32 devices in a mesh: group: 4 (over y, core), fsdp: 8 (over z, x).
Axes of the slice: x: 2, y: 2, z: 4, core: 2. Of those that a mesh axis runs over, the one named last changes fastest.
Arguments:
- tokens: bfloat16 [16384, 768], P(('group', 'fsdp')), may hold values from -6 to 6
- cotangent: bfloat16 [16384, 768], P(('group', 'fsdp')), may hold values from -6 to 6
- parent_seg: int32 [4, 16], P('group'), may hold values from -1 to 15, as said below
- w_qkv: bfloat16 [768, 2304], P(('group', 'fsdp')), may hold values from -0.21875 to 0.21875
- w_out: bfloat16 [768, 768], P(('group', 'fsdp')), may hold values from -3 to 3
- b_out: bfloat16 [768], P(('group', 'fsdp')), may hold values from -4 to 4
- norm1_gain: bfloat16 [768], P(('group', 'fsdp')), may hold values from 0.5 to 1.5
- norm1_bias: bfloat16 [768], P(('group', 'fsdp')), may hold values from -4 to 4
- w_up: bfloat16 [768, 3072], P(('group', 'fsdp')), may hold values from -0.21875 to 0.21875
- b_up: bfloat16 [3072], P(('group', 'fsdp')), may hold values from -4 to 4
- w_down: bfloat16 [3072, 768], P(('group', 'fsdp')), may hold values from -0.109375 to 0.109375
- b_down: bfloat16 [768], P(('group', 'fsdp')), may hold values from -4 to 4
- norm2_gain: bfloat16 [768], P(('group', 'fsdp')), may hold values from 0.5 to 1.5
- norm2_bias: bfloat16 [768], P(('group', 'fsdp')), may hold values from -4 to 4
Outputs:
- output: bfloat16 [16384, 768], P(('group', 'fsdp'))
- tokens_grad: float32 [16384, 768], P(('group', 'fsdp'))
- w_qkv_grad: float32 [768, 2304], P('fsdp')
- w_out_grad: float32 [768, 768], P('fsdp')
- b_out_grad: float32 [768], P('fsdp')
- norm1_gain_grad: float32 [768], P('fsdp')
- norm1_bias_grad: float32 [768], P('fsdp')
- w_up_grad: float32 [768, 3072], P('fsdp')
- b_up_grad: float32 [3072], P('fsdp')
- w_down_grad: float32 [3072, 768], P('fsdp')
- b_down_grad: float32 [768], P('fsdp')
- norm2_gain_grad: float32 [768], P('fsdp')
- norm2_bias_grad: float32 [768], P('fsdp')
The draws below stay inside these ranges and needn't reach their ends.
Inputs may be any that keep to these rules, and one draw needn't show every extreme that they name: parent_seg[g, p] is the position within group row g of the segment whose end state seeds segment p, or -1 for a root. Each row is a forest of trees of 20 segments placed in random positions: a trunk chain of 8, four branches off the trunk's last segment, and two leaves on each branch; where 16 is not a multiple of 20, the row's last tree keeps only its first segments. Following parents reaches a root after at most 9 steps, which some segment of every row needs.
All inputs are finite; a program needn't handle non-finite values.
Results may differ from the reference program's by a relative error of at most 0.018.
Values may be sent and summed in bfloat16 or wider, within the bound.
No kernel may reach another device: no remote copies, remote signals or barrier semaphores. Data moves between devices by JAX's collectives and lax.ppermute only.
A program may use at most 128 MiB of HBM per device.

```python
import math
import jax
import jax.numpy as jnp
from jax import lax

D = 768
H = 12
HD = 64
FF = 3072
SEG = 256
TREE_DEPTH = 10
HORIZON = 2560
ROW_BLOCKS = 16
GROUPS = 4
TOKENS = 16384
N_GROUP = 4


def draw_parent_seg(key, part):
    canon = jnp.arange(ROW_BLOCKS, dtype=jnp.int32)
    tree_start = canon // 20 * 20
    within = canon % 20
    local_parent = jnp.where(within == 0, -1, jnp.where(within < 8, within - 1, jnp.where(within < 12, 7, 8 + (within - 12) // 2)))
    canon_parent = jnp.where(local_parent < 0, -1, tree_start + local_parent)

    def one_row(row_key):
        placing = jax.random.permutation(row_key, ROW_BLOCKS).astype(jnp.int32)
        last_slot = jnp.argmax((placing == ROW_BLOCKS - 1).astype(jnp.int32)).astype(jnp.int32)
        first_place = placing[0]
        placing = placing.at[last_slot].set(first_place).at[0].set(ROW_BLOCKS - 1)
        moved = jnp.where(canon_parent < 0, -1, placing[jnp.maximum(canon_parent, 0)])
        return jnp.zeros((ROW_BLOCKS,), jnp.int32).at[placing].set(moved)
    row_keys = jax.random.split(jax.random.fold_in(key, 17), GROUPS)
    return jax.vmap(one_row)(row_keys)


def spiked(result, stream_key, source, target, blocks, factor):
    owner, partner = [(jnp.arange(result.shape[axis_at]) // (result.shape[axis_at] // blocks)).reshape([-1 if axis == axis_at else 1 for axis in range(result.ndim)]) for axis_at in (source, target)]
    chosen = jax.random.permutation(stream_key, blocks)[partner]
    strong = (owner == chosen) | (owner == (partner + blocks // 2) % blocks)
    return jnp.where(strong, factor * result, result)


def level_of(key, shape, cuts, least, largest):
    factor_of = 1.0
    for dim, shards_of in cuts:
        draws = jax.random.uniform(jax.random.fold_in(jax.random.fold_in(key, 6), dim), (shards_of,), jnp.float32, least / len(cuts), largest / len(cuts))
        factor_of = factor_of * jnp.repeat(jnp.exp(draws), shape[dim] // shards_of).reshape((-1,) + (1,) * (len(shape) - 1 - dim))
    return factor_of


def gaussian(stream_key, extent, deviation, most, cuts=(), kind=jnp.bfloat16):
    array = deviation * jax.random.normal(stream_key, extent, jnp.float32)
    if cuts:
        array = array * level_of(stream_key, extent, cuts, -0.22, 0.18)
    return jnp.clip(array, -most, most).astype(kind)


def heavy_noise(key, shape, deviation, reach, shards, heavy, held_as=jnp.bfloat16):
    result = deviation * jax.random.normal(key, shape, jnp.float32)
    if shards:
        result = result * level_of(key, shape, shards, -0.22, 0.18)
    return jnp.clip(spiked(result, jax.random.fold_in(key, 3), *heavy), -reach, reach).astype(held_as)


def setup_inputs(seed: int = 0) -> dict:
    splits = jax.random.split(jax.random.key(seed), 15)
    tokens = heavy_noise(splits[0], (TOKENS, D), 1.0, 6.0, ((0, 32),), (0, 1, 32, 2.75))
    cotangent = gaussian(splits[1], (TOKENS, D), 1.0, 6.0, ((0, 32),))
    parent_seg = draw_parent_seg(jax.random.fold_in(splits[14], 71), 0)
    w_qkv = gaussian(splits[3], (D, 3 * D), D ** -0.5, 0.21875, ((0, 32),))
    w_out = gaussian(splits[4], (D, D), 4 ** -0.5, 3.0, ((0, 32),))
    b_out = gaussian(splits[5], (D,), 0.3, 4.0, ((0, 32),))
    norm1_gain = jnp.clip(1.0 + 0.1 * jax.random.normal(splits[6], (D,), jnp.float32), 0.5, 1.5).astype(jnp.bfloat16)
    norm1_bias = gaussian(splits[7], (D,), 0.3, 4.0, ((0, 32),))
    w_up = gaussian(splits[8], (D, FF), D ** -0.5, 0.21875, ((0, 32),))
    b_up = gaussian(splits[9], (FF,), 0.3, 4.0, ((0, 32),))
    w_down = gaussian(splits[10], (FF, D), FF ** -0.5, 0.109375, ((0, 32),))
    b_down = gaussian(splits[11], (D,), 0.3, 4.0, ((0, 32),))
    norm2_gain = jnp.clip(1.0 + 0.1 * jax.random.normal(splits[12], (D,), jnp.float32), 0.5, 1.5).astype(jnp.bfloat16)
    norm2_bias = gaussian(splits[13], (D,), 0.3, 4.0, ((0, 32),))
    return dict(tokens=tokens, cotangent=cotangent, parent_seg=parent_seg, w_qkv=w_qkv, w_out=w_out, b_out=b_out, norm1_gain=norm1_gain, norm1_bias=norm1_bias, w_up=w_up, b_up=b_up, w_down=w_down, b_down=b_down, norm2_gain=norm2_gain, norm2_bias=norm2_bias)


ln_epsilon = 1e-05
highest = lax.Precision.HIGHEST

@jax.custom_vjp
def low(v):
    return lax.optimization_barrier(v.astype(jnp.bfloat16)).astype(jnp.float32)

@jax.custom_vjp
def low_back(v):
    return v

def low_keep(v):
    return (low(v), None)

def low_pass(kept, grad):
    return (grad,)

def back_keep(v):
    return (v, None)

def back_low(kept, grad):
    return (low(grad),)
low.defvjp(low_keep, low_pass)
low_back.defvjp(back_keep, back_low)

def path_matrix(parent_seg):
    columns = jnp.arange(ROW_BLOCKS, dtype=jnp.int32)
    step_one = (parent_seg[:, :, None] == columns[None, None, :]).astype(jnp.float32)
    current = step_one
    reached = step_one
    for depth_step in range(TREE_DEPTH - 1):
        current = jnp.einsum('grc,gcd->grd', current, step_one, precision=highest)
        reached = reached + current
    return reached

def layer_norm(resid, gain, shift):
    centred = resid - lax.optimization_barrier(jnp.mean(resid, axis=-1, keepdims=True))
    inv_std = lax.rsqrt(lax.optimization_barrier(jnp.mean(centred * centred, axis=-1, keepdims=True)) + ln_epsilon)
    return centred * inv_std * gain + shift

def block_attend(pieces):
    query_feat, key_feat, value_act, path_state, path_norm = pieces
    positions = jnp.arange(SEG, dtype=jnp.int32)
    causal = positions[:, None] >= positions[None, :]
    scores = jnp.einsum('shf,thf->hst', query_feat, key_feat, precision=highest)
    scores = low_back(jnp.where(causal[None, :, :], scores, 0.0))
    numerator = jnp.einsum('hst,the->she', low(scores), value_act, precision=highest)
    numerator = numerator + jnp.einsum('shf,hfe->she', query_feat, low(path_state), precision=highest)
    denominator = lax.optimization_barrier(jnp.sum(scores, axis=-1)).T + jnp.einsum('shf,hf->sh', query_feat, low(path_norm), precision=highest) + 1.0
    numerator = low_back(numerator)
    return numerator / denominator[:, :, None]

def layer_forward(tokens_f, weights, cosine, sine_rows, ancestry):
    w_qkv, w_out, b_out, norm1_gain, norm1_bias, w_up, b_up, w_down, b_down, norm2_gain, norm2_bias = weights
    row_total = tokens_f.shape[0]
    projected = low_back(jnp.dot(tokens_f, w_qkv, precision=highest))
    query_act = jax.nn.relu(projected[:, :D]).reshape(row_total, H, HD)
    key_act = jax.nn.relu(projected[:, D:2 * D]).reshape(row_total, H, HD)
    value_act = low(projected[:, 2 * D:]).reshape(row_total, H, HD)
    cos_col = cosine[:, None, None]
    sin_col = sine_rows[:, None, None]
    query_feat = low(jnp.concatenate([query_act * cos_col, query_act * sin_col], axis=-1))
    key_feat = low(jnp.concatenate([key_act * cos_col, key_act * sin_col], axis=-1))
    grid_shape = (N_GROUP, ROW_BLOCKS, SEG, H)
    key_grid = key_feat.reshape(grid_shape + (2 * HD,))
    value_grid = value_act.reshape(grid_shape + (HD,))
    incr_state = low_back(jnp.einsum('grshf,grshe->grhfe', key_grid, value_grid, precision=highest))
    incr_norm = lax.optimization_barrier(jnp.sum(key_grid, axis=2))
    path_state = low_back(jnp.einsum('grc,gchfe->grhfe', ancestry, low(incr_state), precision=highest))
    path_norm = low_back(jnp.einsum('grc,gchf->grhf', ancestry, low(incr_norm), precision=highest))
    block_total = N_GROUP * ROW_BLOCKS
    attended = lax.map(jax.checkpoint(block_attend), (query_feat.reshape(block_total, SEG, H, 2 * HD), key_feat.reshape(block_total, SEG, H, 2 * HD), value_act.reshape(block_total, SEG, H, HD), path_state.reshape(block_total, H, 2 * HD, HD), path_norm.reshape(block_total, H, 2 * HD)))
    attended = attended.reshape(row_total, D)
    mixed_out = low_back(jnp.dot(low(attended), w_out, precision=highest) + b_out)
    normed = layer_norm(tokens_f + mixed_out, norm1_gain, norm1_bias)
    upper_pre = low_back(jnp.dot(low(normed), w_up, precision=highest) + b_up)
    gelu_low = low(jax.nn.gelu(upper_pre, approximate=False))
    lowered = low_back(jnp.dot(gelu_low, w_down, precision=highest) + b_down)
    return layer_norm(normed + lowered, norm2_gain, norm2_bias)

def reference(tokens, cotangent, parent_seg, w_qkv, w_out, b_out, norm1_gain, norm1_bias, w_up, b_up, w_down, b_down, norm2_gain, norm2_bias):
    ancestry = path_matrix(parent_seg)
    depths = lax.optimization_barrier(jnp.sum(ancestry, axis=-1))
    position = depths[:, :, None] * SEG + jnp.arange(SEG, dtype=jnp.float32)[None, None, :]
    angles = (position * (math.pi / (2.0 * HORIZON))).reshape(-1)
    cosine = jnp.cos(angles)
    sine_rows = jnp.sin(angles)
    weights = tuple((weight_arg.astype(jnp.float32) for weight_arg in (w_qkv, w_out, b_out, norm1_gain, norm1_bias, w_up, b_up, w_down, b_down, norm2_gain, norm2_bias)))

    def wrapped(tokens_f, *weights_f):
        return layer_forward(tokens_f, weights_f, cosine, sine_rows, ancestry)
    output, pullback = jax.vjp(wrapped, tokens.astype(jnp.float32), *weights)
    gradients = pullback(cotangent.astype(jnp.float32))
    return (output.astype(jnp.bfloat16), gradients[0], gradients[1], gradients[2], gradients[3], gradients[4], gradients[5], gradients[6], gradients[7], gradients[8], gradients[9], gradients[10], gradients[11])
```

```python
import math

import jax
import jax.numpy as jnp
from jax import lax
from jax.experimental import pallas as pl
from jax.experimental.pallas import tpu as pltpu
from jax.sharding import PartitionSpec as P

D = 768
H = 12
HD = 64
SEG = 256
HORIZON = 2560
PAIRS = H // 2
LANES = 2 * HD
EPS = 1e-05

f32 = jnp.float32
bf16 = jnp.bfloat16

B_OUT, GAIN1, BIAS1, B_DOWN, GAIN2, BIAS2, B_UP = range(7)
OUT_AT = D + LANES


def exchange(x, axis, *bits):
    size, offset = lax.axis_size(axis), sum(1 << b for b in bits)
    return lax.ppermute(x, axis, [(i, i ^ offset) for i in range(size)])


def axis_bits(axis):
    return [(axis, b) for b in range(lax.axis_size(axis).bit_length() - 1)]


def tie(x, *others):
    return lax.optimization_barrier((x,) + others)[0]


def trade(pieces):
    size = lax.axis_size("fsdp")
    far = [pieces[0]]
    for m in range(1, size // 2):
        far.append(lax.ppermute(pieces[m], "fsdp", [(i, i ^ (2 * m)) for i in range(size)]))
    return far, exchange(jnp.concatenate([x[1:] for x in far], axis=0), "fsdp", 0)


def near_steps(first_low):
    low, high = axis_bits("fsdp")[:1], axis_bits("group")[1:]
    return low + high if first_low else high + low


def moved(masks, axis, bit):
    step = (1 << bit) * (lax.axis_size("fsdp") if axis == "group" else 1)
    return tuple(m ^ step for m in masks)


def gather_stages(shard):
    lin = lax.axis_index("group") * lax.axis_size("fsdp") + lax.axis_index("fsdp")
    rows, columns = shard.shape
    if rows % 8:
        whole = lax.all_gather(shard, ("group", "fsdp"), axis=0, tiled=True)
        merged = rows
        while merged % 8:
            merged *= 2
        blocks = whole.reshape(-1, merged, columns)
        yield []
        return [[(blocks, tuple(range(blocks.shape[0])))]], jnp.zeros_like(lin)
    blocks, masks = shard[None], (0,)
    for axis, bit in reversed(axis_bits("fsdp")[1:]):
        (other,) = yield [(blocks, axis, bit)]
        blocks = jnp.concatenate([blocks, other], axis=0)
        masks = masks + moved(masks, axis, bit)
    half = columns // 2
    sides = [(blocks[:, :, :half], masks), (blocks[:, :, half:], masks)]
    steps = [near_steps(True), near_steps(False)]
    for n in range(len(steps[0]) - 1):
        others = yield [(b,) + st[n] for (b, _), st in zip(sides, steps)]
        sides = [
            (jnp.concatenate([b, o], axis=0), m + moved(m, *st[n]))
            for (b, m), st, o in zip(sides, steps, others)
        ]
    core = ("group", 0)
    others = yield [(b,) + st[-1] for (b, _), st in zip(sides, steps)] + [
        (b,) + core for b, _ in sides
    ]
    parts = []
    for (b, m), st, o, c in zip(sides, steps, others, others[2:]):
        parts.append([(b, m), (o, moved(m, *st[-1])), (c, moved(m, *core))])
    lasts = yield [(part[1][0],) + core for part in parts]
    for part, last in zip(parts, lasts):
        part.append((last, moved(part[1][1], *core)))
    return parts, lin


class Pipeline:
    def __init__(self):
        self.running = {}
        self.finished = {}
        self.started = ()

    def add(self, name, stages):
        self.running[name] = (stages, None)

    def slot(self, *others, only=None):
        names = [n for n in self.running if only is None or n in only]
        arrived = [x for n in names for x in self.running[n][1] or ()]
        if arrived:
            arrived = lax.optimization_barrier(tuple(arrived) + others)[: len(arrived)]
        at, requests = 0, []
        for n in names:
            stages, results = self.running.pop(n)
            count = len(results or ())
            mine, at = arrived[at : at + count], at + count
            try:
                wanted = next(stages) if results is None else stages.send(mine)
            except StopIteration as done:
                self.finished[n] = done.value
            else:
                self.running[n] = (stages, ())
                requests += [(n, w) for w in wanted]
        operands = tuple(w[0] for _, w in requests)
        if operands and others:
            operands = lax.optimization_barrier(operands + others)[: len(operands)]
        self.started = operands
        for x, (n, (_, axis, *bits)) in zip(operands, requests):
            stages, results = self.running[n]
            self.running[n] = (stages, results + (exchange(x, axis, *bits),))

    def finish(self, name, *others, only=None):
        while name not in self.finished:
            self.slot(*others, only=only)
        return self.finished[name]


VMEM = pl.BlockSpec(memory_space=pltpu.VMEM)
SMEM = pl.BlockSpec(memory_space=pltpu.SMEM)


COSTS = {
    "assemble": 1.5, "project": 5.4, "mix_segments": 1.1, "intra_forward": 5.9, "inter_forward": 5.5,
    "expand": 9.5, "contract": 10.5, "back_to_heads": 11.8, "intra_backward": 10.3,
    "inter_backward": 4.6, "input_grad": 4.0, "weight_grad": 4.0,
}
FLOPS_PER_US = 1.4e9


def call(kernel, name, outs, in_specs, scratch=(), mib=12):
    return pl.pallas_call(
        kernel,
        out_shape=outs,
        in_specs=in_specs,
        out_specs=jax.tree.map(lambda _: VMEM, outs),
        scratch_shapes=scratch,
        compiler_params=pltpu.CompilerParams(vmem_limit_bytes=mib * 1024 * 1024),
        cost_estimate=pl.CostEstimate(
            flops=int(COSTS[name] * FLOPS_PER_US), transcendentals=0, bytes_accessed=0
        ),
        name=name,
    )


def shape_of(shape, dtype):
    return jax.ShapeDtypeStruct(shape, dtype)


def dot(a, b):
    return lax.dot_general(a, b, (((1,), (0,)), ((), ())), preferred_element_type=f32)


def dot_nt(a, b):
    return lax.dot_general(a, b, (((1,), (1,)), ((), ())), preferred_element_type=f32)


def dot_tn(a, b):
    return lax.dot_general(a, b, (((0,), (0,)), ((), ())), preferred_element_type=f32)


def loop(count, body):
    def step(i, carry):
        body(i)
        return carry

    lax.fori_loop(0, count, step, 0)


def rows_at(i):
    return pl.ds(pl.multiple_of(i * SEG, SEG), SEG)


def lanes_at(p):
    return pl.ds(pl.multiple_of(p * LANES, LANES), LANES)


def head_masks(rows):
    lane = lax.broadcasted_iota(jnp.int32, (rows, LANES), 1)
    first = (lane < HD).astype(f32)
    return first.astype(bf16), (1.0 - first).astype(bf16)


def diagonal():
    row = lax.broadcasted_iota(jnp.int32, (LANES, LANES), 0)
    lane = lax.broadcasted_iota(jnp.int32, (LANES, LANES), 1)
    return (row < HD) == (lane < HD)


def head_ones():
    return jnp.where(diagonal(), 1.0, 0.0).astype(bf16)


def split_state(packed):
    same = diagonal()
    cos_part = jnp.where(same, packed, 0.0)
    sin_part = pltpu.roll(jnp.where(same, 0.0, packed), HD, 1)
    return cos_part.astype(bf16), sin_part.astype(bf16)


def state_scratch(fsdp):
    return [pltpu.VMEM((D, LANES), f32), pltpu.VMEM((8 * max(2 * PAIRS, fsdp), LANES), f32)]


def piece_shapes(fsdp, segs):
    return (shape_of((2, segs, D // fsdp + 8, LANES), bf16),) * (fsdp // 2)


def norm_row(n, fsdp):
    per = max(16, fsdp) // fsdp
    return 8 * (n // per) + n % per


def store_states(s, own, left_ref, right_ref, weight_ref, cos_ref, sin_ref, state_scr, norm_scr, out_refs):
    fsdp = 2 * len(out_refs)
    chunk = D // fsdp
    same = diagonal()
    rows = rows_at(s)
    cos, sin = cos_ref[rows, :], sin_ref[rows, :]

    def pair(p):
        lanes = lanes_at(p)
        a = left_ref[rows, lanes]
        b = right_ref[rows, lanes].astype(f32)
        both = jnp.concatenate(
            [(b * cos).astype(bf16), (pltpu.roll(b, HD, 1) * sin).astype(bf16)], axis=1
        )
        product = dot_tn(a, both)
        state_scr[lanes, :] = jnp.where(same, product[:, :LANES], product[:, LANES:])
        wide = a.astype(f32)
        if weight_ref is not None:
            wide = wide * weight_ref[rows, lanes]
        for n, wave in ((p, cos), (PAIRS + p, sin)):
            norm_scr[pl.ds(norm_row(n, fsdp), 1), :] = jnp.sum(wide * wave, axis=0, keepdims=True)

    loop(PAIRS, pair)
    for r in range(fsdp):
        j = own ^ r
        at = pl.ds(pl.multiple_of(chunk * j, 8), chunk)
        norms = pl.ds(pl.multiple_of(8 * j, 8), 8)
        out_refs[r // 2][r % 2, s, 0:chunk, :] = state_scr[at, :].astype(bf16)
        out_refs[r // 2][r % 2, s, chunk : chunk + 8, :] = norm_scr[norms, :].astype(bf16)


def load_states(s, own, far_refs, near_ref, state_scr, norm_scr):
    fsdp = 2 * len(far_refs)
    chunk = D // fsdp
    for r in range(fsdp):
        j = own ^ r
        at = pl.ds(pl.multiple_of(chunk * j, 8), chunk)
        norms = pl.ds(pl.multiple_of(8 * j, 8), 8)
        ref, place = (near_ref, r // 2) if r % 2 else (far_refs[r // 2], 0)
        state_scr[at, :] = ref[place, s, 0:chunk, :].astype(f32)
        norm_scr[norms, :] = ref[place, s, chunk : chunk + 8, :].astype(f32)


def pair_state(p, state_scr, norm_scr, fsdp):
    cos_part, sin_part = split_state(state_scr[lanes_at(p), :])
    norm_cos = norm_scr[pl.ds(norm_row(p, fsdp), 1), :]
    norm_sin = norm_scr[pl.ds(norm_row(PAIRS + p, fsdp), 1), :]
    return cos_part, sin_part, norm_cos, norm_sin


def assemble(parts, lin):
    arrays = [blocks for part in parts for blocks, _ in part]
    places = jnp.concatenate(
        [jnp.array(masks, jnp.int32) for part in parts for _, masks in part]
    ) ^ lin.astype(jnp.int32)
    rows = arrays[0].shape[1]
    count = sum(len(masks) for _, masks in parts[0])
    width = sum(part[0][0].shape[2] for part in parts)
    lefts, left = [], 0
    for part in parts:
        lefts += [left] * len(part)
        left += part[0][0].shape[2]

    def kernel(places_ref, *refs):
        out_ref = refs[-1]
        first = 0
        for ref, at in zip(refs[:-1], lefts):
            number, _, columns = ref.shape

            def place(i, ref=ref, at=at, columns=columns, first=first):
                out_ref[places_ref[first + i], :, at : at + columns] = ref[i]

            loop(number, place)
            first += number

    whole = call(
        kernel, "assemble", shape_of((count, rows, width), bf16), [SMEM] + [VMEM] * len(arrays)
    )(places, *arrays)
    return whole.reshape(count * rows, width)


def project(ids, tokens, w_kv, cos, sin, fsdp):
    rows = tokens.shape[0]
    segs = rows // SEG

    def kernel(ids_ref, tok_ref, w_ref, cos_ref, sin_ref, k_ref, v_ref, *refs):
        inc_refs, (state_scr, norm_scr) = refs[:-2], refs[-2:]
        norm_scr[...] = jnp.zeros_like(norm_scr)

        def segment(s):
            at = rows_at(s)
            x = tok_ref[at, :]
            k_ref[at, :] = jnp.maximum(dot(x, w_ref[:, :D]), 0.0).astype(bf16)
            v_ref[at, :] = dot(x, w_ref[:, D:]).astype(bf16)
            store_states(s, ids_ref[2], k_ref, v_ref, None, cos_ref, sin_ref, state_scr, norm_scr,
                         inc_refs)

        loop(segs, segment)

    act = shape_of((rows, D), bf16)
    k, v, *pieces = call(
        kernel,
        "project",
        (act, act) + piece_shapes(fsdp, segs),
        [SMEM] + [VMEM] * 4,
        state_scratch(fsdp),
    )(ids, tokens, w_kv, cos, sin)
    return k, v, pieces


def mix_segments(spread, far, near):
    fsdp = 2 * len(far)
    _, segs, height, _ = near.shape

    def kernel(spread_ref, *refs):
        far_refs, near_ref, out_refs = refs[: fsdp // 2], refs[fsdp // 2], refs[fsdp // 2 + 1 :]
        for t in range(height // 8):
            at = slice(8 * t, 8 * t + 8)
            stacked = []
            for r in range(fsdp):
                ref, place = (near_ref, r // 2) if r % 2 else (far_refs[r // 2], 0)
                stacked += [ref[place, s, at, :].astype(f32) for s in range(segs)]
            mixed = dot(spread_ref[...], jnp.concatenate(stacked, axis=0).astype(bf16))
            for c in range(fsdp * segs):
                r, s = c // segs, c % segs
                out_refs[r // 2][r % 2, s, at, :] = mixed[8 * c : 8 * c + 8, :].astype(bf16)

    return call(
        kernel, "mix_segments", piece_shapes(fsdp, segs), [VMEM] * (fsdp // 2 + 2)
    )(spread, *far, near)


def intra_forward(tokens, w_q, k, v, wave):
    rows = tokens.shape[0]

    def kernel(tok_ref, w_ref, k_ref, v_ref, wave_ref, q_ref, num_ref, den_ref):
        masks = head_masks(SEG)

        def segment(s):
            at = rows_at(s)
            q_ref[at, :] = jnp.maximum(dot(tok_ref[at, :], w_ref[:, :D]), 0.0).astype(bf16)

            def pair(p):
                lanes = lanes_at(p)
                qs, ks, vs = q_ref[at, lanes], k_ref[at, lanes], v_ref[at, lanes]
                weights, values = [], []
                for m in masks:
                    weights.append((dot_nt(qs, ks * m) * wave_ref[...]).astype(bf16))
                    values.append(jnp.concatenate([vs * m, m], axis=1))
                both = dot(jnp.concatenate(weights, axis=1), jnp.concatenate(values, axis=0))
                num_ref[at, lanes] = both[:, :LANES]
                den_ref[at, lanes] = both[:, LANES:]

            loop(PAIRS, pair)

        loop(rows // SEG, segment)

    wide = shape_of((rows, D), f32)
    return call(
        kernel, "intra_forward", (shape_of((rows, D), bf16), wide, wide), [VMEM] * 5
    )(tokens, w_q, k, v, wave)


def inter_forward(ids, q, num, den, cos, sin, far, near):
    rows = q.shape[0]
    fsdp = 2 * len(far)

    def kernel(ids_ref, q_ref, num_ref, den_ref, cos_ref, sin_ref, *refs):
        far_refs, near_ref = refs[: fsdp // 2], refs[fsdp // 2]
        att_ref, rden_ref, state_scr, norm_scr = refs[fsdp // 2 + 1 :]
        ones = head_ones()
        twice = jnp.concatenate([ones, ones], axis=0)

        def segment(s):
            at = rows_at(s)
            load_states(s, ids_ref[2], far_refs, near_ref, state_scr, norm_scr)

            def pair(p):
                lanes = lanes_at(p)
                cos_part, sin_part, norm_cos, norm_sin = pair_state(p, state_scr, norm_scr, fsdp)
                qs = q_ref[at, lanes].astype(f32)
                q_cos = (qs * cos_ref[at, :]).astype(bf16)
                q_sin = (qs * sin_ref[at, :]).astype(bf16)
                carried = dot(
                    jnp.concatenate([q_cos, q_sin], axis=1),
                    jnp.concatenate([cos_part, sin_part], axis=0),
                )
                along = q_cos.astype(f32) * norm_cos + q_sin.astype(f32) * norm_sin
                high = along.astype(bf16)
                rest = (along - high.astype(f32)).astype(bf16)
                weight = dot(jnp.concatenate([high, rest], axis=1), twice)
                inverse = 1.0 / (den_ref[at, lanes] + weight + 1.0)
                att_ref[at, lanes] = ((num_ref[at, lanes] + carried) * inverse).astype(bf16)
                rden_ref[at, lanes] = inverse

            loop(PAIRS, pair)

        loop(rows // SEG, segment)

    return call(
        kernel,
        "inter_forward",
        (shape_of((rows, D), bf16), shape_of((rows, D), f32)),
        [SMEM] + [VMEM] * (6 + fsdp // 2),
        state_scratch(fsdp),
    )(ids, q, num, den, cos, sin, *far, near)


def standardize(resid):
    centred = resid - jnp.mean(resid, axis=1, keepdims=True)
    inv = lax.rsqrt(jnp.mean(centred * centred, axis=1, keepdims=True) + EPS)
    return centred * inv, inv


def standardize_back(d_hat, hat, inv):
    return inv * (
        d_hat
        - jnp.mean(d_hat, axis=1, keepdims=True)
        - hat * jnp.mean(d_hat * hat, axis=1, keepdims=True)
    )


def expand(att, tokens, w_out, w_up, small):
    rows = att.shape[0]
    ff = w_up.shape[1]

    def kernel(att_ref, tok_ref, out_w_ref, up_ref, small_ref, hat_ref, inv_ref, low_ref, gelu_ref,
               slope_ref):
        def block(i):
            at = rows_at(i)
            mixed = dot(att_ref[at, :], out_w_ref[:, OUT_AT : OUT_AT + D])
            hat, inv = standardize(
                tok_ref[at, :].astype(f32) + mixed + small_ref[B_OUT : B_OUT + 1, :]
            )
            hat_ref[at, :] = hat
            inv_ref[at, :] = jnp.broadcast_to(inv, (SEG, LANES))
            low_ref[at, :] = (
                hat * small_ref[GAIN1 : GAIN1 + 1, :] + small_ref[BIAS1 : BIAS1 + 1, :]
            ).astype(bf16)

            def part(m):
                for c in range(3):
                    columns = pl.ds(pl.multiple_of(m * D + 256 * c, 256), 256)
                    bias = small_ref[pl.ds(B_UP + m, 1), 256 * c : 256 * (c + 1)]
                    upper = dot(low_ref[at, :], up_ref[:, columns]) + bias
                    cdf = 0.5 + 0.5 * lax.erf(upper * math.sqrt(0.5))
                    pdf = jnp.exp(-0.5 * upper * upper) * (1.0 / math.sqrt(2.0 * math.pi))
                    gelu_ref[at, columns] = (upper * cdf).astype(bf16)
                    slope_ref[at, columns] = (cdf + upper * pdf).astype(bf16)

            loop(ff // D, part)

        loop(rows // SEG, block)

    return call(
        kernel,
        "expand",
        (
            shape_of((rows, D), f32),
            shape_of((rows, LANES), f32),
            shape_of((rows, D), bf16),
            shape_of((rows, ff), bf16),
            shape_of((rows, ff), bf16),
        ),
        [VMEM] * 5,
    )(att, tokens, w_out, w_up, small)


def contract(ids, gelu, slope, hat1, cotangent, w_down, small):
    rows, ff = gelu.shape

    def kernel(ids_ref, gelu_ref, slope_ref, hat1_ref, cot_ref, w_ref, small_ref,
               out_ref, dres_ref, dlow_ref, dup_ref, dlow_half_ref, dup_half_ref, sums_ref):
        sums_ref[...] = jnp.zeros_like(sums_ref)

        def block(i):
            at = rows_at(i)
            normed = hat1_ref[at, :] * small_ref[GAIN1 : GAIN1 + 1, :]
            normed += small_ref[BIAS1 : BIAS1 + 1, :]
            resid = normed + dot(gelu_ref[at, :], w_ref[...]) + small_ref[B_DOWN : B_DOWN + 1, :]
            hat, inv = standardize(resid)
            gain = small_ref[GAIN2 : GAIN2 + 1, :]
            out_ref[at, :] = (hat * gain + small_ref[BIAS2 : BIAS2 + 1, :]).astype(bf16)
            cot = cot_ref[at, :].astype(f32)
            sums_ref[GAIN2 : GAIN2 + 1, :] += jnp.sum(cot * hat, axis=0, keepdims=True)
            sums_ref[BIAS2 : BIAS2 + 1, :] += jnp.sum(cot, axis=0, keepdims=True)
            d_res = standardize_back(cot * gain, hat, inv)
            dres_ref[at, :] = d_res
            d_low = d_res.astype(bf16)
            dlow_ref[at, :] = d_low
            sums_ref[B_DOWN : B_DOWN + 1, :] += jnp.sum(d_low.astype(f32), axis=0, keepdims=True)

            def part(m):
                for c in range(3):
                    columns = pl.ds(pl.multiple_of(m * D + 256 * c, 256), 256)
                    d_up = dot_nt(dlow_ref[at, :], w_ref[columns, :])
                    d_up = (d_up * slope_ref[at, columns].astype(f32)).astype(bf16)
                    dup_ref[at, columns] = d_up
                    sums_ref[pl.ds(B_UP + m, 1), 256 * c : 256 * (c + 1)] += jnp.sum(
                        d_up.astype(f32), axis=0, keepdims=True
                    )

            loop(ff // D, part)
            theirs = 1 - ids_ref[0]
            dlow_half_ref[at, :] = dlow_ref[
                at, pl.ds(pl.multiple_of(theirs * (D // 2), 128), D // 2)
            ]
            dup_half_ref[at, :] = dup_ref[
                at, pl.ds(pl.multiple_of(theirs * (ff // 2), 128), ff // 2)
            ]

        loop(rows // SEG, block)

    return call(
        kernel,
        "contract",
        (
            shape_of((rows, D), bf16),
            shape_of((rows, D), f32),
            shape_of((rows, D), bf16),
            shape_of((rows, ff), bf16),
            shape_of((rows, D // 2), bf16),
            shape_of((rows, ff // 2), bf16),
            shape_of((16, D), f32),
        ),
        [SMEM] + [VMEM] * 6,
    )(ids, gelu, slope, hat1, cotangent, w_down, small)


def back_to_heads(ids, d_upper, d_res2, hat1, inv1, rden, att, q, cos, sin, w_out, w_up, small,
                  sums, fsdp):
    rows, ff = d_upper.shape
    segs = rows // SEG

    def kernel(ids_ref, dup_ref, dres_ref, hat_ref, inv_ref, rden_ref, att_ref, q_ref, cos_ref,
               sin_ref, out_w_ref, up_ref, small_ref, sums_in_ref,
               dres1_ref, dmix_ref, dmix_half_ref, dnum_ref, dden_ref, sums_ref, *refs):
        inc_refs, (state_scr, norm_scr) = refs[:-2], refs[-2:]
        sums_ref[...] = sums_in_ref[...]
        norm_scr[...] = jnp.zeros_like(norm_scr)
        ones = head_ones()
        twice = jnp.concatenate([ones, ones], axis=0)

        def block(i):
            at = rows_at(i)
            d_normed = dres_ref[at, :] + dot_nt(dup_ref[at, :], up_ref[...])
            hat = hat_ref[at, :]
            sums_ref[GAIN1 : GAIN1 + 1, :] += jnp.sum(d_normed * hat, axis=0, keepdims=True)
            sums_ref[BIAS1 : BIAS1 + 1, :] += jnp.sum(d_normed, axis=0, keepdims=True)
            d_res = standardize_back(
                d_normed * small_ref[GAIN1 : GAIN1 + 1, :], hat, inv_ref[at, 0:1]
            )
            dres1_ref[at, :] = d_res
            d_mix = d_res.astype(bf16)
            dmix_ref[at, :] = d_mix
            sums_ref[B_OUT : B_OUT + 1, :] += jnp.sum(d_mix.astype(f32), axis=0, keepdims=True)
            d_att = dot_nt(d_mix, out_w_ref[:, OUT_AT : OUT_AT + D])
            inverse = rden_ref[at, :]
            dnum_ref[at, :] = (d_att * inverse).astype(bf16)
            along = d_att * att_ref[at, :].astype(f32)
            for p in range(PAIRS):
                lanes = slice(LANES * p, LANES * (p + 1))
                high = along[:, lanes].astype(bf16)
                rest = (along[:, lanes] - high.astype(f32)).astype(bf16)
                total = dot(jnp.concatenate([high, rest], axis=1), twice)
                dden_ref[at, lanes] = -total * inverse[:, lanes]
            theirs = 1 - ids_ref[0]
            dmix_half_ref[at, :] = dmix_ref[
                at, pl.ds(pl.multiple_of(theirs * (D // 2), 128), D // 2)
            ]
            store_states(i, ids_ref[2], q_ref, dnum_ref, dden_ref, cos_ref, sin_ref, state_scr,
                         norm_scr, inc_refs)

        loop(segs, block)

    return call(
        kernel,
        "back_to_heads",
        (
            shape_of((rows, D), f32),
            shape_of((rows, D), bf16),
            shape_of((rows, D // 2), bf16),
            shape_of((rows, D), bf16),
            shape_of((rows, D), f32),
            shape_of((16, D), f32),
        )
        + piece_shapes(fsdp, segs),
        [SMEM] + [VMEM] * 13,
        state_scratch(fsdp),
    )(ids, d_upper, d_res2, hat1, inv1, rden, att, q, cos, sin, w_out, w_up, small, sums)


def intra_backward(ids, q, k, v, d_num, d_den, cos, sin, wave, wave_t, far, near):
    rows = q.shape[0]
    fsdp = 2 * len(far)

    def kernel(ids_ref, q_ref, k_ref, v_ref, dnum_ref, dden_ref, cos_ref, sin_ref, wave_ref,
               wave_t_ref, *refs):
        far_refs, near_ref = refs[: fsdp // 2], refs[fsdp // 2]
        dq_ref, dq_half_ref, dk_ref, dv_ref, state_scr, norm_scr = refs[fsdp // 2 + 1 :]
        masks = head_masks(SEG)
        lane = lax.broadcasted_iota(jnp.int32, (SEG, LANES), 1) % HD
        picks = [jnp.where(lane < 2, m.astype(f32), 0.0).astype(bf16) for m in masks]

        def segment(s):
            at = rows_at(s)
            load_states(s, ids_ref[2], far_refs, near_ref, state_scr, norm_scr)
            cosine, sine = cos_ref[at, :], sin_ref[at, :]

            def pair(p):
                lanes = lanes_at(p)
                qs, ks, vs = q_ref[at, lanes], k_ref[at, lanes], v_ref[at, lanes]
                dn, dd = dnum_ref[at, lanes], dden_ref[at, lanes]
                high = dd.astype(bf16).astype(f32)
                spread = jnp.where(lane == 0, high, jnp.where(lane == 1, dd - high, 0.0))
                grads = jnp.concatenate([dn, spread.astype(bf16)], axis=1)
                w_ts, d_ss, d_ts, khs, qhs, dns = [], [], [], [], [], []
                for m, pick in zip(masks, picks):
                    kh = ks * m
                    values = jnp.concatenate([vs * m, pick], axis=1)
                    w_ts.append((dot_nt(kh, qs) * wave_t_ref[...]).astype(bf16))
                    d_ss.append((dot_nt(grads, values) * wave_ref[...]).astype(bf16))
                    d_ts.append((dot_nt(values, grads) * wave_t_ref[...]).astype(bf16))
                    khs.append(kh)
                    qhs.append(qs * m)
                    dns.append(dn * m)

                def both(left, right):
                    return dot(jnp.concatenate(left, axis=1), jnp.concatenate(right, axis=0))

                dk_ref[at, lanes] = both(d_ts, qhs)
                dv_ref[at, lanes] = both(w_ts, dns)
                d_q = both(d_ss, khs)
                cos_part, sin_part, norm_cos, norm_sin = pair_state(p, state_scr, norm_scr, fsdp)
                d_q += cosine * (dot_nt(dn, cos_part) + dd * norm_cos)
                d_q += sine * (dot_nt(dn, sin_part) + dd * norm_sin)
                dq_ref[at, lanes] = jnp.where(qs.astype(f32) > 0.0, d_q, 0.0).astype(bf16)

            loop(PAIRS, pair)
            theirs = 1 - ids_ref[0]
            dq_half_ref[at, :] = dq_ref[at, pl.ds(pl.multiple_of(theirs * (D // 2), 128), D // 2)]

        loop(rows // SEG, segment)

    return call(
        kernel,
        "intra_backward",
        (
            shape_of((rows, D), bf16),
            shape_of((rows, D // 2), bf16),
            shape_of((rows, D), f32),
            shape_of((rows, D), f32),
        ),
        [SMEM] + [VMEM] * (10 + fsdp // 2),
        state_scratch(fsdp),
    )(ids, q, k, v, d_num, d_den, cos, sin, wave, wave_t, *far, near)


def inter_backward(ids, k, v, d_k, d_v, cos, sin, far, near):
    rows = k.shape[0]
    fsdp = 2 * len(far)

    def kernel(ids_ref, k_ref, v_ref, dk_ref, dv_ref, cos_ref, sin_ref, *refs):
        far_refs, near_ref = refs[: fsdp // 2], refs[fsdp // 2]
        out_ref, state_scr, norm_scr = refs[fsdp // 2 + 1 :]
        core = ids_ref[0]

        def segment(s):
            at = rows_at(s)
            load_states(s, ids_ref[2], far_refs, near_ref, state_scr, norm_scr)
            cosine, sine = cos_ref[at, :], sin_ref[at, :]

            def pair(p):
                lanes = lanes_at(p)
                cos_part, sin_part, norm_cos, norm_sin = pair_state(p, state_scr, norm_scr, fsdp)
                ks = k_ref[at, lanes].astype(f32)
                vs = v_ref[at, lanes]
                d_k = dk_ref[at, lanes]
                d_k += cosine * (dot_nt(vs, cos_part) + norm_cos)
                d_k += sine * (dot_nt(vs, sin_part) + norm_sin)
                feats = jnp.concatenate(
                    [(ks * cosine).astype(bf16), (ks * sine).astype(bf16)], axis=1
                )
                d_v = dv_ref[at, lanes]
                d_v += dot(feats, jnp.concatenate([cos_part, sin_part], axis=0))
                out_ref[core, at, lanes] = jnp.where(ks > 0.0, d_k, 0.0).astype(bf16)
                out_ref[1 - core, at, lanes] = d_v.astype(bf16)

            loop(PAIRS, pair)

        loop(rows // SEG, segment)

    return call(
        kernel,
        "inter_backward",
        shape_of((2, rows, D), bf16),
        [SMEM] + [VMEM] * (7 + fsdp // 2),
        state_scratch(fsdp),
    )(ids, k, v, d_k, d_v, cos, sin, *far, near)


def input_grad(ids, d_q, d_kv, d_res1, w_q, w_kv):
    rows = d_q.shape[0]

    def kernel(ids_ref, dq_ref, dkv_ref, dres_ref, w_q_ref, w_kv_ref, out_ref):
        core = ids_ref[0]

        def block(i):
            at = rows_at(i)
            total = dres_ref[at, :] + dot_nt(dq_ref[at, :], w_q_ref[:, :D])
            total += dot_nt(dkv_ref[core, at, :], w_kv_ref[:, :D])
            total += dot_nt(dkv_ref[1 - core, at, :], w_kv_ref[:, D:])
            out_ref[at, :] = total

        loop(rows // SEG, block)

    return call(
        kernel, "input_grad", shape_of((rows, D), f32), [SMEM] + [VMEM] * 5
    )(ids, d_q, d_kv, d_res1, w_q, w_kv)


def reversed_bits(index, bits):
    total = 0
    for b in range(bits):
        total = total + (((index >> b) & 1) << (bits - 1 - b))
    return total


def weight_grad(ids, products, fsdp, splits, own_half=True, sums=None):
    height = products[0][0].shape[1]
    widths = [product[3].shape[1] for product in products]
    block = height // fsdp
    bits = fsdp.bit_length() - 1
    share = block // len(splits)
    group = block if block % 128 == 0 else height
    extra = [] if sums is None else [sums]

    def kernel(ids_ref, *refs):
        ins, out_refs = refs[: 4 * len(products)], refs[4 * len(products) + len(extra) :]

        def part(i):
            columns = pl.ds(pl.multiple_of(i * group, 128), group)

            def store(total, left):
                right = left + total.shape[1]
                for j in range(group // block):
                    place = reversed_bits((i * (group // block) + j) ^ ids_ref[2], bits)
                    for n, (split, out_ref) in enumerate(zip(splits, out_refs)):
                        strip = share // split
                        for h in range(split):
                            row = block * j + share * n + strip * h
                            half = h ^ ids_ref[1] if split > 1 else 0
                            out_ref[half, place, :, left:right] = total[
                                row : row + strip, :
                            ].astype(bf16)

            left = 0
            for n, width in enumerate(widths):
                a0_ref, a1_ref, b0_ref, b1_ref = ins[4 * n : 4 * n + 4]
                first = pl.multiple_of(ids_ref[0] * width, 128) if own_half else 0
                total = dot_tn(a0_ref[:, columns], b0_ref[:, pl.ds(first, width)])
                store(total + dot_tn(a1_ref[:, columns], b1_ref[...]), left)
                left += width
            if extra:
                tall = jnp.concatenate(
                    [refs[4 * len(products)][...], jnp.zeros((LANES - 16, height), f32)], axis=0
                )
                store(tall.T, left)

        loop(height // group, part)

    width = sum(widths) + LANES * len(extra)
    return call(
        kernel,
        "weight_grad",
        tuple(shape_of((n, fsdp, share // n, width), bf16) for n in splits),
        [SMEM] + [VMEM] * (4 * len(products) + len(extra)),
    )(ids, *(x for product in products for x in product), *extra)


def add_low(a, b):
    return (a.astype(f32) + b.astype(f32)).astype(bf16)


def halving_stages(keep, send):
    for axis, bit in axis_bits("fsdp"):
        (received,) = yield [(send, axis, bit)]
        half = keep.shape[0] // 2
        if half == 0:
            return add_low(keep[0], received[0])
        keep, send = add_low(keep[:half], received[:half]), add_low(keep[half:], received[half:])


def reduce_stages(x, core):
    half = x.shape[1] // 2
    x = yield from halving_stages(x[0, :half], x[0, half:])
    bits = axis_bits("group")[1:]
    for axis, bit in bits[:-1]:
        (received,) = yield [(x, axis, bit)]
        x = add_low(x, received)
    if not bits:
        return (yield from core_stages(x, core))
    axis, bit = bits[-1]
    above, beside, across = yield [(x, axis, bit), (x, axis, 0), (x, axis, bit, 0)]
    mine = x.astype(f32) + above.astype(f32)
    theirs = beside.astype(f32) + across.astype(f32)
    return ordered(mine, theirs, core == 0, -1)


def share_stages(x, core, chip):
    axis, bit = axis_bits("group")[1]
    half = x.shape[1] // 2
    (received,) = yield [(x[1], axis, bit)]
    keep = add_low(x[0, :half], received[:half])
    x = yield from halving_stages(keep, add_low(x[0, half:], received[half:]))
    above, beside, across = yield [(x, axis, bit), (x, axis, 0), (x, axis, bit, 0)]
    mine = ordered(x, above, chip == 0, 0)
    theirs = ordered(beside, across, chip == 0, 0)
    return ordered(mine, theirs, core == 0, -1).astype(f32)


def ordered(x, other, first, axis):
    return jnp.concatenate([jnp.where(first, x, other), jnp.where(first, other, x)], axis=axis)


def core_stages(x, core):
    (other,) = yield [(x, "group", 0)]
    return ordered(x, other, core == 0, -1).astype(f32)


def ancestor_matrix(parents):
    count = parents.shape[0]
    columns = jnp.arange(count, dtype=jnp.int32)
    step = (parents[:, None] == columns[None, :]).astype(f32)
    same = (columns[:, None] == columns[None, :]).astype(f32)
    reached = step + same
    for _ in range(4):
        reached = (jnp.dot(reached, reached, preferred_element_type=f32) > 0.0).astype(f32)
    return reached - same


def spread_rows(matrix):
    count = matrix.shape[0]
    row = jnp.arange(8 * count, dtype=jnp.int32)
    pick = (row[:, None] // 8 == jnp.arange(count, dtype=jnp.int32)[None, :]).astype(f32)
    wide = jnp.dot(jnp.dot(pick, matrix), pick.T)
    return jnp.where(row[:, None] % 8 == row[None, :] % 8, wide, 0.0).astype(bf16)


def waves(local, segs):
    depth = jnp.sum(local[:segs], axis=1)
    angle = (depth[:, None] * SEG + jnp.arange(SEG, dtype=f32)[None, :]) * (
        math.pi / (2.0 * HORIZON)
    )
    angle = jnp.broadcast_to(angle.reshape(segs * SEG, 1), (segs * SEG, LANES))
    return jnp.cos(angle), jnp.sin(angle)


def gap_wave():
    position = jnp.arange(SEG, dtype=jnp.int32)
    gap = position[:, None] - position[None, :]
    wave = jnp.cos(gap.astype(f32) * (math.pi / (2.0 * HORIZON)))
    return jnp.where(gap >= 0, wave, 0.0), jnp.where(gap <= 0, wave, 0.0)


def vector_columns(vectors, wide):
    rows = vectors[0].shape[0]
    columns = jnp.concatenate([jnp.stack(vectors, axis=1), wide.reshape(-1, rows).T], axis=1)
    return jnp.pad(columns, ((0, 0), (0, LANES - columns.shape[1])))


def vector_rows(columns, rows, longer):
    turned = columns[:, :16].T.astype(f32)
    wide = turned[B_UP : B_UP + longer].reshape(longer, -1, rows)
    wide = jnp.swapaxes(wide, 0, 1).reshape(longer, D)
    return jnp.concatenate([turned[:B_UP], wide, turned[B_UP + longer :]], axis=0)


def wide_by_block(sums, fsdp, longer):
    wide = sums[B_UP : B_UP + longer].reshape(fsdp, longer, D // fsdp)
    wide = jnp.swapaxes(wide, 0, 1).reshape(longer, D)
    return jnp.concatenate([sums[:B_UP], wide, sums[B_UP + longer :]], axis=0)


def body(
    tokens, cotangent, parent_seg, w_qkv, w_out, b_out, norm1_gain, norm1_bias, w_up, b_up,
    w_down, b_down, norm2_gain, norm2_bias,
):
    fsdp = lax.axis_size("fsdp")
    chips = lax.axis_size("group") // 2
    own = lax.axis_index("fsdp")
    group = lax.axis_index("group")
    core, chip = group % 2, group // 2
    rows = tokens.shape[0]
    segs = rows // SEG
    ff = w_up.shape[1]
    ids = jnp.stack([core, chip, own]).astype(jnp.int32)

    ancestry = ancestor_matrix(parent_seg[0])
    count = parent_seg.shape[1]
    place = jnp.arange(count, dtype=jnp.int32)
    there = (own ^ (place // segs)) * segs + place % segs
    select = (there[:, None] == place[None, :]).astype(f32)
    local = jnp.dot(jnp.dot(select, ancestry), select.T)
    from_ancestors, from_descendants = spread_rows(local), spread_rows(local.T)
    cos, sin = waves(local, segs)
    wave, wave_t = gap_wave()

    pipe = Pipeline()
    pipe.add("kv", gather_stages(w_qkv[:, D:]))
    pipe.slot()
    columns = vector_columns(
        (b_out, norm1_gain, norm1_bias, b_down, norm2_gain, norm2_bias), b_up
    )
    pipe.add("qo", gather_stages(jnp.concatenate([w_qkv[:, :D], columns, w_out, columns], axis=1)))
    pipe.add("up", gather_stages(w_up))
    pipe.add("down", gather_stages(w_down))
    pipe.slot(only=("kv",))
    pipe.slot(*pipe.started, only=("qo",))
    pipe.slot(only=("kv",))
    pipe.slot(*pipe.started, only=("qo",))
    pipe.slot(*pipe.started, only=("up",))
    pipe.slot(only=("kv",))
    pipe.slot(*pipe.started, only=("qo",))
    w_kv = assemble(*pipe.finish("kv", only=("kv",)))
    tables = (from_ancestors, from_descendants, wave, wave_t)
    k, v, increments = project(ids, tie(tokens, *tables), w_kv, cos, sin, fsdp)
    far, near = trade(increments)
    pipe.slot(k, only=("qo", "up"))
    pipe.slot(*pipe.started, only=("down",))
    pipe.slot(near, only=("qo",))
    pipe.slot(*pipe.started, only=("up",))
    w_qo = assemble(*pipe.finish("qo", only=("qo",)))
    q, num, den = intra_forward(tokens, w_qo, k, v, wave)
    pipe.slot(q, only=("up", "down"))
    mixed = mix_segments(from_ancestors, far, tie(near, q))
    path = trade(mixed)
    tokens_other = exchange(tie(tokens, q), "group", 0)
    small = vector_rows(tie(w_qo, mixed[0])[:, D:OUT_AT], w_qkv.shape[0], ff // D)
    pipe.slot(path[1], only=("up", "down"))
    att, rden = inter_forward(ids, q, num, den, cos, sin, *path)
    pipe.slot(att, only=("down",))
    att_other = exchange(att, "group", 0)
    w_up_full = assemble(*pipe.finish("up", only=("up",)))
    hat1, inv1, low1, gelu, slope = expand(att, tokens, w_qo, w_up_full, small)
    w_down_full = assemble(*pipe.finish("down", low1, only=("down",)))
    gelu_other = exchange(gelu, "group", 0)
    low1_other = exchange(low1, "group", 0)
    output, d_res2, d_lower, d_upper, d_lower_half, d_upper_half, sums = contract(
        ids, gelu, slope, hat1, cotangent, w_down_full, small
    )
    d_lower_other = exchange(d_lower_half, "group", 0)
    d_upper_other = exchange(d_upper_half, "group", 0)
    d_res1, d_mixed, d_mixed_half, d_num, d_den, sums, *back = back_to_heads(
        ids, d_upper, d_res2, hat1, inv1, rden, att, q, cos, sin, w_qo, w_up_full, small, sums, fsdp
    )
    d_mixed_other = exchange(d_mixed_half, "group", 0)
    far, near = trade(back)
    grads = Pipeline()
    two = chips == 2

    def reduction(part):
        return share_stages(part, core, chip) if two else reduce_stages(part, core)

    split = 2 if two else 1
    (down_part,) = weight_grad(
        ids, [(gelu, gelu_other, tie(d_lower, d_num), d_lower_other)], fsdp, [split]
    )
    grads.add("down", reduction(down_part))
    grads.slot()
    (up_part,) = weight_grad(
        ids, [(low1, low1_other, tie(d_upper, *grads.started), d_upper_other)], fsdp, [1]
    )
    grads.add("up", reduce_stages(up_part, core))
    grads.slot(only=("up",))
    mixed = mix_segments(from_descendants, far, tie(near, *grads.started))
    back = trade(mixed)
    d_q, d_q_half, d_k, d_v = intra_backward(
        ids, tie(q, mixed[0]), k, v, d_num, d_den, cos, sin, wave, wave_t, *path
    )
    d_q_other = exchange(d_q_half, "group", 0)
    grads.slot(d_q)
    (outq_part,) = weight_grad(
        ids,
        [
            (tie(att, *grads.started), att_other, d_mixed, d_mixed_other),
            (tokens, tokens_other, d_q, d_q_other),
        ],
        fsdp, [split], sums=wide_by_block(sums, fsdp, ff // D),
    )
    grads.add("outq", reduction(outq_part))
    grads.slot(only=("outq",))
    d_kv = inter_backward(ids, tie(k, *grads.started), v, d_k, d_v, cos, sin, *back)
    d_kv_other = exchange(d_kv[1], "group", 0)
    grads.slot(d_kv)
    tokens_grad = input_grad(ids, d_q, tie(d_kv, *grads.started), d_res1, w_qo, w_kv)
    kv_parts = weight_grad(
        ids, [(tokens, tokens_other, tie(d_kv[0], tokens_grad), d_kv_other)], fsdp,
        [2, 1] if two else [1], False,
    )
    grads.add("kv0", reduction(kv_parts[0]))
    for part in kv_parts[1:]:
        grads.add("kv1", reduce_stages(part, core))
    while grads.running:
        grads.slot(kv_parts[0])
    done = grads.finished
    kv_grad = jnp.concatenate([done[n] for n in ("kv0", "kv1") if n in done], axis=0)
    ours, others = jnp.split(done["outq"], 2, axis=1)
    half = D // 2
    sums = ours[:, D : D + 16] + others[:, D : D + 16]
    return (
        output,
        tokens_grad,
        jnp.concatenate([ours[:, half:D], others[:, half:D], kv_grad], axis=1),
        jnp.concatenate([ours[:, :half], others[:, :half]], axis=1),
        sums[:, B_OUT],
        sums[:, GAIN1],
        sums[:, BIAS1],
        done["up"],
        sums[:, B_UP : B_UP + ff // D].T.reshape(-1),
        done["down"],
        sums[:, B_DOWN],
        sums[:, GAIN2],
        sums[:, BIAS2],
    )


def solution(mesh):
    both = ("group", "fsdp")
    matrix, vector = P(both, None), P(both)
    in_specs = (
        matrix, matrix, P("group", None), matrix, matrix, vector, vector, vector, matrix, vector,
        matrix, vector, vector, vector,
    )
    rows, line = P("fsdp", None), P("fsdp")
    out_specs = (
        matrix, matrix, rows, rows, line, line, line, rows, line, rows, line, line, line,
    )
    return jax.shard_map(body, mesh=mesh, in_specs=in_specs, out_specs=out_specs, check_vma=False)
```

```python
import math

import jax
import jax.numpy as jnp
from jax import lax
from jax.experimental import pallas as pl
from jax.experimental.pallas import tpu as pltpu
from jax.sharding import PartitionSpec as P

D = 768
H = 12
HD = 64
SEG = 256
HORIZON = 2560
PAIRS = H // 2
LANES = 2 * HD
EPS = 1e-05

f32 = jnp.float32
bf16 = jnp.bfloat16

B_OUT, GAIN1, BIAS1, B_DOWN, GAIN2, BIAS2, B_UP = range(7)
OUT_AT = D + LANES


def exchange(x, axis, *bits):
    size, offset = lax.axis_size(axis), sum(1 << b for b in bits)
    return lax.ppermute(x, axis, [(i, i ^ offset) for i in range(size)])


def axis_bits(axis):
    return [(axis, b) for b in range(lax.axis_size(axis).bit_length() - 1)]


def tie(x, *others):
    return lax.optimization_barrier((x,) + others)[0]


def trade_stages(pieces):
    bits = axis_bits("fsdp")[1:]
    requests = []
    for m in range(1, len(pieces)):
        requests.append((pieces[m], "fsdp") + tuple(b for n, (_, b) in enumerate(bits) if m >> n & 1))
    arrived = yield requests
    far = [pieces[0]] + list(arrived)
    (near,) = yield [(jnp.concatenate([x[1:] for x in far], axis=0), "fsdp", 0)]
    return far, near


def near_steps(first_low):
    low, high = axis_bits("fsdp")[:1], axis_bits("group")[1:]
    return low + high if first_low else high + low


def moved(masks, axis, bit):
    step = (1 << bit) * (lax.axis_size("fsdp") if axis == "group" else 1)
    return tuple(m ^ step for m in masks)


def gather_stages(shard, early=False):
    lin = lax.axis_index("group") * lax.axis_size("fsdp") + lax.axis_index("fsdp")
    rows, columns = shard.shape
    if rows % 8:
        whole = lax.all_gather(shard, ("group", "fsdp"), axis=0, tiled=True)
        merged = rows
        while merged % 8:
            merged *= 2
        blocks = whole.reshape(-1, merged, columns)
        yield []
        return [[(blocks, tuple(range(blocks.shape[0])))]], jnp.zeros_like(lin)
    blocks, masks = shard[None], (0,)
    for axis, bit in reversed(axis_bits("fsdp")[1:]):
        (other,) = yield [(blocks, axis, bit)]
        blocks = jnp.concatenate([blocks, other], axis=0)
        masks = masks + moved(masks, axis, bit)
    half = columns // 2
    sides = [(blocks[:, :, :half], masks), (blocks[:, :, half:], masks)]
    steps = [near_steps(True), near_steps(False)]
    for n in range(len(steps[0]) - 1):
        others = yield [(b,) + st[n] for (b, _), st in zip(sides, steps)]
        sides = [
            (jnp.concatenate([b, o], axis=0), m + moved(m, *st[n]))
            for (b, m), st, o in zip(sides, steps, others)
        ]
    core = ("group", 0)
    others = yield [(b,) + st[-1] for (b, _), st in zip(sides, steps)] + (
        [(b,) + core for b, _ in sides] if early else []
    )
    parts = []
    if early:
        lasts = yield [(o,) + core for o in others[:2]]
        for n, ((b, m), st) in enumerate(zip(sides, steps)):
            there = moved(m, *st[-1])
            parts.append([
                (b, m), (others[n], there), (others[n + 2], moved(m, *core)),
                (lasts[n], moved(there, *core)),
            ])
        return parts, lin
    sides = [
        (jnp.concatenate([b, o], axis=0), m + moved(m, *st[-1]))
        for (b, m), st, o in zip(sides, steps, others)
    ]
    lasts = yield [(b,) + core for b, _ in sides]
    return [[(b, m), (last, moved(m, *core))] for (b, m), last in zip(sides, lasts)], lin


class Pipeline:
    def __init__(self):
        self.running = {}
        self.waiting = {}
        self.finished = {}
        self.started = ()

    def add(self, name, stages):
        self.running[name] = (stages, None)

    def names(self, only):
        return [n for n in self.running if only is None or n in only]

    def arrive(self, *others, only=None):
        names = [n for n in self.names(only) if n not in self.waiting]
        arrived = [x for n in names for x in self.running[n][1] or ()]
        if arrived:
            arrived = lax.optimization_barrier(tuple(arrived) + others)[: len(arrived)]
        at, ready = 0, ()
        for n in names:
            stages, results = self.running.pop(n)
            count = len(results or ())
            mine, at = arrived[at : at + count], at + count
            try:
                wanted = next(stages) if results is None else stages.send(mine)
            except StopIteration as done:
                self.finished[n] = done.value
            else:
                self.running[n] = (stages, ())
                self.waiting[n] = wanted
                ready += tuple(w[0] for w in wanted)
        self.started = ready or self.started

    def slot(self, *others, only=None):
        self.arrive(*others, only=only)
        requests = [(n, w) for n in self.names(only) for w in self.waiting.pop(n)]
        operands = tuple(w[0] for _, w in requests)
        if operands and others:
            operands = lax.optimization_barrier(operands + others)[: len(operands)]
        self.started = operands or self.started
        for x, (n, (_, axis, *bits)) in zip(operands, requests):
            stages, results = self.running[n]
            self.running[n] = (stages, results + (exchange(x, axis, *bits),))

    def read(self, name, *others):
        self.arrive(*others, only=(name,))
        return self.finished[name]

    def finish(self, name, *others, only=None):
        while name not in self.finished:
            self.slot(*others, only=only)
        return self.finished[name]


VMEM = pl.BlockSpec(memory_space=pltpu.VMEM)
SMEM = pl.BlockSpec(memory_space=pltpu.SMEM)


COSTS = {
    "assemble": 1.5, "project": 5.4, "mix_segments": 1.1, "intra_forward": 5.9, "inter_forward": 5.5,
    "expand": 9.5, "contract": 10.5, "back_to_heads": 11.8, "intra_backward": 10.3,
    "inter_backward": 4.6, "input_grad": 4.0, "weight_grad": 4.0, "vector_rows": 1.5,
}
FLOPS_PER_US = 6.0e8


def call(kernel, name, outs, in_specs, scratch=(), mib=8):
    return pl.pallas_call(
        kernel,
        out_shape=outs,
        in_specs=in_specs,
        out_specs=jax.tree.map(lambda _: VMEM, outs),
        scratch_shapes=scratch,
        compiler_params=pltpu.CompilerParams(vmem_limit_bytes=mib * 1024 * 1024),
        cost_estimate=pl.CostEstimate(
            flops=int(COSTS[name] * FLOPS_PER_US), transcendentals=0, bytes_accessed=0
        ),
        name=name,
    )


def shape_of(shape, dtype):
    return jax.ShapeDtypeStruct(shape, dtype)


def dot(a, b):
    return lax.dot_general(a, b, (((1,), (0,)), ((), ())), preferred_element_type=f32)


def dot_nt(a, b):
    return lax.dot_general(a, b, (((1,), (1,)), ((), ())), preferred_element_type=f32)


def dot_tn(a, b):
    return lax.dot_general(a, b, (((0,), (0,)), ((), ())), preferred_element_type=f32)


def loop(count, body):
    def step(i, carry):
        body(i)
        return carry

    lax.fori_loop(0, count, step, 0)


def rows_at(i):
    return pl.ds(pl.multiple_of(i * SEG, SEG), SEG)


def lanes_at(p):
    return pl.ds(pl.multiple_of(p * LANES, LANES), LANES)


def head_masks(rows):
    lane = lax.broadcasted_iota(jnp.int32, (rows, LANES), 1)
    first = (lane < HD).astype(f32)
    return first.astype(bf16), (1.0 - first).astype(bf16)


def diagonal():
    row = lax.broadcasted_iota(jnp.int32, (LANES, LANES), 0)
    lane = lax.broadcasted_iota(jnp.int32, (LANES, LANES), 1)
    return (row < HD) == (lane < HD)


def head_ones():
    return jnp.where(diagonal(), 1.0, 0.0).astype(bf16)


def split_state(packed):
    same = diagonal()
    cos_part = jnp.where(same, packed, 0.0)
    sin_part = pltpu.roll(jnp.where(same, 0.0, packed), HD, 1)
    return cos_part.astype(bf16), sin_part.astype(bf16)


def state_scratch(fsdp):
    return [pltpu.VMEM((D, LANES), f32), pltpu.VMEM((8 * max(2 * PAIRS, fsdp), LANES), f32)]


def piece_shapes(fsdp, segs):
    return (shape_of((2, segs, D // fsdp + 8, LANES), bf16),) * (fsdp // 2)


def norm_row(n, fsdp):
    per = max(16, fsdp) // fsdp
    return 8 * (n // per) + n % per


def store_states(s, own, left_ref, right_ref, weight_ref, cos_ref, sin_ref, state_scr, norm_scr, out_refs):
    fsdp = 2 * len(out_refs)
    chunk = D // fsdp
    same = diagonal()
    rows = rows_at(s)
    cos, sin = cos_ref[rows, :], sin_ref[rows, :]

    def pair(p):
        lanes = lanes_at(p)
        a = left_ref[rows, lanes]
        b = right_ref[rows, lanes].astype(f32)
        both = jnp.concatenate(
            [(b * cos).astype(bf16), (pltpu.roll(b, HD, 1) * sin).astype(bf16)], axis=1
        )
        product = dot_tn(a, both)
        state_scr[lanes, :] = jnp.where(same, product[:, :LANES], product[:, LANES:])
        wide = a.astype(f32)
        if weight_ref is not None:
            wide = wide * weight_ref[rows, lanes]
        for n, wave in ((p, cos), (PAIRS + p, sin)):
            norm_scr[pl.ds(norm_row(n, fsdp), 1), :] = jnp.sum(wide * wave, axis=0, keepdims=True)

    loop(PAIRS, pair)
    for r in range(fsdp):
        j = own ^ r
        at = pl.ds(pl.multiple_of(chunk * j, 8), chunk)
        norms = pl.ds(pl.multiple_of(8 * j, 8), 8)
        out_refs[r // 2][r % 2, s, 0:chunk, :] = state_scr[at, :].astype(bf16)
        out_refs[r // 2][r % 2, s, chunk : chunk + 8, :] = norm_scr[norms, :].astype(bf16)


def load_states(s, own, far_refs, near_ref, state_scr, norm_scr):
    fsdp = 2 * len(far_refs)
    chunk = D // fsdp
    for r in range(fsdp):
        j = own ^ r
        at = pl.ds(pl.multiple_of(chunk * j, 8), chunk)
        norms = pl.ds(pl.multiple_of(8 * j, 8), 8)
        ref, place = (near_ref, r // 2) if r % 2 else (far_refs[r // 2], 0)
        state_scr[at, :] = ref[place, s, 0:chunk, :].astype(f32)
        norm_scr[norms, :] = ref[place, s, chunk : chunk + 8, :].astype(f32)


def pair_state(p, state_scr, norm_scr, fsdp):
    cos_part, sin_part = split_state(state_scr[lanes_at(p), :])
    norm_cos = norm_scr[pl.ds(norm_row(p, fsdp), 1), :]
    norm_sin = norm_scr[pl.ds(norm_row(PAIRS + p, fsdp), 1), :]
    return cos_part, sin_part, norm_cos, norm_sin


def assemble(parts, lin):
    arrays = [blocks for part in parts for blocks, _ in part]
    places = jnp.concatenate(
        [jnp.array(masks, jnp.int32) for part in parts for _, masks in part]
    ) ^ lin.astype(jnp.int32)
    rows = arrays[0].shape[1]
    count = sum(len(masks) for _, masks in parts[0])
    width = sum(part[0][0].shape[2] for part in parts)
    lefts, left = [], 0
    for part in parts:
        lefts += [left] * len(part)
        left += part[0][0].shape[2]

    def kernel(places_ref, *refs):
        out_ref = refs[-1]
        first = 0
        for ref, at in zip(refs[:-1], lefts):
            number, _, columns = ref.shape

            def place(i, ref=ref, at=at, columns=columns, first=first):
                out_ref[places_ref[first + i], :, at : at + columns] = ref[i]

            loop(number, place)
            first += number

    whole = call(
        kernel, "assemble", shape_of((count, rows, width), bf16), [SMEM] + [VMEM] * len(arrays)
    )(places, *arrays)
    return whole.reshape(count * rows, width)


def project(ids, tokens, w_kv, cos, sin, fsdp):
    rows = tokens.shape[0]
    segs = rows // SEG

    def kernel(ids_ref, tok_ref, w_ref, cos_ref, sin_ref, k_ref, v_ref, *refs):
        inc_refs, (state_scr, norm_scr) = refs[:-2], refs[-2:]
        norm_scr[...] = jnp.zeros_like(norm_scr)

        def segment(s):
            at = rows_at(s)
            x = tok_ref[at, :]
            k_ref[at, :] = jnp.maximum(dot(x, w_ref[:, :D]), 0.0).astype(bf16)
            v_ref[at, :] = dot(x, w_ref[:, D:]).astype(bf16)
            store_states(s, ids_ref[2], k_ref, v_ref, None, cos_ref, sin_ref, state_scr, norm_scr,
                         inc_refs)

        loop(segs, segment)

    act = shape_of((rows, D), bf16)
    k, v, *pieces = call(
        kernel,
        "project",
        (act, act) + piece_shapes(fsdp, segs),
        [SMEM] + [VMEM] * 4,
        state_scratch(fsdp),
    )(ids, tokens, w_kv, cos, sin)
    return k, v, pieces


def mix_segments(spread, far, near):
    fsdp = 2 * len(far)
    _, segs, height, _ = near.shape

    def kernel(spread_ref, *refs):
        far_refs, near_ref, out_refs = refs[: fsdp // 2], refs[fsdp // 2], refs[fsdp // 2 + 1 :]
        for t in range(height // 8):
            at = slice(8 * t, 8 * t + 8)
            stacked = []
            for r in range(fsdp):
                ref, place = (near_ref, r // 2) if r % 2 else (far_refs[r // 2], 0)
                stacked += [ref[place, s, at, :].astype(f32) for s in range(segs)]
            mixed = dot(spread_ref[...], jnp.concatenate(stacked, axis=0).astype(bf16))
            for c in range(fsdp * segs):
                r, s = c // segs, c % segs
                out_refs[r // 2][r % 2, s, at, :] = mixed[8 * c : 8 * c + 8, :].astype(bf16)

    return call(
        kernel, "mix_segments", piece_shapes(fsdp, segs), [VMEM] * (fsdp // 2 + 2)
    )(spread, *far, near)


def intra_forward(tokens, w_q, k, v, wave):
    rows = tokens.shape[0]

    def kernel(tok_ref, w_ref, k_ref, v_ref, wave_ref, q_ref, num_ref, den_ref):
        masks = head_masks(SEG)

        def segment(s):
            at = rows_at(s)
            q_ref[at, :] = jnp.maximum(dot(tok_ref[at, :], w_ref[:, :D]), 0.0).astype(bf16)

            def pair(p):
                lanes = lanes_at(p)
                qs, ks, vs = q_ref[at, lanes], k_ref[at, lanes], v_ref[at, lanes]
                weights, values = [], []
                for m in masks:
                    weights.append((dot_nt(qs, ks * m) * wave_ref[...]).astype(bf16))
                    values.append(jnp.concatenate([vs * m, m], axis=1))
                both = dot(jnp.concatenate(weights, axis=1), jnp.concatenate(values, axis=0))
                num_ref[at, lanes] = both[:, :LANES]
                den_ref[at, lanes] = both[:, LANES:]

            loop(PAIRS, pair)

        loop(rows // SEG, segment)

    wide = shape_of((rows, D), f32)
    return call(
        kernel, "intra_forward", (shape_of((rows, D), bf16), wide, wide), [VMEM] * 5
    )(tokens, w_q, k, v, wave)


def inter_forward(ids, q, num, den, cos, sin, far, near):
    rows = q.shape[0]
    fsdp = 2 * len(far)

    def kernel(ids_ref, q_ref, num_ref, den_ref, cos_ref, sin_ref, *refs):
        far_refs, near_ref = refs[: fsdp // 2], refs[fsdp // 2]
        att_ref, rden_ref, state_scr, norm_scr = refs[fsdp // 2 + 1 :]
        ones = head_ones()
        twice = jnp.concatenate([ones, ones], axis=0)

        def segment(s):
            at = rows_at(s)
            load_states(s, ids_ref[2], far_refs, near_ref, state_scr, norm_scr)

            def pair(p):
                lanes = lanes_at(p)
                cos_part, sin_part, norm_cos, norm_sin = pair_state(p, state_scr, norm_scr, fsdp)
                qs = q_ref[at, lanes].astype(f32)
                q_cos = (qs * cos_ref[at, :]).astype(bf16)
                q_sin = (qs * sin_ref[at, :]).astype(bf16)
                carried = dot(
                    jnp.concatenate([q_cos, q_sin], axis=1),
                    jnp.concatenate([cos_part, sin_part], axis=0),
                )
                along = q_cos.astype(f32) * norm_cos + q_sin.astype(f32) * norm_sin
                high = along.astype(bf16)
                rest = (along - high.astype(f32)).astype(bf16)
                weight = dot(jnp.concatenate([high, rest], axis=1), twice)
                inverse = 1.0 / (den_ref[at, lanes] + weight + 1.0)
                att_ref[at, lanes] = ((num_ref[at, lanes] + carried) * inverse).astype(bf16)
                rden_ref[at, lanes] = inverse

            loop(PAIRS, pair)

        loop(rows // SEG, segment)

    return call(
        kernel,
        "inter_forward",
        (shape_of((rows, D), bf16), shape_of((rows, D), f32)),
        [SMEM] + [VMEM] * (6 + fsdp // 2),
        state_scratch(fsdp),
    )(ids, q, num, den, cos, sin, *far, near)


def standardize(resid):
    centred = resid - jnp.mean(resid, axis=1, keepdims=True)
    inv = lax.rsqrt(jnp.mean(centred * centred, axis=1, keepdims=True) + EPS)
    return centred * inv, inv


def standardize_back(d_hat, hat, inv):
    return inv * (
        d_hat
        - jnp.mean(d_hat, axis=1, keepdims=True)
        - hat * jnp.mean(d_hat * hat, axis=1, keepdims=True)
    )


def expand(att, tokens, w_out, w_up, small):
    rows = att.shape[0]
    ff = w_up.shape[1]

    def kernel(att_ref, tok_ref, out_w_ref, up_ref, small_ref, hat_ref, inv_ref, low_ref, gelu_ref,
               slope_ref):
        def block(i):
            at = rows_at(i)
            mixed = dot(att_ref[at, :], out_w_ref[:, OUT_AT : OUT_AT + D])
            hat, inv = standardize(
                tok_ref[at, :].astype(f32) + mixed + small_ref[B_OUT : B_OUT + 1, :]
            )
            hat_ref[at, :] = hat
            inv_ref[at, :] = jnp.broadcast_to(inv, (SEG, LANES))
            low_ref[at, :] = (
                hat * small_ref[GAIN1 : GAIN1 + 1, :] + small_ref[BIAS1 : BIAS1 + 1, :]
            ).astype(bf16)

            def part(m):
                for c in range(3):
                    columns = pl.ds(pl.multiple_of(m * D + 256 * c, 256), 256)
                    bias = small_ref[pl.ds(B_UP + m, 1), 256 * c : 256 * (c + 1)]
                    upper = dot(low_ref[at, :], up_ref[:, columns]) + bias
                    cdf = 0.5 + 0.5 * lax.erf(upper * math.sqrt(0.5))
                    pdf = jnp.exp(-0.5 * upper * upper) * (1.0 / math.sqrt(2.0 * math.pi))
                    gelu_ref[at, columns] = (upper * cdf).astype(bf16)
                    slope_ref[at, columns] = (cdf + upper * pdf).astype(bf16)

            loop(ff // D, part)

        loop(rows // SEG, block)

    return call(
        kernel,
        "expand",
        (
            shape_of((rows, D), f32),
            shape_of((rows, LANES), f32),
            shape_of((rows, D), bf16),
            shape_of((rows, ff), bf16),
            shape_of((rows, ff), bf16),
        ),
        [VMEM] * 5,
    )(att, tokens, w_out, w_up, small)


def contract(ids, gelu, slope, hat1, cotangent, w_down, small):
    rows, ff = gelu.shape

    def kernel(ids_ref, gelu_ref, slope_ref, hat1_ref, cot_ref, w_ref, small_ref,
               out_ref, dres_ref, dlow_ref, dup_ref, dlow_half_ref, dup_half_ref, sums_ref):
        sums_ref[...] = jnp.zeros_like(sums_ref)

        def block(i):
            at = rows_at(i)
            normed = hat1_ref[at, :] * small_ref[GAIN1 : GAIN1 + 1, :]
            normed += small_ref[BIAS1 : BIAS1 + 1, :]
            resid = normed + dot(gelu_ref[at, :], w_ref[...]) + small_ref[B_DOWN : B_DOWN + 1, :]
            hat, inv = standardize(resid)
            gain = small_ref[GAIN2 : GAIN2 + 1, :]
            out_ref[at, :] = (hat * gain + small_ref[BIAS2 : BIAS2 + 1, :]).astype(bf16)
            cot = cot_ref[at, :].astype(f32)
            sums_ref[GAIN2 : GAIN2 + 1, :] += jnp.sum(cot * hat, axis=0, keepdims=True)
            sums_ref[BIAS2 : BIAS2 + 1, :] += jnp.sum(cot, axis=0, keepdims=True)
            d_res = standardize_back(cot * gain, hat, inv)
            dres_ref[at, :] = d_res
            d_low = d_res.astype(bf16)
            dlow_ref[at, :] = d_low
            sums_ref[B_DOWN : B_DOWN + 1, :] += jnp.sum(d_low.astype(f32), axis=0, keepdims=True)

            def part(m):
                for c in range(3):
                    columns = pl.ds(pl.multiple_of(m * D + 256 * c, 256), 256)
                    d_up = dot_nt(dlow_ref[at, :], w_ref[columns, :])
                    d_up = (d_up * slope_ref[at, columns].astype(f32)).astype(bf16)
                    dup_ref[at, columns] = d_up
                    sums_ref[pl.ds(B_UP + m, 1), 256 * c : 256 * (c + 1)] += jnp.sum(
                        d_up.astype(f32), axis=0, keepdims=True
                    )

            loop(ff // D, part)
            theirs = 1 - ids_ref[0]
            dlow_half_ref[at, :] = dlow_ref[
                at, pl.ds(pl.multiple_of(theirs * (D // 2), 128), D // 2)
            ]
            dup_half_ref[at, :] = dup_ref[
                at, pl.ds(pl.multiple_of(theirs * (ff // 2), 128), ff // 2)
            ]

        loop(rows // SEG, block)

    return call(
        kernel,
        "contract",
        (
            shape_of((rows, D), bf16),
            shape_of((rows, D), f32),
            shape_of((rows, D), bf16),
            shape_of((rows, ff), bf16),
            shape_of((rows, D // 2), bf16),
            shape_of((rows, ff // 2), bf16),
            shape_of((16, D), f32),
        ),
        [SMEM] + [VMEM] * 6,
    )(ids, gelu, slope, hat1, cotangent, w_down, small)


def back_to_heads(ids, d_upper, d_res2, hat1, inv1, rden, att, q, cos, sin, w_out, w_up, small,
                  sums, fsdp):
    rows, ff = d_upper.shape
    segs = rows // SEG

    def kernel(ids_ref, dup_ref, dres_ref, hat_ref, inv_ref, rden_ref, att_ref, q_ref, cos_ref,
               sin_ref, out_w_ref, up_ref, small_ref, sums_in_ref,
               dres1_ref, dmix_ref, dmix_half_ref, dnum_ref, dden_ref, sums_ref, *refs):
        inc_refs, (state_scr, norm_scr) = refs[:-2], refs[-2:]
        sums_ref[...] = sums_in_ref[...]
        share = D // fsdp
        for j in range(fsdp):
            for c in range(ff // D):
                at = (j * (ff // D) + c) * share
                m, lane = B_UP + at // D, at % D
                sums_ref[B_UP + c : B_UP + c + 1, share * j : share * (j + 1)] = sums_in_ref[
                    m : m + 1, lane : lane + share
                ]
        norm_scr[...] = jnp.zeros_like(norm_scr)
        ones = head_ones()
        twice = jnp.concatenate([ones, ones], axis=0)

        def block(i):
            at = rows_at(i)
            d_normed = dres_ref[at, :] + dot_nt(dup_ref[at, :], up_ref[...])
            hat = hat_ref[at, :]
            sums_ref[GAIN1 : GAIN1 + 1, :] += jnp.sum(d_normed * hat, axis=0, keepdims=True)
            sums_ref[BIAS1 : BIAS1 + 1, :] += jnp.sum(d_normed, axis=0, keepdims=True)
            d_res = standardize_back(
                d_normed * small_ref[GAIN1 : GAIN1 + 1, :], hat, inv_ref[at, 0:1]
            )
            dres1_ref[at, :] = d_res
            d_mix = d_res.astype(bf16)
            dmix_ref[at, :] = d_mix
            sums_ref[B_OUT : B_OUT + 1, :] += jnp.sum(d_mix.astype(f32), axis=0, keepdims=True)
            d_att = dot_nt(d_mix, out_w_ref[:, OUT_AT : OUT_AT + D])
            inverse = rden_ref[at, :]
            dnum_ref[at, :] = (d_att * inverse).astype(bf16)
            along = d_att * att_ref[at, :].astype(f32)
            for p in range(PAIRS):
                lanes = slice(LANES * p, LANES * (p + 1))
                high = along[:, lanes].astype(bf16)
                rest = (along[:, lanes] - high.astype(f32)).astype(bf16)
                total = dot(jnp.concatenate([high, rest], axis=1), twice)
                dden_ref[at, lanes] = -total * inverse[:, lanes]
            theirs = 1 - ids_ref[0]
            dmix_half_ref[at, :] = dmix_ref[
                at, pl.ds(pl.multiple_of(theirs * (D // 2), 128), D // 2)
            ]
            store_states(i, ids_ref[2], q_ref, dnum_ref, dden_ref, cos_ref, sin_ref, state_scr,
                         norm_scr, inc_refs)

        loop(segs, block)

    return call(
        kernel,
        "back_to_heads",
        (
            shape_of((rows, D), f32),
            shape_of((rows, D), bf16),
            shape_of((rows, D // 2), bf16),
            shape_of((rows, D), bf16),
            shape_of((rows, D), f32),
            shape_of((16, D), f32),
        )
        + piece_shapes(fsdp, segs),
        [SMEM] + [VMEM] * 13,
        state_scratch(fsdp),
    )(ids, d_upper, d_res2, hat1, inv1, rden, att, q, cos, sin, w_out, w_up, small, sums)


def intra_backward(ids, q, k, v, d_num, d_den, cos, sin, wave, wave_t, far, near):
    rows = q.shape[0]
    fsdp = 2 * len(far)

    def kernel(ids_ref, q_ref, k_ref, v_ref, dnum_ref, dden_ref, cos_ref, sin_ref, wave_ref,
               wave_t_ref, *refs):
        far_refs, near_ref = refs[: fsdp // 2], refs[fsdp // 2]
        dq_ref, dq_half_ref, dk_ref, dv_ref, state_scr, norm_scr = refs[fsdp // 2 + 1 :]
        masks = head_masks(SEG)
        lane = lax.broadcasted_iota(jnp.int32, (SEG, LANES), 1) % HD
        picks = [jnp.where(lane < 2, m.astype(f32), 0.0).astype(bf16) for m in masks]

        def segment(s):
            at = rows_at(s)
            load_states(s, ids_ref[2], far_refs, near_ref, state_scr, norm_scr)
            cosine, sine = cos_ref[at, :], sin_ref[at, :]

            def pair(p):
                lanes = lanes_at(p)
                qs, ks, vs = q_ref[at, lanes], k_ref[at, lanes], v_ref[at, lanes]
                dn, dd = dnum_ref[at, lanes], dden_ref[at, lanes]
                high = dd.astype(bf16).astype(f32)
                spread = jnp.where(lane == 0, high, jnp.where(lane == 1, dd - high, 0.0))
                grads = jnp.concatenate([dn, spread.astype(bf16)], axis=1)
                w_ts, d_ss, d_ts, khs, qhs, dns = [], [], [], [], [], []
                for m, pick in zip(masks, picks):
                    kh = ks * m
                    values = jnp.concatenate([vs * m, pick], axis=1)
                    w_ts.append((dot_nt(kh, qs) * wave_t_ref[...]).astype(bf16))
                    d_ss.append((dot_nt(grads, values) * wave_ref[...]).astype(bf16))
                    d_ts.append((dot_nt(values, grads) * wave_t_ref[...]).astype(bf16))
                    khs.append(kh)
                    qhs.append(qs * m)
                    dns.append(dn * m)

                def both(left, right):
                    return dot(jnp.concatenate(left, axis=1), jnp.concatenate(right, axis=0))

                dk_ref[at, lanes] = both(d_ts, qhs)
                dv_ref[at, lanes] = both(w_ts, dns)
                d_q = both(d_ss, khs)
                cos_part, sin_part, norm_cos, norm_sin = pair_state(p, state_scr, norm_scr, fsdp)
                d_q += cosine * (dot_nt(dn, cos_part) + dd * norm_cos)
                d_q += sine * (dot_nt(dn, sin_part) + dd * norm_sin)
                dq_ref[at, lanes] = jnp.where(qs.astype(f32) > 0.0, d_q, 0.0).astype(bf16)

            loop(PAIRS, pair)
            theirs = 1 - ids_ref[0]
            dq_half_ref[at, :] = dq_ref[at, pl.ds(pl.multiple_of(theirs * (D // 2), 128), D // 2)]

        loop(rows // SEG, segment)

    return call(
        kernel,
        "intra_backward",
        (
            shape_of((rows, D), bf16),
            shape_of((rows, D // 2), bf16),
            shape_of((rows, D), f32),
            shape_of((rows, D), f32),
        ),
        [SMEM] + [VMEM] * (10 + fsdp // 2),
        state_scratch(fsdp),
    )(ids, q, k, v, d_num, d_den, cos, sin, wave, wave_t, *far, near)


def inter_backward(ids, k, v, d_k, d_v, cos, sin, far, near):
    rows = k.shape[0]
    fsdp = 2 * len(far)

    def kernel(ids_ref, k_ref, v_ref, dk_ref, dv_ref, cos_ref, sin_ref, *refs):
        far_refs, near_ref = refs[: fsdp // 2], refs[fsdp // 2]
        out_ref, state_scr, norm_scr = refs[fsdp // 2 + 1 :]
        core = ids_ref[0]

        def segment(s):
            at = rows_at(s)
            load_states(s, ids_ref[2], far_refs, near_ref, state_scr, norm_scr)
            cosine, sine = cos_ref[at, :], sin_ref[at, :]

            def pair(p):
                lanes = lanes_at(p)
                cos_part, sin_part, norm_cos, norm_sin = pair_state(p, state_scr, norm_scr, fsdp)
                ks = k_ref[at, lanes].astype(f32)
                vs = v_ref[at, lanes]
                d_k = dk_ref[at, lanes]
                d_k += cosine * (dot_nt(vs, cos_part) + norm_cos)
                d_k += sine * (dot_nt(vs, sin_part) + norm_sin)
                feats = jnp.concatenate(
                    [(ks * cosine).astype(bf16), (ks * sine).astype(bf16)], axis=1
                )
                d_v = dv_ref[at, lanes]
                d_v += dot(feats, jnp.concatenate([cos_part, sin_part], axis=0))
                out_ref[core, at, lanes] = jnp.where(ks > 0.0, d_k, 0.0).astype(bf16)
                out_ref[1 - core, at, lanes] = d_v.astype(bf16)

            loop(PAIRS, pair)

        loop(rows // SEG, segment)

    return call(
        kernel,
        "inter_backward",
        shape_of((2, rows, D), bf16),
        [SMEM] + [VMEM] * (7 + fsdp // 2),
        state_scratch(fsdp),
    )(ids, k, v, d_k, d_v, cos, sin, *far, near)


def input_grad(ids, d_q, d_kv, d_res1, w_q, w_kv):
    rows = d_q.shape[0]

    def kernel(ids_ref, dq_ref, dkv_ref, dres_ref, w_q_ref, w_kv_ref, out_ref):
        core = ids_ref[0]

        def block(i):
            at = rows_at(i)
            total = dres_ref[at, :] + dot_nt(dq_ref[at, :], w_q_ref[:, :D])
            total += dot_nt(dkv_ref[core, at, :], w_kv_ref[:, :D])
            total += dot_nt(dkv_ref[1 - core, at, :], w_kv_ref[:, D:])
            out_ref[at, :] = total

        loop(rows // SEG, block)

    return call(
        kernel, "input_grad", shape_of((rows, D), f32), [SMEM] + [VMEM] * 5
    )(ids, d_q, d_kv, d_res1, w_q, w_kv)


def reversed_bits(index, bits):
    total = 0
    for b in range(bits):
        total = total + (((index >> b) & 1) << (bits - 1 - b))
    return total


def weight_grad(ids, products, fsdp, splits, own_half=True, sums=None):
    height = products[0][0].shape[1]
    widths = [product[3].shape[1] for product in products]
    block = height // fsdp
    bits = fsdp.bit_length() - 1
    share = block // len(splits)
    group = block if block % 128 == 0 else height
    extra = [] if sums is None else [sums]

    def kernel(ids_ref, *refs):
        ins, out_refs = refs[: 4 * len(products)], refs[4 * len(products) + len(extra) :]

        def part(i):
            columns = pl.ds(pl.multiple_of(i * group, 128), group)

            def store(total, left):
                right = left + total.shape[1]
                for j in range(group // block):
                    place = reversed_bits((i * (group // block) + j) ^ ids_ref[2], bits)
                    for n, (split, out_ref) in enumerate(zip(splits, out_refs)):
                        strip = share // split
                        for h in range(split):
                            row = block * j + share * n + strip * h
                            half = h ^ ids_ref[1] if split > 1 else 0
                            out_ref[half, place, :, left:right] = total[
                                row : row + strip, :
                            ].astype(bf16)

            left = 0
            for n, width in enumerate(widths):
                a0_ref, a1_ref, b0_ref, b1_ref = ins[4 * n : 4 * n + 4]
                first = pl.multiple_of(ids_ref[0] * width, 128) if own_half else 0
                total = dot_tn(a0_ref[:, columns], b0_ref[:, pl.ds(first, width)])
                store(total + dot_tn(a1_ref[:, columns], b1_ref[...]), left)
                left += width
            if extra:
                tall = jnp.concatenate(
                    [refs[4 * len(products)][...], jnp.zeros((LANES - 16, height), f32)], axis=0
                )
                store(tall.T, left)

        loop(height // group, part)

    width = sum(widths) + LANES * len(extra)
    return call(
        kernel,
        "weight_grad",
        tuple(shape_of((n, fsdp, share // n, width), bf16) for n in splits),
        [SMEM] + [VMEM] * (4 * len(products) + len(extra)),
    )(ids, *(x for product in products for x in product), *extra)


def add_low(a, b):
    return (a.astype(f32) + b.astype(f32)).astype(bf16)


def core_stage(x):
    (other,) = yield [(x, "group", 0)]
    return other


def halving_stages(keep, send, bits):
    for axis, bit in bits:
        (received,) = yield [(send, axis, bit)]
        half = keep.shape[0] // 2
        if half == 0:
            return add_low(keep[0], received[0])
        keep, send = add_low(keep[:half], received[:half]), add_low(keep[half:], received[half:])


def reduce_stages(x, core, large=False):
    half = x.shape[1] // 2
    bits = axis_bits("fsdp")
    keep, send = x[0, :half], x[0, half:]
    if large and half > 1:
        quarter = half // 2
        axis, bit = bits.pop(0)
        (received,) = yield [(send[quarter:], axis, bit)]
        after = add_low(keep[quarter:], received)
        (received,) = yield [(tie(send[:quarter], after), axis, bit)]
        keep, send = add_low(keep[:quarter], received), after
    x = yield from halving_stages(keep, send, bits)
    for axis, bit in axis_bits("group")[1:]:
        (received,) = yield [(x, axis, bit)]
        x = add_low(x, received)
    other = yield from core_stage(x)
    return ordered(x, other, core == 0, -1).astype(f32)


def share_stages(x, core, chip):
    axis, bit = axis_bits("group")[1]
    half = x.shape[1] // 2
    (received,) = yield [(x[1], axis, bit)]
    keep, send = add_low(x[0, :half], received[:half]), add_low(x[0, half:], received[half:])
    x = yield from halving_stages(keep, send, axis_bits("fsdp"))
    (other,) = yield [(x, axis, bit)]
    x = ordered(x, other, chip == 0, 0)
    other = yield from core_stage(x)
    return ordered(x, other, core == 0, -1).astype(f32)


def ordered(x, other, first, axis):
    return jnp.concatenate([jnp.where(first, x, other), jnp.where(first, other, x)], axis=axis)


def ancestor_matrix(parents):
    count = parents.shape[0]
    columns = jnp.arange(count, dtype=jnp.int32)
    step = (parents[:, None] == columns[None, :]).astype(f32)
    same = (columns[:, None] == columns[None, :]).astype(f32)
    reached = step + same
    for _ in range(4):
        reached = (jnp.dot(reached, reached, preferred_element_type=f32) > 0.0).astype(f32)
    return reached - same


def spread_rows(matrix):
    count = matrix.shape[0]
    row = jnp.arange(8 * count, dtype=jnp.int32)
    pick = (row[:, None] // 8 == jnp.arange(count, dtype=jnp.int32)[None, :]).astype(f32)
    wide = jnp.dot(jnp.dot(pick, matrix), pick.T)
    return jnp.where(row[:, None] % 8 == row[None, :] % 8, wide, 0.0).astype(bf16)


def waves(local, segs):
    depth = jnp.sum(local[:segs], axis=1)
    angle = (depth[:, None] * SEG + jnp.arange(SEG, dtype=f32)[None, :]) * (
        math.pi / (2.0 * HORIZON)
    )
    angle = jnp.broadcast_to(angle.reshape(segs * SEG, 1), (segs * SEG, LANES))
    return jnp.cos(angle), jnp.sin(angle)


def gap_wave(position):
    gap = position[:, None] - position[None, :]
    wave = jnp.cos(gap.astype(f32) * (math.pi / (2.0 * HORIZON)))
    return jnp.where(gap >= 0, wave, 0.0), jnp.where(gap <= 0, wave, 0.0)


def vector_columns(vectors):
    return jnp.pad(jnp.stack(vectors), ((0, LANES - len(vectors)), (0, 0))).T


def wide_row(shard, rows):
    return jnp.pad(shard[None], ((0, rows - 1), (0, LANES - shard.shape[0])))


def vector_rows(weight, rows, share, longer):
    per = D // share

    def kernel(w_ref, out_ref):
        out_ref[...] = jnp.zeros_like(out_ref)
        turned = w_ref[:, D:OUT_AT].astype(f32).T
        out_ref[:B_UP, :] = turned[:B_UP, :]
        for block in range(longer * per):
            m, lane = B_UP + block // per, share * (block % per)
            first = rows * block // 8 * 8
            tile = w_ref[first : first + 8, OUT_AT + D :].astype(f32)
            row = rows * block - first
            out_ref[m : m + 1, lane : lane + share] = tile[row : row + 1, :share]

    return call(kernel, "vector_rows", shape_of((16, D), f32), [VMEM])(weight)


def body(
    tokens, cotangent, parent_seg, w_qkv, w_out, b_out, norm1_gain, norm1_bias, w_up, b_up,
    w_down, b_down, norm2_gain, norm2_bias,
):
    fsdp = lax.axis_size("fsdp")
    chips = lax.axis_size("group") // 2
    own = lax.axis_index("fsdp")
    group = lax.axis_index("group")
    core, chip = group % 2, group // 2
    rows = tokens.shape[0]
    segs = rows // SEG
    ff = w_up.shape[1]
    ids = jnp.stack([core, chip, own]).astype(jnp.int32)

    pipe = Pipeline()
    pipe.add("kv", gather_stages(w_qkv[:, D:], True))
    pipe.add("tokens", core_stage(tokens))
    pipe.slot()
    pipe.slot(only=("kv",))
    begun = pipe.started[0]
    tokens_other = pipe.read("tokens", begun)

    ancestry = ancestor_matrix(tie(parent_seg[0], begun))
    count = parent_seg.shape[1]
    place = jnp.arange(count, dtype=jnp.int32)
    there = (own ^ (place // segs)) * segs + place % segs
    select = (there[:, None] == place[None, :]).astype(f32)
    local = jnp.dot(jnp.dot(select, ancestry), select.T)
    from_ancestors, from_descendants = spread_rows(local), spread_rows(local.T)
    cos, sin = waves(local, segs)
    wave, wave_t = gap_wave(tie(jnp.arange(SEG, dtype=jnp.int32), begun))
    shard_rows = w_qkv.shape[0]
    columns = vector_columns((b_out, norm1_gain, norm1_bias, b_down, norm2_gain, norm2_bias))
    pipe.add("qo", gather_stages(tie(
        jnp.concatenate([w_qkv[:, :D], columns, w_out, wide_row(b_up, shard_rows)], axis=1), begun
    )))
    pipe.add("up", gather_stages(w_up))
    pipe.add("down", gather_stages(w_down))
    pipe.slot(only=("kv", "qo"))
    pipe.slot(only=("kv", "qo"))
    pipe.slot(only=("kv", "qo"))
    pipe.slot(*pipe.started, only=("up",))
    w_kv = assemble(*pipe.finish("kv", only=("kv",)))
    tables = (from_ancestors, from_descendants, wave, wave_t)
    k, v, increments = project(ids, tie(tokens, tokens_other, *tables), w_kv, cos, sin, fsdp)
    pipe.arrive(k, only=("qo", "up"))
    pipe.add("state", trade_stages(increments))
    pipe.slot(*pipe.started, only=("state", "qo"))
    pipe.slot(only=("state", "qo"))
    pipe.slot(*pipe.started, only=("up",))
    pipe.slot(*pipe.started, only=("down",))
    w_qo = assemble(*pipe.finish("qo", only=("qo",)))
    pipe.slot(w_qo, only=("up",))
    pipe.slot(*pipe.started, only=("down",))
    q, num, den = intra_forward(tie(tokens, *pipe.started), w_qo, k, v, wave)
    far, near = pipe.finish("state", q, only=("state",))
    mixed = mix_segments(from_ancestors, far, near)
    pipe.arrive(q, only=("up", "down"))
    pipe.add("path", trade_stages(mixed))
    pipe.slot(*pipe.started, only=("path", "up"))
    small = vector_rows(tie(w_qo, *pipe.started), shard_rows, b_up.shape[0], ff // D)
    pipe.slot(small, only=("path", "up", "down"))
    path = pipe.finish("path", *pipe.started, only=("path",))
    att, rden = inter_forward(ids, q, num, den, cos, sin, *path)
    pipe.add("att", core_stage(att))
    pipe.slot(att, only=("down", "att"))
    w_up_full = assemble(*pipe.finish("up", att, only=("up",)))
    att_other = pipe.read("att", w_up_full)
    hat1, inv1, low1, gelu, slope = expand(
        tie(att, att_other, *pipe.started), tokens, w_qo, w_up_full, small
    )
    pipe.slot(low1, only=("down",))
    w_down_full = assemble(*pipe.finish("down", only=("down",)))
    pipe.add("gelu", core_stage(gelu))
    pipe.add("low1", core_stage(low1))
    pipe.slot(w_down_full, only=("gelu", "low1"))
    output, d_res2, d_lower, d_upper, d_lower_half, d_upper_half, sums = contract(
        ids, gelu, slope, hat1, cotangent, w_down_full, small
    )
    low1_other = pipe.read("low1", sums)
    gelu_other = pipe.read("gelu", sums)
    grads = Pipeline()
    grads.add("d_lower", core_stage(d_lower_half))
    grads.add("d_upper", core_stage(d_upper_half))
    grads.slot(low1_other, gelu_other)
    d_res1, d_mixed, d_mixed_half, d_num, d_den, sums, *back = back_to_heads(
        ids, tie(d_upper, *grads.started), d_res2, hat1, inv1, rden, att, q, cos, sin, w_qo,
        w_up_full, small, sums, fsdp,
    )
    d_lower_other = grads.read("d_lower", d_num)
    d_upper_other = grads.read("d_upper", d_num)
    grads.add("state", trade_stages(back))
    grads.add("d_mixed", core_stage(d_mixed_half))
    grads.slot(d_lower_other, d_upper_other)
    two = chips == 2

    def reduction(part):
        return share_stages(part, core, chip) if two else reduce_stages(part, core)

    split = 2 if two else 1
    (down_part,) = weight_grad(
        ids, [(gelu, gelu_other, tie(d_lower, *grads.started), d_lower_other)], fsdp, [split]
    )
    d_mixed_other = grads.read("d_mixed", down_part)
    grads.add("down", reduction(down_part))
    grads.slot(d_mixed_other, only=("state", "down"))
    (up_part,) = weight_grad(
        ids, [(low1, low1_other, tie(d_upper, *grads.started), d_upper_other)], fsdp, [1]
    )
    far, near = grads.finish("state", up_part, only=("state",))
    grads.add("up", reduce_stages(up_part, core, True))
    grads.slot(near, only=("up",))
    mixed = mix_segments(from_descendants, far, tie(near, *grads.started))
    grads.add("path", trade_stages(mixed))
    grads.slot(only=("path",))
    d_q, d_q_half, d_k, d_v = intra_backward(
        ids, tie(q, *grads.started), k, v, d_num, d_den, cos, sin, wave, wave_t, *path
    )
    grads.add("d_q", core_stage(d_q_half))
    grads.slot(d_q, only=("path", "d_q"))
    grads.slot(*grads.started, only=("up",))
    d_q_other = grads.read("d_q", *grads.started)
    (outq_part,) = weight_grad(
        ids,
        [
            (att, att_other, d_mixed, d_mixed_other),
            (tokens, tokens_other, d_q, d_q_other),
        ],
        fsdp, [split], sums=sums,
    )
    grads.add("outq", reduction(outq_part))
    grads.arrive(outq_part, only=("down",))
    grads.slot(*grads.started, only=("outq",))
    back = grads.finish("path", *grads.started, only=("path",))
    d_kv = inter_backward(ids, k, v, d_k, d_v, cos, sin, *back)
    grads.add("d_kv", core_stage(d_kv[1]))
    grads.slot(only=("d_kv",))
    d_kv_other = grads.read("d_kv")
    kv_parts = weight_grad(
        ids, [(tokens, tokens_other, d_kv[0], d_kv_other)], fsdp, [2, 1] if two else [1], False,
    )
    grads.add("kv0", reduction(kv_parts[0]))
    for part in kv_parts[1:]:
        grads.add("kv1", reduce_stages(part, core))
    kv = ("kv0", "kv1")
    grads.slot(only=kv)
    grads.slot(*kv_parts, only=("up",))
    tokens_grad = input_grad(ids, d_q, tie(d_kv, *grads.started), d_res1, w_qo, w_kv)
    grads.slot(tokens_grad, only=kv)
    grads.slot(*grads.started, only=("down",))
    grads.slot(*grads.started, only=("outq",))
    grads.slot(*grads.started, only=kv)
    grads.slot(*grads.started, only=kv)
    grads.slot(*grads.started, only=("up", "down"))
    grads.slot(*grads.started, only=kv)
    while grads.running:
        grads.slot(*grads.started)
    done = grads.finished
    kv_grad = jnp.concatenate([done[n] for n in ("kv0", "kv1") if n in done], axis=0)
    ours, others = jnp.split(done["outq"], 2, axis=1)
    half = D // 2
    sums = ours[:, D : D + 16] + others[:, D : D + 16]
    return (
        output,
        tokens_grad,
        jnp.concatenate([ours[:, half:D], others[:, half:D], kv_grad], axis=1),
        jnp.concatenate([ours[:, :half], others[:, :half]], axis=1),
        sums[:, B_OUT],
        sums[:, GAIN1],
        sums[:, BIAS1],
        done["up"],
        sums[:, B_UP : B_UP + ff // D].T.reshape(-1),
        done["down"],
        sums[:, B_DOWN],
        sums[:, GAIN2],
        sums[:, BIAS2],
    )


def solution(mesh):
    both = ("group", "fsdp")
    matrix, vector = P(both, None), P(both)
    in_specs = (
        matrix, matrix, P("group", None), matrix, matrix, vector, vector, vector, matrix, vector,
        matrix, vector, vector, vector,
    )
    rows, line = P("fsdp", None), P("fsdp")
    out_specs = (
        matrix, matrix, rows, rows, line, line, line, rows, line, rows, line, line, line,
    )
    return jax.shard_map(body, mesh=mesh, in_specs=in_specs, out_specs=out_specs, check_vma=False)
```

```python
import math

import jax
import jax.numpy as jnp
from jax import lax
from jax.experimental import pallas as pl
from jax.experimental.pallas import tpu as pltpu
from jax.sharding import PartitionSpec as P

D = 768
H = 12
HD = 64
SEG = 256
HORIZON = 2560
PAIRS = H // 2
LANES = 2 * HD
EPS = 1e-05

f32 = jnp.float32
bf16 = jnp.bfloat16

B_OUT, GAIN1, BIAS1, B_DOWN, GAIN2, BIAS2, B_UP = range(7)
OUT_AT = D + LANES


def exchange(x, axis, *bits):
    size, offset = lax.axis_size(axis), sum(1 << b for b in bits)
    return lax.ppermute(x, axis, [(i, i ^ offset) for i in range(size)])


def axis_bits(axis):
    return [(axis, b) for b in range(lax.axis_size(axis).bit_length() - 1)]


def tie(x, *others):
    return lax.optimization_barrier((x,) + others)[0]


def trade_stages(pieces):
    bits = axis_bits("fsdp")[1:]
    requests = []
    for m in range(1, len(pieces)):
        requests.append((pieces[m], "fsdp") + tuple(b for n, (_, b) in enumerate(bits) if m >> n & 1))
    arrived = yield requests
    far = [pieces[0]] + list(arrived)
    (near,) = yield [(jnp.concatenate([x[1:] for x in far], axis=0), "fsdp", 0)]
    return far, near


def near_steps(first_low):
    low, high = axis_bits("fsdp")[:1], axis_bits("group")[1:]
    return low + high if first_low else high + low


def moved(masks, axis, bit):
    step = (1 << bit) * (lax.axis_size("fsdp") if axis == "group" else 1)
    return tuple(m ^ step for m in masks)


def gather_stages(shard, early=False):
    lin = lax.axis_index("group") * lax.axis_size("fsdp") + lax.axis_index("fsdp")
    rows, columns = shard.shape
    if rows % 8:
        whole = lax.all_gather(shard, ("group", "fsdp"), axis=0, tiled=True)
        merged = rows
        while merged % 8:
            merged *= 2
        blocks = whole.reshape(-1, merged, columns)
        yield []
        return [[(blocks, tuple(range(blocks.shape[0])))]], jnp.zeros_like(lin)
    blocks, masks = shard[None], (0,)
    for axis, bit in reversed(axis_bits("fsdp")[1:]):
        (other,) = yield [(blocks, axis, bit)]
        blocks = jnp.concatenate([blocks, other], axis=0)
        masks = masks + moved(masks, axis, bit)
    half = columns // 2
    sides = [(blocks[:, :, :half], masks), (blocks[:, :, half:], masks)]
    steps = [near_steps(True), near_steps(False)]
    for n in range(len(steps[0]) - 1):
        others = yield [(b,) + st[n] for (b, _), st in zip(sides, steps)]
        sides = [
            (jnp.concatenate([b, o], axis=0), m + moved(m, *st[n]))
            for (b, m), st, o in zip(sides, steps, others)
        ]
    core = ("group", 0)
    others = yield [(b,) + st[-1] for (b, _), st in zip(sides, steps)] + (
        [(b,) + core for b, _ in sides] if early else []
    )
    parts = []
    if early:
        lasts = yield [(o,) + core for o in others[:2]]
        for n, ((b, m), st) in enumerate(zip(sides, steps)):
            there = moved(m, *st[-1])
            parts.append([
                (b, m), (others[n], there), (others[n + 2], moved(m, *core)),
                (lasts[n], moved(there, *core)),
            ])
        return parts, lin
    sides = [
        (jnp.concatenate([b, o], axis=0), m + moved(m, *st[-1]))
        for (b, m), st, o in zip(sides, steps, others)
    ]
    lasts = yield [(b,) + core for b, _ in sides]
    return [[(b, m), (last, moved(m, *core))] for (b, m), last in zip(sides, lasts)], lin


class Pipeline:
    def __init__(self):
        self.running = {}
        self.waiting = {}
        self.finished = {}
        self.started = ()

    def add(self, name, stages):
        self.running[name] = (stages, None)

    def names(self, only):
        return [n for n in self.running if only is None or n in only]

    def arrive(self, *others, only=None):
        names = [n for n in self.names(only) if n not in self.waiting]
        arrived = [x for n in names for x in self.running[n][1] or ()]
        if arrived:
            arrived = lax.optimization_barrier(tuple(arrived) + others)[: len(arrived)]
        at, ready = 0, ()
        for n in names:
            stages, results = self.running.pop(n)
            count = len(results or ())
            mine, at = arrived[at : at + count], at + count
            try:
                wanted = next(stages) if results is None else stages.send(mine)
            except StopIteration as done:
                self.finished[n] = done.value
            else:
                self.running[n] = (stages, ())
                self.waiting[n] = wanted
                ready += tuple(w[0] for w in wanted)
        self.started = ready or self.started

    def slot(self, *others, only=None):
        self.arrive(*others, only=only)
        requests = [(n, w) for n in self.names(only) for w in self.waiting.pop(n)]
        operands = tuple(w[0] for _, w in requests)
        if operands and others:
            operands = lax.optimization_barrier(operands + others)[: len(operands)]
        self.started = operands or self.started
        for x, (n, (_, axis, *bits)) in zip(operands, requests):
            stages, results = self.running[n]
            self.running[n] = (stages, results + (exchange(x, axis, *bits),))

    def read(self, name, *others):
        self.arrive(*others, only=(name,))
        return self.finished[name]

    def finish(self, name, *others, only=None):
        while name not in self.finished:
            self.slot(*others, only=only)
        return self.finished[name]


VMEM = pl.BlockSpec(memory_space=pltpu.VMEM)
SMEM = pl.BlockSpec(memory_space=pltpu.SMEM)


COSTS = {"assemble": 1.5, "project": 5.4, "mix_segments": 1.1, "intra_forward": 5.9, "inter_forward": 5.5, "expand": 2.85, "contract": 6.0, "turn": 22.5, "back_to_heads": 11.8, "intra_backward": 10.3, "inter_backward": 4.6, "input_grad": 4.0, "vector_rows": 1.5, "down": 6.0, "up": 1.2, "outq": 2.4, "kv": 3.36}
TAIL = ('kv0+kv1', 'up', 'grad', 'down', 'outq', 'kv1', 'kv0', 'kv1', 'up', 'outq', 'kv0', 'outq', 'down', 'kv0', 'up', 'kv1', 'outq', 'kv0', 'down', 'kv1', 'outq', 'kv0', 'kv1')
FLOPS_PER_US = 6.0e8


def call(kernel, name, outs, in_specs, scratch=(), cost=None, mib=8):
    return pl.pallas_call(
        kernel,
        out_shape=outs,
        in_specs=in_specs,
        out_specs=jax.tree.map(lambda _: VMEM, outs),
        scratch_shapes=scratch,
        compiler_params=pltpu.CompilerParams(vmem_limit_bytes=mib * 1024 * 1024),
        cost_estimate=pl.CostEstimate(
            flops=int((cost or COSTS[name]) * FLOPS_PER_US), transcendentals=0, bytes_accessed=0
        ),
        name=name,
    )


def shape_of(shape, dtype):
    return jax.ShapeDtypeStruct(shape, dtype)


def dot(a, b):
    return lax.dot_general(a, b, (((1,), (0,)), ((), ())), preferred_element_type=f32)


def dot_nt(a, b):
    return lax.dot_general(a, b, (((1,), (1,)), ((), ())), preferred_element_type=f32)


def dot_tn(a, b):
    return lax.dot_general(a, b, (((0,), (0,)), ((), ())), preferred_element_type=f32)


def loop(count, body):
    def step(i, carry):
        body(i)
        return carry

    lax.fori_loop(0, count, step, 0)


def rows_at(i):
    return pl.ds(pl.multiple_of(i * SEG, SEG), SEG)


def lanes_at(p):
    return pl.ds(pl.multiple_of(p * LANES, LANES), LANES)


def head_masks(rows):
    lane = lax.broadcasted_iota(jnp.int32, (rows, LANES), 1)
    first = (lane < HD).astype(f32)
    return first.astype(bf16), (1.0 - first).astype(bf16)


def diagonal():
    row = lax.broadcasted_iota(jnp.int32, (LANES, LANES), 0)
    lane = lax.broadcasted_iota(jnp.int32, (LANES, LANES), 1)
    return (row < HD) == (lane < HD)


def head_ones():
    return jnp.where(diagonal(), 1.0, 0.0).astype(bf16)


def split_state(packed):
    same = diagonal()
    cos_part = jnp.where(same, packed, 0.0)
    sin_part = pltpu.roll(jnp.where(same, 0.0, packed), HD, 1)
    return cos_part.astype(bf16), sin_part.astype(bf16)


def state_scratch(fsdp):
    return [pltpu.VMEM((D, LANES), f32), pltpu.VMEM((8 * max(2 * PAIRS, fsdp), LANES), f32)]


def piece_shapes(fsdp, segs):
    return (shape_of((2, segs, D // fsdp + 8, LANES), bf16),) * (fsdp // 2)


def norm_row(n, fsdp):
    per = max(16, fsdp) // fsdp
    return 8 * (n // per) + n % per


def store_states(s, own, left_ref, right_ref, weight_ref, cos_ref, sin_ref, state_scr, norm_scr, out_refs):
    fsdp = 2 * len(out_refs)
    chunk = D // fsdp
    same = diagonal()
    rows = rows_at(s)
    cos, sin = cos_ref[rows, :], sin_ref[rows, :]

    def pair(p):
        lanes = lanes_at(p)
        a = left_ref[rows, lanes]
        b = right_ref[rows, lanes].astype(f32)
        both = jnp.concatenate(
            [(b * cos).astype(bf16), (pltpu.roll(b, HD, 1) * sin).astype(bf16)], axis=1
        )
        product = dot_tn(a, both)
        state_scr[lanes, :] = jnp.where(same, product[:, :LANES], product[:, LANES:])
        wide = a.astype(f32)
        if weight_ref is not None:
            wide = wide * weight_ref[rows, lanes]
        for n, wave in ((p, cos), (PAIRS + p, sin)):
            norm_scr[pl.ds(norm_row(n, fsdp), 1), :] = jnp.sum(wide * wave, axis=0, keepdims=True)

    loop(PAIRS, pair)
    for r in range(fsdp):
        j = own ^ r
        at = pl.ds(pl.multiple_of(chunk * j, 8), chunk)
        norms = pl.ds(pl.multiple_of(8 * j, 8), 8)
        out_refs[r // 2][r % 2, s, 0:chunk, :] = state_scr[at, :].astype(bf16)
        out_refs[r // 2][r % 2, s, chunk : chunk + 8, :] = norm_scr[norms, :].astype(bf16)


def load_states(s, own, far_refs, near_ref, state_scr, norm_scr):
    fsdp = 2 * len(far_refs)
    chunk = D // fsdp
    for r in range(fsdp):
        j = own ^ r
        at = pl.ds(pl.multiple_of(chunk * j, 8), chunk)
        norms = pl.ds(pl.multiple_of(8 * j, 8), 8)
        ref, place = (near_ref, r // 2) if r % 2 else (far_refs[r // 2], 0)
        state_scr[at, :] = ref[place, s, 0:chunk, :].astype(f32)
        norm_scr[norms, :] = ref[place, s, chunk : chunk + 8, :].astype(f32)


def pair_state(p, state_scr, norm_scr, fsdp):
    cos_part, sin_part = split_state(state_scr[lanes_at(p), :])
    norm_cos = norm_scr[pl.ds(norm_row(p, fsdp), 1), :]
    norm_sin = norm_scr[pl.ds(norm_row(PAIRS + p, fsdp), 1), :]
    return cos_part, sin_part, norm_cos, norm_sin


def assemble(parts, lin):
    arrays = [blocks for part in parts for blocks, _ in part]
    places = jnp.concatenate(
        [jnp.array(masks, jnp.int32) for part in parts for _, masks in part]
    ) ^ lin.astype(jnp.int32)
    rows = arrays[0].shape[1]
    count = sum(len(masks) for _, masks in parts[0])
    width = sum(part[0][0].shape[2] for part in parts)
    lefts, left = [], 0
    for part in parts:
        lefts += [left] * len(part)
        left += part[0][0].shape[2]

    def kernel(places_ref, *refs):
        out_ref = refs[-1]
        first = 0
        for ref, at in zip(refs[:-1], lefts):
            number, _, columns = ref.shape

            def place(i, ref=ref, at=at, columns=columns, first=first):
                out_ref[places_ref[first + i], :, at : at + columns] = ref[i]

            loop(number, place)
            first += number

    whole = call(
        kernel, "assemble", shape_of((count, rows, width), bf16), [SMEM] + [VMEM] * len(arrays)
    )(places, *arrays)
    return whole.reshape(count * rows, width)


def project(ids, tokens, w_kv, cos, sin, fsdp):
    rows = tokens.shape[0]
    segs = rows // SEG

    def kernel(ids_ref, tok_ref, w_ref, cos_ref, sin_ref, k_ref, v_ref, *refs):
        inc_refs, (state_scr, norm_scr) = refs[:-2], refs[-2:]
        norm_scr[...] = jnp.zeros_like(norm_scr)

        def segment(s):
            at = rows_at(s)
            x = tok_ref[at, :]
            k_ref[at, :] = jnp.maximum(dot(x, w_ref[:, :D]), 0.0).astype(bf16)
            v_ref[at, :] = dot(x, w_ref[:, D:]).astype(bf16)
            store_states(s, ids_ref[2], k_ref, v_ref, None, cos_ref, sin_ref, state_scr, norm_scr,
                         inc_refs)

        loop(segs, segment)

    act = shape_of((rows, D), bf16)
    k, v, *pieces = call(
        kernel,
        "project",
        (act, act) + piece_shapes(fsdp, segs),
        [SMEM] + [VMEM] * 4,
        state_scratch(fsdp),
    )(ids, tokens, w_kv, cos, sin)
    return k, v, pieces


def mix_segments(spread, far, near):
    fsdp = 2 * len(far)
    _, segs, height, _ = near.shape

    def kernel(spread_ref, *refs):
        far_refs, near_ref, out_refs = refs[: fsdp // 2], refs[fsdp // 2], refs[fsdp // 2 + 1 :]
        for t in range(height // 8):
            at = slice(8 * t, 8 * t + 8)
            stacked = []
            for r in range(fsdp):
                ref, place = (near_ref, r // 2) if r % 2 else (far_refs[r // 2], 0)
                stacked += [ref[place, s, at, :].astype(f32) for s in range(segs)]
            mixed = dot(spread_ref[...], jnp.concatenate(stacked, axis=0).astype(bf16))
            for c in range(fsdp * segs):
                r, s = c // segs, c % segs
                out_refs[r // 2][r % 2, s, at, :] = mixed[8 * c : 8 * c + 8, :].astype(bf16)

    return call(
        kernel, "mix_segments", piece_shapes(fsdp, segs), [VMEM] * (fsdp // 2 + 2)
    )(spread, *far, near)


def intra_forward(tokens, w_q, k, v, wave):
    rows = tokens.shape[0]

    def kernel(tok_ref, w_ref, k_ref, v_ref, wave_ref, q_ref, num_ref, den_ref):
        masks = head_masks(SEG)

        def segment(s):
            at = rows_at(s)
            q_ref[at, :] = jnp.maximum(dot(tok_ref[at, :], w_ref[:, :D]), 0.0).astype(bf16)

            def pair(p):
                lanes = lanes_at(p)
                qs, ks, vs = q_ref[at, lanes], k_ref[at, lanes], v_ref[at, lanes]
                weights, values = [], []
                for m in masks:
                    weights.append((dot_nt(qs, ks * m) * wave_ref[...]).astype(bf16))
                    values.append(jnp.concatenate([vs * m, m], axis=1))
                both = dot(jnp.concatenate(weights, axis=1), jnp.concatenate(values, axis=0))
                num_ref[at, lanes] = both[:, :LANES]
                den_ref[at, lanes] = both[:, LANES:]

            loop(PAIRS, pair)

        loop(rows // SEG, segment)

    wide = shape_of((rows, D), f32)
    return call(
        kernel, "intra_forward", (shape_of((rows, D), bf16), wide, wide), [VMEM] * 5
    )(tokens, w_q, k, v, wave)


def inter_forward(ids, q, num, den, cos, sin, far, near):
    rows = q.shape[0]
    fsdp = 2 * len(far)

    def kernel(ids_ref, q_ref, num_ref, den_ref, cos_ref, sin_ref, *refs):
        far_refs, near_ref = refs[: fsdp // 2], refs[fsdp // 2]
        att_ref, rden_ref, state_scr, norm_scr = refs[fsdp // 2 + 1 :]
        ones = head_ones()
        twice = jnp.concatenate([ones, ones], axis=0)

        def segment(s):
            at = rows_at(s)
            load_states(s, ids_ref[2], far_refs, near_ref, state_scr, norm_scr)

            def pair(p):
                lanes = lanes_at(p)
                cos_part, sin_part, norm_cos, norm_sin = pair_state(p, state_scr, norm_scr, fsdp)
                qs = q_ref[at, lanes].astype(f32)
                q_cos = (qs * cos_ref[at, :]).astype(bf16)
                q_sin = (qs * sin_ref[at, :]).astype(bf16)
                carried = dot(
                    jnp.concatenate([q_cos, q_sin], axis=1),
                    jnp.concatenate([cos_part, sin_part], axis=0),
                )
                along = q_cos.astype(f32) * norm_cos + q_sin.astype(f32) * norm_sin
                high = along.astype(bf16)
                rest = (along - high.astype(f32)).astype(bf16)
                weight = dot(jnp.concatenate([high, rest], axis=1), twice)
                inverse = 1.0 / (den_ref[at, lanes] + weight + 1.0)
                att_ref[at, lanes] = ((num_ref[at, lanes] + carried) * inverse).astype(bf16)
                rden_ref[at, lanes] = inverse

            loop(PAIRS, pair)

        loop(rows // SEG, segment)

    return call(
        kernel,
        "inter_forward",
        (shape_of((rows, D), bf16), shape_of((rows, D), f32)),
        [SMEM] + [VMEM] * (6 + fsdp // 2),
        state_scratch(fsdp),
    )(ids, q, num, den, cos, sin, *far, near)


def standardize(resid):
    centred = resid - jnp.mean(resid, axis=1, keepdims=True)
    inv = lax.rsqrt(jnp.mean(centred * centred, axis=1, keepdims=True) + EPS)
    return centred * inv, inv


def standardize_back(d_hat, hat, inv):
    return inv * (
        d_hat
        - jnp.mean(d_hat, axis=1, keepdims=True)
        - hat * jnp.mean(d_hat * hat, axis=1, keepdims=True)
    )


def expand(att, tokens, w_out, w_up, small):
    rows = att.shape[0]
    ff = w_up.shape[1]

    def kernel(att_ref, tok_ref, out_w_ref, up_ref, small_ref, hat_ref, inv_ref, low_ref, gelu_ref,
               slope_ref):
        def block(i):
            at = rows_at(i)
            mixed = dot(att_ref[at, :], out_w_ref[:, OUT_AT : OUT_AT + D])
            hat, inv = standardize(
                tok_ref[at, :].astype(f32) + mixed + small_ref[B_OUT : B_OUT + 1, :]
            )
            hat_ref[at, :] = hat
            inv_ref[at, :] = jnp.broadcast_to(inv, (SEG, LANES))
            low_ref[at, :] = (
                hat * small_ref[GAIN1 : GAIN1 + 1, :] + small_ref[BIAS1 : BIAS1 + 1, :]
            ).astype(bf16)

            def part(m):
                for c in range(3):
                    columns = pl.ds(pl.multiple_of(m * D + 256 * c, 256), 256)
                    bias = small_ref[pl.ds(B_UP + m, 1), 256 * c : 256 * (c + 1)]
                    upper = dot(low_ref[at, :], up_ref[:, columns]) + bias
                    cdf = 0.5 + 0.5 * lax.erf(upper * math.sqrt(0.5))
                    pdf = jnp.exp(-0.5 * upper * upper) * (1.0 / math.sqrt(2.0 * math.pi))
                    gelu_ref[at, columns] = (upper * cdf).astype(bf16)
                    slope_ref[at, columns] = (cdf + upper * pdf).astype(bf16)

            loop(ff // D, part)

        loop(rows // SEG, block)

    return call(
        kernel,
        "expand",
        (
            shape_of((rows, D), f32),
            shape_of((rows, LANES), f32),
            shape_of((rows, D), bf16),
            shape_of((rows, ff), bf16),
            shape_of((rows, ff), bf16),
        ),
        [VMEM] * 5,
    )(att, tokens, w_out, w_up, small)


def contract(ids, gelu, hat1, cotangent, w_down, small):
    rows, ff = gelu.shape

    def kernel(ids_ref, gelu_ref, hat1_ref, cot_ref, w_ref, small_ref,
               out_ref, dres_ref, dlow_ref, dlow_half_ref, sums_ref):
        sums_ref[...] = jnp.zeros_like(sums_ref)

        def block(i):
            at = rows_at(i)
            normed = hat1_ref[at, :] * small_ref[GAIN1 : GAIN1 + 1, :]
            normed += small_ref[BIAS1 : BIAS1 + 1, :]
            resid = normed + dot(gelu_ref[at, :], w_ref[...]) + small_ref[B_DOWN : B_DOWN + 1, :]
            hat, inv = standardize(resid)
            gain = small_ref[GAIN2 : GAIN2 + 1, :]
            out_ref[at, :] = (hat * gain + small_ref[BIAS2 : BIAS2 + 1, :]).astype(bf16)
            cot = cot_ref[at, :].astype(f32)
            sums_ref[GAIN2 : GAIN2 + 1, :] += jnp.sum(cot * hat, axis=0, keepdims=True)
            sums_ref[BIAS2 : BIAS2 + 1, :] += jnp.sum(cot, axis=0, keepdims=True)
            d_res = standardize_back(cot * gain, hat, inv)
            dres_ref[at, :] = d_res
            d_low = d_res.astype(bf16)
            dlow_ref[at, :] = d_low
            sums_ref[B_DOWN : B_DOWN + 1, :] += jnp.sum(d_low.astype(f32), axis=0, keepdims=True)
            theirs = 1 - ids_ref[0]
            dlow_half_ref[at, :] = dlow_ref[
                at, pl.ds(pl.multiple_of(theirs * (D // 2), 128), D // 2)
            ]

        loop(rows // SEG, block)

    return call(
        kernel,
        "contract",
        (
            shape_of((rows, D), bf16),
            shape_of((rows, D), f32),
            shape_of((rows, D), bf16),
            shape_of((rows, D // 2), bf16),
            shape_of((16, D), f32),
        ),
        [SMEM] + [VMEM] * 5,
    )(ids, gelu, hat1, cotangent, w_down, small)


def turn(ids, d_lower, slope, w_down, sums):
    rows, ff = slope.shape

    def kernel(ids_ref, dlow_ref, slope_ref, w_ref, sums_in_ref, dup_ref, dup_half_ref, sums_ref):
        sums_ref[...] = sums_in_ref[...]

        def block(i):
            at = rows_at(i)

            def part(m):
                for c in range(3):
                    columns = pl.ds(pl.multiple_of(m * D + 256 * c, 256), 256)
                    d_up = dot_nt(dlow_ref[at, :], w_ref[columns, :])
                    d_up = (d_up * slope_ref[at, columns].astype(f32)).astype(bf16)
                    dup_ref[at, columns] = d_up
                    sums_ref[pl.ds(B_UP + m, 1), 256 * c : 256 * (c + 1)] += jnp.sum(
                        d_up.astype(f32), axis=0, keepdims=True
                    )

            loop(ff // D, part)
            theirs = 1 - ids_ref[0]
            dup_half_ref[at, :] = dup_ref[
                at, pl.ds(pl.multiple_of(theirs * (ff // 2), 128), ff // 2)
            ]

        loop(rows // SEG, block)

    return call(
        kernel,
        "turn",
        (
            shape_of((rows, ff), bf16), shape_of((rows, ff // 2), bf16), shape_of((16, D), f32),
        ),
        [SMEM] + [VMEM] * 4,
    )(ids, d_lower, slope, w_down, sums)


def back_to_heads(ids, d_upper, d_res2, hat1, inv1, rden, att, q, cos, sin, w_out, w_up, small,
                  sums, fsdp):
    rows, ff = d_upper.shape
    segs = rows // SEG

    def kernel(ids_ref, dup_ref, dres_ref, hat_ref, inv_ref, rden_ref, att_ref, q_ref, cos_ref,
               sin_ref, out_w_ref, up_ref, small_ref, sums_in_ref,
               dres1_ref, dmix_ref, dmix_half_ref, dnum_ref, dden_ref, sums_ref, *refs):
        inc_refs, (state_scr, norm_scr) = refs[:-2], refs[-2:]
        sums_ref[...] = sums_in_ref[...]
        share = D // fsdp
        for j in range(fsdp):
            for c in range(ff // D):
                at = (j * (ff // D) + c) * share
                m, lane = B_UP + at // D, at % D
                sums_ref[B_UP + c : B_UP + c + 1, share * j : share * (j + 1)] = sums_in_ref[
                    m : m + 1, lane : lane + share
                ]
        norm_scr[...] = jnp.zeros_like(norm_scr)
        ones = head_ones()
        twice = jnp.concatenate([ones, ones], axis=0)

        def block(i):
            at = rows_at(i)
            d_normed = dres_ref[at, :] + dot_nt(dup_ref[at, :], up_ref[...])
            hat = hat_ref[at, :]
            sums_ref[GAIN1 : GAIN1 + 1, :] += jnp.sum(d_normed * hat, axis=0, keepdims=True)
            sums_ref[BIAS1 : BIAS1 + 1, :] += jnp.sum(d_normed, axis=0, keepdims=True)
            d_res = standardize_back(
                d_normed * small_ref[GAIN1 : GAIN1 + 1, :], hat, inv_ref[at, 0:1]
            )
            dres1_ref[at, :] = d_res
            d_mix = d_res.astype(bf16)
            dmix_ref[at, :] = d_mix
            sums_ref[B_OUT : B_OUT + 1, :] += jnp.sum(d_mix.astype(f32), axis=0, keepdims=True)
            d_att = dot_nt(d_mix, out_w_ref[:, OUT_AT : OUT_AT + D])
            inverse = rden_ref[at, :]
            dnum_ref[at, :] = (d_att * inverse).astype(bf16)
            along = d_att * att_ref[at, :].astype(f32)
            for p in range(PAIRS):
                lanes = slice(LANES * p, LANES * (p + 1))
                high = along[:, lanes].astype(bf16)
                rest = (along[:, lanes] - high.astype(f32)).astype(bf16)
                total = dot(jnp.concatenate([high, rest], axis=1), twice)
                dden_ref[at, lanes] = -total * inverse[:, lanes]
            theirs = 1 - ids_ref[0]
            dmix_half_ref[at, :] = dmix_ref[
                at, pl.ds(pl.multiple_of(theirs * (D // 2), 128), D // 2)
            ]
            store_states(i, ids_ref[2], q_ref, dnum_ref, dden_ref, cos_ref, sin_ref, state_scr,
                         norm_scr, inc_refs)

        loop(segs, block)

    return call(
        kernel,
        "back_to_heads",
        (
            shape_of((rows, D), f32),
            shape_of((rows, D), bf16),
            shape_of((rows, D // 2), bf16),
            shape_of((rows, D), bf16),
            shape_of((rows, D), f32),
            shape_of((16, D), f32),
        )
        + piece_shapes(fsdp, segs),
        [SMEM] + [VMEM] * 13,
        state_scratch(fsdp),
    )(ids, d_upper, d_res2, hat1, inv1, rden, att, q, cos, sin, w_out, w_up, small, sums)


def intra_backward(ids, q, k, v, d_num, d_den, cos, sin, wave, wave_t, far, near):
    rows = q.shape[0]
    fsdp = 2 * len(far)

    def kernel(ids_ref, q_ref, k_ref, v_ref, dnum_ref, dden_ref, cos_ref, sin_ref, wave_ref,
               wave_t_ref, *refs):
        far_refs, near_ref = refs[: fsdp // 2], refs[fsdp // 2]
        dq_ref, dq_half_ref, dk_ref, dv_ref, state_scr, norm_scr = refs[fsdp // 2 + 1 :]
        masks = head_masks(SEG)
        lane = lax.broadcasted_iota(jnp.int32, (SEG, LANES), 1) % HD
        picks = [jnp.where(lane < 2, m.astype(f32), 0.0).astype(bf16) for m in masks]

        def segment(s):
            at = rows_at(s)
            load_states(s, ids_ref[2], far_refs, near_ref, state_scr, norm_scr)
            cosine, sine = cos_ref[at, :], sin_ref[at, :]

            def pair(p):
                lanes = lanes_at(p)
                qs, ks, vs = q_ref[at, lanes], k_ref[at, lanes], v_ref[at, lanes]
                dn, dd = dnum_ref[at, lanes], dden_ref[at, lanes]
                high = dd.astype(bf16).astype(f32)
                spread = jnp.where(lane == 0, high, jnp.where(lane == 1, dd - high, 0.0))
                grads = jnp.concatenate([dn, spread.astype(bf16)], axis=1)
                w_ts, d_ss, d_ts, khs, qhs, dns = [], [], [], [], [], []
                for m, pick in zip(masks, picks):
                    kh = ks * m
                    values = jnp.concatenate([vs * m, pick], axis=1)
                    w_ts.append((dot_nt(kh, qs) * wave_t_ref[...]).astype(bf16))
                    d_ss.append((dot_nt(grads, values) * wave_ref[...]).astype(bf16))
                    d_ts.append((dot_nt(values, grads) * wave_t_ref[...]).astype(bf16))
                    khs.append(kh)
                    qhs.append(qs * m)
                    dns.append(dn * m)

                def both(left, right):
                    return dot(jnp.concatenate(left, axis=1), jnp.concatenate(right, axis=0))

                dk_ref[at, lanes] = both(d_ts, qhs)
                dv_ref[at, lanes] = both(w_ts, dns)
                d_q = both(d_ss, khs)
                cos_part, sin_part, norm_cos, norm_sin = pair_state(p, state_scr, norm_scr, fsdp)
                d_q += cosine * (dot_nt(dn, cos_part) + dd * norm_cos)
                d_q += sine * (dot_nt(dn, sin_part) + dd * norm_sin)
                dq_ref[at, lanes] = jnp.where(qs.astype(f32) > 0.0, d_q, 0.0).astype(bf16)

            loop(PAIRS, pair)
            theirs = 1 - ids_ref[0]
            dq_half_ref[at, :] = dq_ref[at, pl.ds(pl.multiple_of(theirs * (D // 2), 128), D // 2)]

        loop(rows // SEG, segment)

    return call(
        kernel,
        "intra_backward",
        (
            shape_of((rows, D), bf16),
            shape_of((rows, D // 2), bf16),
            shape_of((rows, D), f32),
            shape_of((rows, D), f32),
        ),
        [SMEM] + [VMEM] * (10 + fsdp // 2),
        state_scratch(fsdp),
    )(ids, q, k, v, d_num, d_den, cos, sin, wave, wave_t, *far, near)


def inter_backward(ids, k, v, d_k, d_v, cos, sin, far, near):
    rows = k.shape[0]
    fsdp = 2 * len(far)

    def kernel(ids_ref, k_ref, v_ref, dk_ref, dv_ref, cos_ref, sin_ref, *refs):
        far_refs, near_ref = refs[: fsdp // 2], refs[fsdp // 2]
        out_ref, state_scr, norm_scr = refs[fsdp // 2 + 1 :]
        core = ids_ref[0]

        def segment(s):
            at = rows_at(s)
            load_states(s, ids_ref[2], far_refs, near_ref, state_scr, norm_scr)
            cosine, sine = cos_ref[at, :], sin_ref[at, :]

            def pair(p):
                lanes = lanes_at(p)
                cos_part, sin_part, norm_cos, norm_sin = pair_state(p, state_scr, norm_scr, fsdp)
                ks = k_ref[at, lanes].astype(f32)
                vs = v_ref[at, lanes]
                d_k = dk_ref[at, lanes]
                d_k += cosine * (dot_nt(vs, cos_part) + norm_cos)
                d_k += sine * (dot_nt(vs, sin_part) + norm_sin)
                feats = jnp.concatenate(
                    [(ks * cosine).astype(bf16), (ks * sine).astype(bf16)], axis=1
                )
                d_v = dv_ref[at, lanes]
                d_v += dot(feats, jnp.concatenate([cos_part, sin_part], axis=0))
                out_ref[core, at, lanes] = jnp.where(ks > 0.0, d_k, 0.0).astype(bf16)
                out_ref[1 - core, at, lanes] = d_v.astype(bf16)

            loop(PAIRS, pair)

        loop(rows // SEG, segment)

    return call(
        kernel,
        "inter_backward",
        shape_of((2, rows, D), bf16),
        [SMEM] + [VMEM] * (7 + fsdp // 2),
        state_scratch(fsdp),
    )(ids, k, v, d_k, d_v, cos, sin, *far, near)


def input_grad(ids, d_q, d_kv, d_res1, w_q, w_kv):
    rows = d_q.shape[0]

    def kernel(ids_ref, dq_ref, dkv_ref, dres_ref, w_q_ref, w_kv_ref, out_ref):
        core = ids_ref[0]

        def block(i):
            at = rows_at(i)
            total = dres_ref[at, :] + dot_nt(dq_ref[at, :], w_q_ref[:, :D])
            total += dot_nt(dkv_ref[core, at, :], w_kv_ref[:, :D])
            total += dot_nt(dkv_ref[1 - core, at, :], w_kv_ref[:, D:])
            out_ref[at, :] = total

        loop(rows // SEG, block)

    return call(
        kernel, "input_grad", shape_of((rows, D), f32), [SMEM] + [VMEM] * 5
    )(ids, d_q, d_kv, d_res1, w_q, w_kv)


def reversed_bits(index, bits):
    total = 0
    for b in range(bits):
        total = total + (((index >> b) & 1) << (bits - 1 - b))
    return total


def weight_grad(ids, products, fsdp, splits, key, own_half=True, sums=None):
    height = products[0][0].shape[1]
    widths = [product[3].shape[1] for product in products]
    block = height // fsdp
    bits = fsdp.bit_length() - 1
    share = block // len(splits)
    group = block if block % 128 == 0 else height
    extra = [] if sums is None else [sums]

    def kernel(ids_ref, *refs):
        ins, out_refs = refs[: 4 * len(products)], refs[4 * len(products) + len(extra) :]

        def part(i):
            columns = pl.ds(pl.multiple_of(i * group, 128), group)

            def store(total, left):
                right = left + total.shape[1]
                for j in range(group // block):
                    place = reversed_bits((i * (group // block) + j) ^ ids_ref[2], bits)
                    for n, (split, out_ref) in enumerate(zip(splits, out_refs)):
                        strip = share // split
                        for h in range(split):
                            row = block * j + share * n + strip * h
                            half = h ^ ids_ref[1] if split > 1 else 0
                            out_ref[half, place, :, left:right] = total[
                                row : row + strip, :
                            ].astype(bf16)

            left = 0
            for n, width in enumerate(widths):
                a0_ref, a1_ref, b0_ref, b1_ref = ins[4 * n : 4 * n + 4]
                first = pl.multiple_of(ids_ref[0] * width, 128) if own_half else 0
                total = dot_tn(a0_ref[:, columns], b0_ref[:, pl.ds(first, width)])
                store(total + dot_tn(a1_ref[:, columns], b1_ref[...]), left)
                left += width
            if extra:
                tall = jnp.concatenate(
                    [refs[4 * len(products)][...], jnp.zeros((LANES - 16, height), f32)], axis=0
                )
                store(tall.T, left)

        loop(height // group, part)

    width = sum(widths) + LANES * len(extra)
    return call(
        kernel,
        "weight_grad",
        tuple(shape_of((n, fsdp, share // n, width), bf16) for n in splits),
        [SMEM] + [VMEM] * (4 * len(products) + len(extra)),
        cost=COSTS[key],
    )(ids, *(x for product in products for x in product), *extra)


def add_low(a, b):
    return (a.astype(f32) + b.astype(f32)).astype(bf16)


def core_stage(x):
    (other,) = yield [(x, "group", 0)]
    return other


def halving_stages(keep, send, bits):
    for axis, bit in bits:
        (received,) = yield [(send, axis, bit)]
        half = keep.shape[0] // 2
        if half == 0:
            return add_low(keep[0], received[0])
        keep, send = add_low(keep[:half], received[:half]), add_low(keep[half:], received[half:])


def reduce_stages(x, core, large=False):
    half = x.shape[1] // 2
    bits = axis_bits("fsdp")
    keep, send = x[0, :half], x[0, half:]
    if large and half > 1:
        quarter = half // 2
        axis, bit = bits.pop(0)
        (received,) = yield [(send[quarter:], axis, bit)]
        after = add_low(keep[quarter:], received)
        (received,) = yield [(tie(send[:quarter], after), axis, bit)]
        keep = add_low(keep[:quarter], received)
        send = tie(after, keep)
    x = yield from halving_stages(keep, send, bits)
    for axis, bit in axis_bits("group")[1:]:
        (received,) = yield [(x, axis, bit)]
        x = add_low(x, received)
    other = yield from core_stage(x)
    return ordered(x, other, core == 0, -1).astype(f32)


def share_stages(x, core, chip):
    axis, bit = axis_bits("group")[1]
    half = x.shape[1] // 2
    (received,) = yield [(x[1], axis, bit)]
    keep, send = add_low(x[0, :half], received[:half]), add_low(x[0, half:], received[half:])
    x = yield from halving_stages(keep, send, axis_bits("fsdp"))
    (other,) = yield [(x, axis, bit)]
    x = ordered(x, other, chip == 0, 0)
    other = yield from core_stage(x)
    return ordered(x, other, core == 0, -1).astype(f32)


def ordered(x, other, first, axis):
    return jnp.concatenate([jnp.where(first, x, other), jnp.where(first, other, x)], axis=axis)


def ancestor_matrix(parents):
    count = parents.shape[0]
    columns = jnp.arange(count, dtype=jnp.int32)
    step = (parents[:, None] == columns[None, :]).astype(f32)
    same = (columns[:, None] == columns[None, :]).astype(f32)
    reached = step + same
    for _ in range(4):
        reached = (jnp.dot(reached, reached, preferred_element_type=f32) > 0.0).astype(f32)
    return reached - same


def spread_rows(matrix):
    count = matrix.shape[0]
    row = jnp.arange(8 * count, dtype=jnp.int32)
    pick = (row[:, None] // 8 == jnp.arange(count, dtype=jnp.int32)[None, :]).astype(f32)
    wide = jnp.dot(jnp.dot(pick, matrix), pick.T)
    return jnp.where(row[:, None] % 8 == row[None, :] % 8, wide, 0.0).astype(bf16)


def waves(local, segs):
    depth = jnp.sum(local[:segs], axis=1)
    angle = (depth[:, None] * SEG + jnp.arange(SEG, dtype=f32)[None, :]) * (
        math.pi / (2.0 * HORIZON)
    )
    angle = jnp.broadcast_to(angle.reshape(segs * SEG, 1), (segs * SEG, LANES))
    return jnp.cos(angle), jnp.sin(angle)


def gap_wave(position):
    gap = position[:, None] - position[None, :]
    wave = jnp.cos(gap.astype(f32) * (math.pi / (2.0 * HORIZON)))
    return jnp.where(gap >= 0, wave, 0.0), jnp.where(gap <= 0, wave, 0.0)


def vector_columns(vectors):
    return jnp.pad(jnp.stack(vectors), ((0, LANES - len(vectors)), (0, 0))).T


def wide_row(shard, rows):
    return jnp.pad(shard[None], ((0, rows - 1), (0, LANES - shard.shape[0])))


def vector_rows(weight, rows, share, longer):
    per = D // share

    def kernel(w_ref, out_ref):
        out_ref[...] = jnp.zeros_like(out_ref)
        turned = w_ref[:, D:OUT_AT].astype(f32).T
        out_ref[:B_UP, :] = turned[:B_UP, :]
        for block in range(longer * per):
            m, lane = B_UP + block // per, share * (block % per)
            first = rows * block // 8 * 8
            tile = w_ref[first : first + 8, OUT_AT + D :].astype(f32)
            row = rows * block - first
            out_ref[m : m + 1, lane : lane + share] = tile[row : row + 1, :share]

    return call(kernel, "vector_rows", shape_of((16, D), f32), [VMEM])(weight)


def body(
    tokens, cotangent, parent_seg, w_qkv, w_out, b_out, norm1_gain, norm1_bias, w_up, b_up,
    w_down, b_down, norm2_gain, norm2_bias,
):
    fsdp = lax.axis_size("fsdp")
    chips = lax.axis_size("group") // 2
    own = lax.axis_index("fsdp")
    group = lax.axis_index("group")
    core, chip = group % 2, group // 2
    rows = tokens.shape[0]
    segs = rows // SEG
    ff = w_up.shape[1]
    ids = jnp.stack([core, chip, own]).astype(jnp.int32)

    pipe = Pipeline()
    pipe.add("kv", gather_stages(w_qkv[:, D:]))
    pipe.add("tokens", core_stage(tokens))
    pipe.slot()
    pipe.slot(only=("kv",))
    begun = pipe.started[0]
    tokens_other = pipe.read("tokens", begun)

    ancestry = ancestor_matrix(tie(parent_seg[0], begun))
    count = parent_seg.shape[1]
    place = jnp.arange(count, dtype=jnp.int32)
    there = (own ^ (place // segs)) * segs + place % segs
    select = (there[:, None] == place[None, :]).astype(f32)
    local = jnp.dot(jnp.dot(select, ancestry), select.T)
    from_ancestors, from_descendants = spread_rows(local), spread_rows(local.T)
    cos, sin = waves(local, segs)
    wave, wave_t = gap_wave(tie(jnp.arange(SEG, dtype=jnp.int32), begun))
    shard_rows = w_qkv.shape[0]
    columns = vector_columns((b_out, norm1_gain, norm1_bias, b_down, norm2_gain, norm2_bias))
    pipe.add("qo", gather_stages(tie(
        jnp.concatenate([w_qkv[:, :D], columns, w_out, wide_row(b_up, shard_rows)], axis=1), begun
    )))
    pipe.add("up", gather_stages(w_up))
    pipe.add("down", gather_stages(w_down))
    pipe.slot(only=("kv",))
    pipe.slot(*pipe.started, only=("qo",))
    pipe.slot(only=("kv",))
    pipe.slot(*pipe.started, only=("qo",))
    pipe.slot(*pipe.started, only=("up",))
    pipe.slot(only=("kv", "qo"))
    pipe.slot(*pipe.started, only=("up",))
    w_kv = assemble(*pipe.finish("kv", only=("kv",)))
    tables = (from_ancestors, from_descendants, wave, wave_t)
    k, v, increments = project(
        ids, tie(tokens, tokens_other, *tables, *pipe.started), w_kv, cos, sin, fsdp
    )
    pipe.arrive(k, only=("qo",))
    pipe.add("state", trade_stages(increments))
    pipe.slot(*pipe.started, only=("state", "qo"))
    pipe.slot(only=("state", "qo"))
    pipe.slot(*pipe.started, only=("up",))
    w_qo = assemble(*pipe.finish("qo", only=("qo",)))
    pipe.slot(w_qo, only=("down",))
    q, num, den = intra_forward(tie(tokens, *pipe.started), w_qo, k, v, wave)
    far, near = pipe.finish("state", q, only=("state",))
    mixed = mix_segments(from_ancestors, far, near)
    pipe.arrive(q, only=("up", "down"))
    pipe.add("path", trade_stages(mixed))
    pipe.slot(*pipe.started, only=("path", "up"))
    small = vector_rows(tie(w_qo, *pipe.started), shard_rows, b_up.shape[0], ff // D)
    pipe.slot(small, only=("path", "down"))
    pipe.slot(*pipe.started, only=("up",))
    w_up_full = assemble(*pipe.finish("up", only=("up",)))
    path = pipe.finish("path", w_up_full, only=("path",))
    pipe.slot(path[1], only=("down",))
    att, rden = inter_forward(ids, tie(q, *pipe.started), num, den, cos, sin, *path)
    pipe.slot(att, only=("down",))
    pipe.add("att", core_stage(att))
    pipe.slot(*pipe.started, only=("att",))
    att_other = pipe.read("att", *pipe.started)
    hat1, inv1, low1, gelu, slope = expand(
        tie(att, *pipe.started), tokens, w_qo, w_up_full, small
    )
    pipe.slot(low1, only=("down",))
    w_down_full = assemble(*pipe.finish("down", only=("down",)))
    pipe.add("gelu", core_stage(gelu))
    pipe.add("low1", core_stage(low1))
    pipe.slot(w_down_full, only=("gelu", "low1"))
    output, d_res2, d_lower, d_lower_half, sums = contract(
        ids, gelu, hat1, cotangent, w_down_full, small
    )
    low1_other = pipe.read("low1", d_lower)
    gelu_other = pipe.read("gelu", d_lower)
    grads = Pipeline()
    grads.add("d_lower", core_stage(d_lower_half))
    grads.slot(low1_other, gelu_other)
    d_upper, d_upper_half, sums = turn(
        ids, tie(d_lower, *grads.started), slope, w_down_full, sums
    )
    d_lower_other = grads.read("d_lower", d_upper)
    grads.add("d_upper", core_stage(d_upper_half))
    grads.slot(d_lower_other, only=("d_upper",))
    two = chips == 2

    def reduction(part):
        return share_stages(part, core, chip) if two else reduce_stages(part, core)

    split = 2 if two else 1
    (down_part,) = weight_grad(
        ids, [(gelu, gelu_other, tie(d_lower, *grads.started), d_lower_other)], fsdp, [split],
        "down",
    )
    d_upper_other = grads.read("d_upper", down_part)
    grads.add("down", reduction(down_part))
    grads.slot(d_upper_other, only=("down",))
    (up_part,) = weight_grad(
        ids, [(low1, low1_other, tie(d_upper, *grads.started), d_upper_other)], fsdp, [1], "up",
    )
    grads.add("up", reduce_stages(up_part, core, True))
    grads.slot(only=("up",))
    d_res1, d_mixed, d_mixed_half, d_num, d_den, sums, *back = back_to_heads(
        ids, tie(d_upper, *grads.started), d_res2, hat1, inv1, rden, att, q, cos, sin, w_qo,
        w_up_full, small, sums, fsdp,
    )
    grads.add("state", trade_stages(back))
    grads.slot(only=("state",))
    grads.slot(d_num, only=("up",))
    grads.slot(*grads.started, only=("state",))
    grads.add("d_mixed", core_stage(d_mixed_half))
    grads.slot(*grads.started, only=("d_mixed",))
    grads.slot(*grads.started, only=("down",))
    d_mixed_other = grads.read("d_mixed", *grads.started)
    far, near = grads.finish("state", d_mixed_other, only=("state",))
    mixed = mix_segments(from_descendants, far, near)
    grads.arrive(*mixed, only=("up",))
    grads.add("path", trade_stages(mixed))
    grads.slot(*grads.started, only=("path",))
    d_q, d_q_half, d_k, d_v = intra_backward(
        ids, tie(q, *grads.started), k, v, d_num, d_den, cos, sin, wave, wave_t, *path
    )
    grads.add("d_q", core_stage(d_q_half))
    grads.arrive(d_q, only=("down",))
    grads.slot(*grads.started, only=("path", "d_q"))
    grads.slot(*grads.started, only=("up",))
    d_q_other = grads.read("d_q", *grads.started)
    (outq_part,) = weight_grad(
        ids,
        [
            (att, att_other, d_mixed, d_mixed_other),
            (tokens, tokens_other, d_q, d_q_other),
        ],
        fsdp, [split], "outq", sums=sums,
    )
    grads.add("outq", reduction(outq_part))
    grads.slot(only=("outq",))
    back = grads.finish("path", *grads.started, only=("path",))
    d_kv = inter_backward(ids, k, v, d_k, d_v, cos, sin, *back)
    grads.add("d_kv", core_stage(d_kv[1]))
    grads.slot(only=("d_kv",))
    grads.slot(*grads.started, only=("down",))
    grads.arrive(*grads.started, only=("up",))
    d_kv_other = grads.read("d_kv", *grads.started)
    kv_parts = weight_grad(
        ids, [(tokens, tokens_other, d_kv[0], d_kv_other)], fsdp, [2, 1] if two else [1], "kv",
        False,
    )
    grads.add("kv0", reduction(kv_parts[0]))
    for part in kv_parts[1:]:
        grads.add("kv1", reduce_stages(part, core))
    for step in TAIL:
        if step == "grad":
            tokens_grad = input_grad(ids, d_q, tie(d_kv, *grads.started), d_res1, w_qo, w_kv)
            grads.started = (tokens_grad,)
        elif grads.names(step.split("+")):
            grads.slot(*grads.started, only=step.split("+"))
    while grads.running:
        grads.slot(*grads.started)
    done = grads.finished
    kv_grad = jnp.concatenate([done[n] for n in ("kv0", "kv1") if n in done], axis=0)
    ours, others = jnp.split(done["outq"], 2, axis=1)
    half = D // 2
    sums = ours[:, D : D + 16] + others[:, D : D + 16]
    return (
        output,
        tokens_grad,
        jnp.concatenate([ours[:, half:D], others[:, half:D], kv_grad], axis=1),
        jnp.concatenate([ours[:, :half], others[:, :half]], axis=1),
        sums[:, B_OUT],
        sums[:, GAIN1],
        sums[:, BIAS1],
        done["up"],
        sums[:, B_UP : B_UP + ff // D].T.reshape(-1),
        done["down"],
        sums[:, B_DOWN],
        sums[:, GAIN2],
        sums[:, BIAS2],
    )


def solution(mesh):
    both = ("group", "fsdp")
    matrix, vector = P(both, None), P(both)
    in_specs = (
        matrix, matrix, P("group", None), matrix, matrix, vector, vector, vector, matrix, vector,
        matrix, vector, vector, vector,
    )
    rows, line = P("fsdp", None), P("fsdp")
    out_specs = (
        matrix, matrix, rows, rows, line, line, line, rows, line, rows, line, line, line,
    )
    return jax.shard_map(body, mesh=mesh, in_specs=in_specs, out_specs=out_specs, check_vma=False)
```

```python
import math

import jax
import jax.numpy as jnp
from jax import lax
from jax.experimental import pallas as pl
from jax.experimental.pallas import tpu as pltpu
from jax.sharding import PartitionSpec as P

D = 768
H = 12
HD = 64
SEG = 256
HORIZON = 2560
PAIRS = H // 2
LANES = 2 * HD
EPS = 1e-05

f32 = jnp.float32
bf16 = jnp.bfloat16

B_OUT, GAIN1, BIAS1, B_DOWN, GAIN2, BIAS2, B_UP = range(7)
OUT_AT = D + LANES


def exchange(x, axis, *bits):
    size, offset = lax.axis_size(axis), sum(1 << b for b in bits)
    return lax.ppermute(x, axis, [(i, i ^ offset) for i in range(size)])


def axis_bits(axis):
    return [(axis, b) for b in range(lax.axis_size(axis).bit_length() - 1)]


def tie(x, *others):
    return lax.optimization_barrier((x,) + others)[0]


def trade_stages(pieces):
    bits = axis_bits("fsdp")[1:]
    requests = []
    for m in range(1, len(pieces)):
        requests.append((pieces[m], "fsdp") + tuple(b for n, (_, b) in enumerate(bits) if m >> n & 1))
    arrived = yield requests
    far = [pieces[0]] + list(arrived)
    (near,) = yield [(jnp.concatenate([x[1:] for x in far], axis=0), "fsdp", 0)]
    return far, near


def near_steps(first_low):
    low, high = axis_bits("fsdp")[:1], axis_bits("group")[1:]
    return low + high if first_low else high + low


def moved(masks, axis, bit):
    step = (1 << bit) * (lax.axis_size("fsdp") if axis == "group" else 1)
    return tuple(m ^ step for m in masks)


def gather_stages(shard, early=False):
    lin = lax.axis_index("group") * lax.axis_size("fsdp") + lax.axis_index("fsdp")
    rows, columns = shard.shape
    if rows % 8:
        whole = lax.all_gather(shard, ("group", "fsdp"), axis=0, tiled=True)
        merged = rows
        while merged % 8:
            merged *= 2
        blocks = whole.reshape(-1, merged, columns)
        yield []
        return [[(blocks, tuple(range(blocks.shape[0])))]], jnp.zeros_like(lin)
    blocks, masks = shard[None], (0,)
    for axis, bit in reversed(axis_bits("fsdp")[1:]):
        (other,) = yield [(blocks, axis, bit)]
        blocks = jnp.concatenate([blocks, other], axis=0)
        masks = masks + moved(masks, axis, bit)
    half = columns // 2
    sides = [(blocks[:, :, :half], masks), (blocks[:, :, half:], masks)]
    steps = [near_steps(True), near_steps(False)]
    for n in range(len(steps[0]) - 1):
        others = yield [(b,) + st[n] for (b, _), st in zip(sides, steps)]
        sides = [
            (jnp.concatenate([b, o], axis=0), m + moved(m, *st[n]))
            for (b, m), st, o in zip(sides, steps, others)
        ]
    core = ("group", 0)
    others = yield [(b,) + st[-1] for (b, _), st in zip(sides, steps)] + (
        [(b,) + core for b, _ in sides] if early else []
    )
    parts = []
    if early:
        lasts = yield [(o,) + core for o in others[:2]]
        for n, ((b, m), st) in enumerate(zip(sides, steps)):
            there = moved(m, *st[-1])
            parts.append([
                (b, m), (others[n], there), (others[n + 2], moved(m, *core)),
                (lasts[n], moved(there, *core)),
            ])
        return parts, lin
    sides = [
        (jnp.concatenate([b, o], axis=0), m + moved(m, *st[-1]))
        for (b, m), st, o in zip(sides, steps, others)
    ]
    lasts = yield [(b,) + core for b, _ in sides]
    return [[(b, m), (last, moved(m, *core))] for (b, m), last in zip(sides, lasts)], lin


class Pipeline:
    def __init__(self):
        self.running = {}
        self.waiting = {}
        self.finished = {}
        self.started = ()

    def add(self, name, stages):
        self.running[name] = (stages, None)

    def names(self, only):
        return [n for n in self.running if only is None or n in only]

    def arrive(self, *others, only=None):
        names = [n for n in self.names(only) if n not in self.waiting]
        arrived = [x for n in names for x in self.running[n][1] or ()]
        if arrived:
            arrived = lax.optimization_barrier(tuple(arrived) + others)[: len(arrived)]
        at, ready = 0, ()
        for n in names:
            stages, results = self.running.pop(n)
            count = len(results or ())
            mine, at = arrived[at : at + count], at + count
            try:
                wanted = next(stages) if results is None else stages.send(mine)
            except StopIteration as done:
                self.finished[n] = done.value
            else:
                self.running[n] = (stages, ())
                self.waiting[n] = wanted
                ready += tuple(w[0] for w in wanted)
        self.started = ready or self.started

    def slot(self, *others, only=None):
        self.arrive(*others, only=only)
        requests = [(n, w) for n in self.names(only) for w in self.waiting.pop(n)]
        operands = tuple(w[0] for _, w in requests)
        if operands and others:
            operands = lax.optimization_barrier(operands + others)[: len(operands)]
        self.started = operands or self.started
        for x, (n, (_, axis, *bits)) in zip(operands, requests):
            stages, results = self.running[n]
            self.running[n] = (stages, results + (exchange(x, axis, *bits),))

    def read(self, name, *others):
        self.arrive(*others, only=(name,))
        return self.finished[name]

    def finish(self, name, *others, only=None):
        while name not in self.finished:
            self.slot(*others, only=only)
        return self.finished[name]


VMEM = pl.BlockSpec(memory_space=pltpu.VMEM)
SMEM = pl.BlockSpec(memory_space=pltpu.SMEM)


COSTS = {"assemble": 1.5, "project": 10.8, "mix_segments": 1.1, "intra_forward": 5.9, "inter_forward": 16.5, "expand": 0.285, "contract": 6.0, "turn": 22.5, "back_to_heads": 11.8, "intra_backward": 10.3, "inter_backward": 4.6, "input_grad": 4.0, "vector_rows": 1.5, "down": 6.0, "up": 1.2, "outq": 3.36, "kv": 3.36}
TAIL = ('kv0+kv1', 'up', 'grad', 'down', 'outq', 'kv1', 'kv0', 'kv1', 'up', 'outq', 'kv0', 'down', 'outq', 'kv0', 'kv1', 'up', 'outq', 'kv1', 'kv0', 'down', 'outq', 'close', 'kv0', 'kv1', 'outq', 'close', 'kv0', 'kv1')
FLOPS_PER_US = 6.0e8


def call(kernel, name, outs, in_specs, scratch=(), cost=None, mib=5):
    return pl.pallas_call(
        kernel,
        out_shape=outs,
        in_specs=in_specs,
        out_specs=jax.tree.map(lambda _: VMEM, outs),
        scratch_shapes=scratch,
        compiler_params=pltpu.CompilerParams(vmem_limit_bytes=mib * 1024 * 1024),
        cost_estimate=pl.CostEstimate(
            flops=int((cost or COSTS[name]) * FLOPS_PER_US), transcendentals=0, bytes_accessed=0
        ),
        name=name,
    )


def shape_of(shape, dtype):
    return jax.ShapeDtypeStruct(shape, dtype)


def dot(a, b):
    return lax.dot_general(a, b, (((1,), (0,)), ((), ())), preferred_element_type=f32)


def dot_nt(a, b):
    return lax.dot_general(a, b, (((1,), (1,)), ((), ())), preferred_element_type=f32)


def dot_tn(a, b):
    return lax.dot_general(a, b, (((0,), (0,)), ((), ())), preferred_element_type=f32)


def loop(count, body):
    def step(i, carry):
        body(i)
        return carry

    lax.fori_loop(0, count, step, 0)


def rows_at(i):
    return pl.ds(pl.multiple_of(i * SEG, SEG), SEG)


def lanes_at(p):
    return pl.ds(pl.multiple_of(p * LANES, LANES), LANES)


def head_masks(rows):
    lane = lax.broadcasted_iota(jnp.int32, (rows, LANES), 1)
    first = (lane < HD).astype(f32)
    return first.astype(bf16), (1.0 - first).astype(bf16)


def diagonal():
    row = lax.broadcasted_iota(jnp.int32, (LANES, LANES), 0)
    lane = lax.broadcasted_iota(jnp.int32, (LANES, LANES), 1)
    return (row < HD) == (lane < HD)


def head_ones():
    return jnp.where(diagonal(), 1.0, 0.0).astype(bf16)


def split_state(packed):
    same = diagonal()
    cos_part = jnp.where(same, packed, 0.0)
    sin_part = pltpu.roll(jnp.where(same, 0.0, packed), HD, 1)
    return cos_part.astype(bf16), sin_part.astype(bf16)


def state_scratch(fsdp):
    return [pltpu.VMEM((D, LANES), f32), pltpu.VMEM((8 * max(2 * PAIRS, fsdp), LANES), f32)]


def piece_shapes(fsdp, segs):
    return (shape_of((2, segs, D // fsdp + 8, LANES), bf16),) * (fsdp // 2)


def norm_row(n, fsdp):
    per = max(16, fsdp) // fsdp
    return 8 * (n // per) + n % per


def store_states(s, own, left_ref, right_ref, weight_ref, cos_ref, sin_ref, state_scr, norm_scr, out_refs):
    fsdp = 2 * len(out_refs)
    chunk = D // fsdp
    same = diagonal()
    rows = rows_at(s)
    cos, sin = cos_ref[rows, :], sin_ref[rows, :]

    def pair(p):
        lanes = lanes_at(p)
        a = left_ref[rows, lanes]
        b = right_ref[rows, lanes].astype(f32)
        both = jnp.concatenate(
            [(b * cos).astype(bf16), (pltpu.roll(b, HD, 1) * sin).astype(bf16)], axis=1
        )
        product = dot_tn(a, both)
        state_scr[lanes, :] = jnp.where(same, product[:, :LANES], product[:, LANES:])
        wide = a.astype(f32)
        if weight_ref is not None:
            wide = wide * weight_ref[rows, lanes]
        for n, wave in ((p, cos), (PAIRS + p, sin)):
            norm_scr[pl.ds(norm_row(n, fsdp), 1), :] = jnp.sum(wide * wave, axis=0, keepdims=True)

    loop(PAIRS, pair)
    for r in range(fsdp):
        j = own ^ r
        at = pl.ds(pl.multiple_of(chunk * j, 8), chunk)
        norms = pl.ds(pl.multiple_of(8 * j, 8), 8)
        out_refs[r // 2][r % 2, s, 0:chunk, :] = state_scr[at, :].astype(bf16)
        out_refs[r // 2][r % 2, s, chunk : chunk + 8, :] = norm_scr[norms, :].astype(bf16)


def load_states(s, own, far_refs, near_ref, state_scr, norm_scr):
    fsdp = 2 * len(far_refs)
    chunk = D // fsdp
    for r in range(fsdp):
        j = own ^ r
        at = pl.ds(pl.multiple_of(chunk * j, 8), chunk)
        norms = pl.ds(pl.multiple_of(8 * j, 8), 8)
        ref, place = (near_ref, r // 2) if r % 2 else (far_refs[r // 2], 0)
        state_scr[at, :] = ref[place, s, 0:chunk, :].astype(f32)
        norm_scr[norms, :] = ref[place, s, chunk : chunk + 8, :].astype(f32)


def pair_state(p, state_scr, norm_scr, fsdp):
    cos_part, sin_part = split_state(state_scr[lanes_at(p), :])
    norm_cos = norm_scr[pl.ds(norm_row(p, fsdp), 1), :]
    norm_sin = norm_scr[pl.ds(norm_row(PAIRS + p, fsdp), 1), :]
    return cos_part, sin_part, norm_cos, norm_sin


def assemble(parts, lin):
    arrays = [blocks for part in parts for blocks, _ in part]
    places = jnp.concatenate(
        [jnp.array(masks, jnp.int32) for part in parts for _, masks in part]
    ) ^ lin.astype(jnp.int32)
    rows = arrays[0].shape[1]
    count = sum(len(masks) for _, masks in parts[0])
    width = sum(part[0][0].shape[2] for part in parts)
    lefts, left = [], 0
    for part in parts:
        lefts += [left] * len(part)
        left += part[0][0].shape[2]

    def kernel(places_ref, *refs):
        out_ref = refs[-1]
        first = 0
        for ref, at in zip(refs[:-1], lefts):
            number, _, columns = ref.shape

            def place(i, ref=ref, at=at, columns=columns, first=first):
                out_ref[places_ref[first + i], :, at : at + columns] = ref[i]

            loop(number, place)
            first += number

    whole = call(
        kernel, "assemble", shape_of((count, rows, width), bf16), [SMEM] + [VMEM] * len(arrays)
    )(places, *arrays)
    return whole.reshape(count * rows, width)


def project(ids, tokens, w_kv, cos, sin, fsdp):
    rows = tokens.shape[0]
    segs = rows // SEG

    def kernel(ids_ref, tok_ref, w_ref, cos_ref, sin_ref, k_ref, v_ref, *refs):
        inc_refs, (state_scr, norm_scr) = refs[:-2], refs[-2:]
        norm_scr[...] = jnp.zeros_like(norm_scr)

        def segment(s):
            at = rows_at(s)
            x = tok_ref[at, :]
            k_ref[at, :] = jnp.maximum(dot(x, w_ref[:, :D]), 0.0).astype(bf16)
            v_ref[at, :] = dot(x, w_ref[:, D:]).astype(bf16)
            store_states(s, ids_ref[2], k_ref, v_ref, None, cos_ref, sin_ref, state_scr, norm_scr,
                         inc_refs)

        loop(segs, segment)

    act = shape_of((rows, D), bf16)
    k, v, *pieces = call(
        kernel,
        "project",
        (act, act) + piece_shapes(fsdp, segs),
        [SMEM] + [VMEM] * 4,
        state_scratch(fsdp),
    )(ids, tokens, w_kv, cos, sin)
    return k, v, pieces


def mix_segments(spread, far, near):
    fsdp = 2 * len(far)
    _, segs, height, _ = near.shape

    def kernel(spread_ref, *refs):
        far_refs, near_ref, out_refs = refs[: fsdp // 2], refs[fsdp // 2], refs[fsdp // 2 + 1 :]
        for t in range(height // 8):
            at = slice(8 * t, 8 * t + 8)
            stacked = []
            for r in range(fsdp):
                ref, place = (near_ref, r // 2) if r % 2 else (far_refs[r // 2], 0)
                stacked += [ref[place, s, at, :].astype(f32) for s in range(segs)]
            mixed = dot(spread_ref[...], jnp.concatenate(stacked, axis=0).astype(bf16))
            for c in range(fsdp * segs):
                r, s = c // segs, c % segs
                out_refs[r // 2][r % 2, s, at, :] = mixed[8 * c : 8 * c + 8, :].astype(bf16)

    return call(
        kernel, "mix_segments", piece_shapes(fsdp, segs), [VMEM] * (fsdp // 2 + 2)
    )(spread, *far, near)


def intra_forward(tokens, w_q, k, v, wave):
    rows = tokens.shape[0]

    def kernel(tok_ref, w_ref, k_ref, v_ref, wave_ref, q_ref, num_ref, den_ref):
        masks = head_masks(SEG)

        def segment(s):
            at = rows_at(s)
            q_ref[at, :] = jnp.maximum(dot(tok_ref[at, :], w_ref[:, :D]), 0.0).astype(bf16)

            def pair(p):
                lanes = lanes_at(p)
                qs, ks, vs = q_ref[at, lanes], k_ref[at, lanes], v_ref[at, lanes]
                weights, values = [], []
                for m in masks:
                    weights.append((dot_nt(qs, ks * m) * wave_ref[...]).astype(bf16))
                    values.append(jnp.concatenate([vs * m, m], axis=1))
                both = dot(jnp.concatenate(weights, axis=1), jnp.concatenate(values, axis=0))
                num_ref[at, lanes] = both[:, :LANES]
                den_ref[at, lanes] = both[:, LANES:]

            loop(PAIRS, pair)

        loop(rows // SEG, segment)

    wide = shape_of((rows, D), f32)
    return call(
        kernel, "intra_forward", (shape_of((rows, D), bf16), wide, wide), [VMEM] * 5
    )(tokens, w_q, k, v, wave)


def inter_forward(ids, q, num, den, cos, sin, far, near):
    rows = q.shape[0]
    fsdp = 2 * len(far)

    def kernel(ids_ref, q_ref, num_ref, den_ref, cos_ref, sin_ref, *refs):
        far_refs, near_ref = refs[: fsdp // 2], refs[fsdp // 2]
        att_ref, rden_ref, state_scr, norm_scr = refs[fsdp // 2 + 1 :]
        ones = head_ones()
        twice = jnp.concatenate([ones, ones], axis=0)

        def segment(s):
            at = rows_at(s)
            load_states(s, ids_ref[2], far_refs, near_ref, state_scr, norm_scr)

            def pair(p):
                lanes = lanes_at(p)
                cos_part, sin_part, norm_cos, norm_sin = pair_state(p, state_scr, norm_scr, fsdp)
                qs = q_ref[at, lanes].astype(f32)
                q_cos = (qs * cos_ref[at, :]).astype(bf16)
                q_sin = (qs * sin_ref[at, :]).astype(bf16)
                carried = dot(
                    jnp.concatenate([q_cos, q_sin], axis=1),
                    jnp.concatenate([cos_part, sin_part], axis=0),
                )
                along = q_cos.astype(f32) * norm_cos + q_sin.astype(f32) * norm_sin
                high = along.astype(bf16)
                rest = (along - high.astype(f32)).astype(bf16)
                weight = dot(jnp.concatenate([high, rest], axis=1), twice)
                inverse = 1.0 / (den_ref[at, lanes] + weight + 1.0)
                att_ref[at, lanes] = ((num_ref[at, lanes] + carried) * inverse).astype(bf16)
                rden_ref[at, lanes] = inverse

            loop(PAIRS, pair)

        loop(rows // SEG, segment)

    return call(
        kernel,
        "inter_forward",
        (shape_of((rows, D), bf16), shape_of((rows, D), f32)),
        [SMEM] + [VMEM] * (6 + fsdp // 2),
        state_scratch(fsdp),
    )(ids, q, num, den, cos, sin, *far, near)


def standardize(resid):
    centred = resid - jnp.mean(resid, axis=1, keepdims=True)
    inv = lax.rsqrt(jnp.mean(centred * centred, axis=1, keepdims=True) + EPS)
    return centred * inv, inv


def standardize_back(d_hat, hat, inv):
    return inv * (
        d_hat
        - jnp.mean(d_hat, axis=1, keepdims=True)
        - hat * jnp.mean(d_hat * hat, axis=1, keepdims=True)
    )


def expand(att, tokens, w_out, w_up, small):
    rows = att.shape[0]
    ff = w_up.shape[1]

    def kernel(att_ref, tok_ref, out_w_ref, up_ref, small_ref, hat_ref, inv_ref, low_ref, gelu_ref,
               slope_ref):
        def block(i):
            at = rows_at(i)
            mixed = dot(att_ref[at, :], out_w_ref[:, OUT_AT : OUT_AT + D])
            hat, inv = standardize(
                tok_ref[at, :].astype(f32) + mixed + small_ref[B_OUT : B_OUT + 1, :]
            )
            hat_ref[at, :] = hat
            inv_ref[at, :] = jnp.broadcast_to(inv, (SEG, LANES))
            low_ref[at, :] = (
                hat * small_ref[GAIN1 : GAIN1 + 1, :] + small_ref[BIAS1 : BIAS1 + 1, :]
            ).astype(bf16)

            def part(m):
                for c in range(3):
                    columns = pl.ds(pl.multiple_of(m * D + 256 * c, 256), 256)
                    bias = small_ref[pl.ds(B_UP + m, 1), 256 * c : 256 * (c + 1)]
                    upper = dot(low_ref[at, :], up_ref[:, columns]) + bias
                    cdf = 0.5 + 0.5 * lax.erf(upper * math.sqrt(0.5))
                    pdf = jnp.exp(-0.5 * upper * upper) * (1.0 / math.sqrt(2.0 * math.pi))
                    gelu_ref[at, columns] = (upper * cdf).astype(bf16)
                    slope_ref[at, columns] = (cdf + upper * pdf).astype(bf16)

            loop(ff // D, part)

        loop(rows // SEG, block)

    return call(
        kernel,
        "expand",
        (
            shape_of((rows, D), f32),
            shape_of((rows, LANES), f32),
            shape_of((rows, D), bf16),
            shape_of((rows, ff), bf16),
            shape_of((rows, ff), bf16),
        ),
        [VMEM] * 5,
    )(att, tokens, w_out, w_up, small)


def contract(ids, gelu, hat1, cotangent, w_down, small):
    rows, ff = gelu.shape

    def kernel(ids_ref, gelu_ref, hat1_ref, cot_ref, w_ref, small_ref,
               out_ref, dres_ref, dlow_ref, dlow_half_ref, sums_ref):
        sums_ref[...] = jnp.zeros_like(sums_ref)

        def block(i):
            at = rows_at(i)
            normed = hat1_ref[at, :] * small_ref[GAIN1 : GAIN1 + 1, :]
            normed += small_ref[BIAS1 : BIAS1 + 1, :]
            resid = normed + dot(gelu_ref[at, :], w_ref[...]) + small_ref[B_DOWN : B_DOWN + 1, :]
            hat, inv = standardize(resid)
            gain = small_ref[GAIN2 : GAIN2 + 1, :]
            out_ref[at, :] = (hat * gain + small_ref[BIAS2 : BIAS2 + 1, :]).astype(bf16)
            cot = cot_ref[at, :].astype(f32)
            sums_ref[GAIN2 : GAIN2 + 1, :] += jnp.sum(cot * hat, axis=0, keepdims=True)
            sums_ref[BIAS2 : BIAS2 + 1, :] += jnp.sum(cot, axis=0, keepdims=True)
            d_res = standardize_back(cot * gain, hat, inv)
            dres_ref[at, :] = d_res
            d_low = d_res.astype(bf16)
            dlow_ref[at, :] = d_low
            sums_ref[B_DOWN : B_DOWN + 1, :] += jnp.sum(d_low.astype(f32), axis=0, keepdims=True)
            theirs = 1 - ids_ref[0]
            dlow_half_ref[at, :] = dlow_ref[
                at, pl.ds(pl.multiple_of(theirs * (D // 2), 128), D // 2)
            ]

        loop(rows // SEG, block)

    return call(
        kernel,
        "contract",
        (
            shape_of((rows, D), bf16),
            shape_of((rows, D), f32),
            shape_of((rows, D), bf16),
            shape_of((rows, D // 2), bf16),
            shape_of((16, D), f32),
        ),
        [SMEM] + [VMEM] * 5,
    )(ids, gelu, hat1, cotangent, w_down, small)


def turn(ids, d_lower, slope, w_down, sums):
    rows, ff = slope.shape

    def kernel(ids_ref, dlow_ref, slope_ref, w_ref, sums_in_ref, dup_ref, dup_half_ref, sums_ref):
        sums_ref[...] = sums_in_ref[...]

        def block(i):
            at = rows_at(i)

            def part(m):
                for c in range(3):
                    columns = pl.ds(pl.multiple_of(m * D + 256 * c, 256), 256)
                    d_up = dot_nt(dlow_ref[at, :], w_ref[columns, :])
                    d_up = (d_up * slope_ref[at, columns].astype(f32)).astype(bf16)
                    dup_ref[at, columns] = d_up
                    sums_ref[pl.ds(B_UP + m, 1), 256 * c : 256 * (c + 1)] += jnp.sum(
                        d_up.astype(f32), axis=0, keepdims=True
                    )

            loop(ff // D, part)
            theirs = 1 - ids_ref[0]
            dup_half_ref[at, :] = dup_ref[
                at, pl.ds(pl.multiple_of(theirs * (ff // 2), 128), ff // 2)
            ]

        loop(rows // SEG, block)

    return call(
        kernel,
        "turn",
        (
            shape_of((rows, ff), bf16), shape_of((rows, ff // 2), bf16), shape_of((16, D), f32),
        ),
        [SMEM] + [VMEM] * 4,
    )(ids, d_lower, slope, w_down, sums)


def back_to_heads(ids, d_upper, d_res2, hat1, inv1, rden, att, q, cos, sin, w_out, w_up, small,
                  sums, fsdp):
    rows, ff = d_upper.shape
    segs = rows // SEG

    def kernel(ids_ref, dup_ref, dres_ref, hat_ref, inv_ref, rden_ref, att_ref, q_ref, cos_ref,
               sin_ref, out_w_ref, up_ref, small_ref, sums_in_ref,
               dres1_ref, dmix_ref, dmix_half_ref, dnum_ref, dden_ref, sums_ref, *refs):
        inc_refs, (state_scr, norm_scr) = refs[:-2], refs[-2:]
        sums_ref[...] = sums_in_ref[...]
        share = D // fsdp
        for j in range(fsdp):
            for c in range(ff // D):
                at = (j * (ff // D) + c) * share
                m, lane = B_UP + at // D, at % D
                sums_ref[B_UP + c : B_UP + c + 1, share * j : share * (j + 1)] = sums_in_ref[
                    m : m + 1, lane : lane + share
                ]
        norm_scr[...] = jnp.zeros_like(norm_scr)
        ones = head_ones()
        twice = jnp.concatenate([ones, ones], axis=0)

        def block(i):
            at = rows_at(i)
            d_normed = dres_ref[at, :] + dot_nt(dup_ref[at, :], up_ref[...])
            hat = hat_ref[at, :]
            sums_ref[GAIN1 : GAIN1 + 1, :] += jnp.sum(d_normed * hat, axis=0, keepdims=True)
            sums_ref[BIAS1 : BIAS1 + 1, :] += jnp.sum(d_normed, axis=0, keepdims=True)
            d_res = standardize_back(
                d_normed * small_ref[GAIN1 : GAIN1 + 1, :], hat, inv_ref[at, 0:1]
            )
            dres1_ref[at, :] = d_res
            d_mix = d_res.astype(bf16)
            dmix_ref[at, :] = d_mix
            sums_ref[B_OUT : B_OUT + 1, :] += jnp.sum(d_mix.astype(f32), axis=0, keepdims=True)
            d_att = dot_nt(d_mix, out_w_ref[:, OUT_AT : OUT_AT + D])
            inverse = rden_ref[at, :]
            dnum_ref[at, :] = (d_att * inverse).astype(bf16)
            along = d_att * att_ref[at, :].astype(f32)
            for p in range(PAIRS):
                lanes = slice(LANES * p, LANES * (p + 1))
                high = along[:, lanes].astype(bf16)
                rest = (along[:, lanes] - high.astype(f32)).astype(bf16)
                total = dot(jnp.concatenate([high, rest], axis=1), twice)
                dden_ref[at, lanes] = -total * inverse[:, lanes]
            theirs = 1 - ids_ref[0]
            dmix_half_ref[at, :] = dmix_ref[
                at, pl.ds(pl.multiple_of(theirs * (D // 2), 128), D // 2)
            ]
            store_states(i, ids_ref[2], q_ref, dnum_ref, dden_ref, cos_ref, sin_ref, state_scr,
                         norm_scr, inc_refs)

        loop(segs, block)

    return call(
        kernel,
        "back_to_heads",
        (
            shape_of((rows, D), f32),
            shape_of((rows, D), bf16),
            shape_of((rows, D // 2), bf16),
            shape_of((rows, D), bf16),
            shape_of((rows, D), f32),
            shape_of((16, D), f32),
        )
        + piece_shapes(fsdp, segs),
        [SMEM] + [VMEM] * 13,
        state_scratch(fsdp),
    )(ids, d_upper, d_res2, hat1, inv1, rden, att, q, cos, sin, w_out, w_up, small, sums)


def intra_backward(ids, q, k, v, d_num, d_den, cos, sin, wave, wave_t, far, near):
    rows = q.shape[0]
    fsdp = 2 * len(far)

    def kernel(ids_ref, q_ref, k_ref, v_ref, dnum_ref, dden_ref, cos_ref, sin_ref, wave_ref,
               wave_t_ref, *refs):
        far_refs, near_ref = refs[: fsdp // 2], refs[fsdp // 2]
        dq_ref, dq_half_ref, dk_ref, dv_ref, state_scr, norm_scr = refs[fsdp // 2 + 1 :]
        masks = head_masks(SEG)
        lane = lax.broadcasted_iota(jnp.int32, (SEG, LANES), 1) % HD
        picks = [jnp.where(lane < 2, m.astype(f32), 0.0).astype(bf16) for m in masks]

        def segment(s):
            at = rows_at(s)
            load_states(s, ids_ref[2], far_refs, near_ref, state_scr, norm_scr)
            cosine, sine = cos_ref[at, :], sin_ref[at, :]

            def pair(p):
                lanes = lanes_at(p)
                qs, ks, vs = q_ref[at, lanes], k_ref[at, lanes], v_ref[at, lanes]
                dn, dd = dnum_ref[at, lanes], dden_ref[at, lanes]
                high = dd.astype(bf16).astype(f32)
                spread = jnp.where(lane == 0, high, jnp.where(lane == 1, dd - high, 0.0))
                grads = jnp.concatenate([dn, spread.astype(bf16)], axis=1)
                w_ts, d_ss, d_ts, khs, qhs, dns = [], [], [], [], [], []
                for m, pick in zip(masks, picks):
                    kh = ks * m
                    values = jnp.concatenate([vs * m, pick], axis=1)
                    w_ts.append((dot_nt(kh, qs) * wave_t_ref[...]).astype(bf16))
                    d_ss.append((dot_nt(grads, values) * wave_ref[...]).astype(bf16))
                    d_ts.append((dot_nt(values, grads) * wave_t_ref[...]).astype(bf16))
                    khs.append(kh)
                    qhs.append(qs * m)
                    dns.append(dn * m)

                def both(left, right):
                    return dot(jnp.concatenate(left, axis=1), jnp.concatenate(right, axis=0))

                dk_ref[at, lanes] = both(d_ts, qhs)
                dv_ref[at, lanes] = both(w_ts, dns)
                d_q = both(d_ss, khs)
                cos_part, sin_part, norm_cos, norm_sin = pair_state(p, state_scr, norm_scr, fsdp)
                d_q += cosine * (dot_nt(dn, cos_part) + dd * norm_cos)
                d_q += sine * (dot_nt(dn, sin_part) + dd * norm_sin)
                dq_ref[at, lanes] = jnp.where(qs.astype(f32) > 0.0, d_q, 0.0).astype(bf16)

            loop(PAIRS, pair)
            theirs = 1 - ids_ref[0]
            dq_half_ref[at, :] = dq_ref[at, pl.ds(pl.multiple_of(theirs * (D // 2), 128), D // 2)]

        loop(rows // SEG, segment)

    return call(
        kernel,
        "intra_backward",
        (
            shape_of((rows, D), bf16),
            shape_of((rows, D // 2), bf16),
            shape_of((rows, D), f32),
            shape_of((rows, D), f32),
        ),
        [SMEM] + [VMEM] * (10 + fsdp // 2),
        state_scratch(fsdp),
    )(ids, q, k, v, d_num, d_den, cos, sin, wave, wave_t, *far, near)


def inter_backward(ids, k, v, d_k, d_v, cos, sin, far, near):
    rows = k.shape[0]
    fsdp = 2 * len(far)

    def kernel(ids_ref, k_ref, v_ref, dk_ref, dv_ref, cos_ref, sin_ref, *refs):
        far_refs, near_ref = refs[: fsdp // 2], refs[fsdp // 2]
        out_ref, state_scr, norm_scr = refs[fsdp // 2 + 1 :]
        core = ids_ref[0]

        def segment(s):
            at = rows_at(s)
            load_states(s, ids_ref[2], far_refs, near_ref, state_scr, norm_scr)
            cosine, sine = cos_ref[at, :], sin_ref[at, :]

            def pair(p):
                lanes = lanes_at(p)
                cos_part, sin_part, norm_cos, norm_sin = pair_state(p, state_scr, norm_scr, fsdp)
                ks = k_ref[at, lanes].astype(f32)
                vs = v_ref[at, lanes]
                d_k = dk_ref[at, lanes]
                d_k += cosine * (dot_nt(vs, cos_part) + norm_cos)
                d_k += sine * (dot_nt(vs, sin_part) + norm_sin)
                feats = jnp.concatenate(
                    [(ks * cosine).astype(bf16), (ks * sine).astype(bf16)], axis=1
                )
                d_v = dv_ref[at, lanes]
                d_v += dot(feats, jnp.concatenate([cos_part, sin_part], axis=0))
                out_ref[core, at, lanes] = jnp.where(ks > 0.0, d_k, 0.0).astype(bf16)
                out_ref[1 - core, at, lanes] = d_v.astype(bf16)

            loop(PAIRS, pair)

        loop(rows // SEG, segment)

    return call(
        kernel,
        "inter_backward",
        shape_of((2, rows, D), bf16),
        [SMEM] + [VMEM] * (7 + fsdp // 2),
        state_scratch(fsdp),
    )(ids, k, v, d_k, d_v, cos, sin, *far, near)


def input_grad(ids, d_q, d_kv, d_res1, w_q, w_kv):
    rows = d_q.shape[0]

    def kernel(ids_ref, dq_ref, dkv_ref, dres_ref, w_q_ref, w_kv_ref, out_ref):
        core = ids_ref[0]

        def block(i):
            at = rows_at(i)
            total = dres_ref[at, :] + dot_nt(dq_ref[at, :], w_q_ref[:, :D])
            total += dot_nt(dkv_ref[core, at, :], w_kv_ref[:, :D])
            total += dot_nt(dkv_ref[1 - core, at, :], w_kv_ref[:, D:])
            out_ref[at, :] = total

        loop(rows // SEG, block)

    return call(
        kernel, "input_grad", shape_of((rows, D), f32), [SMEM] + [VMEM] * 5
    )(ids, d_q, d_kv, d_res1, w_q, w_kv)


def reversed_bits(index, bits):
    total = 0
    for b in range(bits):
        total = total + (((index >> b) & 1) << (bits - 1 - b))
    return total


def weight_grad(ids, products, fsdp, splits, key, own_half=True, sums=None):
    height = products[0][0].shape[1]
    widths = [product[3].shape[1] for product in products]
    block = height // fsdp
    bits = fsdp.bit_length() - 1
    share = block // len(splits)
    group = block if block % 128 == 0 else height
    extra = [] if sums is None else [sums]

    def kernel(ids_ref, *refs):
        ins, out_refs = refs[: 4 * len(products)], refs[4 * len(products) + len(extra) :]

        def part(i):
            columns = pl.ds(pl.multiple_of(i * group, 128), group)

            def store(total, left):
                right = left + total.shape[1]
                for j in range(group // block):
                    place = reversed_bits((i * (group // block) + j) ^ ids_ref[2], bits)
                    for n, (split, out_ref) in enumerate(zip(splits, out_refs)):
                        strip = share // split
                        for h in range(split):
                            row = block * j + share * n + strip * h
                            half = h ^ ids_ref[1] if split > 1 else 0
                            out_ref[half, place, :, left:right] = total[
                                row : row + strip, :
                            ].astype(bf16)

            left = 0
            for n, width in enumerate(widths):
                a0_ref, a1_ref, b0_ref, b1_ref = ins[4 * n : 4 * n + 4]
                first = pl.multiple_of(ids_ref[0] * width, 128) if own_half else 0
                total = dot_tn(a0_ref[:, columns], b0_ref[:, pl.ds(first, width)])
                store(total + dot_tn(a1_ref[:, columns], b1_ref[...]), left)
                left += width
            if extra:
                tall = jnp.concatenate(
                    [refs[4 * len(products)][...], jnp.zeros((LANES - 16, height), f32)], axis=0
                )
                store(tall.T, left)

        loop(height // group, part)

    width = sum(widths) + LANES * len(extra)
    return call(
        kernel,
        "weight_grad",
        tuple(shape_of((n, fsdp, share // n, width), bf16) for n in splits),
        [SMEM] + [VMEM] * (4 * len(products) + len(extra)),
        cost=COSTS[key],
    )(ids, *(x for product in products for x in product), *extra)


def add_low(a, b):
    return (a.astype(f32) + b.astype(f32)).astype(bf16)


def core_stage(x):
    (other,) = yield [(x, "group", 0)]
    return other


def halving_stages(keep, send, bits):
    for axis, bit in bits:
        (received,) = yield [(send, axis, bit)]
        half = keep.shape[0] // 2
        if half == 0:
            return add_low(keep[0], received[0])
        keep, send = add_low(keep[:half], received[:half]), add_low(keep[half:], received[half:])


def reduce_stages(x, core, large=False):
    half = x.shape[1] // 2
    bits = axis_bits("fsdp")
    keep, send = x[0, :half], x[0, half:]
    if large and half >= 4:
        axis, bit = bits.pop(0)
        middle, first = half // 2, half // 4
        (received,) = yield [(send[first:], axis, bit)]
        after = add_low(keep[middle:], received[middle - first :])
        beside = add_low(keep[first:middle], received[: middle - first])
        rest, after = lax.optimization_barrier((send[:first], after))
        (received,) = yield [(rest, axis, bit)]
        keep = jnp.concatenate([add_low(keep[:first], received), beside], axis=0)
        send, keep = lax.optimization_barrier((after, keep))
    x = yield from halving_stages(keep, send, bits)
    for axis, bit in axis_bits("group")[1:]:
        (received,) = yield [(x, axis, bit)]
        x = add_low(x, received)
    other = yield from core_stage(x)
    return ordered(x, other, core == 0, -1).astype(f32)


def share_stages(x, core, chip):
    axis, bit = axis_bits("group")[1]
    half = x.shape[1] // 2
    (received,) = yield [(x[1], axis, bit)]
    keep, send = add_low(x[0, :half], received[:half]), add_low(x[0, half:], received[half:])
    x = yield from halving_stages(keep, send, axis_bits("fsdp"))
    (other,) = yield [(x, axis, bit)]
    x = ordered(x, other, chip == 0, 0)
    other = yield from core_stage(x)
    return ordered(x, other, core == 0, -1).astype(f32)


def ordered(x, other, first, axis):
    return jnp.concatenate([jnp.where(first, x, other), jnp.where(first, other, x)], axis=axis)


def ancestor_matrix(parents):
    count = parents.shape[0]
    columns = jnp.arange(count, dtype=jnp.int32)
    step = (parents[:, None] == columns[None, :]).astype(f32)
    same = (columns[:, None] == columns[None, :]).astype(f32)
    reached = step + same
    for _ in range(4):
        reached = (jnp.dot(reached, reached, preferred_element_type=f32) > 0.0).astype(f32)
    return reached - same


def spread_rows(matrix):
    count = matrix.shape[0]
    row = jnp.arange(8 * count, dtype=jnp.int32)
    pick = (row[:, None] // 8 == jnp.arange(count, dtype=jnp.int32)[None, :]).astype(f32)
    wide = jnp.dot(jnp.dot(pick, matrix), pick.T)
    return jnp.where(row[:, None] % 8 == row[None, :] % 8, wide, 0.0).astype(bf16)


def waves(local, segs):
    depth = jnp.sum(local[:segs], axis=1)
    angle = (depth[:, None] * SEG + jnp.arange(SEG, dtype=f32)[None, :]) * (
        math.pi / (2.0 * HORIZON)
    )
    angle = jnp.broadcast_to(angle.reshape(segs * SEG, 1), (segs * SEG, LANES))
    return jnp.cos(angle), jnp.sin(angle)


def gap_wave(position):
    gap = position[:, None] - position[None, :]
    wave = jnp.cos(gap.astype(f32) * (math.pi / (2.0 * HORIZON)))
    return jnp.where(gap >= 0, wave, 0.0), jnp.where(gap <= 0, wave, 0.0)


def vector_columns(vectors):
    return jnp.pad(jnp.stack(vectors), ((0, LANES - len(vectors)), (0, 0))).T


def wide_row(shard, rows):
    return jnp.pad(shard[None], ((0, rows - 1), (0, LANES - shard.shape[0])))


def vector_rows(weight, rows, share, longer):
    per = D // share

    def kernel(w_ref, out_ref):
        out_ref[...] = jnp.zeros_like(out_ref)
        turned = w_ref[:, D:OUT_AT].astype(f32).T
        out_ref[:B_UP, :] = turned[:B_UP, :]
        for block in range(longer * per):
            m, lane = B_UP + block // per, share * (block % per)
            first = rows * block // 8 * 8
            tile = w_ref[first : first + 8, OUT_AT + D :].astype(f32)
            row = rows * block - first
            out_ref[m : m + 1, lane : lane + share] = tile[row : row + 1, :share]

    return call(kernel, "vector_rows", shape_of((16, D), f32), [VMEM])(weight)


def body(
    tokens, cotangent, parent_seg, w_qkv, w_out, b_out, norm1_gain, norm1_bias, w_up, b_up,
    w_down, b_down, norm2_gain, norm2_bias,
):
    fsdp = lax.axis_size("fsdp")
    chips = lax.axis_size("group") // 2
    own = lax.axis_index("fsdp")
    group = lax.axis_index("group")
    core, chip = group % 2, group // 2
    rows = tokens.shape[0]
    segs = rows // SEG
    ff = w_up.shape[1]
    ids = jnp.stack([core, chip, own]).astype(jnp.int32)

    pipe = Pipeline()
    pipe.add("kv", gather_stages(w_qkv[:, D:]))
    pipe.add("tokens", core_stage(tokens))
    pipe.slot()
    pipe.slot(only=("kv",))
    begun = pipe.started[0]
    tokens_other = pipe.read("tokens", begun)

    ancestry = ancestor_matrix(tie(parent_seg[0], begun))
    count = parent_seg.shape[1]
    place = jnp.arange(count, dtype=jnp.int32)
    there = (own ^ (place // segs)) * segs + place % segs
    select = (there[:, None] == place[None, :]).astype(f32)
    local = jnp.dot(jnp.dot(select, ancestry), select.T)
    from_ancestors, from_descendants = spread_rows(local), spread_rows(local.T)
    cos, sin = waves(local, segs)
    wave, wave_t = gap_wave(tie(jnp.arange(SEG, dtype=jnp.int32), begun))
    shard_rows = w_qkv.shape[0]
    columns = vector_columns((b_out, norm1_gain, norm1_bias, b_down, norm2_gain, norm2_bias))
    pipe.add("qo", gather_stages(tie(
        jnp.concatenate([w_qkv[:, :D], columns, w_out, wide_row(b_up, shard_rows)], axis=1), begun
    )))
    pipe.add("up", gather_stages(w_up))
    pipe.add("down", gather_stages(w_down))
    pipe.slot(only=("kv",))
    pipe.slot(*pipe.started, only=("qo",))
    pipe.slot(only=("kv",))
    pipe.slot(*pipe.started, only=("qo",))
    pipe.slot(*pipe.started, only=("up",))
    pipe.slot(only=("kv", "qo"))
    pipe.slot(*pipe.started, only=("up",))
    w_kv = assemble(*pipe.finish("kv", only=("kv",)))
    tables = (from_ancestors, from_descendants, wave, wave_t)
    k, v, increments = project(
        ids, tie(tokens, tokens_other, *tables, *pipe.started), w_kv, cos, sin, fsdp
    )
    pipe.arrive(k, only=("qo",))
    pipe.add("state", trade_stages(increments))
    pipe.slot(*pipe.started, only=("state", "qo"))
    pipe.slot(only=("state", "qo"))
    pipe.slot(*pipe.started, only=("up",))
    w_qo = assemble(*pipe.finish("qo", only=("qo",)))
    pipe.slot(w_qo, only=("down",))
    q, num, den = intra_forward(tie(tokens, *pipe.started), w_qo, k, v, wave)
    far, near = pipe.finish("state", q, only=("state",))
    mixed = mix_segments(from_ancestors, far, near)
    pipe.arrive(q, only=("up", "down"))
    pipe.add("path", trade_stages(mixed))
    pipe.slot(*pipe.started, only=("path", "up"))
    small = vector_rows(tie(w_qo, *pipe.started), shard_rows, b_up.shape[0], ff // D)
    pipe.slot(small, only=("path", "down"))
    pipe.slot(*pipe.started, only=("up",))
    w_up_full = assemble(*pipe.finish("up", only=("up",)))
    path = pipe.finish("path", w_up_full, only=("path",))
    pipe.slot(path[1], only=("down",))
    att, rden = inter_forward(ids, tie(q, *pipe.started), num, den, cos, sin, *path)
    pipe.add("att", core_stage(att))
    pipe.slot(only=("att",))
    pipe.slot(att, only=("down",))
    att_other = pipe.read("att", *pipe.started)
    hat1, inv1, low1, gelu, slope = expand(
        tie(att, att_other, *pipe.started), tokens, w_qo, w_up_full, small
    )
    pipe.slot(low1, only=("down",))
    w_down_full = assemble(*pipe.finish("down", only=("down",)))
    pipe.add("gelu", core_stage(gelu))
    pipe.add("low1", core_stage(low1))
    pipe.slot(w_down_full, only=("gelu", "low1"))
    output, d_res2, d_lower, d_lower_half, sums = contract(
        ids, gelu, hat1, cotangent, w_down_full, small
    )
    low1_other = pipe.read("low1", d_lower)
    gelu_other = pipe.read("gelu", d_lower)
    grads = Pipeline()
    grads.add("d_lower", core_stage(d_lower_half))
    grads.slot(low1_other, gelu_other)
    d_upper, d_upper_half, sums = turn(
        ids, tie(d_lower, *grads.started), slope, w_down_full, sums
    )
    d_lower_other = grads.read("d_lower", d_upper)
    grads.add("d_upper", core_stage(d_upper_half))
    grads.slot(d_lower_other, only=("d_upper",))
    two = chips == 2

    def reduction(part):
        return share_stages(part, core, chip) if two else reduce_stages(part, core)

    split = 2 if two else 1
    (down_part,) = weight_grad(
        ids, [(gelu, gelu_other, tie(d_lower, *grads.started), d_lower_other)], fsdp, [split],
        "down",
    )
    d_upper_other = grads.read("d_upper", down_part)
    grads.add("down", reduction(down_part))
    grads.slot(d_upper_other, only=("down",))
    (up_part,) = weight_grad(
        ids, [(low1, low1_other, tie(d_upper, *grads.started), d_upper_other)], fsdp, [1], "up",
    )
    grads.add("up", reduce_stages(up_part, core, True))
    grads.slot(only=("up",))
    d_res1, d_mixed, d_mixed_half, d_num, d_den, sums, *back = back_to_heads(
        ids, tie(d_upper, *grads.started), d_res2, hat1, inv1, rden, att, q, cos, sin, w_qo,
        w_up_full, small, sums, fsdp,
    )
    grads.add("state", trade_stages(back))
    grads.slot(only=("state",))
    grads.slot(d_num, only=("state",))
    grads.add("d_mixed", core_stage(d_mixed_half))
    grads.slot(*grads.started, only=("d_mixed",))
    grads.slot(*grads.started, only=("up",))
    grads.slot(*grads.started, only=("down",))
    d_mixed_other = grads.read("d_mixed", *grads.started)
    far, near = grads.finish("state", d_mixed_other, only=("state",))
    mixed = mix_segments(from_descendants, far, near)
    grads.add("path", trade_stages(mixed))
    grads.slot(only=("path",))
    d_q, d_q_half, d_k, d_v = intra_backward(
        ids, tie(q, *grads.started), k, v, d_num, d_den, cos, sin, wave, wave_t, *path
    )
    grads.add("d_q", core_stage(d_q_half))
    grads.arrive(d_q, only=("up",))
    grads.slot(*grads.started, only=("path", "d_q"))
    grads.slot(*grads.started, only=("up",))
    grads.arrive(*grads.started, only=("down",))
    d_q_other = grads.read("d_q", *grads.started)
    (outq_part,) = weight_grad(
        ids,
        [
            (att, att_other, d_mixed, d_mixed_other),
            (tokens, tokens_other, d_q, d_q_other),
        ],
        fsdp, [split], "outq", sums=sums,
    )
    grads.add("outq", reduction(outq_part))
    grads.slot(only=("outq",))
    back = grads.finish("path", *grads.started, only=("path",))
    d_kv = inter_backward(ids, k, v, d_k, d_v, cos, sin, *back)
    grads.add("d_kv", core_stage(d_kv[1]))
    grads.slot(only=("d_kv",))
    grads.slot(*grads.started, only=("down",))
    grads.arrive(*grads.started, only=("up",))
    d_kv_other = grads.read("d_kv", *grads.started)
    kv_parts = weight_grad(
        ids, [(tokens, tokens_other, d_kv[0], d_kv_other)], fsdp, [2, 1] if two else [1], "kv",
        False,
    )
    grads.add("kv0", reduction(kv_parts[0]))
    for part in kv_parts[1:]:
        grads.add("kv1", reduce_stages(part, core))
    half = D // 2
    closed = ()

    def close(outq):
        ours, others = jnp.split(outq, 2, axis=1)
        sums = ours[:, D : D + 16] + others[:, D : D + 16]
        q_grad = jnp.concatenate([ours[:, half:D], others[:, half:D]], axis=1)
        out_grad = jnp.concatenate([ours[:, :half], others[:, :half]], axis=1)
        return q_grad, out_grad, sums.T, sums[:, B_UP : B_UP + ff // D].T.reshape(-1)

    for step in TAIL:
        if step == "grad":
            tokens_grad = input_grad(ids, d_q, tie(d_kv, *grads.started), d_res1, w_qo, w_kv)
            grads.started = (tokens_grad,)
        elif step == "close":
            if not closed and "outq" in grads.finished:
                closed = close(grads.finished["outq"])
                grads.started += closed
        elif grads.names(step.split("+")):
            grads.slot(*grads.started, only=step.split("+"))
    while grads.running:
        grads.slot(*grads.started)
    done = grads.finished
    q_grad, out_grad, sums, b_up_grad = closed or close(done["outq"])
    kv_grad = jnp.concatenate([done[n] for n in ("kv0", "kv1") if n in done], axis=0)
    return (
        output,
        tokens_grad,
        jnp.concatenate([q_grad, kv_grad], axis=1),
        out_grad,
        sums[B_OUT],
        sums[GAIN1],
        sums[BIAS1],
        done["up"],
        b_up_grad,
        done["down"],
        sums[B_DOWN],
        sums[GAIN2],
        sums[BIAS2],
    )


def solution(mesh):
    both = ("group", "fsdp")
    matrix, vector = P(both, None), P(both)
    in_specs = (
        matrix, matrix, P("group", None), matrix, matrix, vector, vector, vector, matrix, vector,
        matrix, vector, vector, vector,
    )
    rows, line = P("fsdp", None), P("fsdp")
    out_specs = (
        matrix, matrix, rows, rows, line, line, line, rows, line, rows, line, line, line,
    )
    return jax.shard_map(body, mesh=mesh, in_specs=in_specs, out_specs=out_specs, check_vma=False)
```

```python
import math

import jax
import jax.numpy as jnp
from jax import lax
from jax.experimental import pallas as pl
from jax.experimental.pallas import tpu as pltpu
from jax.sharding import PartitionSpec as P

D = 768
H = 12
HD = 64
SEG = 256
HORIZON = 2560
PAIRS = H // 2
LANES = 2 * HD
EPS = 1e-05

f32 = jnp.float32
bf16 = jnp.bfloat16

B_OUT, GAIN1, BIAS1, B_DOWN, GAIN2, BIAS2, B_UP = range(7)
OUT_AT = D + LANES


def exchange(x, axis, *bits):
    size, offset = lax.axis_size(axis), sum(1 << b for b in bits)
    return lax.ppermute(x, axis, [(i, i ^ offset) for i in range(size)])


def axis_bits(axis):
    return [(axis, b) for b in range(lax.axis_size(axis).bit_length() - 1)]


def tie(x, *others):
    return lax.optimization_barrier((x,) + others)[0]


def trade_stages(pieces):
    bits = axis_bits("fsdp")[1:]
    requests = []
    for m in range(1, len(pieces)):
        requests.append((pieces[m], "fsdp") + tuple(b for n, (_, b) in enumerate(bits) if m >> n & 1))
    arrived = yield requests
    far = [pieces[0]] + list(arrived)
    (near,) = yield [(jnp.concatenate([x[1:] for x in far], axis=0), "fsdp", 0)]
    return far, near


def near_steps(first_low):
    low, high = axis_bits("fsdp")[:1], axis_bits("group")[1:]
    return low + high if first_low else high + low


def moved(masks, axis, bit):
    step = (1 << bit) * (lax.axis_size("fsdp") if axis == "group" else 1)
    return tuple(m ^ step for m in masks)


def gather_stages(shard, early=False):
    lin = lax.axis_index("group") * lax.axis_size("fsdp") + lax.axis_index("fsdp")
    rows, columns = shard.shape
    if rows % 8:
        whole = lax.all_gather(shard, ("group", "fsdp"), axis=0, tiled=True)
        merged = rows
        while merged % 8:
            merged *= 2
        blocks = whole.reshape(-1, merged, columns)
        yield []
        return [[(blocks, tuple(range(blocks.shape[0])))]], jnp.zeros_like(lin)
    blocks, masks = shard[None], (0,)
    for axis, bit in reversed(axis_bits("fsdp")[1:]):
        (other,) = yield [(blocks, axis, bit)]
        blocks = jnp.concatenate([blocks, other], axis=0)
        masks = masks + moved(masks, axis, bit)
    half = columns // 2
    sides = [(blocks[:, :, :half], masks), (blocks[:, :, half:], masks)]
    steps = [near_steps(True), near_steps(False)]
    for n in range(len(steps[0]) - 1):
        others = yield [(b,) + st[n] for (b, _), st in zip(sides, steps)]
        sides = [
            (jnp.concatenate([b, o], axis=0), m + moved(m, *st[n]))
            for (b, m), st, o in zip(sides, steps, others)
        ]
    core = ("group", 0)
    others = yield [(b,) + st[-1] for (b, _), st in zip(sides, steps)] + (
        [(b,) + core for b, _ in sides] if early else []
    )
    parts = []
    if early:
        lasts = yield [(o,) + core for o in others[:2]]
        for n, ((b, m), st) in enumerate(zip(sides, steps)):
            there = moved(m, *st[-1])
            parts.append([
                (b, m), (others[n], there), (others[n + 2], moved(m, *core)),
                (lasts[n], moved(there, *core)),
            ])
        return parts, lin
    sides = [
        (jnp.concatenate([b, o], axis=0), m + moved(m, *st[-1]))
        for (b, m), st, o in zip(sides, steps, others)
    ]
    lasts = yield [(b,) + core for b, _ in sides]
    return [[(b, m), (last, moved(m, *core))] for (b, m), last in zip(sides, lasts)], lin


class Pipeline:
    def __init__(self):
        self.running = {}
        self.waiting = {}
        self.finished = {}
        self.started = ()

    def add(self, name, stages):
        self.running[name] = (stages, None)

    def names(self, only):
        return [n for n in self.running if only is None or n in only]

    def arrive(self, *others, only=None):
        names = [n for n in self.names(only) if n not in self.waiting]
        arrived = [x for n in names for x in self.running[n][1] or ()]
        if arrived:
            arrived = lax.optimization_barrier(tuple(arrived) + others)[: len(arrived)]
        at, ready = 0, ()
        for n in names:
            stages, results = self.running.pop(n)
            count = len(results or ())
            mine, at = arrived[at : at + count], at + count
            try:
                wanted = next(stages) if results is None else stages.send(mine)
            except StopIteration as done:
                self.finished[n] = done.value
            else:
                self.running[n] = (stages, ())
                self.waiting[n] = wanted
                ready += tuple(w[0] for w in wanted)
        self.started = ready or self.started

    def slot(self, *others, only=None):
        self.arrive(*others, only=only)
        requests = [(n, w) for n in self.names(only) for w in self.waiting.pop(n)]
        operands = tuple(w[0] for _, w in requests)
        if operands and others:
            operands = lax.optimization_barrier(operands + others)[: len(operands)]
        self.started = operands or self.started
        for x, (n, (_, axis, *bits)) in zip(operands, requests):
            stages, results = self.running[n]
            self.running[n] = (stages, results + (exchange(x, axis, *bits),))

    def read(self, name, *others):
        self.arrive(*others, only=(name,))
        return self.finished[name]

    def finish(self, name, *others, only=None):
        while name not in self.finished:
            self.slot(*others, only=only)
        return self.finished[name]


VMEM = pl.BlockSpec(memory_space=pltpu.VMEM)
SMEM = pl.BlockSpec(memory_space=pltpu.SMEM)


COSTS = {"assemble": 1.5, "project": 10.8, "mix_segments": 1.1, "intra_forward": 5.9, "inter_forward": 16.5, "expand": 0.285, "contract": 6.0, "turn": 22.5, "back_to_heads": 11.8, "intra_backward": 10.3, "inter_backward": 4.6, "input_grad": 4.0, "vector_rows": 1.5, "down": 6.0, "up": 1.2, "outq": 3.36, "kv": 3.36}
TAIL = (
    "kv0+kv1",
    "grad",
    "outq",
    "down",
    "kv1",
    "up",
    "kv0",
    "outq",
    "kv1",
    "down",
    "kv0",
    "up",
    "outq",
    "kv1",
    "kv0",
    "up",
    "down",
    "outq",
    "kv1",
    "kv0",
    "outq",
    "kv1",
    "down",
    "kv0",
    "outq",
    "kv1",
    "kv0",
)
FLOPS_PER_US = 6.0e8


def call(kernel, name, outs, in_specs, scratch=(), cost=None, mib=5):
    return pl.pallas_call(
        kernel,
        out_shape=outs,
        in_specs=in_specs,
        out_specs=jax.tree.map(lambda _: VMEM, outs),
        scratch_shapes=scratch,
        compiler_params=pltpu.CompilerParams(vmem_limit_bytes=mib * 1024 * 1024),
        cost_estimate=pl.CostEstimate(
            flops=int((cost or COSTS[name]) * FLOPS_PER_US), transcendentals=0, bytes_accessed=0
        ),
        name=name,
    )


def shape_of(shape, dtype):
    return jax.ShapeDtypeStruct(shape, dtype)


def dot(a, b):
    return lax.dot_general(a, b, (((1,), (0,)), ((), ())), preferred_element_type=f32)


def dot_nt(a, b):
    return lax.dot_general(a, b, (((1,), (1,)), ((), ())), preferred_element_type=f32)


def dot_tn(a, b):
    return lax.dot_general(a, b, (((0,), (0,)), ((), ())), preferred_element_type=f32)


def loop(count, body):
    def step(i, carry):
        body(i)
        return carry

    lax.fori_loop(0, count, step, 0)


def rows_at(i):
    return pl.ds(pl.multiple_of(i * SEG, SEG), SEG)


def lanes_at(p):
    return pl.ds(pl.multiple_of(p * LANES, LANES), LANES)


def head_masks(rows):
    lane = lax.broadcasted_iota(jnp.int32, (rows, LANES), 1)
    first = (lane < HD).astype(f32)
    return first.astype(bf16), (1.0 - first).astype(bf16)


def diagonal():
    row = lax.broadcasted_iota(jnp.int32, (LANES, LANES), 0)
    lane = lax.broadcasted_iota(jnp.int32, (LANES, LANES), 1)
    return (row < HD) == (lane < HD)


def head_ones():
    return jnp.where(diagonal(), 1.0, 0.0).astype(bf16)


def split_state(packed):
    same = diagonal()
    cos_part = jnp.where(same, packed, 0.0)
    sin_part = pltpu.roll(jnp.where(same, 0.0, packed), HD, 1)
    return cos_part.astype(bf16), sin_part.astype(bf16)


def state_scratch(fsdp):
    return [pltpu.VMEM((D, LANES), f32), pltpu.VMEM((8 * max(2 * PAIRS, fsdp), LANES), f32)]


def piece_shapes(fsdp, segs):
    return (shape_of((2, segs, D // fsdp + 8, LANES), bf16),) * (fsdp // 2)


def norm_row(n, fsdp):
    per = max(16, fsdp) // fsdp
    return 8 * (n // per) + n % per


def store_states(s, own, left_ref, right_ref, weight_ref, cos_ref, sin_ref, state_scr, norm_scr, out_refs):
    fsdp = 2 * len(out_refs)
    chunk = D // fsdp
    same = diagonal()
    rows = rows_at(s)
    cos, sin = cos_ref[rows, :], sin_ref[rows, :]

    def pair(p):
        lanes = lanes_at(p)
        a = left_ref[rows, lanes]
        b = right_ref[rows, lanes].astype(f32)
        both = jnp.concatenate(
            [(b * cos).astype(bf16), (pltpu.roll(b, HD, 1) * sin).astype(bf16)], axis=1
        )
        product = dot_tn(a, both)
        state_scr[lanes, :] = jnp.where(same, product[:, :LANES], product[:, LANES:])
        wide = a.astype(f32)
        if weight_ref is not None:
            wide = wide * weight_ref[rows, lanes]
        for n, wave in ((p, cos), (PAIRS + p, sin)):
            norm_scr[pl.ds(norm_row(n, fsdp), 1), :] = jnp.sum(wide * wave, axis=0, keepdims=True)

    loop(PAIRS, pair)
    for r in range(fsdp):
        j = own ^ r
        at = pl.ds(pl.multiple_of(chunk * j, 8), chunk)
        norms = pl.ds(pl.multiple_of(8 * j, 8), 8)
        out_refs[r // 2][r % 2, s, 0:chunk, :] = state_scr[at, :].astype(bf16)
        out_refs[r // 2][r % 2, s, chunk : chunk + 8, :] = norm_scr[norms, :].astype(bf16)


def load_states(s, own, far_refs, near_ref, state_scr, norm_scr):
    fsdp = 2 * len(far_refs)
    chunk = D // fsdp
    for r in range(fsdp):
        j = own ^ r
        at = pl.ds(pl.multiple_of(chunk * j, 8), chunk)
        norms = pl.ds(pl.multiple_of(8 * j, 8), 8)
        ref, place = (near_ref, r // 2) if r % 2 else (far_refs[r // 2], 0)
        state_scr[at, :] = ref[place, s, 0:chunk, :].astype(f32)
        norm_scr[norms, :] = ref[place, s, chunk : chunk + 8, :].astype(f32)


def pair_state(p, state_scr, norm_scr, fsdp):
    cos_part, sin_part = split_state(state_scr[lanes_at(p), :])
    norm_cos = norm_scr[pl.ds(norm_row(p, fsdp), 1), :]
    norm_sin = norm_scr[pl.ds(norm_row(PAIRS + p, fsdp), 1), :]
    return cos_part, sin_part, norm_cos, norm_sin


def assemble(parts, lin):
    arrays = [blocks for part in parts for blocks, _ in part]
    places = jnp.concatenate(
        [jnp.array(masks, jnp.int32) for part in parts for _, masks in part]
    ) ^ lin.astype(jnp.int32)
    rows = arrays[0].shape[1]
    count = sum(len(masks) for _, masks in parts[0])
    width = sum(part[0][0].shape[2] for part in parts)
    lefts, left = [], 0
    for part in parts:
        lefts += [left] * len(part)
        left += part[0][0].shape[2]

    def kernel(places_ref, *refs):
        out_ref = refs[-1]
        first = 0
        for ref, at in zip(refs[:-1], lefts):
            number, _, columns = ref.shape

            def place(i, ref=ref, at=at, columns=columns, first=first):
                out_ref[places_ref[first + i], :, at : at + columns] = ref[i]

            loop(number, place)
            first += number

    whole = call(
        kernel, "assemble", shape_of((count, rows, width), bf16), [SMEM] + [VMEM] * len(arrays)
    )(places, *arrays)
    return whole.reshape(count * rows, width)


def project(ids, tokens, w_kv, cos, sin, fsdp):
    rows = tokens.shape[0]
    segs = rows // SEG

    def kernel(ids_ref, tok_ref, w_ref, cos_ref, sin_ref, k_ref, v_ref, *refs):
        inc_refs, (state_scr, norm_scr) = refs[:-2], refs[-2:]
        norm_scr[...] = jnp.zeros_like(norm_scr)

        def segment(s):
            at = rows_at(s)
            x = tok_ref[at, :]
            k_ref[at, :] = jnp.maximum(dot(x, w_ref[:, :D]), 0.0).astype(bf16)
            v_ref[at, :] = dot(x, w_ref[:, D:]).astype(bf16)
            store_states(s, ids_ref[2], k_ref, v_ref, None, cos_ref, sin_ref, state_scr, norm_scr,
                         inc_refs)

        loop(segs, segment)

    act = shape_of((rows, D), bf16)
    k, v, *pieces = call(
        kernel,
        "project",
        (act, act) + piece_shapes(fsdp, segs),
        [SMEM] + [VMEM] * 4,
        state_scratch(fsdp),
    )(ids, tokens, w_kv, cos, sin)
    return k, v, pieces


def mix_segments(spread, far, near):
    fsdp = 2 * len(far)
    _, segs, height, _ = near.shape

    def kernel(spread_ref, *refs):
        far_refs, near_ref, out_refs = refs[: fsdp // 2], refs[fsdp // 2], refs[fsdp // 2 + 1 :]
        for t in range(height // 8):
            at = slice(8 * t, 8 * t + 8)
            stacked = []
            for r in range(fsdp):
                ref, place = (near_ref, r // 2) if r % 2 else (far_refs[r // 2], 0)
                stacked += [ref[place, s, at, :].astype(f32) for s in range(segs)]
            mixed = dot(spread_ref[...], jnp.concatenate(stacked, axis=0).astype(bf16))
            for c in range(fsdp * segs):
                r, s = c // segs, c % segs
                out_refs[r // 2][r % 2, s, at, :] = mixed[8 * c : 8 * c + 8, :].astype(bf16)

    return call(
        kernel, "mix_segments", piece_shapes(fsdp, segs), [VMEM] * (fsdp // 2 + 2)
    )(spread, *far, near)


def intra_forward(tokens, w_q, k, v, wave):
    rows = tokens.shape[0]

    def kernel(tok_ref, w_ref, k_ref, v_ref, wave_ref, q_ref, num_ref, den_ref):
        masks = head_masks(SEG)

        def segment(s):
            at = rows_at(s)
            q_ref[at, :] = jnp.maximum(dot(tok_ref[at, :], w_ref[:, :D]), 0.0).astype(bf16)

            def pair(p):
                lanes = lanes_at(p)
                qs, ks, vs = q_ref[at, lanes], k_ref[at, lanes], v_ref[at, lanes]
                weights, values = [], []
                for m in masks:
                    weights.append((dot_nt(qs, ks * m) * wave_ref[...]).astype(bf16))
                    values.append(jnp.concatenate([vs * m, m], axis=1))
                both = dot(jnp.concatenate(weights, axis=1), jnp.concatenate(values, axis=0))
                num_ref[at, lanes] = both[:, :LANES]
                den_ref[at, lanes] = both[:, LANES:]

            loop(PAIRS, pair)

        loop(rows // SEG, segment)

    wide = shape_of((rows, D), f32)
    return call(
        kernel, "intra_forward", (shape_of((rows, D), bf16), wide, wide), [VMEM] * 5
    )(tokens, w_q, k, v, wave)


def inter_forward(ids, q, num, den, cos, sin, far, near):
    rows = q.shape[0]
    fsdp = 2 * len(far)

    def kernel(ids_ref, q_ref, num_ref, den_ref, cos_ref, sin_ref, *refs):
        far_refs, near_ref = refs[: fsdp // 2], refs[fsdp // 2]
        att_ref, rden_ref, state_scr, norm_scr = refs[fsdp // 2 + 1 :]
        ones = head_ones()
        twice = jnp.concatenate([ones, ones], axis=0)

        def segment(s):
            at = rows_at(s)
            load_states(s, ids_ref[2], far_refs, near_ref, state_scr, norm_scr)

            def pair(p):
                lanes = lanes_at(p)
                cos_part, sin_part, norm_cos, norm_sin = pair_state(p, state_scr, norm_scr, fsdp)
                qs = q_ref[at, lanes].astype(f32)
                q_cos = (qs * cos_ref[at, :]).astype(bf16)
                q_sin = (qs * sin_ref[at, :]).astype(bf16)
                carried = dot(
                    jnp.concatenate([q_cos, q_sin], axis=1),
                    jnp.concatenate([cos_part, sin_part], axis=0),
                )
                along = q_cos.astype(f32) * norm_cos + q_sin.astype(f32) * norm_sin
                high = along.astype(bf16)
                rest = (along - high.astype(f32)).astype(bf16)
                weight = dot(jnp.concatenate([high, rest], axis=1), twice)
                inverse = 1.0 / (den_ref[at, lanes] + weight + 1.0)
                att_ref[at, lanes] = ((num_ref[at, lanes] + carried) * inverse).astype(bf16)
                rden_ref[at, lanes] = inverse

            loop(PAIRS, pair)

        loop(rows // SEG, segment)

    return call(
        kernel,
        "inter_forward",
        (shape_of((rows, D), bf16), shape_of((rows, D), f32)),
        [SMEM] + [VMEM] * (6 + fsdp // 2),
        state_scratch(fsdp),
    )(ids, q, num, den, cos, sin, *far, near)


def standardize(resid):
    centred = resid - jnp.mean(resid, axis=1, keepdims=True)
    inv = lax.rsqrt(jnp.mean(centred * centred, axis=1, keepdims=True) + EPS)
    return centred * inv, inv


def standardize_back(d_hat, hat, inv):
    return inv * (
        d_hat
        - jnp.mean(d_hat, axis=1, keepdims=True)
        - hat * jnp.mean(d_hat * hat, axis=1, keepdims=True)
    )


def expand(att, tokens, w_out, w_up, small):
    rows = att.shape[0]
    ff = w_up.shape[1]

    def kernel(att_ref, tok_ref, out_w_ref, up_ref, small_ref, hat_ref, inv_ref, low_ref, gelu_ref,
               slope_ref):
        def block(i):
            at = rows_at(i)
            mixed = dot(att_ref[at, :], out_w_ref[:, OUT_AT : OUT_AT + D])
            hat, inv = standardize(
                tok_ref[at, :].astype(f32) + mixed + small_ref[B_OUT : B_OUT + 1, :]
            )
            hat_ref[at, :] = hat
            inv_ref[at, :] = jnp.broadcast_to(inv, (SEG, LANES))
            low_ref[at, :] = (
                hat * small_ref[GAIN1 : GAIN1 + 1, :] + small_ref[BIAS1 : BIAS1 + 1, :]
            ).astype(bf16)

            def part(m):
                for c in range(3):
                    columns = pl.ds(pl.multiple_of(m * D + 256 * c, 256), 256)
                    bias = small_ref[pl.ds(B_UP + m, 1), 256 * c : 256 * (c + 1)]
                    upper = dot(low_ref[at, :], up_ref[:, columns]) + bias
                    cdf = 0.5 + 0.5 * lax.erf(upper * math.sqrt(0.5))
                    pdf = jnp.exp(-0.5 * upper * upper) * (1.0 / math.sqrt(2.0 * math.pi))
                    gelu_ref[at, columns] = (upper * cdf).astype(bf16)
                    slope_ref[at, columns] = (cdf + upper * pdf).astype(bf16)

            loop(ff // D, part)

        loop(rows // SEG, block)

    return call(
        kernel,
        "expand",
        (
            shape_of((rows, D), f32),
            shape_of((rows, LANES), f32),
            shape_of((rows, D), bf16),
            shape_of((rows, ff), bf16),
            shape_of((rows, ff), bf16),
        ),
        [VMEM] * 5,
    )(att, tokens, w_out, w_up, small)


def contract(ids, gelu, hat1, cotangent, w_down, small):
    rows, ff = gelu.shape

    def kernel(ids_ref, gelu_ref, hat1_ref, cot_ref, w_ref, small_ref,
               out_ref, dres_ref, dlow_ref, dlow_half_ref, sums_ref):
        sums_ref[...] = jnp.zeros_like(sums_ref)

        def block(i):
            at = rows_at(i)
            normed = hat1_ref[at, :] * small_ref[GAIN1 : GAIN1 + 1, :]
            normed += small_ref[BIAS1 : BIAS1 + 1, :]
            resid = normed + dot(gelu_ref[at, :], w_ref[...]) + small_ref[B_DOWN : B_DOWN + 1, :]
            hat, inv = standardize(resid)
            gain = small_ref[GAIN2 : GAIN2 + 1, :]
            out_ref[at, :] = (hat * gain + small_ref[BIAS2 : BIAS2 + 1, :]).astype(bf16)
            cot = cot_ref[at, :].astype(f32)
            sums_ref[GAIN2 : GAIN2 + 1, :] += jnp.sum(cot * hat, axis=0, keepdims=True)
            sums_ref[BIAS2 : BIAS2 + 1, :] += jnp.sum(cot, axis=0, keepdims=True)
            d_res = standardize_back(cot * gain, hat, inv)
            dres_ref[at, :] = d_res
            d_low = d_res.astype(bf16)
            dlow_ref[at, :] = d_low
            sums_ref[B_DOWN : B_DOWN + 1, :] += jnp.sum(d_low.astype(f32), axis=0, keepdims=True)
            theirs = 1 - ids_ref[0]
            dlow_half_ref[at, :] = dlow_ref[
                at, pl.ds(pl.multiple_of(theirs * (D // 2), 128), D // 2)
            ]

        loop(rows // SEG, block)

    return call(
        kernel,
        "contract",
        (
            shape_of((rows, D), bf16),
            shape_of((rows, D), f32),
            shape_of((rows, D), bf16),
            shape_of((rows, D // 2), bf16),
            shape_of((16, D), f32),
        ),
        [SMEM] + [VMEM] * 5,
    )(ids, gelu, hat1, cotangent, w_down, small)


def turn(ids, d_lower, slope, w_down, sums):
    rows, ff = slope.shape

    def kernel(ids_ref, dlow_ref, slope_ref, w_ref, sums_in_ref, dup_ref, dup_half_ref, sums_ref):
        sums_ref[...] = sums_in_ref[...]

        def block(i):
            at = rows_at(i)

            def part(m):
                for c in range(3):
                    columns = pl.ds(pl.multiple_of(m * D + 256 * c, 256), 256)
                    d_up = dot_nt(dlow_ref[at, :], w_ref[columns, :])
                    d_up = (d_up * slope_ref[at, columns].astype(f32)).astype(bf16)
                    dup_ref[at, columns] = d_up
                    sums_ref[pl.ds(B_UP + m, 1), 256 * c : 256 * (c + 1)] += jnp.sum(
                        d_up.astype(f32), axis=0, keepdims=True
                    )

            loop(ff // D, part)
            theirs = 1 - ids_ref[0]
            dup_half_ref[at, :] = dup_ref[
                at, pl.ds(pl.multiple_of(theirs * (ff // 2), 128), ff // 2)
            ]

        loop(rows // SEG, block)

    return call(
        kernel,
        "turn",
        (
            shape_of((rows, ff), bf16), shape_of((rows, ff // 2), bf16), shape_of((16, D), f32),
        ),
        [SMEM] + [VMEM] * 4,
    )(ids, d_lower, slope, w_down, sums)


def back_to_heads(ids, d_upper, d_res2, hat1, inv1, rden, att, q, cos, sin, w_out, w_up, small,
                  sums, fsdp):
    rows, ff = d_upper.shape
    segs = rows // SEG

    def kernel(ids_ref, dup_ref, dres_ref, hat_ref, inv_ref, rden_ref, att_ref, q_ref, cos_ref,
               sin_ref, out_w_ref, up_ref, small_ref, sums_in_ref,
               dres1_ref, dmix_ref, dmix_half_ref, dnum_ref, dden_ref, sums_ref, *refs):
        inc_refs, (state_scr, norm_scr) = refs[:-2], refs[-2:]
        sums_ref[...] = sums_in_ref[...]
        share = D // fsdp
        for j in range(fsdp):
            for c in range(ff // D):
                at = (j * (ff // D) + c) * share
                m, lane = B_UP + at // D, at % D
                sums_ref[B_UP + c : B_UP + c + 1, share * j : share * (j + 1)] = sums_in_ref[
                    m : m + 1, lane : lane + share
                ]
        norm_scr[...] = jnp.zeros_like(norm_scr)
        ones = head_ones()
        twice = jnp.concatenate([ones, ones], axis=0)

        def block(i):
            at = rows_at(i)
            d_normed = dres_ref[at, :] + dot_nt(dup_ref[at, :], up_ref[...])
            hat = hat_ref[at, :]
            sums_ref[GAIN1 : GAIN1 + 1, :] += jnp.sum(d_normed * hat, axis=0, keepdims=True)
            sums_ref[BIAS1 : BIAS1 + 1, :] += jnp.sum(d_normed, axis=0, keepdims=True)
            d_res = standardize_back(
                d_normed * small_ref[GAIN1 : GAIN1 + 1, :], hat, inv_ref[at, 0:1]
            )
            dres1_ref[at, :] = d_res
            d_mix = d_res.astype(bf16)
            dmix_ref[at, :] = d_mix
            sums_ref[B_OUT : B_OUT + 1, :] += jnp.sum(d_mix.astype(f32), axis=0, keepdims=True)
            d_att = dot_nt(d_mix, out_w_ref[:, OUT_AT : OUT_AT + D])
            inverse = rden_ref[at, :]
            dnum_ref[at, :] = (d_att * inverse).astype(bf16)
            along = d_att * att_ref[at, :].astype(f32)
            for p in range(PAIRS):
                lanes = slice(LANES * p, LANES * (p + 1))
                high = along[:, lanes].astype(bf16)
                rest = (along[:, lanes] - high.astype(f32)).astype(bf16)
                total = dot(jnp.concatenate([high, rest], axis=1), twice)
                dden_ref[at, lanes] = -total * inverse[:, lanes]
            theirs = 1 - ids_ref[0]
            dmix_half_ref[at, :] = dmix_ref[
                at, pl.ds(pl.multiple_of(theirs * (D // 2), 128), D // 2)
            ]
            store_states(i, ids_ref[2], q_ref, dnum_ref, dden_ref, cos_ref, sin_ref, state_scr,
                         norm_scr, inc_refs)

        loop(segs, block)

    return call(
        kernel,
        "back_to_heads",
        (
            shape_of((rows, D), f32),
            shape_of((rows, D), bf16),
            shape_of((rows, D // 2), bf16),
            shape_of((rows, D), bf16),
            shape_of((rows, D), f32),
            shape_of((16, D), f32),
        )
        + piece_shapes(fsdp, segs),
        [SMEM] + [VMEM] * 13,
        state_scratch(fsdp),
    )(ids, d_upper, d_res2, hat1, inv1, rden, att, q, cos, sin, w_out, w_up, small, sums)


def intra_backward(ids, q, k, v, d_num, d_den, cos, sin, wave, wave_t, far, near):
    rows = q.shape[0]
    fsdp = 2 * len(far)

    def kernel(ids_ref, q_ref, k_ref, v_ref, dnum_ref, dden_ref, cos_ref, sin_ref, wave_ref,
               wave_t_ref, *refs):
        far_refs, near_ref = refs[: fsdp // 2], refs[fsdp // 2]
        dq_ref, dq_half_ref, dk_ref, dv_ref, state_scr, norm_scr = refs[fsdp // 2 + 1 :]
        masks = head_masks(SEG)
        lane = lax.broadcasted_iota(jnp.int32, (SEG, LANES), 1) % HD
        picks = [jnp.where(lane < 2, m.astype(f32), 0.0).astype(bf16) for m in masks]

        def segment(s):
            at = rows_at(s)
            load_states(s, ids_ref[2], far_refs, near_ref, state_scr, norm_scr)
            cosine, sine = cos_ref[at, :], sin_ref[at, :]

            def pair(p):
                lanes = lanes_at(p)
                qs, ks, vs = q_ref[at, lanes], k_ref[at, lanes], v_ref[at, lanes]
                dn, dd = dnum_ref[at, lanes], dden_ref[at, lanes]
                high = dd.astype(bf16).astype(f32)
                spread = jnp.where(lane == 0, high, jnp.where(lane == 1, dd - high, 0.0))
                grads = jnp.concatenate([dn, spread.astype(bf16)], axis=1)
                w_ts, d_ss, d_ts, khs, qhs, dns = [], [], [], [], [], []
                for m, pick in zip(masks, picks):
                    kh = ks * m
                    values = jnp.concatenate([vs * m, pick], axis=1)
                    w_ts.append((dot_nt(kh, qs) * wave_t_ref[...]).astype(bf16))
                    d_ss.append((dot_nt(grads, values) * wave_ref[...]).astype(bf16))
                    d_ts.append((dot_nt(values, grads) * wave_t_ref[...]).astype(bf16))
                    khs.append(kh)
                    qhs.append(qs * m)
                    dns.append(dn * m)

                def both(left, right):
                    return dot(jnp.concatenate(left, axis=1), jnp.concatenate(right, axis=0))

                dk_ref[at, lanes] = both(d_ts, qhs)
                dv_ref[at, lanes] = both(w_ts, dns)
                d_q = both(d_ss, khs)
                cos_part, sin_part, norm_cos, norm_sin = pair_state(p, state_scr, norm_scr, fsdp)
                d_q += cosine * (dot_nt(dn, cos_part) + dd * norm_cos)
                d_q += sine * (dot_nt(dn, sin_part) + dd * norm_sin)
                dq_ref[at, lanes] = jnp.where(qs.astype(f32) > 0.0, d_q, 0.0).astype(bf16)

            loop(PAIRS, pair)
            theirs = 1 - ids_ref[0]
            dq_half_ref[at, :] = dq_ref[at, pl.ds(pl.multiple_of(theirs * (D // 2), 128), D // 2)]

        loop(rows // SEG, segment)

    return call(
        kernel,
        "intra_backward",
        (
            shape_of((rows, D), bf16),
            shape_of((rows, D // 2), bf16),
            shape_of((rows, D), f32),
            shape_of((rows, D), f32),
        ),
        [SMEM] + [VMEM] * (10 + fsdp // 2),
        state_scratch(fsdp),
    )(ids, q, k, v, d_num, d_den, cos, sin, wave, wave_t, *far, near)


def inter_backward(ids, k, v, d_k, d_v, cos, sin, far, near):
    rows = k.shape[0]
    fsdp = 2 * len(far)

    def kernel(ids_ref, k_ref, v_ref, dk_ref, dv_ref, cos_ref, sin_ref, *refs):
        far_refs, near_ref = refs[: fsdp // 2], refs[fsdp // 2]
        out_ref, state_scr, norm_scr = refs[fsdp // 2 + 1 :]
        core = ids_ref[0]

        def segment(s):
            at = rows_at(s)
            load_states(s, ids_ref[2], far_refs, near_ref, state_scr, norm_scr)
            cosine, sine = cos_ref[at, :], sin_ref[at, :]

            def pair(p):
                lanes = lanes_at(p)
                cos_part, sin_part, norm_cos, norm_sin = pair_state(p, state_scr, norm_scr, fsdp)
                ks = k_ref[at, lanes].astype(f32)
                vs = v_ref[at, lanes]
                d_k = dk_ref[at, lanes]
                d_k += cosine * (dot_nt(vs, cos_part) + norm_cos)
                d_k += sine * (dot_nt(vs, sin_part) + norm_sin)
                feats = jnp.concatenate(
                    [(ks * cosine).astype(bf16), (ks * sine).astype(bf16)], axis=1
                )
                d_v = dv_ref[at, lanes]
                d_v += dot(feats, jnp.concatenate([cos_part, sin_part], axis=0))
                out_ref[core, at, lanes] = jnp.where(ks > 0.0, d_k, 0.0).astype(bf16)
                out_ref[1 - core, at, lanes] = d_v.astype(bf16)

            loop(PAIRS, pair)

        loop(rows // SEG, segment)

    return call(
        kernel,
        "inter_backward",
        shape_of((2, rows, D), bf16),
        [SMEM] + [VMEM] * (7 + fsdp // 2),
        state_scratch(fsdp),
    )(ids, k, v, d_k, d_v, cos, sin, *far, near)


def input_grad(ids, d_q, d_kv, d_res1, w_q, w_kv):
    rows = d_q.shape[0]

    def kernel(ids_ref, dq_ref, dkv_ref, dres_ref, w_q_ref, w_kv_ref, out_ref):
        core = ids_ref[0]

        def block(i):
            at = rows_at(i)
            total = dres_ref[at, :] + dot_nt(dq_ref[at, :], w_q_ref[:, :D])
            total += dot_nt(dkv_ref[core, at, :], w_kv_ref[:, :D])
            total += dot_nt(dkv_ref[1 - core, at, :], w_kv_ref[:, D:])
            out_ref[at, :] = total

        loop(rows // SEG, block)

    return call(
        kernel, "input_grad", shape_of((rows, D), f32), [SMEM] + [VMEM] * 5
    )(ids, d_q, d_kv, d_res1, w_q, w_kv)


def reversed_bits(index, bits):
    total = 0
    for b in range(bits):
        total = total + (((index >> b) & 1) << (bits - 1 - b))
    return total


def weight_grad(ids, products, fsdp, splits, key, own_half=True, sums=None):
    height = products[0][0].shape[1]
    widths = [product[3].shape[1] for product in products]
    block = height // fsdp
    bits = fsdp.bit_length() - 1
    share = block // len(splits)
    group = block if block % 128 == 0 else height
    extra = [] if sums is None else [sums]

    def kernel(ids_ref, *refs):
        ins, out_refs = refs[: 4 * len(products)], refs[4 * len(products) + len(extra) :]

        def part(i):
            columns = pl.ds(pl.multiple_of(i * group, 128), group)

            def store(total, left):
                right = left + total.shape[1]
                for j in range(group // block):
                    place = reversed_bits((i * (group // block) + j) ^ ids_ref[2], bits)
                    for n, (split, out_ref) in enumerate(zip(splits, out_refs)):
                        strip = share // split
                        for h in range(split):
                            row = block * j + share * n + strip * h
                            half = h ^ ids_ref[1] if split > 1 else 0
                            out_ref[half, place, :, left:right] = total[
                                row : row + strip, :
                            ].astype(bf16)

            left = 0
            for n, width in enumerate(widths):
                a0_ref, a1_ref, b0_ref, b1_ref = ins[4 * n : 4 * n + 4]
                first = pl.multiple_of(ids_ref[0] * width, 128) if own_half else 0
                total = dot_tn(a0_ref[:, columns], b0_ref[:, pl.ds(first, width)])
                store(total + dot_tn(a1_ref[:, columns], b1_ref[...]), left)
                left += width
            if extra:
                tall = jnp.concatenate(
                    [refs[4 * len(products)][...], jnp.zeros((LANES - 16, height), f32)], axis=0
                )
                store(tall.T, left)

        loop(height // group, part)

    width = sum(widths) + LANES * len(extra)
    return call(
        kernel,
        "weight_grad",
        tuple(shape_of((n, fsdp, share // n, width), bf16) for n in splits),
        [SMEM] + [VMEM] * (4 * len(products) + len(extra)),
        cost=COSTS[key],
    )(ids, *(x for product in products for x in product), *extra)


def add_low(a, b):
    return (a.astype(f32) + b.astype(f32)).astype(bf16)


def core_stage(x):
    (other,) = yield [(x, "group", 0)]
    return other


def halving_stages(keep, send, bits):
    for axis, bit in bits:
        (received,) = yield [(send, axis, bit)]
        half = keep.shape[0] // 2
        if half == 0:
            return add_low(keep[0], received[0])
        keep, send = add_low(keep[:half], received[:half]), add_low(keep[half:], received[half:])


def reduce_stages(x, core):
    half = x.shape[1] // 2
    bits = axis_bits("fsdp")
    keep, send = x[0, :half], x[0, half:]
    x = yield from halving_stages(keep, send, bits)
    for axis, bit in axis_bits("group")[1:]:
        (received,) = yield [(x, axis, bit)]
        x = add_low(x, received)
    other = yield from core_stage(x)
    return ordered(x, other, core == 0, -1).astype(f32)


def share_stages(x, core, chip, twice=False):
    axis, bit = axis_bits("group")[1]
    half = x.shape[1] // 2
    if twice:
        (received,) = yield [(x[1, half:], axis, bit)]
        rest, send = lax.optimization_barrier((x[1, :half], add_low(x[0, half:], received)))
        (received,) = yield [(rest, axis, bit)]
        send, keep = lax.optimization_barrier((send, add_low(x[0, :half], received)))
    else:
        (received,) = yield [(x[1], axis, bit)]
        keep, send = add_low(x[0, :half], received[:half]), add_low(x[0, half:], received[half:])
    x = yield from halving_stages(keep, send, axis_bits("fsdp"))
    (other,) = yield [(x, axis, bit)]
    x = ordered(x, other, chip == 0, 0)
    other = yield from core_stage(x)
    return ordered(x, other, core == 0, -1).astype(f32)


def large_stages(x, core, chip):
    (axis, bit), *bits = axis_bits("fsdp")
    group_axis, group_bit = axis_bits("group")[1]
    half = x.shape[1] // 2
    first = half // 4
    keep, send = x[:, :half], x[:, half:]
    (received,) = yield [(send[:, first:], axis, bit)]
    later = add_low(keep[:, first:], received)
    rest, later = lax.optimization_barrier((send[:, :first], later))
    (received,) = yield [(rest, axis, bit)]
    head = add_low(keep[:, :first], received)
    theirs = jnp.concatenate([head[1], later[1]], axis=0)
    (received,) = yield [(theirs, group_axis, group_bit)]
    head, later = head[0], later[0]
    quarter = half // 2
    ours = jnp.concatenate([head, later[: quarter - first]], axis=0)
    keep = add_low(ours, received[:quarter])
    send = add_low(later[quarter - first :], received[quarter:])
    x = yield from halving_stages(keep, send, bits)
    (other,) = yield [(x, group_axis, group_bit)]
    x = ordered(x, other, chip == 0, 0)
    other = yield from core_stage(x)
    return ordered(x, other, core == 0, -1).astype(f32)


def ordered(x, other, first, axis):
    return jnp.concatenate([jnp.where(first, x, other), jnp.where(first, other, x)], axis=axis)


def ancestor_matrix(parents):
    count = parents.shape[0]
    columns = jnp.arange(count, dtype=jnp.int32)
    step = (parents[:, None] == columns[None, :]).astype(f32)
    same = (columns[:, None] == columns[None, :]).astype(f32)
    reached = step + same
    for _ in range(4):
        reached = (jnp.dot(reached, reached, preferred_element_type=f32) > 0.0).astype(f32)
    return reached - same


def spread_rows(matrix):
    count = matrix.shape[0]
    row = jnp.arange(8 * count, dtype=jnp.int32)
    pick = (row[:, None] // 8 == jnp.arange(count, dtype=jnp.int32)[None, :]).astype(f32)
    wide = jnp.dot(jnp.dot(pick, matrix), pick.T)
    return jnp.where(row[:, None] % 8 == row[None, :] % 8, wide, 0.0).astype(bf16)


def waves(local, segs):
    depth = jnp.sum(local[:segs], axis=1)
    angle = (depth[:, None] * SEG + jnp.arange(SEG, dtype=f32)[None, :]) * (
        math.pi / (2.0 * HORIZON)
    )
    angle = jnp.broadcast_to(angle.reshape(segs * SEG, 1), (segs * SEG, LANES))
    return jnp.cos(angle), jnp.sin(angle)


def gap_wave(position):
    gap = position[:, None] - position[None, :]
    wave = jnp.cos(gap.astype(f32) * (math.pi / (2.0 * HORIZON)))
    return jnp.where(gap >= 0, wave, 0.0), jnp.where(gap <= 0, wave, 0.0)


def vector_columns(vectors):
    return jnp.pad(jnp.stack(vectors), ((0, LANES - len(vectors)), (0, 0))).T


def wide_row(shard, rows):
    return jnp.pad(shard[None], ((0, rows - 1), (0, LANES - shard.shape[0])))


def vector_rows(weight, rows, share, longer):
    per = D // share

    def kernel(w_ref, out_ref):
        out_ref[...] = jnp.zeros_like(out_ref)
        turned = w_ref[:, D:OUT_AT].astype(f32).T
        out_ref[:B_UP, :] = turned[:B_UP, :]
        for block in range(longer * per):
            m, lane = B_UP + block // per, share * (block % per)
            first = rows * block // 8 * 8
            tile = w_ref[first : first + 8, OUT_AT + D :].astype(f32)
            row = rows * block - first
            out_ref[m : m + 1, lane : lane + share] = tile[row : row + 1, :share]

    return call(kernel, "vector_rows", shape_of((16, D), f32), [VMEM])(weight)


def body(
    tokens, cotangent, parent_seg, w_qkv, w_out, b_out, norm1_gain, norm1_bias, w_up, b_up,
    w_down, b_down, norm2_gain, norm2_bias,
):
    fsdp = lax.axis_size("fsdp")
    chips = lax.axis_size("group") // 2
    own = lax.axis_index("fsdp")
    group = lax.axis_index("group")
    core, chip = group % 2, group // 2
    rows = tokens.shape[0]
    segs = rows // SEG
    ff = w_up.shape[1]
    ids = jnp.stack([core, chip, own]).astype(jnp.int32)

    pipe = Pipeline()
    pipe.add("kv", gather_stages(w_qkv[:, D:]))
    pipe.add("tokens", core_stage(tokens))
    pipe.slot()
    pipe.slot(only=("kv",))
    begun = pipe.started[0]
    tokens_other = pipe.read("tokens", begun)

    ancestry = ancestor_matrix(tie(parent_seg[0], begun))
    count = parent_seg.shape[1]
    place = jnp.arange(count, dtype=jnp.int32)
    there = (own ^ (place // segs)) * segs + place % segs
    select = (there[:, None] == place[None, :]).astype(f32)
    local = jnp.dot(jnp.dot(select, ancestry), select.T)
    from_ancestors, from_descendants = spread_rows(local), spread_rows(local.T)
    cos, sin = waves(local, segs)
    wave, wave_t = gap_wave(tie(jnp.arange(SEG, dtype=jnp.int32), begun))
    shard_rows = w_qkv.shape[0]
    columns = vector_columns((b_out, norm1_gain, norm1_bias, b_down, norm2_gain, norm2_bias))
    pipe.add("qo", gather_stages(tie(
        jnp.concatenate([w_qkv[:, :D], columns, w_out, wide_row(b_up, shard_rows)], axis=1), begun
    )))
    pipe.add("up", gather_stages(w_up))
    pipe.add("down", gather_stages(w_down))
    pipe.slot(only=("kv",))
    pipe.slot(*pipe.started, only=("qo",))
    pipe.slot(only=("kv",))
    pipe.slot(*pipe.started, only=("qo",))
    pipe.slot(*pipe.started, only=("up",))
    pipe.slot(only=("kv", "qo"))
    pipe.slot(*pipe.started, only=("up",))
    w_kv = assemble(*pipe.finish("kv", only=("kv",)))
    tables = (from_ancestors, from_descendants, wave, wave_t)
    k, v, increments = project(
        ids, tie(tokens, tokens_other, *tables, *pipe.started), w_kv, cos, sin, fsdp
    )
    pipe.arrive(k, only=("qo",))
    pipe.add("state", trade_stages(increments))
    pipe.slot(*pipe.started, only=("state", "qo"))
    pipe.slot(only=("state", "qo"))
    pipe.slot(*pipe.started, only=("up",))
    w_qo = assemble(*pipe.finish("qo", only=("qo",)))
    pipe.slot(w_qo, only=("down",))
    q, num, den = intra_forward(tie(tokens, *pipe.started), w_qo, k, v, wave)
    far, near = pipe.finish("state", q, only=("state",))
    mixed = mix_segments(from_ancestors, far, near)
    pipe.arrive(q, only=("up", "down"))
    pipe.add("path", trade_stages(mixed))
    pipe.slot(*pipe.started, only=("path", "up"))
    small = vector_rows(tie(w_qo, *pipe.started), shard_rows, b_up.shape[0], ff // D)
    pipe.slot(small, only=("path", "down"))
    pipe.slot(*pipe.started, only=("up",))
    w_up_full = assemble(*pipe.finish("up", only=("up",)))
    path = pipe.finish("path", w_up_full, only=("path",))
    pipe.slot(path[1], only=("down",))
    att, rden = inter_forward(ids, tie(q, *pipe.started), num, den, cos, sin, *path)
    pipe.add("att", core_stage(att))
    pipe.slot(only=("att",))
    pipe.slot(att, only=("down",))
    att_other = pipe.read("att", *pipe.started)
    hat1, inv1, low1, gelu, slope = expand(
        tie(att, att_other, *pipe.started), tokens, w_qo, w_up_full, small
    )
    pipe.slot(low1, only=("down",))
    w_down_full = assemble(*pipe.finish("down", only=("down",)))
    pipe.add("gelu", core_stage(gelu))
    pipe.add("low1", core_stage(low1))
    pipe.slot(w_down_full, only=("gelu", "low1"))
    output, d_res2, d_lower, d_lower_half, sums = contract(
        ids, gelu, hat1, cotangent, w_down_full, small
    )
    low1_other = pipe.read("low1", d_lower)
    gelu_other = pipe.read("gelu", d_lower)
    grads = Pipeline()
    grads.add("d_lower", core_stage(d_lower_half))
    grads.slot(low1_other, gelu_other)
    d_upper, d_upper_half, sums = turn(
        ids, tie(d_lower, *grads.started), slope, w_down_full, sums
    )
    d_lower_other = grads.read("d_lower", d_upper)
    grads.add("d_upper", core_stage(d_upper_half))
    grads.slot(d_lower_other, only=("d_upper",))
    two = chips == 2

    def reduction(part, twice=False):
        return share_stages(part, core, chip, twice) if two else reduce_stages(part, core)

    split = 2 if two else 1
    (down_part,) = weight_grad(
        ids, [(gelu, gelu_other, tie(d_lower, *grads.started), d_lower_other)], fsdp, [split],
        "down",
    )
    d_upper_other = grads.read("d_upper", down_part)
    grads.add("down", reduction(down_part, True))
    grads.slot(d_upper_other, only=("down",))
    (up_part,) = weight_grad(
        ids, [(low1, low1_other, tie(d_upper, *grads.started), d_upper_other)], fsdp, [split], "up",
    )
    large = two and fsdp >= 8
    grads.add("up", large_stages(up_part, core, chip) if large else reduction(up_part))
    grads.slot(only=("up",))
    d_res1, d_mixed, d_mixed_half, d_num, d_den, sums, *back = back_to_heads(
        ids, tie(d_upper, *grads.started), d_res2, hat1, inv1, rden, att, q, cos, sin, w_qo,
        w_up_full, small, sums, fsdp,
    )
    grads.add("state", trade_stages(back))
    grads.slot(only=("state",))
    if two:
        grads.slot(d_num, only=("down",))
    grads.slot(*grads.started, d_num, only=("state",))
    grads.add("d_mixed", core_stage(d_mixed_half))
    grads.slot(*grads.started, only=("d_mixed",))
    grads.slot(*grads.started, only=("up",))
    grads.slot(*grads.started, only=("down",))
    d_mixed_other = grads.read("d_mixed", *grads.started)
    far, near = grads.finish("state", d_mixed_other, only=("state",))
    mixed = mix_segments(from_descendants, far, near)
    grads.add("path", trade_stages(mixed))
    grads.slot(only=("path",))
    grads.slot(*grads.started, only=("up",))
    d_q, d_q_half, d_k, d_v = intra_backward(
        ids, tie(q, *grads.started), k, v, d_num, d_den, cos, sin, wave, wave_t, *path
    )
    grads.add("d_q", core_stage(d_q_half))
    grads.slot(d_q, only=("path", "d_q"))
    grads.arrive(*grads.started, only=("up", "down"))
    d_q_other = grads.read("d_q", *grads.started)
    (outq_part,) = weight_grad(
        ids,
        [
            (att, att_other, d_mixed, d_mixed_other),
            (tokens, tokens_other, d_q, d_q_other),
        ],
        fsdp, [split], "outq", sums=sums,
    )
    grads.add("outq", reduction(outq_part))
    grads.slot(only=("outq",))
    grads.slot(*grads.started, only=("up",))
    back = grads.finish("path", *grads.started, only=("path",))
    d_kv = inter_backward(ids, k, v, d_k, d_v, cos, sin, *back)
    grads.add("d_kv", core_stage(d_kv[1]))
    grads.arrive(d_kv, only=("up",))
    grads.slot(*grads.started, only=("d_kv",))
    grads.slot(*grads.started, only=("up",))
    grads.slot(*grads.started, only=("down",))
    d_kv_other = grads.read("d_kv", *grads.started)
    kv_parts = weight_grad(
        ids, [(tokens, tokens_other, d_kv[0], d_kv_other)], fsdp, [2, 1] if two else [1], "kv",
        False,
    )
    grads.add("kv0", reduction(kv_parts[0]))
    for part in kv_parts[1:]:
        grads.add("kv1", reduce_stages(part, core))
    half = D // 2
    closed = ()

    def close(outq):
        ours, others = jnp.split(outq, 2, axis=1)
        sums = ours[:, D : D + 16] + others[:, D : D + 16]
        q_grad = jnp.concatenate([ours[:, half:D], others[:, half:D]], axis=1)
        out_grad = jnp.concatenate([ours[:, :half], others[:, :half]], axis=1)
        return q_grad, out_grad, sums.T, sums[:, B_UP : B_UP + ff // D].T.reshape(-1)

    written = set()

    def write():
        nonlocal closed
        if not closed and "outq" in grads.finished:
            closed = close(grads.finished["outq"])
            grads.started += closed
        for n in ("up", "down"):
            if n in grads.finished and n not in written:
                written.add(n)
                grads.started += (grads.finished[n],)

    for step in TAIL:
        if step == "grad":
            tokens_grad = input_grad(ids, d_q, tie(d_kv, *grads.started), d_res1, w_qo, w_kv)
            grads.started = (tokens_grad,)
        elif grads.names(step.split("+")):
            grads.slot(*grads.started, only=step.split("+"))
            write()
    while grads.running:
        grads.slot(*grads.started)
        write()
    done = grads.finished
    q_grad, out_grad, sums, b_up_grad = closed or close(done["outq"])
    kv_grad = jnp.concatenate([done[n] for n in ("kv0", "kv1") if n in done], axis=0)
    return (
        output,
        tokens_grad,
        jnp.concatenate([q_grad, kv_grad], axis=1),
        out_grad,
        sums[B_OUT],
        sums[GAIN1],
        sums[BIAS1],
        done["up"],
        b_up_grad,
        done["down"],
        sums[B_DOWN],
        sums[GAIN2],
        sums[BIAS2],
    )


def solution(mesh):
    both = ("group", "fsdp")
    matrix, vector = P(both, None), P(both)
    in_specs = (
        matrix, matrix, P("group", None), matrix, matrix, vector, vector, vector, matrix, vector,
        matrix, vector, vector, vector,
    )
    rows, line = P("fsdp", None), P("fsdp")
    out_specs = (
        matrix, matrix, rows, rows, line, line, line, rows, line, rows, line, line, line,
    )
    return jax.shard_map(body, mesh=mesh, in_specs=in_specs, out_specs=out_specs, check_vma=False)
```

```python
import math

import jax
import jax.numpy as jnp
from jax import lax
from jax.experimental import pallas as pl
from jax.experimental.pallas import tpu as pltpu
from jax.sharding import PartitionSpec as P

D = 768
H = 12
HD = 64
SEG = 256
HORIZON = 2560
PAIRS = H // 2
LANES = 2 * HD
EPS = 1e-05

f32 = jnp.float32
bf16 = jnp.bfloat16

B_OUT, GAIN1, BIAS1, B_DOWN, GAIN2, BIAS2, B_UP = range(7)
OUT_AT = D + LANES


def exchange(x, axis, *bits):
    size, offset = lax.axis_size(axis), sum(1 << b for b in bits)
    return lax.ppermute(x, axis, [(i, i ^ offset) for i in range(size)])


def axis_bits(axis):
    return [(axis, b) for b in range(lax.axis_size(axis).bit_length() - 1)]


def tie(x, *others):
    return lax.optimization_barrier((x,) + others)[0]


def trade_stages(pieces):
    bits = axis_bits("fsdp")[1:]
    requests = []
    for m in range(1, len(pieces)):
        requests.append((pieces[m], "fsdp") + tuple(b for n, (_, b) in enumerate(bits) if m >> n & 1))
    arrived = yield requests
    far = [pieces[0]] + list(arrived)
    (near,) = yield [(jnp.concatenate([x[1:] for x in far], axis=0), "fsdp", 0)]
    return far, near


def near_steps(first_low):
    low, high = axis_bits("fsdp")[:1], axis_bits("group")[1:]
    return low + high if first_low else high + low


def moved(masks, axis, bit):
    step = (1 << bit) * (lax.axis_size("fsdp") if axis == "group" else 1)
    return tuple(m ^ step for m in masks)


def gather_stages(shard, early=False):
    lin = lax.axis_index("group") * lax.axis_size("fsdp") + lax.axis_index("fsdp")
    rows, columns = shard.shape
    if rows % 8:
        whole = lax.all_gather(shard, ("group", "fsdp"), axis=0, tiled=True)
        merged = rows
        while merged % 8:
            merged *= 2
        blocks = whole.reshape(-1, merged, columns)
        yield []
        return [[(blocks, tuple(range(blocks.shape[0])))]], jnp.zeros_like(lin)
    blocks, masks = shard[None], (0,)
    for axis, bit in reversed(axis_bits("fsdp")[1:]):
        (other,) = yield [(blocks, axis, bit)]
        blocks = jnp.concatenate([blocks, other], axis=0)
        masks = masks + moved(masks, axis, bit)
    half = columns // 2
    sides = [(blocks[:, :, :half], masks), (blocks[:, :, half:], masks)]
    steps = [near_steps(True), near_steps(False)]
    for n in range(len(steps[0]) - 1):
        others = yield [(b,) + st[n] for (b, _), st in zip(sides, steps)]
        sides = [
            (jnp.concatenate([b, o], axis=0), m + moved(m, *st[n]))
            for (b, m), st, o in zip(sides, steps, others)
        ]
    core = ("group", 0)
    others = yield [(b,) + st[-1] for (b, _), st in zip(sides, steps)] + (
        [(b,) + core for b, _ in sides] if early else []
    )
    parts = []
    if early:
        lasts = yield [(o,) + core for o in others[:2]]
        for n, ((b, m), st) in enumerate(zip(sides, steps)):
            there = moved(m, *st[-1])
            parts.append([
                (b, m), (others[n], there), (others[n + 2], moved(m, *core)),
                (lasts[n], moved(there, *core)),
            ])
        return parts, lin
    sides = [
        (jnp.concatenate([b, o], axis=0), m + moved(m, *st[-1]))
        for (b, m), st, o in zip(sides, steps, others)
    ]
    lasts = yield [(b,) + core for b, _ in sides]
    return [[(b, m), (last, moved(m, *core))] for (b, m), last in zip(sides, lasts)], lin


class Pipeline:
    def __init__(self):
        self.running = {}
        self.waiting = {}
        self.finished = {}
        self.started = ()

    def add(self, name, stages):
        self.running[name] = (stages, None)

    def names(self, only):
        return [n for n in self.running if only is None or n in only]

    def arrive(self, *others, only=None):
        names = [n for n in self.names(only) if n not in self.waiting]
        arrived = [x for n in names for x in self.running[n][1] or ()]
        if arrived:
            arrived = lax.optimization_barrier(tuple(arrived) + others)[: len(arrived)]
        at, ready = 0, ()
        for n in names:
            stages, results = self.running.pop(n)
            count = len(results or ())
            mine, at = arrived[at : at + count], at + count
            try:
                wanted = next(stages) if results is None else stages.send(mine)
            except StopIteration as done:
                self.finished[n] = done.value
            else:
                self.running[n] = (stages, ())
                self.waiting[n] = wanted
                ready += tuple(w[0] for w in wanted)
        self.started = ready or self.started

    def slot(self, *others, only=None):
        self.arrive(*others, only=only)
        requests = [(n, w) for n in self.names(only) for w in self.waiting.pop(n)]
        operands = tuple(w[0] for _, w in requests)
        if operands and others:
            operands = lax.optimization_barrier(operands + others)[: len(operands)]
        self.started = operands or self.started
        for x, (n, (_, axis, *bits)) in zip(operands, requests):
            stages, results = self.running[n]
            self.running[n] = (stages, results + (exchange(x, axis, *bits),))

    def read(self, name, *others):
        self.arrive(*others, only=(name,))
        return self.finished[name]

    def finish(self, name, *others, only=None):
        while name not in self.finished:
            self.slot(*others, only=only)
        return self.finished[name]


VMEM = pl.BlockSpec(memory_space=pltpu.VMEM)
SMEM = pl.BlockSpec(memory_space=pltpu.SMEM)


COSTS = {"assemble": 1.5, "project": 10.8, "mix_segments": 1.1, "intra_forward": 5.9, "inter_forward": 16.5, "expand": 0.285, "contract": 6.0, "turn": 22.5, "back_to_heads": 11.8, "intra_backward": 10.3, "inter_backward": 4.6, "input_grad": 4.0, "vector_rows": 1.5, "down": 6.0, "up": 1.2, "outq": 3.36, "kv": 3.36}
TAIL = (
    "kv0+kv1",
    "grad",
    "outq",
    "down",
    "kv1",
    "up",
    "kv0",
    "outq",
    "kv1",
    "down",
    "kv0",
    "up",
    "outq",
    "kv1",
    "kv0",
    "up",
    "down",
    "outq",
    "kv1",
    "kv0",
    "outq",
    "kv1",
    "down",
    "kv0",
    "outq",
    "kv1",
    "kv0",
)
FLOPS_PER_US = 6.0e8


def call(kernel, name, outs, in_specs, scratch=(), cost=None, mib=5):
    return pl.pallas_call(
        kernel,
        out_shape=outs,
        in_specs=in_specs,
        out_specs=jax.tree.map(lambda _: VMEM, outs),
        scratch_shapes=scratch,
        compiler_params=pltpu.CompilerParams(vmem_limit_bytes=mib * 1024 * 1024),
        cost_estimate=pl.CostEstimate(
            flops=int((cost or COSTS[name]) * FLOPS_PER_US), transcendentals=0, bytes_accessed=0
        ),
        name=name,
    )


def shape_of(shape, dtype):
    return jax.ShapeDtypeStruct(shape, dtype)


def dot(a, b):
    return lax.dot_general(a, b, (((1,), (0,)), ((), ())), preferred_element_type=f32)


def dot_nt(a, b):
    return lax.dot_general(a, b, (((1,), (1,)), ((), ())), preferred_element_type=f32)


def dot_tn(a, b):
    return lax.dot_general(a, b, (((0,), (0,)), ((), ())), preferred_element_type=f32)


def loop(count, body):
    def step(i, carry):
        body(i)
        return carry

    lax.fori_loop(0, count, step, 0)


def rows_at(i):
    return pl.ds(pl.multiple_of(i * SEG, SEG), SEG)


def lanes_at(p):
    return pl.ds(pl.multiple_of(p * LANES, LANES), LANES)


def head_masks(rows):
    lane = lax.broadcasted_iota(jnp.int32, (rows, LANES), 1)
    first = (lane < HD).astype(f32)
    return first.astype(bf16), (1.0 - first).astype(bf16)


def diagonal():
    row = lax.broadcasted_iota(jnp.int32, (LANES, LANES), 0)
    lane = lax.broadcasted_iota(jnp.int32, (LANES, LANES), 1)
    return (row < HD) == (lane < HD)


def head_ones():
    return jnp.where(diagonal(), 1.0, 0.0).astype(bf16)


def split_state(packed):
    same = diagonal()
    cos_part = jnp.where(same, packed, 0.0)
    sin_part = pltpu.roll(jnp.where(same, 0.0, packed), HD, 1)
    return cos_part.astype(bf16), sin_part.astype(bf16)


def state_scratch(fsdp):
    return [pltpu.VMEM((D, LANES), f32), pltpu.VMEM((8 * max(2 * PAIRS, fsdp), LANES), f32)]


def piece_shapes(fsdp, segs):
    return (shape_of((2, segs, D // fsdp + 8, LANES), bf16),) * (fsdp // 2)


def norm_row(n, fsdp):
    per = max(16, fsdp) // fsdp
    return 8 * (n // per) + n % per


def store_states(s, own, left_ref, right_ref, weight_ref, cos_ref, sin_ref, state_scr, norm_scr, out_refs):
    fsdp = 2 * len(out_refs)
    chunk = D // fsdp
    same = diagonal()
    rows = rows_at(s)
    cos, sin = cos_ref[rows, :], sin_ref[rows, :]

    def pair(p):
        lanes = lanes_at(p)
        a = left_ref[rows, lanes]
        b = right_ref[rows, lanes].astype(f32)
        both = jnp.concatenate(
            [(b * cos).astype(bf16), (pltpu.roll(b, HD, 1) * sin).astype(bf16)], axis=1
        )
        product = dot_tn(a, both)
        state_scr[lanes, :] = jnp.where(same, product[:, :LANES], product[:, LANES:])
        wide = a.astype(f32)
        if weight_ref is not None:
            wide = wide * weight_ref[rows, lanes]
        for n, wave in ((p, cos), (PAIRS + p, sin)):
            norm_scr[pl.ds(norm_row(n, fsdp), 1), :] = jnp.sum(wide * wave, axis=0, keepdims=True)

    loop(PAIRS, pair)
    for r in range(fsdp):
        j = own ^ r
        at = pl.ds(pl.multiple_of(chunk * j, 8), chunk)
        norms = pl.ds(pl.multiple_of(8 * j, 8), 8)
        out_refs[r // 2][r % 2, s, 0:chunk, :] = state_scr[at, :].astype(bf16)
        out_refs[r // 2][r % 2, s, chunk : chunk + 8, :] = norm_scr[norms, :].astype(bf16)


def load_states(s, own, far_refs, near_ref, state_scr, norm_scr):
    fsdp = 2 * len(far_refs)
    chunk = D // fsdp
    for r in range(fsdp):
        j = own ^ r
        at = pl.ds(pl.multiple_of(chunk * j, 8), chunk)
        norms = pl.ds(pl.multiple_of(8 * j, 8), 8)
        ref, place = (near_ref, r // 2) if r % 2 else (far_refs[r // 2], 0)
        state_scr[at, :] = ref[place, s, 0:chunk, :].astype(f32)
        norm_scr[norms, :] = ref[place, s, chunk : chunk + 8, :].astype(f32)


def pair_state(p, state_scr, norm_scr, fsdp):
    cos_part, sin_part = split_state(state_scr[lanes_at(p), :])
    norm_cos = norm_scr[pl.ds(norm_row(p, fsdp), 1), :]
    norm_sin = norm_scr[pl.ds(norm_row(PAIRS + p, fsdp), 1), :]
    return cos_part, sin_part, norm_cos, norm_sin


def assemble(parts, lin):
    arrays = [blocks for part in parts for blocks, _ in part]
    places = jnp.concatenate(
        [jnp.array(masks, jnp.int32) for part in parts for _, masks in part]
    ) ^ lin.astype(jnp.int32)
    rows = arrays[0].shape[1]
    count = sum(len(masks) for _, masks in parts[0])
    width = sum(part[0][0].shape[2] for part in parts)
    lefts, left = [], 0
    for part in parts:
        lefts += [left] * len(part)
        left += part[0][0].shape[2]

    def kernel(places_ref, *refs):
        out_ref = refs[-1]
        first = 0
        for ref, at in zip(refs[:-1], lefts):
            number, _, columns = ref.shape

            def place(i, ref=ref, at=at, columns=columns, first=first):
                out_ref[places_ref[first + i], :, at : at + columns] = ref[i]

            loop(number, place)
            first += number

    whole = call(
        kernel, "assemble", shape_of((count, rows, width), bf16), [SMEM] + [VMEM] * len(arrays)
    )(places, *arrays)
    return whole.reshape(count * rows, width)


def project(ids, tokens, w_kv, cos, sin, fsdp):
    rows = tokens.shape[0]
    segs = rows // SEG

    def kernel(ids_ref, tok_ref, w_ref, cos_ref, sin_ref, k_ref, v_ref, *refs):
        inc_refs, (state_scr, norm_scr) = refs[:-2], refs[-2:]
        norm_scr[...] = jnp.zeros_like(norm_scr)

        def segment(s):
            at = rows_at(s)
            x = tok_ref[at, :]
            k_ref[at, :] = jnp.maximum(dot(x, w_ref[:, :D]), 0.0).astype(bf16)
            v_ref[at, :] = dot(x, w_ref[:, D:]).astype(bf16)
            store_states(s, ids_ref[2], k_ref, v_ref, None, cos_ref, sin_ref, state_scr, norm_scr,
                         inc_refs)

        loop(segs, segment)

    act = shape_of((rows, D), bf16)
    k, v, *pieces = call(
        kernel,
        "project",
        (act, act) + piece_shapes(fsdp, segs),
        [SMEM] + [VMEM] * 4,
        state_scratch(fsdp),
    )(ids, tokens, w_kv, cos, sin)
    return k, v, pieces


def mix_segments(spread, far, near):
    fsdp = 2 * len(far)
    _, segs, height, _ = near.shape

    def kernel(spread_ref, *refs):
        far_refs, near_ref, out_refs = refs[: fsdp // 2], refs[fsdp // 2], refs[fsdp // 2 + 1 :]
        for t in range(height // 8):
            at = slice(8 * t, 8 * t + 8)
            stacked = []
            for r in range(fsdp):
                ref, place = (near_ref, r // 2) if r % 2 else (far_refs[r // 2], 0)
                stacked += [ref[place, s, at, :].astype(f32) for s in range(segs)]
            mixed = dot(spread_ref[...], jnp.concatenate(stacked, axis=0).astype(bf16))
            for c in range(fsdp * segs):
                r, s = c // segs, c % segs
                out_refs[r // 2][r % 2, s, at, :] = mixed[8 * c : 8 * c + 8, :].astype(bf16)

    return call(
        kernel, "mix_segments", piece_shapes(fsdp, segs), [VMEM] * (fsdp // 2 + 2)
    )(spread, *far, near)


def intra_forward(tokens, w_q, k, v, wave):
    rows = tokens.shape[0]

    def kernel(tok_ref, w_ref, k_ref, v_ref, wave_ref, q_ref, num_ref, den_ref):
        masks = head_masks(SEG)

        def segment(s):
            at = rows_at(s)
            q_ref[at, :] = jnp.maximum(dot(tok_ref[at, :], w_ref[:, :D]), 0.0).astype(bf16)

            def pair(p):
                lanes = lanes_at(p)
                qs, ks, vs = q_ref[at, lanes], k_ref[at, lanes], v_ref[at, lanes]
                weights, values = [], []
                for m in masks:
                    weights.append((dot_nt(qs, ks * m) * wave_ref[...]).astype(bf16))
                    values.append(jnp.concatenate([vs * m, m], axis=1))
                both = dot(jnp.concatenate(weights, axis=1), jnp.concatenate(values, axis=0))
                num_ref[at, lanes] = both[:, :LANES]
                den_ref[at, lanes] = both[:, LANES:]

            loop(PAIRS, pair)

        loop(rows // SEG, segment)

    wide = shape_of((rows, D), f32)
    return call(
        kernel, "intra_forward", (shape_of((rows, D), bf16), wide, wide), [VMEM] * 5
    )(tokens, w_q, k, v, wave)


def inter_forward(ids, q, num, den, cos, sin, far, near):
    rows = q.shape[0]
    fsdp = 2 * len(far)

    def kernel(ids_ref, q_ref, num_ref, den_ref, cos_ref, sin_ref, *refs):
        far_refs, near_ref = refs[: fsdp // 2], refs[fsdp // 2]
        att_ref, rden_ref, state_scr, norm_scr = refs[fsdp // 2 + 1 :]
        ones = head_ones()
        twice = jnp.concatenate([ones, ones], axis=0)

        def segment(s):
            at = rows_at(s)
            load_states(s, ids_ref[2], far_refs, near_ref, state_scr, norm_scr)

            def pair(p):
                lanes = lanes_at(p)
                cos_part, sin_part, norm_cos, norm_sin = pair_state(p, state_scr, norm_scr, fsdp)
                qs = q_ref[at, lanes].astype(f32)
                q_cos = (qs * cos_ref[at, :]).astype(bf16)
                q_sin = (qs * sin_ref[at, :]).astype(bf16)
                carried = dot(
                    jnp.concatenate([q_cos, q_sin], axis=1),
                    jnp.concatenate([cos_part, sin_part], axis=0),
                )
                along = q_cos.astype(f32) * norm_cos + q_sin.astype(f32) * norm_sin
                high = along.astype(bf16)
                rest = (along - high.astype(f32)).astype(bf16)
                weight = dot(jnp.concatenate([high, rest], axis=1), twice)
                inverse = 1.0 / (den_ref[at, lanes] + weight + 1.0)
                att_ref[at, lanes] = ((num_ref[at, lanes] + carried) * inverse).astype(bf16)
                rden_ref[at, lanes] = inverse

            loop(PAIRS, pair)

        loop(rows // SEG, segment)

    return call(
        kernel,
        "inter_forward",
        (shape_of((rows, D), bf16), shape_of((rows, D), f32)),
        [SMEM] + [VMEM] * (6 + fsdp // 2),
        state_scratch(fsdp),
    )(ids, q, num, den, cos, sin, *far, near)


def standardize(resid):
    centred = resid - jnp.mean(resid, axis=1, keepdims=True)
    inv = lax.rsqrt(jnp.mean(centred * centred, axis=1, keepdims=True) + EPS)
    return centred * inv, inv


def standardize_back(d_hat, hat, inv):
    return inv * (
        d_hat
        - jnp.mean(d_hat, axis=1, keepdims=True)
        - hat * jnp.mean(d_hat * hat, axis=1, keepdims=True)
    )


def expand(att, tokens, w_out, w_up, small):
    rows = att.shape[0]
    ff = w_up.shape[1]

    def kernel(att_ref, tok_ref, out_w_ref, up_ref, small_ref, hat_ref, inv_ref, low_ref, gelu_ref,
               slope_ref):
        def block(i):
            at = rows_at(i)
            mixed = dot(att_ref[at, :], out_w_ref[:, OUT_AT : OUT_AT + D])
            hat, inv = standardize(
                tok_ref[at, :].astype(f32) + mixed + small_ref[B_OUT : B_OUT + 1, :]
            )
            hat_ref[at, :] = hat
            inv_ref[at, :] = jnp.broadcast_to(inv, (SEG, LANES))
            low_ref[at, :] = (
                hat * small_ref[GAIN1 : GAIN1 + 1, :] + small_ref[BIAS1 : BIAS1 + 1, :]
            ).astype(bf16)

            def part(m):
                for c in range(3):
                    columns = pl.ds(pl.multiple_of(m * D + 256 * c, 256), 256)
                    bias = small_ref[pl.ds(B_UP + m, 1), 256 * c : 256 * (c + 1)]
                    upper = dot(low_ref[at, :], up_ref[:, columns]) + bias
                    cdf = 0.5 + 0.5 * lax.erf(upper * math.sqrt(0.5))
                    pdf = jnp.exp(-0.5 * upper * upper) * (1.0 / math.sqrt(2.0 * math.pi))
                    gelu_ref[at, columns] = (upper * cdf).astype(bf16)
                    slope_ref[at, columns] = (cdf + upper * pdf).astype(bf16)

            loop(ff // D, part)

        loop(rows // SEG, block)

    return call(
        kernel,
        "expand",
        (
            shape_of((rows, D), f32),
            shape_of((rows, LANES), f32),
            shape_of((rows, D), bf16),
            shape_of((rows, ff), bf16),
            shape_of((rows, ff), bf16),
        ),
        [VMEM] * 5,
    )(att, tokens, w_out, w_up, small)


def contract(ids, gelu, hat1, cotangent, w_down, small):
    rows, ff = gelu.shape

    def kernel(ids_ref, gelu_ref, hat1_ref, cot_ref, w_ref, small_ref,
               out_ref, dres_ref, dlow_ref, dlow_half_ref, sums_ref):
        sums_ref[...] = jnp.zeros_like(sums_ref)

        def block(i):
            at = rows_at(i)
            normed = hat1_ref[at, :] * small_ref[GAIN1 : GAIN1 + 1, :]
            normed += small_ref[BIAS1 : BIAS1 + 1, :]
            resid = normed + dot(gelu_ref[at, :], w_ref[...]) + small_ref[B_DOWN : B_DOWN + 1, :]
            hat, inv = standardize(resid)
            gain = small_ref[GAIN2 : GAIN2 + 1, :]
            out_ref[at, :] = (hat * gain + small_ref[BIAS2 : BIAS2 + 1, :]).astype(bf16)
            cot = cot_ref[at, :].astype(f32)
            sums_ref[GAIN2 : GAIN2 + 1, :] += jnp.sum(cot * hat, axis=0, keepdims=True)
            sums_ref[BIAS2 : BIAS2 + 1, :] += jnp.sum(cot, axis=0, keepdims=True)
            d_res = standardize_back(cot * gain, hat, inv)
            dres_ref[at, :] = d_res
            d_low = d_res.astype(bf16)
            dlow_ref[at, :] = d_low
            sums_ref[B_DOWN : B_DOWN + 1, :] += jnp.sum(d_low.astype(f32), axis=0, keepdims=True)
            theirs = 1 - ids_ref[0]
            dlow_half_ref[at, :] = dlow_ref[
                at, pl.ds(pl.multiple_of(theirs * (D // 2), 128), D // 2)
            ]

        loop(rows // SEG, block)

    return call(
        kernel,
        "contract",
        (
            shape_of((rows, D), bf16),
            shape_of((rows, D), f32),
            shape_of((rows, D), bf16),
            shape_of((rows, D // 2), bf16),
            shape_of((16, D), f32),
        ),
        [SMEM] + [VMEM] * 5,
    )(ids, gelu, hat1, cotangent, w_down, small)


def turn(ids, d_lower, slope, w_down, sums):
    rows, ff = slope.shape

    def kernel(ids_ref, dlow_ref, slope_ref, w_ref, sums_in_ref, dup_ref, dup_half_ref, sums_ref):
        sums_ref[...] = sums_in_ref[...]

        def block(i):
            at = rows_at(i)

            def part(m):
                for c in range(3):
                    columns = pl.ds(pl.multiple_of(m * D + 256 * c, 256), 256)
                    d_up = dot_nt(dlow_ref[at, :], w_ref[columns, :])
                    d_up = (d_up * slope_ref[at, columns].astype(f32)).astype(bf16)
                    dup_ref[at, columns] = d_up
                    sums_ref[pl.ds(B_UP + m, 1), 256 * c : 256 * (c + 1)] += jnp.sum(
                        d_up.astype(f32), axis=0, keepdims=True
                    )

            loop(ff // D, part)
            theirs = 1 - ids_ref[0]
            dup_half_ref[at, :] = dup_ref[
                at, pl.ds(pl.multiple_of(theirs * (ff // 2), 128), ff // 2)
            ]

        loop(rows // SEG, block)

    return call(
        kernel,
        "turn",
        (
            shape_of((rows, ff), bf16), shape_of((rows, ff // 2), bf16), shape_of((16, D), f32),
        ),
        [SMEM] + [VMEM] * 4,
    )(ids, d_lower, slope, w_down, sums)


def back_to_heads(ids, d_upper, d_res2, hat1, inv1, rden, att, q, cos, sin, w_out, w_up, small,
                  sums, fsdp):
    rows, ff = d_upper.shape
    segs = rows // SEG

    def kernel(ids_ref, dup_ref, dres_ref, hat_ref, inv_ref, rden_ref, att_ref, q_ref, cos_ref,
               sin_ref, out_w_ref, up_ref, small_ref, sums_in_ref,
               dres1_ref, dmix_ref, dmix_half_ref, dnum_ref, dden_ref, sums_ref, *refs):
        inc_refs, (state_scr, norm_scr) = refs[:-2], refs[-2:]
        sums_ref[...] = sums_in_ref[...]
        share = D // fsdp
        for j in range(fsdp):
            for c in range(ff // D):
                at = (j * (ff // D) + c) * share
                m, lane = B_UP + at // D, at % D
                sums_ref[B_UP + c : B_UP + c + 1, share * j : share * (j + 1)] = sums_in_ref[
                    m : m + 1, lane : lane + share
                ]
        norm_scr[...] = jnp.zeros_like(norm_scr)
        ones = head_ones()
        twice = jnp.concatenate([ones, ones], axis=0)

        def block(i):
            at = rows_at(i)
            d_normed = dres_ref[at, :] + dot_nt(dup_ref[at, :], up_ref[...])
            hat = hat_ref[at, :]
            sums_ref[GAIN1 : GAIN1 + 1, :] += jnp.sum(d_normed * hat, axis=0, keepdims=True)
            sums_ref[BIAS1 : BIAS1 + 1, :] += jnp.sum(d_normed, axis=0, keepdims=True)
            d_res = standardize_back(
                d_normed * small_ref[GAIN1 : GAIN1 + 1, :], hat, inv_ref[at, 0:1]
            )
            dres1_ref[at, :] = d_res
            d_mix = d_res.astype(bf16)
            dmix_ref[at, :] = d_mix
            sums_ref[B_OUT : B_OUT + 1, :] += jnp.sum(d_mix.astype(f32), axis=0, keepdims=True)
            d_att = dot_nt(d_mix, out_w_ref[:, OUT_AT : OUT_AT + D])
            inverse = rden_ref[at, :]
            dnum_ref[at, :] = (d_att * inverse).astype(bf16)
            along = d_att * att_ref[at, :].astype(f32)
            for p in range(PAIRS):
                lanes = slice(LANES * p, LANES * (p + 1))
                high = along[:, lanes].astype(bf16)
                rest = (along[:, lanes] - high.astype(f32)).astype(bf16)
                total = dot(jnp.concatenate([high, rest], axis=1), twice)
                dden_ref[at, lanes] = -total * inverse[:, lanes]
            theirs = 1 - ids_ref[0]
            dmix_half_ref[at, :] = dmix_ref[
                at, pl.ds(pl.multiple_of(theirs * (D // 2), 128), D // 2)
            ]
            store_states(i, ids_ref[2], q_ref, dnum_ref, dden_ref, cos_ref, sin_ref, state_scr,
                         norm_scr, inc_refs)

        loop(segs, block)

    return call(
        kernel,
        "back_to_heads",
        (
            shape_of((rows, D), f32),
            shape_of((rows, D), bf16),
            shape_of((rows, D // 2), bf16),
            shape_of((rows, D), bf16),
            shape_of((rows, D), f32),
            shape_of((16, D), f32),
        )
        + piece_shapes(fsdp, segs),
        [SMEM] + [VMEM] * 13,
        state_scratch(fsdp),
    )(ids, d_upper, d_res2, hat1, inv1, rden, att, q, cos, sin, w_out, w_up, small, sums)


def intra_backward(ids, q, k, v, d_num, d_den, cos, sin, wave, wave_t, far, near):
    rows = q.shape[0]
    fsdp = 2 * len(far)

    def kernel(ids_ref, q_ref, k_ref, v_ref, dnum_ref, dden_ref, cos_ref, sin_ref, wave_ref,
               wave_t_ref, *refs):
        far_refs, near_ref = refs[: fsdp // 2], refs[fsdp // 2]
        dq_ref, dq_half_ref, dk_ref, dv_ref, state_scr, norm_scr = refs[fsdp // 2 + 1 :]
        masks = head_masks(SEG)
        lane = lax.broadcasted_iota(jnp.int32, (SEG, LANES), 1) % HD
        picks = [jnp.where(lane < 2, m.astype(f32), 0.0).astype(bf16) for m in masks]

        def segment(s):
            at = rows_at(s)
            load_states(s, ids_ref[2], far_refs, near_ref, state_scr, norm_scr)
            cosine, sine = cos_ref[at, :], sin_ref[at, :]

            def pair(p):
                lanes = lanes_at(p)
                qs, ks, vs = q_ref[at, lanes], k_ref[at, lanes], v_ref[at, lanes]
                dn, dd = dnum_ref[at, lanes], dden_ref[at, lanes]
                high = dd.astype(bf16).astype(f32)
                spread = jnp.where(lane == 0, high, jnp.where(lane == 1, dd - high, 0.0))
                grads = jnp.concatenate([dn, spread.astype(bf16)], axis=1)
                w_ts, d_ss, d_ts, khs, qhs, dns = [], [], [], [], [], []
                for m, pick in zip(masks, picks):
                    kh = ks * m
                    values = jnp.concatenate([vs * m, pick], axis=1)
                    w_ts.append((dot_nt(kh, qs) * wave_t_ref[...]).astype(bf16))
                    d_ss.append((dot_nt(grads, values) * wave_ref[...]).astype(bf16))
                    d_ts.append((dot_nt(values, grads) * wave_t_ref[...]).astype(bf16))
                    khs.append(kh)
                    qhs.append(qs * m)
                    dns.append(dn * m)

                def both(left, right):
                    return dot(jnp.concatenate(left, axis=1), jnp.concatenate(right, axis=0))

                dk_ref[at, lanes] = both(d_ts, qhs)
                dv_ref[at, lanes] = both(w_ts, dns)
                d_q = both(d_ss, khs)
                cos_part, sin_part, norm_cos, norm_sin = pair_state(p, state_scr, norm_scr, fsdp)
                d_q += cosine * (dot_nt(dn, cos_part) + dd * norm_cos)
                d_q += sine * (dot_nt(dn, sin_part) + dd * norm_sin)
                dq_ref[at, lanes] = jnp.where(qs.astype(f32) > 0.0, d_q, 0.0).astype(bf16)

            loop(PAIRS, pair)
            theirs = 1 - ids_ref[0]
            dq_half_ref[at, :] = dq_ref[at, pl.ds(pl.multiple_of(theirs * (D // 2), 128), D // 2)]

        loop(rows // SEG, segment)

    return call(
        kernel,
        "intra_backward",
        (
            shape_of((rows, D), bf16),
            shape_of((rows, D // 2), bf16),
            shape_of((rows, D), f32),
            shape_of((rows, D), f32),
        ),
        [SMEM] + [VMEM] * (10 + fsdp // 2),
        state_scratch(fsdp),
    )(ids, q, k, v, d_num, d_den, cos, sin, wave, wave_t, *far, near)


def inter_backward(ids, k, v, d_k, d_v, cos, sin, far, near):
    rows = k.shape[0]
    fsdp = 2 * len(far)

    def kernel(ids_ref, k_ref, v_ref, dk_ref, dv_ref, cos_ref, sin_ref, *refs):
        far_refs, near_ref = refs[: fsdp // 2], refs[fsdp // 2]
        out_ref, state_scr, norm_scr = refs[fsdp // 2 + 1 :]
        core = ids_ref[0]

        def segment(s):
            at = rows_at(s)
            load_states(s, ids_ref[2], far_refs, near_ref, state_scr, norm_scr)
            cosine, sine = cos_ref[at, :], sin_ref[at, :]

            def pair(p):
                lanes = lanes_at(p)
                cos_part, sin_part, norm_cos, norm_sin = pair_state(p, state_scr, norm_scr, fsdp)
                ks = k_ref[at, lanes].astype(f32)
                vs = v_ref[at, lanes]
                d_k = dk_ref[at, lanes]
                d_k += cosine * (dot_nt(vs, cos_part) + norm_cos)
                d_k += sine * (dot_nt(vs, sin_part) + norm_sin)
                feats = jnp.concatenate(
                    [(ks * cosine).astype(bf16), (ks * sine).astype(bf16)], axis=1
                )
                d_v = dv_ref[at, lanes]
                d_v += dot(feats, jnp.concatenate([cos_part, sin_part], axis=0))
                out_ref[core, at, lanes] = jnp.where(ks > 0.0, d_k, 0.0).astype(bf16)
                out_ref[1 - core, at, lanes] = d_v.astype(bf16)

            loop(PAIRS, pair)

        loop(rows // SEG, segment)

    return call(
        kernel,
        "inter_backward",
        shape_of((2, rows, D), bf16),
        [SMEM] + [VMEM] * (7 + fsdp // 2),
        state_scratch(fsdp),
    )(ids, k, v, d_k, d_v, cos, sin, *far, near)


def input_grad(ids, d_q, d_kv, d_res1, w_q, w_kv):
    rows = d_q.shape[0]

    def kernel(ids_ref, dq_ref, dkv_ref, dres_ref, w_q_ref, w_kv_ref, out_ref):
        core = ids_ref[0]

        def block(i):
            at = rows_at(i)
            total = dres_ref[at, :] + dot_nt(dq_ref[at, :], w_q_ref[:, :D])
            total += dot_nt(dkv_ref[core, at, :], w_kv_ref[:, :D])
            total += dot_nt(dkv_ref[1 - core, at, :], w_kv_ref[:, D:])
            out_ref[at, :] = total

        loop(rows // SEG, block)

    return call(
        kernel, "input_grad", shape_of((rows, D), f32), [SMEM] + [VMEM] * 5
    )(ids, d_q, d_kv, d_res1, w_q, w_kv)


def reversed_bits(index, bits):
    total = 0
    for b in range(bits):
        total = total + (((index >> b) & 1) << (bits - 1 - b))
    return total


def weight_grad(ids, products, fsdp, splits, key, own_half=True, sums=None):
    height = products[0][0].shape[1]
    widths = [product[3].shape[1] for product in products]
    block = height // fsdp
    bits = fsdp.bit_length() - 1
    share = block // len(splits)
    group = min(4, fsdp) * block if block % 128 == 0 else height
    extra = [] if sums is None else [sums]

    def kernel(ids_ref, *refs):
        ins, out_refs = refs[: 4 * len(products)], refs[4 * len(products) + len(extra) :]

        def part(i):
            columns = pl.ds(pl.multiple_of(i * group, 128), group)

            def store(total, left):
                right = left + total.shape[1]
                for j in range(group // block):
                    place = reversed_bits((i * (group // block) + j) ^ ids_ref[2], bits)
                    for n, (split, out_ref) in enumerate(zip(splits, out_refs)):
                        strip = share // split
                        for h in range(split):
                            row = block * j + share * n + strip * h
                            half = h ^ ids_ref[1] if split > 1 else 0
                            out_ref[half, place, :, left:right] = total[
                                row : row + strip, :
                            ].astype(bf16)

            left = 0
            for n, width in enumerate(widths):
                a0_ref, a1_ref, b0_ref, b1_ref = ins[4 * n : 4 * n + 4]
                first = pl.multiple_of(ids_ref[0] * width, 128) if own_half else 0
                total = dot_tn(a0_ref[:, columns], b0_ref[:, pl.ds(first, width)])
                store(total + dot_tn(a1_ref[:, columns], b1_ref[...]), left)
                left += width
            if extra:
                tall = jnp.concatenate(
                    [refs[4 * len(products)][...], jnp.zeros((LANES - 16, height), f32)], axis=0
                )
                store(tall.T, left)

        loop(height // group, part)

    width = sum(widths) + LANES * len(extra)
    return call(
        kernel,
        "weight_grad",
        tuple(shape_of((n, fsdp, share // n, width), bf16) for n in splits),
        [SMEM] + [VMEM] * (4 * len(products) + len(extra)),
        cost=COSTS[key],
    )(ids, *(x for product in products for x in product), *extra)


def add_low(a, b):
    return (a.astype(f32) + b.astype(f32)).astype(bf16)


def core_stage(x):
    (other,) = yield [(x, "group", 0)]
    return other


def halving_stages(keep, send, bits):
    for axis, bit in bits:
        (received,) = yield [(send, axis, bit)]
        half = keep.shape[0] // 2
        if half == 0:
            return add_low(keep[0], received[0])
        keep, send = add_low(keep[:half], received[:half]), add_low(keep[half:], received[half:])


def reduce_stages(x, core):
    half = x.shape[1] // 2
    bits = axis_bits("fsdp")
    keep, send = x[0, :half], x[0, half:]
    x = yield from halving_stages(keep, send, bits)
    for axis, bit in axis_bits("group")[1:]:
        (received,) = yield [(x, axis, bit)]
        x = add_low(x, received)
    other = yield from core_stage(x)
    return ordered(x, other, core == 0, -1).astype(f32)


def share_stages(x, core, chip, twice=False):
    axis, bit = axis_bits("group")[1]
    half = x.shape[1] // 2
    if twice:
        (received,) = yield [(x[1, half:], axis, bit)]
        rest, send = lax.optimization_barrier((x[1, :half], add_low(x[0, half:], received)))
        (received,) = yield [(rest, axis, bit)]
        send, keep = lax.optimization_barrier((send, add_low(x[0, :half], received)))
    else:
        (received,) = yield [(x[1], axis, bit)]
        keep, send = add_low(x[0, :half], received[:half]), add_low(x[0, half:], received[half:])
    x = yield from halving_stages(keep, send, axis_bits("fsdp"))
    (other,) = yield [(x, axis, bit)]
    x = ordered(x, other, chip == 0, 0)
    other = yield from core_stage(x)
    return ordered(x, other, core == 0, -1).astype(f32)


def large_stages(x, core, chip):
    (axis, bit), *bits = axis_bits("fsdp")
    group_axis, group_bit = axis_bits("group")[1]
    half = x.shape[1] // 2
    first = half // 4
    keep, send = x[:, :half], x[:, half:]
    (received,) = yield [(send[:, first:], axis, bit)]
    later = add_low(keep[:, first:], received)
    rest, later = lax.optimization_barrier((send[:, :first], later))
    (received,) = yield [(rest, axis, bit)]
    head = add_low(keep[:, :first], received)
    theirs = jnp.concatenate([head[1], later[1]], axis=0)
    (received,) = yield [(theirs, group_axis, group_bit)]
    head, later = head[0], later[0]
    quarter = half // 2
    ours = jnp.concatenate([head, later[: quarter - first]], axis=0)
    keep = add_low(ours, received[:quarter])
    send = add_low(later[quarter - first :], received[quarter:])
    x = yield from halving_stages(keep, send, bits)
    (other,) = yield [(x, group_axis, group_bit)]
    x = ordered(x, other, chip == 0, 0)
    other = yield from core_stage(x)
    return ordered(x, other, core == 0, -1).astype(f32)


def ordered(x, other, first, axis):
    return jnp.concatenate([jnp.where(first, x, other), jnp.where(first, other, x)], axis=axis)


def ancestor_matrix(parents):
    count = parents.shape[0]
    columns = jnp.arange(count, dtype=jnp.int32)
    step = (parents[:, None] == columns[None, :]).astype(f32)
    same = (columns[:, None] == columns[None, :]).astype(f32)
    reached = step + same
    for _ in range(4):
        reached = (jnp.dot(reached, reached, preferred_element_type=f32) > 0.0).astype(f32)
    return reached - same


def spread_rows(matrix):
    count = matrix.shape[0]
    row = jnp.arange(8 * count, dtype=jnp.int32)
    pick = (row[:, None] // 8 == jnp.arange(count, dtype=jnp.int32)[None, :]).astype(f32)
    wide = jnp.dot(jnp.dot(pick, matrix), pick.T)
    return jnp.where(row[:, None] % 8 == row[None, :] % 8, wide, 0.0).astype(bf16)


def waves(local, segs):
    depth = jnp.sum(local[:segs], axis=1)
    angle = (depth[:, None] * SEG + jnp.arange(SEG, dtype=f32)[None, :]) * (
        math.pi / (2.0 * HORIZON)
    )
    angle = jnp.broadcast_to(angle.reshape(segs * SEG, 1), (segs * SEG, LANES))
    return jnp.cos(angle), jnp.sin(angle)


def gap_wave(position):
    gap = position[:, None] - position[None, :]
    wave = jnp.cos(gap.astype(f32) * (math.pi / (2.0 * HORIZON)))
    return jnp.where(gap >= 0, wave, 0.0), jnp.where(gap <= 0, wave, 0.0)


def vector_columns(vectors):
    return jnp.pad(jnp.stack(vectors), ((0, LANES - len(vectors)), (0, 0))).T


def wide_row(shard, rows):
    return jnp.pad(shard[None], ((0, rows - 1), (0, LANES - shard.shape[0])))


def vector_rows(weight, rows, share, longer):
    per = D // share

    def kernel(w_ref, out_ref):
        out_ref[...] = jnp.zeros_like(out_ref)
        turned = w_ref[:, D:OUT_AT].astype(f32).T
        out_ref[:B_UP, :] = turned[:B_UP, :]
        for block in range(longer * per):
            m, lane = B_UP + block // per, share * (block % per)
            first = rows * block // 8 * 8
            tile = w_ref[first : first + 8, OUT_AT + D :].astype(f32)
            row = rows * block - first
            out_ref[m : m + 1, lane : lane + share] = tile[row : row + 1, :share]

    return call(kernel, "vector_rows", shape_of((16, D), f32), [VMEM])(weight)


def body(
    tokens, cotangent, parent_seg, w_qkv, w_out, b_out, norm1_gain, norm1_bias, w_up, b_up,
    w_down, b_down, norm2_gain, norm2_bias,
):
    fsdp = lax.axis_size("fsdp")
    chips = lax.axis_size("group") // 2
    own = lax.axis_index("fsdp")
    group = lax.axis_index("group")
    core, chip = group % 2, group // 2
    rows = tokens.shape[0]
    segs = rows // SEG
    ff = w_up.shape[1]
    ids = jnp.stack([core, chip, own]).astype(jnp.int32)

    pipe = Pipeline()
    pipe.add("kv", gather_stages(w_qkv[:, D:]))
    pipe.add("tokens", core_stage(tokens))
    pipe.slot()
    pipe.slot(only=("kv",))
    begun = pipe.started[0]
    tokens_other = pipe.read("tokens", begun)

    ancestry = ancestor_matrix(tie(parent_seg[0], begun))
    count = parent_seg.shape[1]
    place = jnp.arange(count, dtype=jnp.int32)
    there = (own ^ (place // segs)) * segs + place % segs
    select = (there[:, None] == place[None, :]).astype(f32)
    local = jnp.dot(jnp.dot(select, ancestry), select.T)
    from_ancestors, from_descendants = spread_rows(local), spread_rows(local.T)
    cos, sin = waves(local, segs)
    wave, wave_t = gap_wave(tie(jnp.arange(SEG, dtype=jnp.int32), begun))
    shard_rows = w_qkv.shape[0]
    columns = vector_columns((b_out, norm1_gain, norm1_bias, b_down, norm2_gain, norm2_bias))
    pipe.add("qo", gather_stages(tie(
        jnp.concatenate([w_qkv[:, :D], columns, w_out, wide_row(b_up, shard_rows)], axis=1), begun
    )))
    pipe.add("up", gather_stages(w_up))
    pipe.add("down", gather_stages(w_down))
    pipe.slot(only=("kv",))
    pipe.slot(*pipe.started, only=("qo",))
    pipe.slot(only=("kv",))
    pipe.slot(*pipe.started, only=("qo",))
    pipe.slot(*pipe.started, only=("up",))
    pipe.slot(only=("kv", "qo"))
    pipe.slot(*pipe.started, only=("up",))
    w_kv = assemble(*pipe.finish("kv", only=("kv",)))
    tables = (from_ancestors, from_descendants, wave, wave_t)
    k, v, increments = project(
        ids, tie(tokens, tokens_other, *tables, *pipe.started), w_kv, cos, sin, fsdp
    )
    pipe.arrive(k, only=("qo",))
    pipe.add("state", trade_stages(increments))
    pipe.slot(*pipe.started, only=("state", "qo"))
    pipe.slot(only=("state", "qo"))
    pipe.slot(*pipe.started, only=("up",))
    w_qo = assemble(*pipe.finish("qo", only=("qo",)))
    pipe.slot(w_qo, only=("down",))
    q, num, den = intra_forward(tie(tokens, *pipe.started), w_qo, k, v, wave)
    far, near = pipe.finish("state", q, only=("state",))
    mixed = mix_segments(from_ancestors, far, near)
    pipe.arrive(q, only=("up", "down"))
    pipe.add("path", trade_stages(mixed))
    pipe.slot(*pipe.started, only=("path", "up"))
    small = vector_rows(tie(w_qo, *pipe.started), shard_rows, b_up.shape[0], ff // D)
    pipe.slot(small, only=("path", "down"))
    pipe.slot(*pipe.started, only=("up",))
    w_up_full = assemble(*pipe.finish("up", only=("up",)))
    path = pipe.finish("path", w_up_full, only=("path",))
    pipe.slot(path[1], only=("down",))
    att, rden = inter_forward(ids, tie(q, *pipe.started), num, den, cos, sin, *path)
    pipe.add("att", core_stage(att))
    pipe.slot(only=("att",))
    pipe.slot(att, only=("down",))
    att_other = pipe.read("att", *pipe.started)
    hat1, inv1, low1, gelu, slope = expand(
        tie(att, att_other, *pipe.started), tokens, w_qo, w_up_full, small
    )
    pipe.slot(low1, only=("down",))
    w_down_full = assemble(*pipe.finish("down", only=("down",)))
    pipe.add("gelu", core_stage(gelu))
    pipe.add("low1", core_stage(low1))
    pipe.slot(w_down_full, only=("gelu", "low1"))
    output, d_res2, d_lower, d_lower_half, sums = contract(
        ids, gelu, hat1, cotangent, w_down_full, small
    )
    low1_other = pipe.read("low1", d_lower)
    gelu_other = pipe.read("gelu", d_lower)
    grads = Pipeline()
    grads.add("d_lower", core_stage(d_lower_half))
    grads.slot(low1_other, gelu_other)
    d_upper, d_upper_half, sums = turn(
        ids, tie(d_lower, *grads.started), slope, w_down_full, sums
    )
    d_lower_other = grads.read("d_lower", d_upper)
    grads.add("d_upper", core_stage(d_upper_half))
    grads.slot(d_lower_other, only=("d_upper",))
    two = chips == 2

    def reduction(part, twice=False):
        return share_stages(part, core, chip, twice) if two else reduce_stages(part, core)

    split = 2 if two else 1
    (down_part,) = weight_grad(
        ids, [(gelu, gelu_other, tie(d_lower, *grads.started), d_lower_other)], fsdp, [split],
        "down",
    )
    d_upper_other = grads.read("d_upper", down_part)
    grads.add("down", reduction(down_part, True))
    grads.slot(d_upper_other, only=("down",))
    (up_part,) = weight_grad(
        ids, [(low1, low1_other, tie(d_upper, *grads.started), d_upper_other)], fsdp, [split], "up",
    )
    large = two and fsdp >= 8
    grads.add("up", large_stages(up_part, core, chip) if large else reduction(up_part))
    grads.slot(only=("up",))
    d_res1, d_mixed, d_mixed_half, d_num, d_den, sums, *back = back_to_heads(
        ids, tie(d_upper, *grads.started), d_res2, hat1, inv1, rden, att, q, cos, sin, w_qo,
        w_up_full, small, sums, fsdp,
    )
    grads.add("state", trade_stages(back))
    grads.slot(only=("state",))
    if two:
        grads.slot(d_num, only=("down",))
    grads.slot(*grads.started, d_num, only=("state",))
    grads.add("d_mixed", core_stage(d_mixed_half))
    grads.slot(*grads.started, only=("d_mixed",))
    grads.slot(*grads.started, only=("up",))
    grads.slot(*grads.started, only=("down",))
    d_mixed_other = grads.read("d_mixed", *grads.started)
    far, near = grads.finish("state", d_mixed_other, only=("state",))
    mixed = mix_segments(from_descendants, far, near)
    grads.add("path", trade_stages(mixed))
    grads.slot(only=("path",))
    grads.slot(*grads.started, only=("up",))
    d_q, d_q_half, d_k, d_v = intra_backward(
        ids, tie(q, *grads.started), k, v, d_num, d_den, cos, sin, wave, wave_t, *path
    )
    grads.add("d_q", core_stage(d_q_half))
    grads.slot(d_q, only=("path", "d_q"))
    grads.arrive(*grads.started, only=("up", "down"))
    d_q_other = grads.read("d_q", *grads.started)
    (outq_part,) = weight_grad(
        ids,
        [
            (att, att_other, d_mixed, d_mixed_other),
            (tokens, tokens_other, d_q, d_q_other),
        ],
        fsdp, [split], "outq", sums=sums,
    )
    grads.add("outq", reduction(outq_part))
    grads.slot(only=("outq",))
    grads.slot(*grads.started, only=("up",))
    back = grads.finish("path", *grads.started, only=("path",))
    d_kv = inter_backward(ids, k, v, d_k, d_v, cos, sin, *back)
    grads.add("d_kv", core_stage(d_kv[1]))
    grads.arrive(d_kv, only=("up",))
    grads.slot(*grads.started, only=("d_kv",))
    grads.slot(*grads.started, only=("up",))
    grads.slot(*grads.started, only=("down",))
    d_kv_other = grads.read("d_kv", *grads.started)
    kv_parts = weight_grad(
        ids, [(tokens, tokens_other, d_kv[0], d_kv_other)], fsdp, [2, 1] if two else [1], "kv",
        False,
    )
    grads.add("kv0", reduction(kv_parts[0]))
    for part in kv_parts[1:]:
        grads.add("kv1", reduce_stages(part, core))
    half = D // 2
    closed = ()

    def close(outq):
        ours, others = jnp.split(outq, 2, axis=1)
        sums = ours[:, D : D + 16] + others[:, D : D + 16]
        q_grad = jnp.concatenate([ours[:, half:D], others[:, half:D]], axis=1)
        out_grad = jnp.concatenate([ours[:, :half], others[:, :half]], axis=1)
        return q_grad, out_grad, sums.T, sums[:, B_UP : B_UP + ff // D].T.reshape(-1)

    written = set()

    def write():
        nonlocal closed
        if not closed and "outq" in grads.finished:
            closed = close(grads.finished["outq"])
            grads.started += closed
        for n in ("up", "down"):
            if n in grads.finished and n not in written:
                written.add(n)
                grads.started += (grads.finished[n],)

    for step in TAIL:
        if step == "grad":
            tokens_grad = input_grad(ids, d_q, tie(d_kv, *grads.started), d_res1, w_qo, w_kv)
            grads.started = (tokens_grad,)
        elif grads.names(step.split("+")):
            grads.slot(*grads.started, only=step.split("+"))
            write()
    while grads.running:
        grads.slot(*grads.started)
        write()
    done = grads.finished
    q_grad, out_grad, sums, b_up_grad = closed or close(done["outq"])
    kv_grad = jnp.concatenate([done[n] for n in ("kv0", "kv1") if n in done], axis=0)
    return (
        output,
        tokens_grad,
        jnp.concatenate([q_grad, kv_grad], axis=1),
        out_grad,
        sums[B_OUT],
        sums[GAIN1],
        sums[BIAS1],
        done["up"],
        b_up_grad,
        done["down"],
        sums[B_DOWN],
        sums[GAIN2],
        sums[BIAS2],
    )


def solution(mesh):
    both = ("group", "fsdp")
    matrix, vector = P(both, None), P(both)
    in_specs = (
        matrix, matrix, P("group", None), matrix, matrix, vector, vector, vector, matrix, vector,
        matrix, vector, vector, vector,
    )
    rows, line = P("fsdp", None), P("fsdp")
    out_specs = (
        matrix, matrix, rows, rows, line, line, line, rows, line, rows, line, line, line,
    )
    return jax.shard_map(body, mesh=mesh, in_specs=in_specs, out_specs=out_specs, check_vma=False)
```

```python
import math

import jax
import jax.numpy as jnp
from jax import lax
from jax.experimental import pallas as pl
from jax.experimental.pallas import tpu as pltpu
from jax.sharding import PartitionSpec as P

D = 768
H = 12
HD = 64
SEG = 256
HORIZON = 2560
PAIRS = H // 2
LANES = 2 * HD
EPS = 1e-05

f32 = jnp.float32
bf16 = jnp.bfloat16

B_OUT, GAIN1, BIAS1, B_DOWN, GAIN2, BIAS2, B_UP = range(7)
OUT_AT = D + LANES


def exchange(x, axis, *bits):
    size, offset = lax.axis_size(axis), sum(1 << b for b in bits)
    return lax.ppermute(x, axis, [(i, i ^ offset) for i in range(size)])


def axis_bits(axis):
    return [(axis, b) for b in range(lax.axis_size(axis).bit_length() - 1)]


def tie(x, *others):
    return lax.optimization_barrier((x,) + others)[0]


def trade_stages(pieces):
    bits = axis_bits("fsdp")[1:]
    requests = []
    for m in range(1, len(pieces)):
        requests.append((pieces[m], "fsdp") + tuple(b for n, (_, b) in enumerate(bits) if m >> n & 1))
    arrived = yield requests
    far = [pieces[0]] + list(arrived)
    (near,) = yield [(jnp.concatenate([x[1:] for x in far], axis=0), "fsdp", 0)]
    return far, near


def near_steps(first_low):
    low, high = axis_bits("fsdp")[:1], axis_bits("group")[1:]
    return low + high if first_low else high + low


def moved(masks, axis, bit):
    step = (1 << bit) * (lax.axis_size("fsdp") if axis == "group" else 1)
    return tuple(m ^ step for m in masks)


def gather_stages(shard, early=False):
    lin = lax.axis_index("group") * lax.axis_size("fsdp") + lax.axis_index("fsdp")
    rows, columns = shard.shape
    if rows % 8:
        whole = lax.all_gather(shard, ("group", "fsdp"), axis=0, tiled=True)
        merged = rows
        while merged % 8:
            merged *= 2
        blocks = whole.reshape(-1, merged, columns)
        yield []
        return [[(blocks, tuple(range(blocks.shape[0])))]], jnp.zeros_like(lin)
    blocks, masks = shard[None], (0,)
    for axis, bit in reversed(axis_bits("fsdp")[1:]):
        (other,) = yield [(blocks, axis, bit)]
        blocks = jnp.concatenate([blocks, other], axis=0)
        masks = masks + moved(masks, axis, bit)
    half = columns // 2
    sides = [(blocks[:, :, :half], masks), (blocks[:, :, half:], masks)]
    steps = [near_steps(True), near_steps(False)]
    for n in range(len(steps[0]) - 1):
        others = yield [(b,) + st[n] for (b, _), st in zip(sides, steps)]
        sides = [
            (jnp.concatenate([b, o], axis=0), m + moved(m, *st[n]))
            for (b, m), st, o in zip(sides, steps, others)
        ]
    core = ("group", 0)
    others = yield [(b,) + st[-1] for (b, _), st in zip(sides, steps)] + (
        [(b,) + core for b, _ in sides] if early else []
    )
    parts = []
    if early:
        lasts = yield [(o,) + core for o in others[:2]]
        for n, ((b, m), st) in enumerate(zip(sides, steps)):
            there = moved(m, *st[-1])
            parts.append([
                (b, m), (others[n], there), (others[n + 2], moved(m, *core)),
                (lasts[n], moved(there, *core)),
            ])
        return parts, lin
    sides = [
        (jnp.concatenate([b, o], axis=0), m + moved(m, *st[-1]))
        for (b, m), st, o in zip(sides, steps, others)
    ]
    lasts = yield [(b,) + core for b, _ in sides]
    return [[(b, m), (last, moved(m, *core))] for (b, m), last in zip(sides, lasts)], lin


class Pipeline:
    def __init__(self):
        self.running = {}
        self.waiting = {}
        self.finished = {}
        self.started = ()

    def add(self, name, stages):
        self.running[name] = (stages, None)

    def names(self, only):
        return [n for n in self.running if only is None or n in only]

    def arrive(self, *others, only=None):
        names = [n for n in self.names(only) if n not in self.waiting]
        arrived = [x for n in names for x in self.running[n][1] or ()]
        if arrived:
            arrived = lax.optimization_barrier(tuple(arrived) + others)[: len(arrived)]
        at, ready = 0, ()
        for n in names:
            stages, results = self.running.pop(n)
            count = len(results or ())
            mine, at = arrived[at : at + count], at + count
            try:
                wanted = next(stages) if results is None else stages.send(mine)
            except StopIteration as done:
                self.finished[n] = done.value
            else:
                self.running[n] = (stages, ())
                self.waiting[n] = wanted
                ready += tuple(w[0] for w in wanted)
        self.started = ready or self.started

    def slot(self, *others, only=None):
        self.arrive(*others, only=only)
        requests = [(n, w) for n in self.names(only) for w in self.waiting.pop(n)]
        operands = tuple(w[0] for _, w in requests)
        if operands and others:
            operands = lax.optimization_barrier(operands + others)[: len(operands)]
        self.started = operands or self.started
        for x, (n, (_, axis, *bits)) in zip(operands, requests):
            stages, results = self.running[n]
            self.running[n] = (stages, results + (exchange(x, axis, *bits),))

    def read(self, name, *others):
        self.arrive(*others, only=(name,))
        return self.finished[name]

    def finish(self, name, *others, only=None):
        while name not in self.finished:
            self.slot(*others, only=only)
        return self.finished[name]


VMEM = pl.BlockSpec(memory_space=pltpu.VMEM)
SMEM = pl.BlockSpec(memory_space=pltpu.SMEM)


COSTS = {"assemble": 1.5, "project": 10.8, "mix_segments": 1.1, "intra_forward": 5.9, "inter_forward": 16.5, "expand": 0.285, "contract": 6.0, "turn": 22.5, "back_to_heads": 11.8, "intra_backward": 10.3, "inter_backward": 4.6, "input_grad": 4.0, "vector_rows": 1.5, "down": 6.0, "up": 1.2, "outq": 3.36, "kv": 3.36}
TAIL = (
    "kv0+kv1",
    "grad",
    "outq",
    "down",
    "kv1",
    "up",
    "kv0",
    "outq",
    "kv1",
    "down",
    "kv0",
    "up",
    "outq",
    "kv1",
    "kv0",
    "up",
    "down",
    "outq",
    "kv1",
    "kv0",
    "outq",
    "kv1",
    "down",
    "kv0",
    "outq",
    "kv1",
    "kv0",
)
FLOPS_PER_US = 6.0e8


def call(kernel, name, outs, in_specs, scratch=(), cost=None, mib=5):
    return pl.pallas_call(
        kernel,
        out_shape=outs,
        in_specs=in_specs,
        out_specs=jax.tree.map(lambda _: VMEM, outs),
        scratch_shapes=scratch,
        compiler_params=pltpu.CompilerParams(vmem_limit_bytes=mib * 1024 * 1024),
        cost_estimate=pl.CostEstimate(
            flops=int((cost or COSTS[name]) * FLOPS_PER_US), transcendentals=0, bytes_accessed=0
        ),
        name=name,
    )


def shape_of(shape, dtype):
    return jax.ShapeDtypeStruct(shape, dtype)


def dot(a, b):
    return lax.dot_general(a, b, (((1,), (0,)), ((), ())), preferred_element_type=f32)


def dot_nt(a, b):
    return lax.dot_general(a, b, (((1,), (1,)), ((), ())), preferred_element_type=f32)


def dot_tn(a, b):
    return lax.dot_general(a, b, (((0,), (0,)), ((), ())), preferred_element_type=f32)


def loop(count, body, unroll=1):
    def step(i, carry):
        body(i)
        return carry

    lax.fori_loop(0, count, step, 0, unroll=unroll)


def rows_at(i):
    return pl.ds(pl.multiple_of(i * SEG, SEG), SEG)


def lanes_at(p):
    return pl.ds(pl.multiple_of(p * LANES, LANES), LANES)


def head_masks(rows):
    lane = lax.broadcasted_iota(jnp.int32, (rows, LANES), 1)
    first = (lane < HD).astype(f32)
    return first.astype(bf16), (1.0 - first).astype(bf16)


def diagonal():
    row = lax.broadcasted_iota(jnp.int32, (LANES, LANES), 0)
    lane = lax.broadcasted_iota(jnp.int32, (LANES, LANES), 1)
    return (row < HD) == (lane < HD)


def head_ones():
    return jnp.where(diagonal(), 1.0, 0.0).astype(bf16)


def split_state(packed):
    same = diagonal()
    cos_part = jnp.where(same, packed, 0.0)
    sin_part = pltpu.roll(jnp.where(same, 0.0, packed), HD, 1)
    return cos_part.astype(bf16), sin_part.astype(bf16)


def state_scratch(fsdp):
    return [pltpu.VMEM((D, LANES), f32), pltpu.VMEM((8 * max(2 * PAIRS, fsdp), LANES), f32)]


def piece_shapes(fsdp, segs):
    return (shape_of((2, segs, D // fsdp + 8, LANES), bf16),) * (fsdp // 2)


def norm_row(n, fsdp):
    per = max(16, fsdp) // fsdp
    return 8 * (n // per) + n % per


def store_states(s, own, left_ref, right_ref, weight_ref, cos_ref, sin_ref, state_scr, norm_scr, out_refs):
    fsdp = 2 * len(out_refs)
    chunk = D // fsdp
    same = diagonal()
    rows = rows_at(s)
    cos, sin = cos_ref[rows, :], sin_ref[rows, :]

    def pair(p):
        lanes = lanes_at(p)
        a = left_ref[rows, lanes]
        b = right_ref[rows, lanes].astype(f32)
        both = jnp.concatenate(
            [(b * cos).astype(bf16), (pltpu.roll(b, HD, 1) * sin).astype(bf16)], axis=1
        )
        product = dot_tn(a, both)
        state_scr[lanes, :] = jnp.where(same, product[:, :LANES], product[:, LANES:])
        wide = a.astype(f32)
        if weight_ref is not None:
            wide = wide * weight_ref[rows, lanes]
        for n, wave in ((p, cos), (PAIRS + p, sin)):
            norm_scr[pl.ds(norm_row(n, fsdp), 1), :] = jnp.sum(wide * wave, axis=0, keepdims=True)

    loop(PAIRS, pair, 3)
    for r in range(fsdp):
        j = own ^ r
        at = pl.ds(pl.multiple_of(chunk * j, 8), chunk)
        norms = pl.ds(pl.multiple_of(8 * j, 8), 8)
        out_refs[r // 2][r % 2, s, 0:chunk, :] = state_scr[at, :].astype(bf16)
        out_refs[r // 2][r % 2, s, chunk : chunk + 8, :] = norm_scr[norms, :].astype(bf16)


def load_states(s, own, far_refs, near_ref, state_scr, norm_scr):
    fsdp = 2 * len(far_refs)
    chunk = D // fsdp
    for r in range(fsdp):
        j = own ^ r
        at = pl.ds(pl.multiple_of(chunk * j, 8), chunk)
        norms = pl.ds(pl.multiple_of(8 * j, 8), 8)
        ref, place = (near_ref, r // 2) if r % 2 else (far_refs[r // 2], 0)
        state_scr[at, :] = ref[place, s, 0:chunk, :].astype(f32)
        norm_scr[norms, :] = ref[place, s, chunk : chunk + 8, :].astype(f32)


def pair_state(p, state_scr, norm_scr, fsdp):
    cos_part, sin_part = split_state(state_scr[lanes_at(p), :])
    norm_cos = norm_scr[pl.ds(norm_row(p, fsdp), 1), :]
    norm_sin = norm_scr[pl.ds(norm_row(PAIRS + p, fsdp), 1), :]
    return cos_part, sin_part, norm_cos, norm_sin


def assemble(parts, lin):
    arrays = [blocks for part in parts for blocks, _ in part]
    places = jnp.concatenate(
        [jnp.array(masks, jnp.int32) for part in parts for _, masks in part]
    ) ^ lin.astype(jnp.int32)
    rows = arrays[0].shape[1]
    count = sum(len(masks) for _, masks in parts[0])
    width = sum(part[0][0].shape[2] for part in parts)
    lefts, left = [], 0
    for part in parts:
        lefts += [left] * len(part)
        left += part[0][0].shape[2]

    def kernel(places_ref, *refs):
        out_ref = refs[-1]
        first = 0
        for ref, at in zip(refs[:-1], lefts):
            number, _, columns = ref.shape

            def place(i, ref=ref, at=at, columns=columns, first=first):
                out_ref[places_ref[first + i], :, at : at + columns] = ref[i]

            loop(number, place)
            first += number

    whole = call(
        kernel, "assemble", shape_of((count, rows, width), bf16), [SMEM] + [VMEM] * len(arrays)
    )(places, *arrays)
    return whole.reshape(count * rows, width)


def project(ids, tokens, w_kv, cos, sin, fsdp):
    rows = tokens.shape[0]
    segs = rows // SEG

    def kernel(ids_ref, tok_ref, w_ref, cos_ref, sin_ref, k_ref, v_ref, *refs):
        inc_refs, (state_scr, norm_scr) = refs[:-2], refs[-2:]
        norm_scr[...] = jnp.zeros_like(norm_scr)

        def segment(s):
            at = rows_at(s)
            x = tok_ref[at, :]
            k_ref[at, :] = jnp.maximum(dot(x, w_ref[:, :D]), 0.0).astype(bf16)
            v_ref[at, :] = dot(x, w_ref[:, D:]).astype(bf16)
            store_states(s, ids_ref[2], k_ref, v_ref, None, cos_ref, sin_ref, state_scr, norm_scr,
                         inc_refs)

        loop(segs, segment)

    act = shape_of((rows, D), bf16)
    k, v, *pieces = call(
        kernel,
        "project",
        (act, act) + piece_shapes(fsdp, segs),
        [SMEM] + [VMEM] * 4,
        state_scratch(fsdp),
    )(ids, tokens, w_kv, cos, sin)
    return k, v, pieces


def mix_segments(spread, far, near):
    fsdp = 2 * len(far)
    _, segs, height, _ = near.shape

    def kernel(spread_ref, *refs):
        far_refs, near_ref, out_refs = refs[: fsdp // 2], refs[fsdp // 2], refs[fsdp // 2 + 1 :]
        for t in range(height // 8):
            at = slice(8 * t, 8 * t + 8)
            stacked = []
            for r in range(fsdp):
                ref, place = (near_ref, r // 2) if r % 2 else (far_refs[r // 2], 0)
                stacked += [ref[place, s, at, :].astype(f32) for s in range(segs)]
            mixed = dot(spread_ref[...], jnp.concatenate(stacked, axis=0).astype(bf16))
            for c in range(fsdp * segs):
                r, s = c // segs, c % segs
                out_refs[r // 2][r % 2, s, at, :] = mixed[8 * c : 8 * c + 8, :].astype(bf16)

    return call(
        kernel, "mix_segments", piece_shapes(fsdp, segs), [VMEM] * (fsdp // 2 + 2)
    )(spread, *far, near)


def intra_forward(tokens, w_q, k, v, wave):
    rows = tokens.shape[0]

    def kernel(tok_ref, w_ref, k_ref, v_ref, wave_ref, q_ref, num_ref, den_ref):
        masks = head_masks(SEG)

        def segment(s):
            at = rows_at(s)
            q_ref[at, :] = jnp.maximum(dot(tok_ref[at, :], w_ref[:, :D]), 0.0).astype(bf16)

            def pair(p):
                lanes = lanes_at(p)
                qs, ks, vs = q_ref[at, lanes], k_ref[at, lanes], v_ref[at, lanes]
                weights, values = [], []
                for m in masks:
                    weights.append((dot_nt(qs, ks * m) * wave_ref[...]).astype(bf16))
                    values.append(jnp.concatenate([vs * m, m], axis=1))
                both = dot(jnp.concatenate(weights, axis=1), jnp.concatenate(values, axis=0))
                num_ref[at, lanes] = both[:, :LANES]
                den_ref[at, lanes] = both[:, LANES:]

            loop(PAIRS, pair, 3)

        loop(rows // SEG, segment)

    wide = shape_of((rows, D), f32)
    return call(
        kernel, "intra_forward", (shape_of((rows, D), bf16), wide, wide), [VMEM] * 5
    )(tokens, w_q, k, v, wave)


def inter_forward(ids, q, num, den, cos, sin, far, near):
    rows = q.shape[0]
    fsdp = 2 * len(far)

    def kernel(ids_ref, q_ref, num_ref, den_ref, cos_ref, sin_ref, *refs):
        far_refs, near_ref = refs[: fsdp // 2], refs[fsdp // 2]
        att_ref, rden_ref, state_scr, norm_scr = refs[fsdp // 2 + 1 :]
        ones = head_ones()
        twice = jnp.concatenate([ones, ones], axis=0)

        def segment(s):
            at = rows_at(s)
            load_states(s, ids_ref[2], far_refs, near_ref, state_scr, norm_scr)

            def pair(p):
                lanes = lanes_at(p)
                cos_part, sin_part, norm_cos, norm_sin = pair_state(p, state_scr, norm_scr, fsdp)
                qs = q_ref[at, lanes].astype(f32)
                q_cos = (qs * cos_ref[at, :]).astype(bf16)
                q_sin = (qs * sin_ref[at, :]).astype(bf16)
                carried = dot(
                    jnp.concatenate([q_cos, q_sin], axis=1),
                    jnp.concatenate([cos_part, sin_part], axis=0),
                )
                along = q_cos.astype(f32) * norm_cos + q_sin.astype(f32) * norm_sin
                high = along.astype(bf16)
                rest = (along - high.astype(f32)).astype(bf16)
                weight = dot(jnp.concatenate([high, rest], axis=1), twice)
                inverse = 1.0 / (den_ref[at, lanes] + weight + 1.0)
                att_ref[at, lanes] = ((num_ref[at, lanes] + carried) * inverse).astype(bf16)
                rden_ref[at, lanes] = inverse

            loop(PAIRS, pair, 3)

        loop(rows // SEG, segment)

    return call(
        kernel,
        "inter_forward",
        (shape_of((rows, D), bf16), shape_of((rows, D), f32)),
        [SMEM] + [VMEM] * (6 + fsdp // 2),
        state_scratch(fsdp),
    )(ids, q, num, den, cos, sin, *far, near)


def standardize(resid):
    centred = resid - jnp.mean(resid, axis=1, keepdims=True)
    inv = lax.rsqrt(jnp.mean(centred * centred, axis=1, keepdims=True) + EPS)
    return centred * inv, inv


def standardize_back(d_hat, hat, inv):
    return inv * (
        d_hat
        - jnp.mean(d_hat, axis=1, keepdims=True)
        - hat * jnp.mean(d_hat * hat, axis=1, keepdims=True)
    )


def expand(att, tokens, w_out, w_up, small):
    rows = att.shape[0]
    ff = w_up.shape[1]

    def kernel(att_ref, tok_ref, out_w_ref, up_ref, small_ref, hat_ref, inv_ref, low_ref, gelu_ref,
               slope_ref):
        def block(i):
            at = rows_at(i)
            mixed = dot(att_ref[at, :], out_w_ref[:, OUT_AT : OUT_AT + D])
            hat, inv = standardize(
                tok_ref[at, :].astype(f32) + mixed + small_ref[B_OUT : B_OUT + 1, :]
            )
            hat_ref[at, :] = hat
            inv_ref[at, :] = jnp.broadcast_to(inv, (SEG, LANES))
            low_ref[at, :] = (
                hat * small_ref[GAIN1 : GAIN1 + 1, :] + small_ref[BIAS1 : BIAS1 + 1, :]
            ).astype(bf16)

            def part(m):
                for c in range(3):
                    columns = pl.ds(pl.multiple_of(m * D + 256 * c, 256), 256)
                    bias = small_ref[pl.ds(B_UP + m, 1), 256 * c : 256 * (c + 1)]
                    upper = dot(low_ref[at, :], up_ref[:, columns]) + bias
                    cdf = 0.5 + 0.5 * lax.erf(upper * math.sqrt(0.5))
                    pdf = jnp.exp(-0.5 * upper * upper) * (1.0 / math.sqrt(2.0 * math.pi))
                    gelu_ref[at, columns] = (upper * cdf).astype(bf16)
                    slope_ref[at, columns] = (cdf + upper * pdf).astype(bf16)

            loop(ff // D, part)

        loop(rows // SEG, block)

    return call(
        kernel,
        "expand",
        (
            shape_of((rows, D), f32),
            shape_of((rows, LANES), f32),
            shape_of((rows, D), bf16),
            shape_of((rows, ff), bf16),
            shape_of((rows, ff), bf16),
        ),
        [VMEM] * 5,
    )(att, tokens, w_out, w_up, small)


def contract(ids, gelu, hat1, cotangent, w_down, small):
    rows, ff = gelu.shape

    def kernel(ids_ref, gelu_ref, hat1_ref, cot_ref, w_ref, small_ref,
               out_ref, dres_ref, dlow_ref, dlow_half_ref, sums_ref):
        sums_ref[...] = jnp.zeros_like(sums_ref)

        def block(i):
            at = rows_at(i)
            normed = hat1_ref[at, :] * small_ref[GAIN1 : GAIN1 + 1, :]
            normed += small_ref[BIAS1 : BIAS1 + 1, :]
            resid = normed + dot(gelu_ref[at, :], w_ref[...]) + small_ref[B_DOWN : B_DOWN + 1, :]
            hat, inv = standardize(resid)
            gain = small_ref[GAIN2 : GAIN2 + 1, :]
            out_ref[at, :] = (hat * gain + small_ref[BIAS2 : BIAS2 + 1, :]).astype(bf16)
            cot = cot_ref[at, :].astype(f32)
            sums_ref[GAIN2 : GAIN2 + 1, :] += jnp.sum(cot * hat, axis=0, keepdims=True)
            sums_ref[BIAS2 : BIAS2 + 1, :] += jnp.sum(cot, axis=0, keepdims=True)
            d_res = standardize_back(cot * gain, hat, inv)
            dres_ref[at, :] = d_res
            d_low = d_res.astype(bf16)
            dlow_ref[at, :] = d_low
            sums_ref[B_DOWN : B_DOWN + 1, :] += jnp.sum(d_low.astype(f32), axis=0, keepdims=True)
            theirs = 1 - ids_ref[0]
            dlow_half_ref[at, :] = dlow_ref[
                at, pl.ds(pl.multiple_of(theirs * (D // 2), 128), D // 2)
            ]

        loop(rows // SEG, block)

    return call(
        kernel,
        "contract",
        (
            shape_of((rows, D), bf16),
            shape_of((rows, D), f32),
            shape_of((rows, D), bf16),
            shape_of((rows, D // 2), bf16),
            shape_of((16, D), f32),
        ),
        [SMEM] + [VMEM] * 5,
    )(ids, gelu, hat1, cotangent, w_down, small)


def turn(ids, d_lower, slope, w_down, sums):
    rows, ff = slope.shape

    def kernel(ids_ref, dlow_ref, slope_ref, w_ref, sums_in_ref, dup_ref, dup_half_ref, sums_ref):
        sums_ref[...] = sums_in_ref[...]

        def block(i):
            at = rows_at(i)

            def part(m):
                for c in range(3):
                    columns = pl.ds(pl.multiple_of(m * D + 256 * c, 256), 256)
                    d_up = dot_nt(dlow_ref[at, :], w_ref[columns, :])
                    d_up = (d_up * slope_ref[at, columns].astype(f32)).astype(bf16)
                    dup_ref[at, columns] = d_up
                    sums_ref[pl.ds(B_UP + m, 1), 256 * c : 256 * (c + 1)] += jnp.sum(
                        d_up.astype(f32), axis=0, keepdims=True
                    )

            loop(ff // D, part)
            theirs = 1 - ids_ref[0]
            dup_half_ref[at, :] = dup_ref[
                at, pl.ds(pl.multiple_of(theirs * (ff // 2), 128), ff // 2)
            ]

        loop(rows // SEG, block)

    return call(
        kernel,
        "turn",
        (
            shape_of((rows, ff), bf16), shape_of((rows, ff // 2), bf16), shape_of((16, D), f32),
        ),
        [SMEM] + [VMEM] * 4,
    )(ids, d_lower, slope, w_down, sums)


def back_to_heads(ids, d_upper, d_res2, hat1, inv1, rden, att, q, cos, sin, w_out, w_up, small,
                  sums, fsdp):
    rows, ff = d_upper.shape
    segs = rows // SEG

    def kernel(ids_ref, dup_ref, dres_ref, hat_ref, inv_ref, rden_ref, att_ref, q_ref, cos_ref,
               sin_ref, out_w_ref, up_ref, small_ref, sums_in_ref,
               dres1_ref, dmix_ref, dmix_half_ref, dnum_ref, dden_ref, sums_ref, *refs):
        inc_refs, (state_scr, norm_scr) = refs[:-2], refs[-2:]
        sums_ref[...] = sums_in_ref[...]
        share = D // fsdp
        for j in range(fsdp):
            for c in range(ff // D):
                at = (j * (ff // D) + c) * share
                m, lane = B_UP + at // D, at % D
                sums_ref[B_UP + c : B_UP + c + 1, share * j : share * (j + 1)] = sums_in_ref[
                    m : m + 1, lane : lane + share
                ]
        norm_scr[...] = jnp.zeros_like(norm_scr)
        ones = head_ones()
        twice = jnp.concatenate([ones, ones], axis=0)

        def block(i):
            at = rows_at(i)
            d_normed = dres_ref[at, :] + dot_nt(dup_ref[at, :], up_ref[...])
            hat = hat_ref[at, :]
            sums_ref[GAIN1 : GAIN1 + 1, :] += jnp.sum(d_normed * hat, axis=0, keepdims=True)
            sums_ref[BIAS1 : BIAS1 + 1, :] += jnp.sum(d_normed, axis=0, keepdims=True)
            d_res = standardize_back(
                d_normed * small_ref[GAIN1 : GAIN1 + 1, :], hat, inv_ref[at, 0:1]
            )
            dres1_ref[at, :] = d_res
            d_mix = d_res.astype(bf16)
            dmix_ref[at, :] = d_mix
            sums_ref[B_OUT : B_OUT + 1, :] += jnp.sum(d_mix.astype(f32), axis=0, keepdims=True)
            d_att = dot_nt(d_mix, out_w_ref[:, OUT_AT : OUT_AT + D])
            inverse = rden_ref[at, :]
            dnum_ref[at, :] = (d_att * inverse).astype(bf16)
            along = d_att * att_ref[at, :].astype(f32)
            for p in range(PAIRS):
                lanes = slice(LANES * p, LANES * (p + 1))
                high = along[:, lanes].astype(bf16)
                rest = (along[:, lanes] - high.astype(f32)).astype(bf16)
                total = dot(jnp.concatenate([high, rest], axis=1), twice)
                dden_ref[at, lanes] = -total * inverse[:, lanes]
            theirs = 1 - ids_ref[0]
            dmix_half_ref[at, :] = dmix_ref[
                at, pl.ds(pl.multiple_of(theirs * (D // 2), 128), D // 2)
            ]
            store_states(i, ids_ref[2], q_ref, dnum_ref, dden_ref, cos_ref, sin_ref, state_scr,
                         norm_scr, inc_refs)

        loop(segs, block)

    return call(
        kernel,
        "back_to_heads",
        (
            shape_of((rows, D), f32),
            shape_of((rows, D), bf16),
            shape_of((rows, D // 2), bf16),
            shape_of((rows, D), bf16),
            shape_of((rows, D), f32),
            shape_of((16, D), f32),
        )
        + piece_shapes(fsdp, segs),
        [SMEM] + [VMEM] * 13,
        state_scratch(fsdp),
    )(ids, d_upper, d_res2, hat1, inv1, rden, att, q, cos, sin, w_out, w_up, small, sums)


def intra_backward(ids, q, k, v, d_num, d_den, cos, sin, wave, wave_t, far, near):
    rows = q.shape[0]
    fsdp = 2 * len(far)

    def kernel(ids_ref, q_ref, k_ref, v_ref, dnum_ref, dden_ref, cos_ref, sin_ref, wave_ref,
               wave_t_ref, *refs):
        far_refs, near_ref = refs[: fsdp // 2], refs[fsdp // 2]
        dq_ref, dq_half_ref, dk_ref, dv_ref, state_scr, norm_scr = refs[fsdp // 2 + 1 :]
        masks = head_masks(SEG)
        lane = lax.broadcasted_iota(jnp.int32, (SEG, LANES), 1) % HD
        picks = [jnp.where(lane < 2, m.astype(f32), 0.0).astype(bf16) for m in masks]

        def segment(s):
            at = rows_at(s)
            load_states(s, ids_ref[2], far_refs, near_ref, state_scr, norm_scr)
            cosine, sine = cos_ref[at, :], sin_ref[at, :]

            def pair(p):
                lanes = lanes_at(p)
                qs, ks, vs = q_ref[at, lanes], k_ref[at, lanes], v_ref[at, lanes]
                dn, dd = dnum_ref[at, lanes], dden_ref[at, lanes]
                high = dd.astype(bf16).astype(f32)
                spread = jnp.where(lane == 0, high, jnp.where(lane == 1, dd - high, 0.0))
                grads = jnp.concatenate([dn, spread.astype(bf16)], axis=1)
                w_ts, d_ss, d_ts, khs, qhs, dns = [], [], [], [], [], []
                for m, pick in zip(masks, picks):
                    kh = ks * m
                    values = jnp.concatenate([vs * m, pick], axis=1)
                    w_ts.append((dot_nt(kh, qs) * wave_t_ref[...]).astype(bf16))
                    d_ss.append((dot_nt(grads, values) * wave_ref[...]).astype(bf16))
                    d_ts.append((dot_nt(values, grads) * wave_t_ref[...]).astype(bf16))
                    khs.append(kh)
                    qhs.append(qs * m)
                    dns.append(dn * m)

                def both(left, right):
                    return dot(jnp.concatenate(left, axis=1), jnp.concatenate(right, axis=0))

                dk_ref[at, lanes] = both(d_ts, qhs)
                dv_ref[at, lanes] = both(w_ts, dns)
                d_q = both(d_ss, khs)
                cos_part, sin_part, norm_cos, norm_sin = pair_state(p, state_scr, norm_scr, fsdp)
                d_q += cosine * (dot_nt(dn, cos_part) + dd * norm_cos)
                d_q += sine * (dot_nt(dn, sin_part) + dd * norm_sin)
                dq_ref[at, lanes] = jnp.where(qs.astype(f32) > 0.0, d_q, 0.0).astype(bf16)

            loop(PAIRS, pair, 3)
            theirs = 1 - ids_ref[0]
            dq_half_ref[at, :] = dq_ref[at, pl.ds(pl.multiple_of(theirs * (D // 2), 128), D // 2)]

        loop(rows // SEG, segment)

    return call(
        kernel,
        "intra_backward",
        (
            shape_of((rows, D), bf16),
            shape_of((rows, D // 2), bf16),
            shape_of((rows, D), f32),
            shape_of((rows, D), f32),
        ),
        [SMEM] + [VMEM] * (10 + fsdp // 2),
        state_scratch(fsdp),
    )(ids, q, k, v, d_num, d_den, cos, sin, wave, wave_t, *far, near)


def inter_backward(ids, k, v, d_k, d_v, cos, sin, far, near):
    rows = k.shape[0]
    fsdp = 2 * len(far)

    def kernel(ids_ref, k_ref, v_ref, dk_ref, dv_ref, cos_ref, sin_ref, *refs):
        far_refs, near_ref = refs[: fsdp // 2], refs[fsdp // 2]
        out_ref, state_scr, norm_scr = refs[fsdp // 2 + 1 :]
        core = ids_ref[0]

        def segment(s):
            at = rows_at(s)
            load_states(s, ids_ref[2], far_refs, near_ref, state_scr, norm_scr)
            cosine, sine = cos_ref[at, :], sin_ref[at, :]

            def pair(p):
                lanes = lanes_at(p)
                cos_part, sin_part, norm_cos, norm_sin = pair_state(p, state_scr, norm_scr, fsdp)
                ks = k_ref[at, lanes].astype(f32)
                vs = v_ref[at, lanes]
                d_k = dk_ref[at, lanes]
                d_k += cosine * (dot_nt(vs, cos_part) + norm_cos)
                d_k += sine * (dot_nt(vs, sin_part) + norm_sin)
                feats = jnp.concatenate(
                    [(ks * cosine).astype(bf16), (ks * sine).astype(bf16)], axis=1
                )
                d_v = dv_ref[at, lanes]
                d_v += dot(feats, jnp.concatenate([cos_part, sin_part], axis=0))
                out_ref[core, at, lanes] = jnp.where(ks > 0.0, d_k, 0.0).astype(bf16)
                out_ref[1 - core, at, lanes] = d_v.astype(bf16)

            loop(PAIRS, pair, 3)

        loop(rows // SEG, segment)

    return call(
        kernel,
        "inter_backward",
        shape_of((2, rows, D), bf16),
        [SMEM] + [VMEM] * (7 + fsdp // 2),
        state_scratch(fsdp),
    )(ids, k, v, d_k, d_v, cos, sin, *far, near)


def input_grad(ids, d_q, d_kv, d_res1, w_q, w_kv):
    rows = d_q.shape[0]

    def kernel(ids_ref, dq_ref, dkv_ref, dres_ref, w_q_ref, w_kv_ref, out_ref):
        core = ids_ref[0]

        def block(i):
            at = rows_at(i)
            total = dres_ref[at, :] + dot_nt(dq_ref[at, :], w_q_ref[:, :D])
            total += dot_nt(dkv_ref[core, at, :], w_kv_ref[:, :D])
            total += dot_nt(dkv_ref[1 - core, at, :], w_kv_ref[:, D:])
            out_ref[at, :] = total

        loop(rows // SEG, block)

    return call(
        kernel, "input_grad", shape_of((rows, D), f32), [SMEM] + [VMEM] * 5
    )(ids, d_q, d_kv, d_res1, w_q, w_kv)


def reversed_bits(index, bits):
    total = 0
    for b in range(bits):
        total = total + (((index >> b) & 1) << (bits - 1 - b))
    return total


def weight_grad(ids, products, fsdp, splits, key, own_half=True, sums=None):
    height = products[0][0].shape[1]
    widths = [product[3].shape[1] for product in products]
    block = height // fsdp
    bits = fsdp.bit_length() - 1
    share = block // len(splits)
    group = min(4, fsdp) * block if block % 128 == 0 else height
    extra = [] if sums is None else [sums]

    def kernel(ids_ref, *refs):
        ins, out_refs = refs[: 4 * len(products)], refs[4 * len(products) + len(extra) :]

        def part(i):
            columns = pl.ds(pl.multiple_of(i * group, 128), group)

            def store(total, left):
                right = left + total.shape[1]
                for j in range(group // block):
                    place = reversed_bits((i * (group // block) + j) ^ ids_ref[2], bits)
                    for n, (split, out_ref) in enumerate(zip(splits, out_refs)):
                        strip = share // split
                        for h in range(split):
                            row = block * j + share * n + strip * h
                            half = h ^ ids_ref[1] if split > 1 else 0
                            out_ref[half, place, :, left:right] = total[
                                row : row + strip, :
                            ].astype(bf16)

            left = 0
            for n, width in enumerate(widths):
                a0_ref, a1_ref, b0_ref, b1_ref = ins[4 * n : 4 * n + 4]
                first = pl.multiple_of(ids_ref[0] * width, 128) if own_half else 0
                total = dot_tn(a0_ref[:, columns], b0_ref[:, pl.ds(first, width)])
                store(total + dot_tn(a1_ref[:, columns], b1_ref[...]), left)
                left += width
            if extra:
                tall = jnp.concatenate(
                    [refs[4 * len(products)][...], jnp.zeros((LANES - 16, height), f32)], axis=0
                )
                store(tall.T, left)

        loop(height // group, part)

    width = sum(widths) + LANES * len(extra)
    return call(
        kernel,
        "weight_grad",
        tuple(shape_of((n, fsdp, share // n, width), bf16) for n in splits),
        [SMEM] + [VMEM] * (4 * len(products) + len(extra)),
        cost=COSTS[key],
    )(ids, *(x for product in products for x in product), *extra)


def add_low(a, b):
    return (a.astype(f32) + b.astype(f32)).astype(bf16)


def core_stage(x):
    (other,) = yield [(x, "group", 0)]
    return other


def halving_stages(keep, send, bits):
    for axis, bit in bits:
        (received,) = yield [(send, axis, bit)]
        half = keep.shape[0] // 2
        if half == 0:
            return add_low(keep[0], received[0])
        keep, send = add_low(keep[:half], received[:half]), add_low(keep[half:], received[half:])


def reduce_stages(x, core):
    half = x.shape[1] // 2
    bits = axis_bits("fsdp")
    keep, send = x[0, :half], x[0, half:]
    x = yield from halving_stages(keep, send, bits)
    for axis, bit in axis_bits("group")[1:]:
        (received,) = yield [(x, axis, bit)]
        x = add_low(x, received)
    other = yield from core_stage(x)
    return ordered(x, other, core == 0, -1).astype(f32)


def share_stages(x, core, chip, twice=False):
    axis, bit = axis_bits("group")[1]
    half = x.shape[1] // 2
    if twice:
        (received,) = yield [(x[1, half:], axis, bit)]
        rest, send = lax.optimization_barrier((x[1, :half], add_low(x[0, half:], received)))
        (received,) = yield [(rest, axis, bit)]
        send, keep = lax.optimization_barrier((send, add_low(x[0, :half], received)))
    else:
        (received,) = yield [(x[1], axis, bit)]
        keep, send = add_low(x[0, :half], received[:half]), add_low(x[0, half:], received[half:])
    x = yield from halving_stages(keep, send, axis_bits("fsdp"))
    (other,) = yield [(x, axis, bit)]
    x = ordered(x, other, chip == 0, 0)
    other = yield from core_stage(x)
    return ordered(x, other, core == 0, -1).astype(f32)


def large_stages(x, core, chip):
    (axis, bit), *bits = axis_bits("fsdp")
    group_axis, group_bit = axis_bits("group")[1]
    half = x.shape[1] // 2
    first = half // 4
    keep, send = x[:, :half], x[:, half:]
    (received,) = yield [(send[:, first:], axis, bit)]
    later = add_low(keep[:, first:], received)
    rest, later = lax.optimization_barrier((send[:, :first], later))
    (received,) = yield [(rest, axis, bit)]
    head = add_low(keep[:, :first], received)
    theirs = jnp.concatenate([head[1], later[1]], axis=0)
    (received,) = yield [(theirs, group_axis, group_bit)]
    head, later = head[0], later[0]
    quarter = half // 2
    ours = jnp.concatenate([head, later[: quarter - first]], axis=0)
    keep = add_low(ours, received[:quarter])
    send = add_low(later[quarter - first :], received[quarter:])
    x = yield from halving_stages(keep, send, bits)
    (other,) = yield [(x, group_axis, group_bit)]
    x = ordered(x, other, chip == 0, 0)
    other = yield from core_stage(x)
    return ordered(x, other, core == 0, -1).astype(f32)


def ordered(x, other, first, axis):
    return jnp.concatenate([jnp.where(first, x, other), jnp.where(first, other, x)], axis=axis)


def ancestor_matrix(parents):
    count = parents.shape[0]
    columns = jnp.arange(count, dtype=jnp.int32)
    step = (parents[:, None] == columns[None, :]).astype(f32)
    same = (columns[:, None] == columns[None, :]).astype(f32)
    reached = step + same
    for _ in range(4):
        reached = (jnp.dot(reached, reached, preferred_element_type=f32) > 0.0).astype(f32)
    return reached - same


def spread_rows(matrix):
    count = matrix.shape[0]
    row = jnp.arange(8 * count, dtype=jnp.int32)
    pick = (row[:, None] // 8 == jnp.arange(count, dtype=jnp.int32)[None, :]).astype(f32)
    wide = jnp.dot(jnp.dot(pick, matrix), pick.T)
    return jnp.where(row[:, None] % 8 == row[None, :] % 8, wide, 0.0).astype(bf16)


def waves(local, segs):
    depth = jnp.sum(local[:segs], axis=1)
    angle = (depth[:, None] * SEG + jnp.arange(SEG, dtype=f32)[None, :]) * (
        math.pi / (2.0 * HORIZON)
    )
    angle = jnp.broadcast_to(angle.reshape(segs * SEG, 1), (segs * SEG, LANES))
    return jnp.cos(angle), jnp.sin(angle)


def gap_wave(position):
    gap = position[:, None] - position[None, :]
    wave = jnp.cos(gap.astype(f32) * (math.pi / (2.0 * HORIZON)))
    return jnp.where(gap >= 0, wave, 0.0), jnp.where(gap <= 0, wave, 0.0)


def vector_columns(vectors):
    return jnp.pad(jnp.stack(vectors), ((0, LANES - len(vectors)), (0, 0))).T


def wide_row(shard, rows):
    return jnp.pad(shard[None], ((0, rows - 1), (0, LANES - shard.shape[0])))


def vector_rows(weight, rows, share, longer):
    per = D // share

    def kernel(w_ref, out_ref):
        out_ref[...] = jnp.zeros_like(out_ref)
        turned = w_ref[:, D:OUT_AT].astype(f32).T
        out_ref[:B_UP, :] = turned[:B_UP, :]
        for block in range(longer * per):
            m, lane = B_UP + block // per, share * (block % per)
            first = rows * block // 8 * 8
            tile = w_ref[first : first + 8, OUT_AT + D :].astype(f32)
            row = rows * block - first
            out_ref[m : m + 1, lane : lane + share] = tile[row : row + 1, :share]

    return call(kernel, "vector_rows", shape_of((16, D), f32), [VMEM])(weight)


def body(
    tokens, cotangent, parent_seg, w_qkv, w_out, b_out, norm1_gain, norm1_bias, w_up, b_up,
    w_down, b_down, norm2_gain, norm2_bias,
):
    fsdp = lax.axis_size("fsdp")
    chips = lax.axis_size("group") // 2
    own = lax.axis_index("fsdp")
    group = lax.axis_index("group")
    core, chip = group % 2, group // 2
    rows = tokens.shape[0]
    segs = rows // SEG
    ff = w_up.shape[1]
    ids = jnp.stack([core, chip, own]).astype(jnp.int32)

    pipe = Pipeline()
    pipe.add("kv", gather_stages(w_qkv[:, D:]))
    pipe.add("tokens", core_stage(tokens))
    pipe.slot()
    pipe.slot(only=("kv",))
    begun = pipe.started[0]
    tokens_other = pipe.read("tokens", begun)

    ancestry = ancestor_matrix(tie(parent_seg[0], begun))
    count = parent_seg.shape[1]
    place = jnp.arange(count, dtype=jnp.int32)
    there = (own ^ (place // segs)) * segs + place % segs
    select = (there[:, None] == place[None, :]).astype(f32)
    local = jnp.dot(jnp.dot(select, ancestry), select.T)
    from_ancestors, from_descendants = spread_rows(local), spread_rows(local.T)
    cos, sin = waves(local, segs)
    wave, wave_t = gap_wave(tie(jnp.arange(SEG, dtype=jnp.int32), begun))
    shard_rows = w_qkv.shape[0]
    columns = vector_columns((b_out, norm1_gain, norm1_bias, b_down, norm2_gain, norm2_bias))
    pipe.add("qo", gather_stages(tie(
        jnp.concatenate([w_qkv[:, :D], columns, w_out, wide_row(b_up, shard_rows)], axis=1), begun
    )))
    pipe.add("up", gather_stages(w_up))
    pipe.add("down", gather_stages(w_down))
    pipe.slot(only=("kv",))
    pipe.slot(*pipe.started, only=("qo",))
    pipe.slot(only=("kv",))
    pipe.slot(*pipe.started, only=("qo",))
    pipe.slot(*pipe.started, only=("up",))
    pipe.slot(only=("kv", "qo"))
    pipe.slot(*pipe.started, only=("up",))
    w_kv = assemble(*pipe.finish("kv", only=("kv",)))
    tables = (from_ancestors, from_descendants, wave, wave_t)
    k, v, increments = project(
        ids, tie(tokens, tokens_other, *tables, *pipe.started), w_kv, cos, sin, fsdp
    )
    pipe.arrive(k, only=("qo",))
    pipe.add("state", trade_stages(increments))
    pipe.slot(*pipe.started, only=("state", "qo"))
    pipe.slot(only=("state", "qo"))
    pipe.slot(*pipe.started, only=("up",))
    w_qo = assemble(*pipe.finish("qo", only=("qo",)))
    pipe.slot(w_qo, only=("down",))
    q, num, den = intra_forward(tie(tokens, *pipe.started), w_qo, k, v, wave)
    far, near = pipe.finish("state", q, only=("state",))
    mixed = mix_segments(from_ancestors, far, near)
    pipe.arrive(q, only=("up", "down"))
    pipe.add("path", trade_stages(mixed))
    pipe.slot(*pipe.started, only=("path", "up"))
    small = vector_rows(tie(w_qo, *pipe.started), shard_rows, b_up.shape[0], ff // D)
    pipe.slot(small, only=("path", "down"))
    pipe.slot(*pipe.started, only=("up",))
    w_up_full = assemble(*pipe.finish("up", only=("up",)))
    path = pipe.finish("path", w_up_full, only=("path",))
    pipe.slot(path[1], only=("down",))
    att, rden = inter_forward(ids, tie(q, *pipe.started), num, den, cos, sin, *path)
    pipe.add("att", core_stage(att))
    pipe.slot(only=("att",))
    pipe.slot(att, only=("down",))
    att_other = pipe.read("att", *pipe.started)
    hat1, inv1, low1, gelu, slope = expand(
        tie(att, att_other, *pipe.started), tokens, w_qo, w_up_full, small
    )
    pipe.slot(low1, only=("down",))
    w_down_full = assemble(*pipe.finish("down", only=("down",)))
    pipe.add("gelu", core_stage(gelu))
    pipe.add("low1", core_stage(low1))
    pipe.slot(w_down_full, only=("gelu", "low1"))
    output, d_res2, d_lower, d_lower_half, sums = contract(
        ids, gelu, hat1, cotangent, w_down_full, small
    )
    low1_other = pipe.read("low1", d_lower)
    gelu_other = pipe.read("gelu", d_lower)
    grads = Pipeline()
    grads.add("d_lower", core_stage(d_lower_half))
    grads.slot(low1_other, gelu_other)
    d_upper, d_upper_half, sums = turn(
        ids, tie(d_lower, *grads.started), slope, w_down_full, sums
    )
    d_lower_other = grads.read("d_lower", d_upper)
    grads.add("d_upper", core_stage(d_upper_half))
    grads.slot(d_lower_other, only=("d_upper",))
    two = chips == 2

    def reduction(part, twice=False):
        return share_stages(part, core, chip, twice) if two else reduce_stages(part, core)

    split = 2 if two else 1
    (down_part,) = weight_grad(
        ids, [(gelu, gelu_other, tie(d_lower, *grads.started), d_lower_other)], fsdp, [split],
        "down",
    )
    d_upper_other = grads.read("d_upper", down_part)
    grads.add("down", reduction(down_part, True))
    grads.slot(d_upper_other, only=("down",))
    (up_part,) = weight_grad(
        ids, [(low1, low1_other, tie(d_upper, *grads.started), d_upper_other)], fsdp, [split], "up",
    )
    large = two and fsdp >= 8
    grads.add("up", large_stages(up_part, core, chip) if large else reduction(up_part))
    grads.slot(only=("up",))
    d_res1, d_mixed, d_mixed_half, d_num, d_den, sums, *back = back_to_heads(
        ids, tie(d_upper, *grads.started), d_res2, hat1, inv1, rden, att, q, cos, sin, w_qo,
        w_up_full, small, sums, fsdp,
    )
    grads.add("state", trade_stages(back))
    grads.slot(only=("state",))
    if two:
        grads.slot(d_num, only=("down",))
    grads.slot(*grads.started, d_num, only=("state",))
    grads.add("d_mixed", core_stage(d_mixed_half))
    grads.slot(*grads.started, only=("d_mixed",))
    grads.slot(*grads.started, only=("up",))
    grads.slot(*grads.started, only=("down",))
    d_mixed_other = grads.read("d_mixed", *grads.started)
    far, near = grads.finish("state", d_mixed_other, only=("state",))
    mixed = mix_segments(from_descendants, far, near)
    grads.add("path", trade_stages(mixed))
    grads.slot(only=("path",))
    grads.slot(*grads.started, only=("up",))
    d_q, d_q_half, d_k, d_v = intra_backward(
        ids, tie(q, *grads.started), k, v, d_num, d_den, cos, sin, wave, wave_t, *path
    )
    grads.add("d_q", core_stage(d_q_half))
    grads.slot(d_q, only=("path", "d_q"))
    grads.arrive(*grads.started, only=("up", "down"))
    d_q_other = grads.read("d_q", *grads.started)
    (outq_part,) = weight_grad(
        ids,
        [
            (att, att_other, d_mixed, d_mixed_other),
            (tokens, tokens_other, d_q, d_q_other),
        ],
        fsdp, [split], "outq", sums=sums,
    )
    grads.add("outq", reduction(outq_part))
    grads.slot(only=("outq",))
    grads.slot(*grads.started, only=("up",))
    back = grads.finish("path", *grads.started, only=("path",))
    d_kv = inter_backward(ids, k, v, d_k, d_v, cos, sin, *back)
    grads.add("d_kv", core_stage(d_kv[1]))
    grads.arrive(d_kv, only=("up",))
    grads.slot(*grads.started, only=("d_kv",))
    grads.slot(*grads.started, only=("up",))
    grads.slot(*grads.started, only=("down",))
    d_kv_other = grads.read("d_kv", *grads.started)
    kv_parts = weight_grad(
        ids, [(tokens, tokens_other, d_kv[0], d_kv_other)], fsdp, [2, 1] if two else [1], "kv",
        False,
    )
    grads.add("kv0", reduction(kv_parts[0]))
    for part in kv_parts[1:]:
        grads.add("kv1", reduce_stages(part, core))
    half = D // 2
    closed = ()

    def close(outq):
        ours, others = jnp.split(outq, 2, axis=1)
        sums = ours[:, D : D + 16] + others[:, D : D + 16]
        q_grad = jnp.concatenate([ours[:, half:D], others[:, half:D]], axis=1)
        out_grad = jnp.concatenate([ours[:, :half], others[:, :half]], axis=1)
        return q_grad, out_grad, sums.T, sums[:, B_UP : B_UP + ff // D].T.reshape(-1)

    written = set()

    def write():
        nonlocal closed
        if not closed and "outq" in grads.finished:
            closed = close(grads.finished["outq"])
            grads.started += closed
        for n in ("up", "down"):
            if n in grads.finished and n not in written:
                written.add(n)
                grads.started += (grads.finished[n],)

    for step in TAIL:
        if step == "grad":
            tokens_grad = input_grad(ids, d_q, tie(d_kv, *grads.started), d_res1, w_qo, w_kv)
            grads.started = (tokens_grad,)
        elif grads.names(step.split("+")):
            grads.slot(*grads.started, only=step.split("+"))
            write()
    while grads.running:
        grads.slot(*grads.started)
        write()
    done = grads.finished
    q_grad, out_grad, sums, b_up_grad = closed or close(done["outq"])
    kv_grad = jnp.concatenate([done[n] for n in ("kv0", "kv1") if n in done], axis=0)
    return (
        output,
        tokens_grad,
        jnp.concatenate([q_grad, kv_grad], axis=1),
        out_grad,
        sums[B_OUT],
        sums[GAIN1],
        sums[BIAS1],
        done["up"],
        b_up_grad,
        done["down"],
        sums[B_DOWN],
        sums[GAIN2],
        sums[BIAS2],
    )


def solution(mesh):
    both = ("group", "fsdp")
    matrix, vector = P(both, None), P(both)
    in_specs = (
        matrix, matrix, P("group", None), matrix, matrix, vector, vector, vector, matrix, vector,
        matrix, vector, vector, vector,
    )
    rows, line = P("fsdp", None), P("fsdp")
    out_specs = (
        matrix, matrix, rows, rows, line, line, line, rows, line, rows, line, line, line,
    )
    return jax.shard_map(body, mesh=mesh, in_specs=in_specs, out_specs=out_specs, check_vma=False)
```

```python
import math

import jax
import jax.numpy as jnp
from jax import lax
from jax.experimental import pallas as pl
from jax.experimental.pallas import tpu as pltpu
from jax.sharding import PartitionSpec as P

D = 768
H = 12
HD = 64
SEG = 256
HORIZON = 2560
PAIRS = H // 2
LANES = 2 * HD
EPS = 1e-05

f32 = jnp.float32
bf16 = jnp.bfloat16

B_OUT, GAIN1, BIAS1, B_DOWN, GAIN2, BIAS2, B_UP = range(7)
OUT_AT = D + LANES


def exchange(x, axis, *bits):
    size, offset = lax.axis_size(axis), sum(1 << b for b in bits)
    return lax.ppermute(x, axis, [(i, i ^ offset) for i in range(size)])


def axis_bits(axis):
    return [(axis, b) for b in range(lax.axis_size(axis).bit_length() - 1)]


def tie(x, *others):
    return lax.optimization_barrier((x,) + others)[0]


def trade_stages(pieces):
    bits = axis_bits("fsdp")[1:]
    requests = []
    for m in range(1, len(pieces)):
        requests.append((pieces[m], "fsdp") + tuple(b for n, (_, b) in enumerate(bits) if m >> n & 1))
    arrived = yield requests
    far = [pieces[0]] + list(arrived)
    (near,) = yield [(jnp.concatenate([x[1:] for x in far], axis=0), "fsdp", 0)]
    return far, near


def near_steps(first_low):
    low, high = axis_bits("fsdp")[:1], axis_bits("group")[1:]
    return low + high if first_low else high + low


def moved(masks, axis, bit):
    step = (1 << bit) * (lax.axis_size("fsdp") if axis == "group" else 1)
    return tuple(m ^ step for m in masks)


def gather_stages(shard, early=False):
    lin = lax.axis_index("group") * lax.axis_size("fsdp") + lax.axis_index("fsdp")
    rows, columns = shard.shape
    if rows % 8:
        whole = lax.all_gather(shard, ("group", "fsdp"), axis=0, tiled=True)
        merged = rows
        while merged % 8:
            merged *= 2
        blocks = whole.reshape(-1, merged, columns)
        yield []
        return [[(blocks, tuple(range(blocks.shape[0])))]], jnp.zeros_like(lin)
    blocks, masks = shard[None], (0,)
    for axis, bit in reversed(axis_bits("fsdp")[1:]):
        (other,) = yield [(blocks, axis, bit)]
        blocks = jnp.concatenate([blocks, other], axis=0)
        masks = masks + moved(masks, axis, bit)
    half = columns // 2
    sides = [(blocks[:, :, :half], masks), (blocks[:, :, half:], masks)]
    steps = [near_steps(True), near_steps(False)]
    for n in range(len(steps[0]) - 1):
        others = yield [(b,) + st[n] for (b, _), st in zip(sides, steps)]
        sides = [
            (jnp.concatenate([b, o], axis=0), m + moved(m, *st[n]))
            for (b, m), st, o in zip(sides, steps, others)
        ]
    core = ("group", 0)
    others = yield [(b,) + st[-1] for (b, _), st in zip(sides, steps)] + (
        [(b,) + core for b, _ in sides] if early else []
    )
    parts = []
    if early:
        lasts = yield [(o,) + core for o in others[:2]]
        for n, ((b, m), st) in enumerate(zip(sides, steps)):
            there = moved(m, *st[-1])
            parts.append([
                (b, m), (others[n], there), (others[n + 2], moved(m, *core)),
                (lasts[n], moved(there, *core)),
            ])
        return parts, lin
    sides = [
        (jnp.concatenate([b, o], axis=0), m + moved(m, *st[-1]))
        for (b, m), st, o in zip(sides, steps, others)
    ]
    lasts = yield [(b,) + core for b, _ in sides]
    return [[(b, m), (last, moved(m, *core))] for (b, m), last in zip(sides, lasts)], lin


class Pipeline:
    def __init__(self):
        self.running = {}
        self.waiting = {}
        self.finished = {}
        self.started = ()

    def add(self, name, stages):
        self.running[name] = (stages, None)

    def names(self, only):
        return [n for n in self.running if only is None or n in only]

    def arrive(self, *others, only=None):
        names = [n for n in self.names(only) if n not in self.waiting]
        arrived = [x for n in names for x in self.running[n][1] or ()]
        if arrived:
            arrived = lax.optimization_barrier(tuple(arrived) + others)[: len(arrived)]
        at, ready = 0, ()
        for n in names:
            stages, results = self.running.pop(n)
            count = len(results or ())
            mine, at = arrived[at : at + count], at + count
            try:
                wanted = next(stages) if results is None else stages.send(mine)
            except StopIteration as done:
                self.finished[n] = done.value
            else:
                self.running[n] = (stages, ())
                self.waiting[n] = wanted
                ready += tuple(w[0] for w in wanted)
        self.started = ready or self.started

    def slot(self, *others, only=None):
        self.arrive(*others, only=only)
        requests = [(n, w) for n in self.names(only) for w in self.waiting.pop(n)]
        operands = tuple(w[0] for _, w in requests)
        if operands and others:
            operands = lax.optimization_barrier(operands + others)[: len(operands)]
        self.started = operands or self.started
        for x, (n, (_, axis, *bits)) in zip(operands, requests):
            stages, results = self.running[n]
            self.running[n] = (stages, results + (exchange(x, axis, *bits),))

    def read(self, name, *others):
        self.arrive(*others, only=(name,))
        return self.finished[name]

    def finish(self, name, *others, only=None):
        while name not in self.finished:
            self.slot(*others, only=only)
        return self.finished[name]


VMEM = pl.BlockSpec(memory_space=pltpu.VMEM)
SMEM = pl.BlockSpec(memory_space=pltpu.SMEM)


COSTS = {"assemble": 1.5, "project": 10.8, "mix_segments": 1.1, "intra_forward": 5.9, "inter_forward": 16.5, "expand": 0.285, "contract": 6.0, "turn": 22.5, "back_to_heads": 11.8, "intra_backward": 10.3, "inter_backward": 4.6, "input_grad": 4.0, "vector_rows": 1.5, "down": 6.0, "up": 1.2, "outq": 3.36, "kv": 3.36}
TAIL = (
    "kv0+kv1",
    "grad",
    "outq",
    "down",
    "kv1",
    "up",
    "kv0",
    "outq",
    "kv1",
    "down",
    "kv0",
    "up",
    "outq",
    "kv1",
    "kv0",
    "up",
    "down",
    "outq",
    "kv1",
    "kv0",
    "outq",
    "kv1",
    "down",
    "kv0",
    "outq",
    "kv1",
    "kv0",
)
FLOPS_PER_US = 6.0e8


def call(kernel, name, outs, in_specs, scratch=(), cost=None, mib=5):
    return pl.pallas_call(
        kernel,
        out_shape=outs,
        in_specs=in_specs,
        out_specs=jax.tree.map(lambda _: VMEM, outs),
        scratch_shapes=scratch,
        compiler_params=pltpu.CompilerParams(vmem_limit_bytes=mib * 1024 * 1024),
        cost_estimate=pl.CostEstimate(
            flops=int((cost or COSTS[name]) * FLOPS_PER_US), transcendentals=0, bytes_accessed=0
        ),
        name=name,
    )


def shape_of(shape, dtype):
    return jax.ShapeDtypeStruct(shape, dtype)


def dot(a, b):
    return lax.dot_general(a, b, (((1,), (0,)), ((), ())), preferred_element_type=f32)


def dot_nt(a, b):
    return lax.dot_general(a, b, (((1,), (1,)), ((), ())), preferred_element_type=f32)


def dot_tn(a, b):
    return lax.dot_general(a, b, (((0,), (0,)), ((), ())), preferred_element_type=f32)


def loop(count, body, unroll=1):
    def step(i, carry):
        body(i)
        return carry

    lax.fori_loop(0, count, step, 0, unroll=unroll)


def rows_at(i):
    return pl.ds(pl.multiple_of(i * SEG, SEG), SEG)


def lanes_at(p):
    return pl.ds(pl.multiple_of(p * LANES, LANES), LANES)


def head_masks(rows):
    lane = lax.broadcasted_iota(jnp.int32, (rows, LANES), 1)
    first = (lane < HD).astype(f32)
    return first.astype(bf16), (1.0 - first).astype(bf16)


def diagonal():
    row = lax.broadcasted_iota(jnp.int32, (LANES, LANES), 0)
    lane = lax.broadcasted_iota(jnp.int32, (LANES, LANES), 1)
    return (row < HD) == (lane < HD)


def head_ones():
    return jnp.where(diagonal(), 1.0, 0.0).astype(bf16)


def split_state(packed):
    same = diagonal()
    cos_part = jnp.where(same, packed, 0.0)
    sin_part = pltpu.roll(jnp.where(same, 0.0, packed), HD, 1)
    return cos_part.astype(bf16), sin_part.astype(bf16)


def state_scratch(fsdp):
    return [pltpu.VMEM((D, LANES), f32), pltpu.VMEM((8 * max(2 * PAIRS, fsdp), LANES), f32)]


def piece_shapes(fsdp, segs):
    return (shape_of((2, segs, D // fsdp + 8, LANES), bf16),) * (fsdp // 2)


def norm_row(n, fsdp):
    per = max(16, fsdp) // fsdp
    return 8 * (n // per) + n % per


def store_states(s, own, left_ref, right_ref, weight_ref, cos_ref, sin_ref, state_scr, norm_scr, out_refs):
    fsdp = 2 * len(out_refs)
    chunk = D // fsdp
    same = diagonal()
    rows = rows_at(s)
    cos, sin = cos_ref[rows, :], sin_ref[rows, :]

    def pair(p):
        lanes = lanes_at(p)
        a = left_ref[rows, lanes]
        b = right_ref[rows, lanes].astype(f32)
        both = jnp.concatenate(
            [(b * cos).astype(bf16), (pltpu.roll(b, HD, 1) * sin).astype(bf16)], axis=1
        )
        product = dot_tn(a, both)
        state_scr[lanes, :] = jnp.where(same, product[:, :LANES], product[:, LANES:])
        wide = a.astype(f32)
        if weight_ref is not None:
            wide = wide * weight_ref[rows, lanes]
        for n, wave in ((p, cos), (PAIRS + p, sin)):
            norm_scr[pl.ds(norm_row(n, fsdp), 1), :] = jnp.sum(wide * wave, axis=0, keepdims=True)

    loop(PAIRS, pair, 3)
    for r in range(fsdp):
        j = own ^ r
        at = pl.ds(pl.multiple_of(chunk * j, 8), chunk)
        norms = pl.ds(pl.multiple_of(8 * j, 8), 8)
        out_refs[r // 2][r % 2, s, 0:chunk, :] = state_scr[at, :].astype(bf16)
        out_refs[r // 2][r % 2, s, chunk : chunk + 8, :] = norm_scr[norms, :].astype(bf16)


def load_states(s, own, far_refs, near_ref, state_scr, norm_scr):
    fsdp = 2 * len(far_refs)
    chunk = D // fsdp
    for r in range(fsdp):
        j = own ^ r
        at = pl.ds(pl.multiple_of(chunk * j, 8), chunk)
        norms = pl.ds(pl.multiple_of(8 * j, 8), 8)
        ref, place = (near_ref, r // 2) if r % 2 else (far_refs[r // 2], 0)
        state_scr[at, :] = ref[place, s, 0:chunk, :].astype(f32)
        norm_scr[norms, :] = ref[place, s, chunk : chunk + 8, :].astype(f32)


def pair_state(p, state_scr, norm_scr, fsdp):
    cos_part, sin_part = split_state(state_scr[lanes_at(p), :])
    norm_cos = norm_scr[pl.ds(norm_row(p, fsdp), 1), :]
    norm_sin = norm_scr[pl.ds(norm_row(PAIRS + p, fsdp), 1), :]
    return cos_part, sin_part, norm_cos, norm_sin


def assemble(parts, lin):
    arrays = [blocks for part in parts for blocks, _ in part]
    places = jnp.concatenate(
        [jnp.array(masks, jnp.int32) for part in parts for _, masks in part]
    ) ^ lin.astype(jnp.int32)
    rows = arrays[0].shape[1]
    count = sum(len(masks) for _, masks in parts[0])
    width = sum(part[0][0].shape[2] for part in parts)
    lefts, left = [], 0
    for part in parts:
        lefts += [left] * len(part)
        left += part[0][0].shape[2]

    def kernel(places_ref, *refs):
        out_ref = refs[-1]
        first = 0
        for ref, at in zip(refs[:-1], lefts):
            number, _, columns = ref.shape

            def place(i, ref=ref, at=at, columns=columns, first=first):
                out_ref[places_ref[first + i], :, at : at + columns] = ref[i]

            loop(number, place)
            first += number

    whole = call(
        kernel, "assemble", shape_of((count, rows, width), bf16), [SMEM] + [VMEM] * len(arrays)
    )(places, *arrays)
    return whole.reshape(count * rows, width)


def project(ids, tokens, w_kv, cos, sin, fsdp):
    rows = tokens.shape[0]
    segs = rows // SEG

    def kernel(ids_ref, tok_ref, w_ref, cos_ref, sin_ref, k_ref, v_ref, *refs):
        inc_refs, (state_scr, norm_scr) = refs[:-2], refs[-2:]
        norm_scr[...] = jnp.zeros_like(norm_scr)

        def segment(s):
            at = rows_at(s)
            x = tok_ref[at, :]
            k_ref[at, :] = jnp.maximum(dot(x, w_ref[:, :D]), 0.0).astype(bf16)
            v_ref[at, :] = dot(x, w_ref[:, D:]).astype(bf16)
            store_states(s, ids_ref[2], k_ref, v_ref, None, cos_ref, sin_ref, state_scr, norm_scr,
                         inc_refs)

        loop(segs, segment)

    act = shape_of((rows, D), bf16)
    k, v, *pieces = call(
        kernel,
        "project",
        (act, act) + piece_shapes(fsdp, segs),
        [SMEM] + [VMEM] * 4,
        state_scratch(fsdp),
    )(ids, tokens, w_kv, cos, sin)
    return k, v, pieces


def mix_segments(spread, far, near):
    fsdp = 2 * len(far)
    _, segs, height, _ = near.shape

    def kernel(spread_ref, *refs):
        far_refs, near_ref, out_refs = refs[: fsdp // 2], refs[fsdp // 2], refs[fsdp // 2 + 1 :]
        for t in range(height // 8):
            at = slice(8 * t, 8 * t + 8)
            stacked = []
            for r in range(fsdp):
                ref, place = (near_ref, r // 2) if r % 2 else (far_refs[r // 2], 0)
                stacked += [ref[place, s, at, :].astype(f32) for s in range(segs)]
            mixed = dot(spread_ref[...], jnp.concatenate(stacked, axis=0).astype(bf16))
            for c in range(fsdp * segs):
                r, s = c // segs, c % segs
                out_refs[r // 2][r % 2, s, at, :] = mixed[8 * c : 8 * c + 8, :].astype(bf16)

    return call(
        kernel, "mix_segments", piece_shapes(fsdp, segs), [VMEM] * (fsdp // 2 + 2)
    )(spread, *far, near)


def intra_forward(tokens, w_q, k, v, wave):
    rows = tokens.shape[0]

    def kernel(tok_ref, w_ref, k_ref, v_ref, wave_ref, q_ref, num_ref, den_ref):
        masks = head_masks(SEG)

        def segment(s):
            at = rows_at(s)
            q_ref[at, :] = jnp.maximum(dot(tok_ref[at, :], w_ref[:, :D]), 0.0).astype(bf16)

            def pair(p):
                lanes = lanes_at(p)
                qs, ks, vs = q_ref[at, lanes], k_ref[at, lanes], v_ref[at, lanes]
                weights, values = [], []
                for m in masks:
                    weights.append((dot_nt(qs, ks * m) * wave_ref[...]).astype(bf16))
                    values.append(jnp.concatenate([vs * m, m], axis=1))
                both = dot(jnp.concatenate(weights, axis=1), jnp.concatenate(values, axis=0))
                num_ref[at, lanes] = both[:, :LANES]
                den_ref[at, lanes] = both[:, LANES:]

            loop(PAIRS, pair, 3)

        loop(rows // SEG, segment)

    wide = shape_of((rows, D), f32)
    return call(
        kernel, "intra_forward", (shape_of((rows, D), bf16), wide, wide), [VMEM] * 5
    )(tokens, w_q, k, v, wave)


def inter_forward(ids, q, num, den, cos, sin, far, near):
    rows = q.shape[0]
    fsdp = 2 * len(far)

    def kernel(ids_ref, q_ref, num_ref, den_ref, cos_ref, sin_ref, *refs):
        far_refs, near_ref = refs[: fsdp // 2], refs[fsdp // 2]
        att_ref, rden_ref, state_scr, norm_scr = refs[fsdp // 2 + 1 :]
        ones = head_ones()
        twice = jnp.concatenate([ones, ones], axis=0)

        def segment(s):
            at = rows_at(s)
            load_states(s, ids_ref[2], far_refs, near_ref, state_scr, norm_scr)

            def pair(p):
                lanes = lanes_at(p)
                cos_part, sin_part, norm_cos, norm_sin = pair_state(p, state_scr, norm_scr, fsdp)
                qs = q_ref[at, lanes].astype(f32)
                q_cos = (qs * cos_ref[at, :]).astype(bf16)
                q_sin = (qs * sin_ref[at, :]).astype(bf16)
                carried = dot(
                    jnp.concatenate([q_cos, q_sin], axis=1),
                    jnp.concatenate([cos_part, sin_part], axis=0),
                )
                along = q_cos.astype(f32) * norm_cos + q_sin.astype(f32) * norm_sin
                high = along.astype(bf16)
                rest = (along - high.astype(f32)).astype(bf16)
                weight = dot(jnp.concatenate([high, rest], axis=1), twice)
                inverse = 1.0 / (den_ref[at, lanes] + weight + 1.0)
                att_ref[at, lanes] = ((num_ref[at, lanes] + carried) * inverse).astype(bf16)
                rden_ref[at, lanes] = inverse

            loop(PAIRS, pair, 3)

        loop(rows // SEG, segment)

    return call(
        kernel,
        "inter_forward",
        (shape_of((rows, D), bf16), shape_of((rows, D), f32)),
        [SMEM] + [VMEM] * (6 + fsdp // 2),
        state_scratch(fsdp),
    )(ids, q, num, den, cos, sin, *far, near)


def standardize(resid):
    centred = resid - jnp.mean(resid, axis=1, keepdims=True)
    inv = lax.rsqrt(jnp.mean(centred * centred, axis=1, keepdims=True) + EPS)
    return centred * inv, inv


def standardize_back(d_hat, hat, inv):
    return inv * (
        d_hat
        - jnp.mean(d_hat, axis=1, keepdims=True)
        - hat * jnp.mean(d_hat * hat, axis=1, keepdims=True)
    )


def expand(att, tokens, w_out, w_up, small):
    rows = att.shape[0]
    ff = w_up.shape[1]

    def kernel(att_ref, tok_ref, out_w_ref, up_ref, small_ref, hat_ref, inv_ref, low_ref, gelu_ref,
               slope_ref):
        def block(i):
            at = rows_at(i)
            mixed = dot(att_ref[at, :], out_w_ref[:, OUT_AT : OUT_AT + D])
            hat, inv = standardize(
                tok_ref[at, :].astype(f32) + mixed + small_ref[B_OUT : B_OUT + 1, :]
            )
            hat_ref[at, :] = hat
            inv_ref[at, :] = jnp.broadcast_to(inv, (SEG, LANES))
            low_ref[at, :] = (
                hat * small_ref[GAIN1 : GAIN1 + 1, :] + small_ref[BIAS1 : BIAS1 + 1, :]
            ).astype(bf16)

            def part(m):
                for c in range(3):
                    columns = pl.ds(pl.multiple_of(m * D + 256 * c, 256), 256)
                    bias = small_ref[pl.ds(B_UP + m, 1), 256 * c : 256 * (c + 1)]
                    upper = dot(low_ref[at, :], up_ref[:, columns]) + bias
                    cdf = 0.5 + 0.5 * lax.erf(upper * math.sqrt(0.5))
                    pdf = jnp.exp(-0.5 * upper * upper) * (1.0 / math.sqrt(2.0 * math.pi))
                    gelu_ref[at, columns] = (upper * cdf).astype(bf16)
                    slope_ref[at, columns] = (cdf + upper * pdf).astype(bf16)

            loop(ff // D, part, 2)

        loop(rows // SEG, block)

    return call(
        kernel,
        "expand",
        (
            shape_of((rows, D), f32),
            shape_of((rows, LANES), f32),
            shape_of((rows, D), bf16),
            shape_of((rows, ff), bf16),
            shape_of((rows, ff), bf16),
        ),
        [VMEM] * 5,
    )(att, tokens, w_out, w_up, small)


def contract(ids, gelu, hat1, cotangent, w_down, small):
    rows, ff = gelu.shape

    def kernel(ids_ref, gelu_ref, hat1_ref, cot_ref, w_ref, small_ref,
               out_ref, dres_ref, dlow_ref, dlow_half_ref, sums_ref):
        sums_ref[...] = jnp.zeros_like(sums_ref)

        def block(i):
            at = rows_at(i)
            normed = hat1_ref[at, :] * small_ref[GAIN1 : GAIN1 + 1, :]
            normed += small_ref[BIAS1 : BIAS1 + 1, :]
            resid = normed + dot(gelu_ref[at, :], w_ref[...]) + small_ref[B_DOWN : B_DOWN + 1, :]
            hat, inv = standardize(resid)
            gain = small_ref[GAIN2 : GAIN2 + 1, :]
            out_ref[at, :] = (hat * gain + small_ref[BIAS2 : BIAS2 + 1, :]).astype(bf16)
            cot = cot_ref[at, :].astype(f32)
            sums_ref[GAIN2 : GAIN2 + 1, :] += jnp.sum(cot * hat, axis=0, keepdims=True)
            sums_ref[BIAS2 : BIAS2 + 1, :] += jnp.sum(cot, axis=0, keepdims=True)
            d_res = standardize_back(cot * gain, hat, inv)
            dres_ref[at, :] = d_res
            d_low = d_res.astype(bf16)
            dlow_ref[at, :] = d_low
            sums_ref[B_DOWN : B_DOWN + 1, :] += jnp.sum(d_low.astype(f32), axis=0, keepdims=True)
            theirs = 1 - ids_ref[0]
            dlow_half_ref[at, :] = dlow_ref[
                at, pl.ds(pl.multiple_of(theirs * (D // 2), 128), D // 2)
            ]

        loop(rows // SEG, block)

    return call(
        kernel,
        "contract",
        (
            shape_of((rows, D), bf16),
            shape_of((rows, D), f32),
            shape_of((rows, D), bf16),
            shape_of((rows, D // 2), bf16),
            shape_of((16, D), f32),
        ),
        [SMEM] + [VMEM] * 5,
    )(ids, gelu, hat1, cotangent, w_down, small)


def turn(ids, d_lower, slope, w_down, sums):
    rows, ff = slope.shape

    def kernel(ids_ref, dlow_ref, slope_ref, w_ref, sums_in_ref, dup_ref, dup_half_ref, sums_ref):
        sums_ref[...] = sums_in_ref[...]

        def block(i):
            at = rows_at(i)

            def part(m):
                for c in range(3):
                    columns = pl.ds(pl.multiple_of(m * D + 256 * c, 256), 256)
                    d_up = dot_nt(dlow_ref[at, :], w_ref[columns, :])
                    d_up = (d_up * slope_ref[at, columns].astype(f32)).astype(bf16)
                    dup_ref[at, columns] = d_up
                    sums_ref[pl.ds(B_UP + m, 1), 256 * c : 256 * (c + 1)] += jnp.sum(
                        d_up.astype(f32), axis=0, keepdims=True
                    )

            loop(ff // D, part, 2)
            theirs = 1 - ids_ref[0]
            dup_half_ref[at, :] = dup_ref[
                at, pl.ds(pl.multiple_of(theirs * (ff // 2), 128), ff // 2)
            ]

        loop(rows // SEG, block)

    return call(
        kernel,
        "turn",
        (
            shape_of((rows, ff), bf16), shape_of((rows, ff // 2), bf16), shape_of((16, D), f32),
        ),
        [SMEM] + [VMEM] * 4,
    )(ids, d_lower, slope, w_down, sums)


def back_to_heads(ids, d_upper, d_res2, hat1, inv1, rden, att, q, cos, sin, w_out, w_up, small,
                  sums, fsdp):
    rows, ff = d_upper.shape
    segs = rows // SEG

    def kernel(ids_ref, dup_ref, dres_ref, hat_ref, inv_ref, rden_ref, att_ref, q_ref, cos_ref,
               sin_ref, out_w_ref, up_ref, small_ref, sums_in_ref,
               dres1_ref, dmix_ref, dmix_half_ref, dnum_ref, dden_ref, sums_ref, *refs):
        inc_refs, (state_scr, norm_scr) = refs[:-2], refs[-2:]
        sums_ref[...] = sums_in_ref[...]
        share = D // fsdp
        for j in range(fsdp):
            for c in range(ff // D):
                at = (j * (ff // D) + c) * share
                m, lane = B_UP + at // D, at % D
                sums_ref[B_UP + c : B_UP + c + 1, share * j : share * (j + 1)] = sums_in_ref[
                    m : m + 1, lane : lane + share
                ]
        norm_scr[...] = jnp.zeros_like(norm_scr)
        ones = head_ones()
        twice = jnp.concatenate([ones, ones], axis=0)

        def block(i):
            at = rows_at(i)
            d_normed = dres_ref[at, :] + dot_nt(dup_ref[at, :], up_ref[...])
            hat = hat_ref[at, :]
            sums_ref[GAIN1 : GAIN1 + 1, :] += jnp.sum(d_normed * hat, axis=0, keepdims=True)
            sums_ref[BIAS1 : BIAS1 + 1, :] += jnp.sum(d_normed, axis=0, keepdims=True)
            d_res = standardize_back(
                d_normed * small_ref[GAIN1 : GAIN1 + 1, :], hat, inv_ref[at, 0:1]
            )
            dres1_ref[at, :] = d_res
            d_mix = d_res.astype(bf16)
            dmix_ref[at, :] = d_mix
            sums_ref[B_OUT : B_OUT + 1, :] += jnp.sum(d_mix.astype(f32), axis=0, keepdims=True)
            d_att = dot_nt(d_mix, out_w_ref[:, OUT_AT : OUT_AT + D])
            inverse = rden_ref[at, :]
            dnum_ref[at, :] = (d_att * inverse).astype(bf16)
            along = d_att * att_ref[at, :].astype(f32)
            for p in range(PAIRS):
                lanes = slice(LANES * p, LANES * (p + 1))
                high = along[:, lanes].astype(bf16)
                rest = (along[:, lanes] - high.astype(f32)).astype(bf16)
                total = dot(jnp.concatenate([high, rest], axis=1), twice)
                dden_ref[at, lanes] = -total * inverse[:, lanes]
            theirs = 1 - ids_ref[0]
            dmix_half_ref[at, :] = dmix_ref[
                at, pl.ds(pl.multiple_of(theirs * (D // 2), 128), D // 2)
            ]
            store_states(i, ids_ref[2], q_ref, dnum_ref, dden_ref, cos_ref, sin_ref, state_scr,
                         norm_scr, inc_refs)

        loop(segs, block)

    return call(
        kernel,
        "back_to_heads",
        (
            shape_of((rows, D), f32),
            shape_of((rows, D), bf16),
            shape_of((rows, D // 2), bf16),
            shape_of((rows, D), bf16),
            shape_of((rows, D), f32),
            shape_of((16, D), f32),
        )
        + piece_shapes(fsdp, segs),
        [SMEM] + [VMEM] * 13,
        state_scratch(fsdp),
    )(ids, d_upper, d_res2, hat1, inv1, rden, att, q, cos, sin, w_out, w_up, small, sums)


def intra_backward(ids, q, k, v, d_num, d_den, cos, sin, wave, wave_t, far, near):
    rows = q.shape[0]
    fsdp = 2 * len(far)

    def kernel(ids_ref, q_ref, k_ref, v_ref, dnum_ref, dden_ref, cos_ref, sin_ref, wave_ref,
               wave_t_ref, *refs):
        far_refs, near_ref = refs[: fsdp // 2], refs[fsdp // 2]
        dq_ref, dq_half_ref, dk_ref, dv_ref, state_scr, norm_scr = refs[fsdp // 2 + 1 :]
        masks = head_masks(SEG)
        lane = lax.broadcasted_iota(jnp.int32, (SEG, LANES), 1) % HD
        picks = [jnp.where(lane < 2, m.astype(f32), 0.0).astype(bf16) for m in masks]

        def segment(s):
            at = rows_at(s)
            load_states(s, ids_ref[2], far_refs, near_ref, state_scr, norm_scr)
            cosine, sine = cos_ref[at, :], sin_ref[at, :]

            def pair(p):
                lanes = lanes_at(p)
                qs, ks, vs = q_ref[at, lanes], k_ref[at, lanes], v_ref[at, lanes]
                dn, dd = dnum_ref[at, lanes], dden_ref[at, lanes]
                high = dd.astype(bf16).astype(f32)
                spread = jnp.where(lane == 0, high, jnp.where(lane == 1, dd - high, 0.0))
                grads = jnp.concatenate([dn, spread.astype(bf16)], axis=1)
                w_ts, d_ss, d_ts, khs, qhs, dns = [], [], [], [], [], []
                for m, pick in zip(masks, picks):
                    kh = ks * m
                    values = jnp.concatenate([vs * m, pick], axis=1)
                    w_ts.append((dot_nt(kh, qs) * wave_t_ref[...]).astype(bf16))
                    d_ss.append((dot_nt(grads, values) * wave_ref[...]).astype(bf16))
                    d_ts.append((dot_nt(values, grads) * wave_t_ref[...]).astype(bf16))
                    khs.append(kh)
                    qhs.append(qs * m)
                    dns.append(dn * m)

                def both(left, right):
                    return dot(jnp.concatenate(left, axis=1), jnp.concatenate(right, axis=0))

                dk_ref[at, lanes] = both(d_ts, qhs)
                dv_ref[at, lanes] = both(w_ts, dns)
                d_q = both(d_ss, khs)
                cos_part, sin_part, norm_cos, norm_sin = pair_state(p, state_scr, norm_scr, fsdp)
                d_q += cosine * (dot_nt(dn, cos_part) + dd * norm_cos)
                d_q += sine * (dot_nt(dn, sin_part) + dd * norm_sin)
                dq_ref[at, lanes] = jnp.where(qs.astype(f32) > 0.0, d_q, 0.0).astype(bf16)

            loop(PAIRS, pair, 3)
            theirs = 1 - ids_ref[0]
            dq_half_ref[at, :] = dq_ref[at, pl.ds(pl.multiple_of(theirs * (D // 2), 128), D // 2)]

        loop(rows // SEG, segment)

    return call(
        kernel,
        "intra_backward",
        (
            shape_of((rows, D), bf16),
            shape_of((rows, D // 2), bf16),
            shape_of((rows, D), f32),
            shape_of((rows, D), f32),
        ),
        [SMEM] + [VMEM] * (10 + fsdp // 2),
        state_scratch(fsdp),
    )(ids, q, k, v, d_num, d_den, cos, sin, wave, wave_t, *far, near)


def inter_backward(ids, k, v, d_k, d_v, cos, sin, far, near):
    rows = k.shape[0]
    fsdp = 2 * len(far)

    def kernel(ids_ref, k_ref, v_ref, dk_ref, dv_ref, cos_ref, sin_ref, *refs):
        far_refs, near_ref = refs[: fsdp // 2], refs[fsdp // 2]
        out_ref, state_scr, norm_scr = refs[fsdp // 2 + 1 :]
        core = ids_ref[0]

        def segment(s):
            at = rows_at(s)
            load_states(s, ids_ref[2], far_refs, near_ref, state_scr, norm_scr)
            cosine, sine = cos_ref[at, :], sin_ref[at, :]

            def pair(p):
                lanes = lanes_at(p)
                cos_part, sin_part, norm_cos, norm_sin = pair_state(p, state_scr, norm_scr, fsdp)
                ks = k_ref[at, lanes].astype(f32)
                vs = v_ref[at, lanes]
                d_k = dk_ref[at, lanes]
                d_k += cosine * (dot_nt(vs, cos_part) + norm_cos)
                d_k += sine * (dot_nt(vs, sin_part) + norm_sin)
                feats = jnp.concatenate(
                    [(ks * cosine).astype(bf16), (ks * sine).astype(bf16)], axis=1
                )
                d_v = dv_ref[at, lanes]
                d_v += dot(feats, jnp.concatenate([cos_part, sin_part], axis=0))
                out_ref[core, at, lanes] = jnp.where(ks > 0.0, d_k, 0.0).astype(bf16)
                out_ref[1 - core, at, lanes] = d_v.astype(bf16)

            loop(PAIRS, pair, 3)

        loop(rows // SEG, segment)

    return call(
        kernel,
        "inter_backward",
        shape_of((2, rows, D), bf16),
        [SMEM] + [VMEM] * (7 + fsdp // 2),
        state_scratch(fsdp),
    )(ids, k, v, d_k, d_v, cos, sin, *far, near)


def input_grad(ids, d_q, d_kv, d_res1, w_q, w_kv):
    rows = d_q.shape[0]

    def kernel(ids_ref, dq_ref, dkv_ref, dres_ref, w_q_ref, w_kv_ref, out_ref):
        core = ids_ref[0]

        def block(i):
            at = rows_at(i)
            total = dres_ref[at, :] + dot_nt(dq_ref[at, :], w_q_ref[:, :D])
            total += dot_nt(dkv_ref[core, at, :], w_kv_ref[:, :D])
            total += dot_nt(dkv_ref[1 - core, at, :], w_kv_ref[:, D:])
            out_ref[at, :] = total

        loop(rows // SEG, block)

    return call(
        kernel, "input_grad", shape_of((rows, D), f32), [SMEM] + [VMEM] * 5
    )(ids, d_q, d_kv, d_res1, w_q, w_kv)


def reversed_bits(index, bits):
    total = 0
    for b in range(bits):
        total = total + (((index >> b) & 1) << (bits - 1 - b))
    return total


def weight_grad(ids, products, fsdp, splits, key, own_half=True, sums=None):
    height = products[0][0].shape[1]
    widths = [product[3].shape[1] for product in products]
    block = height // fsdp
    bits = fsdp.bit_length() - 1
    share = block // len(splits)
    group = min(4, fsdp) * block if block % 128 == 0 else height
    extra = [] if sums is None else [sums]

    def kernel(ids_ref, *refs):
        ins, out_refs = refs[: 4 * len(products)], refs[4 * len(products) + len(extra) :]

        def part(i):
            columns = pl.ds(pl.multiple_of(i * group, 128), group)

            def store(total, left):
                right = left + total.shape[1]
                for j in range(group // block):
                    place = reversed_bits((i * (group // block) + j) ^ ids_ref[2], bits)
                    for n, (split, out_ref) in enumerate(zip(splits, out_refs)):
                        strip = share // split
                        for h in range(split):
                            row = block * j + share * n + strip * h
                            half = h ^ ids_ref[1] if split > 1 else 0
                            out_ref[half, place, :, left:right] = total[
                                row : row + strip, :
                            ].astype(bf16)

            left = 0
            for n, width in enumerate(widths):
                a0_ref, a1_ref, b0_ref, b1_ref = ins[4 * n : 4 * n + 4]
                first = pl.multiple_of(ids_ref[0] * width, 128) if own_half else 0
                total = dot_tn(a0_ref[:, columns], b0_ref[:, pl.ds(first, width)])
                store(total + dot_tn(a1_ref[:, columns], b1_ref[...]), left)
                left += width
            if extra:
                tall = jnp.concatenate(
                    [refs[4 * len(products)][...], jnp.zeros((LANES - 16, height), f32)], axis=0
                )
                store(tall.T, left)

        loop(height // group, part)

    width = sum(widths) + LANES * len(extra)
    return call(
        kernel,
        "weight_grad",
        tuple(shape_of((n, fsdp, share // n, width), bf16) for n in splits),
        [SMEM] + [VMEM] * (4 * len(products) + len(extra)),
        cost=COSTS[key],
    )(ids, *(x for product in products for x in product), *extra)


def add_low(a, b):
    return (a.astype(f32) + b.astype(f32)).astype(bf16)


def core_stage(x):
    (other,) = yield [(x, "group", 0)]
    return other


def halving_stages(keep, send, bits):
    for axis, bit in bits:
        (received,) = yield [(send, axis, bit)]
        half = keep.shape[0] // 2
        if half == 0:
            return add_low(keep[0], received[0])
        keep, send = add_low(keep[:half], received[:half]), add_low(keep[half:], received[half:])


def reduce_stages(x, core):
    half = x.shape[1] // 2
    bits = axis_bits("fsdp")
    keep, send = x[0, :half], x[0, half:]
    x = yield from halving_stages(keep, send, bits)
    for axis, bit in axis_bits("group")[1:]:
        (received,) = yield [(x, axis, bit)]
        x = add_low(x, received)
    other = yield from core_stage(x)
    return ordered(x, other, core == 0, -1).astype(f32)


def share_stages(x, core, chip, twice=False):
    axis, bit = axis_bits("group")[1]
    half = x.shape[1] // 2
    if twice:
        (received,) = yield [(x[1, half:], axis, bit)]
        rest, send = lax.optimization_barrier((x[1, :half], add_low(x[0, half:], received)))
        (received,) = yield [(rest, axis, bit)]
        send, keep = lax.optimization_barrier((send, add_low(x[0, :half], received)))
    else:
        (received,) = yield [(x[1], axis, bit)]
        keep, send = add_low(x[0, :half], received[:half]), add_low(x[0, half:], received[half:])
    x = yield from halving_stages(keep, send, axis_bits("fsdp"))
    (other,) = yield [(x, axis, bit)]
    x = ordered(x, other, chip == 0, 0)
    other = yield from core_stage(x)
    return ordered(x, other, core == 0, -1).astype(f32)


def large_stages(x, core, chip):
    (axis, bit), *bits = axis_bits("fsdp")
    group_axis, group_bit = axis_bits("group")[1]
    half = x.shape[1] // 2
    first = half // 4
    keep, send = x[:, :half], x[:, half:]
    (received,) = yield [(send[:, first:], axis, bit)]
    later = add_low(keep[:, first:], received)
    rest, later = lax.optimization_barrier((send[:, :first], later))
    (received,) = yield [(rest, axis, bit)]
    head = add_low(keep[:, :first], received)
    theirs = jnp.concatenate([head[1], later[1]], axis=0)
    (received,) = yield [(theirs, group_axis, group_bit)]
    head, later = head[0], later[0]
    quarter = half // 2
    ours = jnp.concatenate([head, later[: quarter - first]], axis=0)
    keep = add_low(ours, received[:quarter])
    send = add_low(later[quarter - first :], received[quarter:])
    x = yield from halving_stages(keep, send, bits)
    (other,) = yield [(x, group_axis, group_bit)]
    x = ordered(x, other, chip == 0, 0)
    other = yield from core_stage(x)
    return ordered(x, other, core == 0, -1).astype(f32)


def ordered(x, other, first, axis):
    return jnp.concatenate([jnp.where(first, x, other), jnp.where(first, other, x)], axis=axis)


def ancestor_matrix(parents):
    count = parents.shape[0]
    columns = jnp.arange(count, dtype=jnp.int32)
    step = (parents[:, None] == columns[None, :]).astype(f32)
    same = (columns[:, None] == columns[None, :]).astype(f32)
    reached = step + same
    for _ in range(4):
        reached = (jnp.dot(reached, reached, preferred_element_type=f32) > 0.0).astype(f32)
    return reached - same


def spread_rows(matrix):
    count = matrix.shape[0]
    row = jnp.arange(8 * count, dtype=jnp.int32)
    pick = (row[:, None] // 8 == jnp.arange(count, dtype=jnp.int32)[None, :]).astype(f32)
    wide = jnp.dot(jnp.dot(pick, matrix), pick.T)
    return jnp.where(row[:, None] % 8 == row[None, :] % 8, wide, 0.0).astype(bf16)


def waves(local, segs):
    depth = jnp.sum(local[:segs], axis=1)
    angle = (depth[:, None] * SEG + jnp.arange(SEG, dtype=f32)[None, :]) * (
        math.pi / (2.0 * HORIZON)
    )
    angle = jnp.broadcast_to(angle.reshape(segs * SEG, 1), (segs * SEG, LANES))
    return jnp.cos(angle), jnp.sin(angle)


def gap_wave(position):
    gap = position[:, None] - position[None, :]
    wave = jnp.cos(gap.astype(f32) * (math.pi / (2.0 * HORIZON)))
    return jnp.where(gap >= 0, wave, 0.0), jnp.where(gap <= 0, wave, 0.0)


def vector_columns(vectors):
    return jnp.pad(jnp.stack(vectors), ((0, LANES - len(vectors)), (0, 0))).T


def wide_row(shard, rows):
    return jnp.pad(shard[None], ((0, rows - 1), (0, LANES - shard.shape[0])))


def vector_rows(weight, rows, share, longer):
    per = D // share

    def kernel(w_ref, out_ref):
        out_ref[...] = jnp.zeros_like(out_ref)
        turned = w_ref[:, D:OUT_AT].astype(f32).T
        out_ref[:B_UP, :] = turned[:B_UP, :]
        for block in range(longer * per):
            m, lane = B_UP + block // per, share * (block % per)
            first = rows * block // 8 * 8
            tile = w_ref[first : first + 8, OUT_AT + D :].astype(f32)
            row = rows * block - first
            out_ref[m : m + 1, lane : lane + share] = tile[row : row + 1, :share]

    return call(kernel, "vector_rows", shape_of((16, D), f32), [VMEM])(weight)


def body(
    tokens, cotangent, parent_seg, w_qkv, w_out, b_out, norm1_gain, norm1_bias, w_up, b_up,
    w_down, b_down, norm2_gain, norm2_bias,
):
    fsdp = lax.axis_size("fsdp")
    chips = lax.axis_size("group") // 2
    own = lax.axis_index("fsdp")
    group = lax.axis_index("group")
    core, chip = group % 2, group // 2
    rows = tokens.shape[0]
    segs = rows // SEG
    ff = w_up.shape[1]
    ids = jnp.stack([core, chip, own]).astype(jnp.int32)

    pipe = Pipeline()
    pipe.add("kv", gather_stages(w_qkv[:, D:]))
    pipe.add("tokens", core_stage(tokens))
    pipe.slot()
    pipe.slot(only=("kv",))
    begun = pipe.started[0]
    tokens_other = pipe.read("tokens", begun)

    ancestry = ancestor_matrix(tie(parent_seg[0], begun))
    count = parent_seg.shape[1]
    place = jnp.arange(count, dtype=jnp.int32)
    there = (own ^ (place // segs)) * segs + place % segs
    select = (there[:, None] == place[None, :]).astype(f32)
    local = jnp.dot(jnp.dot(select, ancestry), select.T)
    from_ancestors, from_descendants = spread_rows(local), spread_rows(local.T)
    cos, sin = waves(local, segs)
    wave, wave_t = gap_wave(tie(jnp.arange(SEG, dtype=jnp.int32), begun))
    shard_rows = w_qkv.shape[0]
    columns = vector_columns((b_out, norm1_gain, norm1_bias, b_down, norm2_gain, norm2_bias))
    pipe.add("qo", gather_stages(tie(
        jnp.concatenate([w_qkv[:, :D], columns, w_out, wide_row(b_up, shard_rows)], axis=1), begun
    )))
    pipe.add("up", gather_stages(w_up))
    pipe.add("down", gather_stages(w_down))
    pipe.slot(only=("kv",))
    pipe.slot(*pipe.started, only=("qo",))
    pipe.slot(only=("kv",))
    pipe.slot(*pipe.started, only=("qo",))
    pipe.slot(*pipe.started, only=("up",))
    pipe.slot(only=("kv", "qo"))
    pipe.slot(*pipe.started, only=("up",))
    w_kv = assemble(*pipe.finish("kv", only=("kv",)))
    tables = (from_ancestors, from_descendants, wave, wave_t)
    k, v, increments = project(
        ids, tie(tokens, tokens_other, *tables, *pipe.started), w_kv, cos, sin, fsdp
    )
    pipe.arrive(k, only=("qo",))
    pipe.add("state", trade_stages(increments))
    pipe.slot(*pipe.started, only=("state", "qo"))
    pipe.slot(only=("state", "qo"))
    pipe.slot(*pipe.started, only=("up",))
    w_qo = assemble(*pipe.finish("qo", only=("qo",)))
    pipe.slot(w_qo, only=("down",))
    q, num, den = intra_forward(tie(tokens, *pipe.started), w_qo, k, v, wave)
    far, near = pipe.finish("state", q, only=("state",))
    mixed = mix_segments(from_ancestors, far, near)
    pipe.arrive(q, only=("up", "down"))
    pipe.add("path", trade_stages(mixed))
    pipe.slot(*pipe.started, only=("path", "up"))
    small = vector_rows(tie(w_qo, *pipe.started), shard_rows, b_up.shape[0], ff // D)
    pipe.slot(small, only=("path", "down"))
    pipe.slot(*pipe.started, only=("up",))
    w_up_full = assemble(*pipe.finish("up", only=("up",)))
    path = pipe.finish("path", w_up_full, only=("path",))
    pipe.slot(path[1], only=("down",))
    att, rden = inter_forward(ids, tie(q, *pipe.started), num, den, cos, sin, *path)
    pipe.add("att", core_stage(att))
    pipe.slot(only=("att",))
    pipe.slot(att, only=("down",))
    att_other = pipe.read("att", *pipe.started)
    hat1, inv1, low1, gelu, slope = expand(
        tie(att, att_other, *pipe.started), tokens, w_qo, w_up_full, small
    )
    pipe.slot(low1, only=("down",))
    w_down_full = assemble(*pipe.finish("down", only=("down",)))
    pipe.add("gelu", core_stage(gelu))
    pipe.add("low1", core_stage(low1))
    pipe.slot(w_down_full, only=("gelu", "low1"))
    output, d_res2, d_lower, d_lower_half, sums = contract(
        ids, gelu, hat1, cotangent, w_down_full, small
    )
    low1_other = pipe.read("low1", d_lower)
    gelu_other = pipe.read("gelu", d_lower)
    grads = Pipeline()
    grads.add("d_lower", core_stage(d_lower_half))
    grads.slot(low1_other, gelu_other)
    d_upper, d_upper_half, sums = turn(
        ids, tie(d_lower, *grads.started), slope, w_down_full, sums
    )
    d_lower_other = grads.read("d_lower", d_upper)
    grads.add("d_upper", core_stage(d_upper_half))
    grads.slot(d_lower_other, only=("d_upper",))
    two = chips == 2

    def reduction(part, twice=False):
        return share_stages(part, core, chip, twice) if two else reduce_stages(part, core)

    split = 2 if two else 1
    (down_part,) = weight_grad(
        ids, [(gelu, gelu_other, tie(d_lower, *grads.started), d_lower_other)], fsdp, [split],
        "down",
    )
    d_upper_other = grads.read("d_upper", down_part)
    grads.add("down", reduction(down_part, True))
    grads.slot(d_upper_other, only=("down",))
    (up_part,) = weight_grad(
        ids, [(low1, low1_other, tie(d_upper, *grads.started), d_upper_other)], fsdp, [split], "up",
    )
    large = two and fsdp >= 8
    grads.add("up", large_stages(up_part, core, chip) if large else reduction(up_part))
    grads.slot(only=("up",))
    d_res1, d_mixed, d_mixed_half, d_num, d_den, sums, *back = back_to_heads(
        ids, tie(d_upper, *grads.started), d_res2, hat1, inv1, rden, att, q, cos, sin, w_qo,
        w_up_full, small, sums, fsdp,
    )
    grads.add("state", trade_stages(back))
    grads.slot(only=("state",))
    if two:
        grads.slot(d_num, only=("down",))
    grads.slot(*grads.started, d_num, only=("state",))
    grads.add("d_mixed", core_stage(d_mixed_half))
    grads.slot(*grads.started, only=("d_mixed",))
    grads.slot(*grads.started, only=("up",))
    grads.slot(*grads.started, only=("down",))
    d_mixed_other = grads.read("d_mixed", *grads.started)
    far, near = grads.finish("state", d_mixed_other, only=("state",))
    mixed = mix_segments(from_descendants, far, near)
    grads.add("path", trade_stages(mixed))
    grads.slot(only=("path",))
    grads.slot(*grads.started, only=("up",))
    d_q, d_q_half, d_k, d_v = intra_backward(
        ids, tie(q, *grads.started), k, v, d_num, d_den, cos, sin, wave, wave_t, *path
    )
    grads.add("d_q", core_stage(d_q_half))
    grads.slot(d_q, only=("path", "d_q"))
    grads.arrive(*grads.started, only=("up", "down"))
    d_q_other = grads.read("d_q", *grads.started)
    (outq_part,) = weight_grad(
        ids,
        [
            (att, att_other, d_mixed, d_mixed_other),
            (tokens, tokens_other, d_q, d_q_other),
        ],
        fsdp, [split], "outq", sums=sums,
    )
    grads.add("outq", reduction(outq_part))
    grads.slot(only=("outq",))
    grads.slot(*grads.started, only=("up",))
    back = grads.finish("path", *grads.started, only=("path",))
    d_kv = inter_backward(ids, k, v, d_k, d_v, cos, sin, *back)
    grads.add("d_kv", core_stage(d_kv[1]))
    grads.arrive(d_kv, only=("up",))
    grads.slot(*grads.started, only=("d_kv",))
    grads.slot(*grads.started, only=("up",))
    grads.slot(*grads.started, only=("down",))
    d_kv_other = grads.read("d_kv", *grads.started)
    kv_parts = weight_grad(
        ids, [(tokens, tokens_other, d_kv[0], d_kv_other)], fsdp, [2, 1] if two else [1], "kv",
        False,
    )
    grads.add("kv0", reduction(kv_parts[0]))
    for part in kv_parts[1:]:
        grads.add("kv1", reduce_stages(part, core))
    half = D // 2
    closed = ()

    def close(outq):
        ours, others = jnp.split(outq, 2, axis=1)
        sums = ours[:, D : D + 16] + others[:, D : D + 16]
        q_grad = jnp.concatenate([ours[:, half:D], others[:, half:D]], axis=1)
        out_grad = jnp.concatenate([ours[:, :half], others[:, :half]], axis=1)
        return q_grad, out_grad, sums.T, sums[:, B_UP : B_UP + ff // D].T.reshape(-1)

    written = set()

    def write():
        nonlocal closed
        if not closed and "outq" in grads.finished:
            closed = close(grads.finished["outq"])
            grads.started += closed
        for n in ("up", "down"):
            if n in grads.finished and n not in written:
                written.add(n)
                grads.started += (grads.finished[n],)

    for step in TAIL:
        if step == "grad":
            tokens_grad = input_grad(ids, d_q, tie(d_kv, *grads.started), d_res1, w_qo, w_kv)
            grads.started = (tokens_grad,)
        elif grads.names(step.split("+")):
            grads.slot(*grads.started, only=step.split("+"))
            write()
    while grads.running:
        grads.slot(*grads.started)
        write()
    done = grads.finished
    q_grad, out_grad, sums, b_up_grad = closed or close(done["outq"])
    kv_grad = jnp.concatenate([done[n] for n in ("kv0", "kv1") if n in done], axis=0)
    return (
        output,
        tokens_grad,
        jnp.concatenate([q_grad, kv_grad], axis=1),
        out_grad,
        sums[B_OUT],
        sums[GAIN1],
        sums[BIAS1],
        done["up"],
        b_up_grad,
        done["down"],
        sums[B_DOWN],
        sums[GAIN2],
        sums[BIAS2],
    )


def solution(mesh):
    both = ("group", "fsdp")
    matrix, vector = P(both, None), P(both)
    in_specs = (
        matrix, matrix, P("group", None), matrix, matrix, vector, vector, vector, matrix, vector,
        matrix, vector, vector, vector,
    )
    rows, line = P("fsdp", None), P("fsdp")
    out_specs = (
        matrix, matrix, rows, rows, line, line, line, rows, line, rows, line, line, line,
    )
    return jax.shard_map(body, mesh=mesh, in_specs=in_specs, out_specs=out_specs, check_vma=False)
```
